32 devices in a mesh: dp: 4 (over y, x), mp: 8 (over z, core).
Axes of the slice: x: 2, y: 2, z: 4, core: 2. Of those that a mesh axis runs over, the one named last changes fastest.
Arguments:
- tokens: bfloat16 [4096, 2048], P(('dp', 'mp')), may hold values from -9 to 9
- seg_ids: int32 [4096], P('dp'), may hold values from 0 to 12, as said below
- positions: int32 [4096], P('dp'), may hold values from 0 to 1023, as said below
- w_query: bfloat16 [2048, 2048], P(None, 'mp'), may hold values from -0.125 to 0.125
- w_key: bfloat16 [2048, 512], replicated, may hold values from -0.125 to 0.125
- w_value: bfloat16 [2048, 512], replicated, may hold values from -0.125 to 0.125
- w_output: bfloat16 [2048, 2048], P('mp'), may hold values from -0.75 to 0.75
- w_gate: bfloat16 [2048, 8192], P(None, 'mp'), may hold values from -0.125 to 0.125
- w_up: bfloat16 [2048, 8192], P(None, 'mp'), may hold values from -0.125 to 0.125
- w_down: bfloat16 [8192, 2048], P('mp'), may hold values from -0.0625 to 0.0625
- attn_gain: float32 [2048], replicated, may hold values from 0.5 to 1.5
- ffn_gain: float32 [2048], replicated, may hold values from 0.5 to 1.5
- query_gain: float32 [64], replicated, may hold values from 0.1 to 1.9
- key_gain: float32 [64], replicated, may hold values from 0.1 to 1.9
- out_grad: bfloat16 [4096, 2048], P(('dp', 'mp')), may hold values from -6 to 6
Outputs:
- output: bfloat16 [4096, 2048], P(('dp', 'mp'))
- grad_tokens: bfloat16 [4096, 2048], P(('dp', 'mp'))
- grad_w_query: float32 [2048, 2048], P(None, 'mp')
- grad_w_key: float32 [2048, 512], replicated
- grad_w_value: float32 [2048, 512], replicated
- grad_w_output: float32 [2048, 2048], P('mp')
- grad_w_gate: float32 [2048, 8192], P(None, 'mp')
- grad_w_up: float32 [2048, 8192], P(None, 'mp')
- grad_w_down: float32 [8192, 2048], P('mp')
- grad_attn_gain: float32 [2048], replicated
- grad_ffn_gain: float32 [2048], replicated
- grad_query_gain: float32 [64], replicated
- grad_key_gain: float32 [64], replicated
- residual_rms: float32 [1], replicated
- branch_rms: float32 [2, 4096], P(None, ('dp', 'mp'))
The draws below stay inside these ranges and needn't reach their ends.
Inputs may be any that keep to these rules, and one draw needn't show every extreme that they name: `seg_ids`: never falling along the tokens; the first token of every block of 1024 consecutive tokens starts a new segment; the first block is one segment, every other block holds exactly 4. `positions`: 0 at the first token of a segment, one more at each following token of it.
All inputs are finite; a program needn't handle non-finite values.
Results may differ from the reference program's by a relative error of at most 0.015.
Values may be sent and summed in bfloat16 or wider, within the bound.
A program may use at most 256 MiB of HBM per device.

```python
import jax
import jax.numpy as jnp
from jax import lax

D = 2048
HEADS = 32
KV = 8
HD = 64
FF = 8192
ROW = 1024
TOKENS = 4096
N_DP = 4


def segment_layout(key):
    layout_key = jax.random.fold_in(key, 11)
    row_keys = jax.random.split(layout_key, N_DP)

    def pick_cuts(row_key):
        return (jax.random.permutation(row_key, ROW - 1)[:3] + 1).astype(jnp.int32)
    cuts = jax.vmap(pick_cuts)(row_keys)
    local = jnp.arange(ROW, dtype=jnp.int32)
    row_number = jnp.arange(N_DP, dtype=jnp.int32)
    inner = jnp.any(local[None, :, None] == cuts[:, None, :], -1) & (row_number > 0)[:, None]
    starts = (inner | (local == 0)[None, :]).reshape(TOKENS)
    token_index = jnp.arange(TOKENS, dtype=jnp.int32)
    segment_ids = jnp.cumsum(starts.astype(jnp.int32)) - 1
    segment_start = lax.cummax(jnp.where(starts, token_index, 0), axis=0)
    return (segment_ids.astype(jnp.int32), (token_index - segment_start).astype(jnp.int32))


def draw_seg_ids(key, part):
    return segment_layout(key)[0]


def draw_positions(key, part):
    return segment_layout(key)[1]


def draw_tokens(key, part):
    place = jnp.arange(TOKENS, dtype=jnp.float32) / TOKENS
    noise = jnp.clip(jax.random.normal(key, (TOKENS, D), jnp.float32), -6.0, 6.0)
    row_scale = 0.5 * 3.0 ** place
    return (noise * row_scale[:, None]).astype(jnp.bfloat16)


def levels(own_key, shape, cuts, least, largest):
    level = 1.0
    for dim, parts in cuts:
        draws = jax.random.uniform(jax.random.fold_in(jax.random.fold_in(own_key, 6), dim), (parts,), jnp.float32, least / len(cuts), largest / len(cuts))
        level = level * jnp.repeat(jnp.exp(draws), shape[dim] // parts).reshape((-1,) + (1,) * (len(shape) - 1 - dim))
    return level


def gaussian(key, shape, deviation, limit, cuts=(), held_as=jnp.bfloat16):
    values = deviation * jax.random.normal(key, shape, jnp.float32)
    if cuts:
        values = values * levels(key, shape, cuts, -0.22, 0.18)
    return jnp.clip(values, -limit, limit).astype(held_as)


def setup_inputs(seed: int = 0) -> dict:
    keys = jax.random.split(jax.random.key(seed), 16)
    return {
        "tokens": draw_tokens(jax.random.fold_in(keys[15], 71), 0),
        "seg_ids": draw_seg_ids(jax.random.fold_in(keys[15], 71), 0),
        "positions": draw_positions(jax.random.fold_in(keys[15], 71), 0),
        "w_query": gaussian(keys[3], (D, HEADS * HD), D ** -0.5, 0.125, ((1, 8),)),
        "w_key": gaussian(keys[4], (D, KV * HD), D ** -0.5, 0.125),
        "w_value": gaussian(keys[5], (D, KV * HD), D ** -0.5, 0.125),
        "w_output": gaussian(keys[6], (HEADS * HD, D), (HEADS * HD // 32) ** -0.5, 0.75, ((0, 8),)),
        "w_gate": gaussian(keys[7], (D, FF), D ** -0.5, 0.125, ((1, 8),)),
        "w_up": gaussian(keys[8], (D, FF), D ** -0.5, 0.125, ((1, 8),)),
        "w_down": gaussian(keys[9], (FF, D), FF ** -0.5, 0.0625, ((0, 8),)),
        "attn_gain": jnp.clip(1.0 + 0.1 * jax.random.normal(keys[10], (D,), jnp.float32), 0.5, 1.5),
        "ffn_gain": jnp.clip(1.0 + 0.1 * jax.random.normal(keys[11], (D,), jnp.float32), 0.5, 1.5),
        "query_gain": jnp.clip(1.0 + 0.18 * jax.random.normal(keys[12], (HD,), jnp.float32), 0.1, 1.9),
        "key_gain": jnp.clip(1.0 + 0.18 * jax.random.normal(keys[13], (HD,), jnp.float32), 0.1, 1.9),
        "out_grad": gaussian(keys[14], (TOKENS, D), 1.0, 6.0, ((0, 32),)),
    }


@jax.custom_vjp
def low(v):
    return lax.optimization_barrier(v.astype(jnp.bfloat16)).astype(jnp.float32)

@jax.custom_vjp
def low_back(v):
    return v

def low_keep(v):
    return (low(v), None)

def low_pass(kept, grad):
    return (grad,)

def back_keep(v):
    return (v, None)

def back_low(kept, grad):
    return (low(grad),)
low.defvjp(low_keep, low_pass)
low_back.defvjp(back_keep, back_low)
HIGHEST_PRECISION = lax.Precision.HIGHEST
EPSILON = 1e-06
ROPE_BASE = 10000.0
MASKED = -1e+30

def product(left, right):
    return jnp.dot(left, right, precision=HIGHEST_PRECISION, preferred_element_type=jnp.float32)

def unit_rms(values):
    return values * lax.rsqrt(lax.optimization_barrier(jnp.mean(values * values, -1, keepdims=True)) + EPSILON)

def rope_tables(position_row):
    half = HD // 2
    freq = ROPE_BASE ** (-jnp.arange(half, dtype=jnp.float32) / half)
    angle = position_row.astype(jnp.float32)[:, None] * freq[None, :]
    return (jnp.cos(angle)[:, None, :], jnp.sin(angle)[:, None, :])

def rotate(values, cosine, sine):
    half = HD // 2
    first_half = values[..., :half]
    second_half = values[..., half:]
    return jnp.concatenate([first_half * cosine - second_half * sine, second_half * cosine + first_half * sine], -1)

def layer_row(params, tokens_row, segment_row, position_row):
    w_query, w_key, w_value, w_output, w_gate, w_up, w_down, attn_gain, ffn_gain, query_gain, key_gain = params
    h_one = low(unit_rms(tokens_row) * attn_gain)
    query = low_back(product(h_one, w_query)).reshape(ROW, HEADS, HD)
    key = low_back(product(h_one, w_key)).reshape(ROW, KV, HD)
    value = low(low_back(product(h_one, w_value))).reshape(ROW, KV, HD)
    cosine, sine = rope_tables(position_row)
    query_rot = low(rotate(unit_rms(query) * query_gain, cosine, sine))
    key_rot = low(rotate(unit_rms(key) * key_gain, cosine, sine))
    group_size = HEADS // KV
    key_wide = jnp.repeat(key_rot, group_size, axis=1)
    value_wide = jnp.repeat(value, group_size, axis=1)
    block = min(512, ROW)
    block_count = ROW // block
    token_index = jnp.arange(ROW).astype(jnp.int32)

    def attend(inputs):
        query_block, start = inputs
        scores = jnp.einsum('qhd,khd->hqk', query_block, key_wide, precision=HIGHEST_PRECISION) * HD ** (-0.5)
        scores = low_back(scores)
        segment_block = lax.dynamic_slice_in_dim(segment_row, start, block)
        index_block = start + jnp.arange(block).astype(jnp.int32)
        allowed = (segment_block[:, None] == segment_row[None, :]) & (token_index[None, :] <= index_block[:, None])
        scores = jnp.where(allowed[None], scores, MASKED)
        weights = low(jax.nn.softmax(scores, axis=-1))
        return jnp.einsum('hqk,khd->qhd', weights, value_wide, precision=HIGHEST_PRECISION)
    starts = (jnp.arange(block_count) * block).astype(jnp.int32)
    context = lax.map(jax.checkpoint(attend), (query_rot.reshape(block_count, block, HEADS, HD), starts))
    context = low(low_back(context.reshape(ROW, HEADS * HD)))
    attn_branch = low_back(product(context, w_output))
    residual_mid = tokens_row + attn_branch
    h_two = low(unit_rms(residual_mid) * ffn_gain)
    gate = low_back(product(h_two, w_gate))
    up = low_back(product(h_two, w_up))
    hidden = low(jax.nn.silu(gate) * up)
    ffn_branch = low_back(product(hidden, w_down))
    return (residual_mid + ffn_branch, attn_branch, ffn_branch)

def reference(tokens, seg_ids, positions, w_query, w_key, w_value, w_output, w_gate, w_up, w_down, attn_gain, ffn_gain, query_gain, key_gain, out_grad):
    params = tuple((p.astype(jnp.float32) for p in (w_query, w_key, w_value, w_output, w_gate, w_up, w_down, attn_gain, ffn_gain, query_gain, key_gain)))
    tokens_f = tokens.astype(jnp.float32)
    token_rows = tokens_f.reshape(N_DP, ROW, D)
    segment_rows = seg_ids.reshape(N_DP, ROW)
    position_rows = positions.reshape(N_DP, ROW)
    grad_rows = out_grad.astype(jnp.float32).reshape(N_DP, ROW, D)

    def per_row(carry, inputs):
        tokens_row, segment_row, position_row, grad_row = inputs

        def forward(params_in, tokens_in):
            return layer_row(params_in, tokens_in, segment_row, position_row)
        outputs, pullback = jax.vjp(forward, params, tokens_row)
        attn_branch = outputs[1]
        ffn_branch = outputs[2]
        grad_params, grad_in = pullback((grad_row, jnp.zeros_like(attn_branch), jnp.zeros_like(ffn_branch)))
        carry = jax.tree.map(jnp.add, carry, grad_params)
        stats = jnp.stack([jnp.sqrt(lax.optimization_barrier(jnp.mean(attn_branch * attn_branch, -1))), jnp.sqrt(lax.optimization_barrier(jnp.mean(ffn_branch * ffn_branch, -1)))])
        return (carry, (outputs[0], grad_in, stats))
    zeros = jax.tree.map(jnp.zeros_like, params)
    grads, (out_rows, grad_in_rows, stat_rows) = lax.scan(per_row, zeros, (token_rows, segment_rows, position_rows, grad_rows))
    output = out_rows.reshape(TOKENS, D).astype(jnp.bfloat16)
    grad_tokens = grad_in_rows.reshape(TOKENS, D).astype(jnp.bfloat16)
    branch_rms = jnp.transpose(stat_rows, (1, 0, 2)).reshape(2, TOKENS)
    residual_rms = jnp.sqrt(jnp.sum(tokens_f * tokens_f) / (TOKENS * D)).reshape(1)
    return (output, grad_tokens, grads[0], grads[1], grads[2], grads[3], grads[4], grads[5], grads[6], grads[7], grads[8], grads[9], grads[10], residual_rms, branch_rms)
```

```python
import functools

import jax
import jax.numpy as jnp
from jax import lax
from jax.experimental import pallas as pl
from jax.experimental.pallas import tpu as pltpu
from jax.sharding import PartitionSpec as P

HEADS = 32
KV = 8
HD = 64
EPSILON = 1e-06
ROPE_BASE = 10000.0
BLOCK = 256
F32 = jnp.float32
BF16 = jnp.bfloat16
MESH = pl.DeviceIdType.MESH


ANY = pl.BlockSpec(memory_space=pl.ANY)
VMEM = pl.BlockSpec(memory_space=pltpu.VMEM)


class Place:
    def __init__(self, members, parts):
        me = lax.axis_index("mp")
        self.dp, self.pos, self.core = lax.axis_index("dp"), me // 2, lax.rem(me, 2)
        self.length, self.parts = members // 2, parts
        self.last = self.length - 1

    def at(self, pos, core):
        return (self.dp, pos * 2 + core)

    def partner(self, bit):
        mine = lax.rem(self.dp // (1 << bit), 2)
        return mine, (self.dp + (1 - 2 * mine) * (1 << bit), self.pos * 2 + self.core)

    def bits(self):
        return self.parts.bit_length() - 1

    def meet(self, line, across):
        barrier = pltpu.get_barrier_semaphore()

        def tell(device):
            pl.semaphore_signal(barrier, inc=1, device_id=device, device_id_type=MESH)

        peers = 0
        if line:
            tell(self.at(self.pos, 1 - self.core))

            @pl.when(self.pos > 0)
            def _():
                tell(self.at(self.pos - 1, self.core))

            @pl.when(self.pos < self.last)
            def _():
                tell(self.at(self.pos + 1, self.core))

            peers = 1 + jnp.minimum(self.pos, 1) + jnp.minimum(self.last - self.pos, 1)
        if across:
            for bit in range(self.bits()):
                tell(self.partner(bit)[1])
            peers = peers + self.bits()
        pl.semaphore_wait(barrier, peers)


def remote(src, dst, send_sem, recv_sem, device):
    return pltpu.make_async_remote_copy(
        src_ref=src, dst_ref=dst, send_sem=send_sem, recv_sem=recv_sem, device_id=device, device_id_type=MESH
    )


class Gather:
    line, across = True, False

    def __init__(self, x, members):
        length = members // 2
        sems = pltpu.SemaphoreType.DMA((length,))
        self.inputs = [(x, ANY)]
        self.outputs = [(jax.ShapeDtypeStruct((members * x.shape[0],) + x.shape[1:], x.dtype), ANY)]
        self.scratch = [pltpu.SemaphoreType.DMA, sems, sems, sems, pltpu.SemaphoreType.DMA((members,))]

    def run(self, here, x_ref, o_ref, own_sem, left_sem, right_sem, side_sem, recv_sem):
        pos, core, length = here.pos, here.core, here.length
        rows = x_ref.shape[0]

        def block(p, c):
            return o_ref.at[pl.ds(pl.multiple_of((p * 2 + c) * rows, rows), rows)]

        def send(src, p, sem, to_p, to_c):
            remote(src, block(p, core), sem.at[p], recv_sem.at[p * 2 + core], here.at(to_p, to_c)).start()

        def arrived(p, c):
            pltpu.make_async_copy(x_ref, block(p, c), recv_sem.at[p * 2 + c]).wait()

        def sent(sem, p):
            pltpu.make_async_copy(x_ref, block(pos, core), sem.at[p]).wait()

        @pl.when(pos > 0)
        def _():
            send(x_ref, pos, left_sem, pos - 1, core)

        @pl.when(pos < here.last)
        def _():
            send(x_ref, pos, right_sem, pos + 1, core)

        send(x_ref, pos, side_sem, pos, 1 - core)
        own = pltpu.make_async_copy(x_ref, block(pos, core), own_sem)
        own.start()
        for step in range(1, length):
            yield
            right, left = pos + step, pos - step

            @pl.when(right < length)
            def _():
                arrived(right, core)

                @pl.when(pos > 0)
                def _():
                    send(block(right, core), right, left_sem, pos - 1, core)

                send(block(right, core), right, side_sem, pos, 1 - core)

            @pl.when(left >= 0)
            def _():
                arrived(left, core)

                @pl.when(pos < here.last)
                def _():
                    send(block(left, core), left, right_sem, pos + 1, core)

                send(block(left, core), left, side_sem, pos, 1 - core)

        yield
        own.wait()

        def drain(p, carry):
            arrived(p, 1 - core)
            sent(side_sem, p)

            @pl.when((p >= pos) & (pos > 0))
            def _():
                sent(left_sem, p)

            @pl.when((p <= pos) & (pos < here.last))
            def _():
                sent(right_sem, p)

            return carry

        lax.fori_loop(0, length, drain, 0)


class Scatter:
    line, across = True, False

    def __init__(self, parts, members):
        length = members // 2
        rows, width = parts.shape[0] // members, parts.shape[1]
        self.rows = rows
        self.inputs = [(parts, VMEM)]
        self.outputs = [(jax.ShapeDtypeStruct((rows, width), F32), VMEM)]
        self.scratch = [pltpu.VMEM((length, rows, width), parts.dtype)] * 5
        self.scratch += [pltpu.SemaphoreType.DMA((length,))] * 6

    def run(self, here, p_ref, o_ref, side_buf, left_in, right_in, left_out, right_out,
            side_send, side_recv, right_send, right_recv, left_send, left_recv):
        pos, core, length, last = here.pos, here.core, here.length, here.last
        rows, tile = self.rows, 32

        def side_copy(p):
            block = p_ref.at[pl.ds(pl.multiple_of((p * 2 + 1 - core) * rows, rows), rows)]
            return remote(block, side_buf.at[p], side_send.at[p], side_recv.at[p], here.at(pos, 1 - core))

        def line_copy(p, right):
            if right:
                return remote(right_out.at[p], right_in.at[p], right_send.at[p], right_recv.at[p], here.at(pos + 1, core))
            return remote(left_out.at[p], left_in.at[p], left_send.at[p], left_recv.at[p], here.at(pos - 1, core))

        def push(i, carry):
            @pl.when(last - i > pos)
            def _():
                side_copy(last - i).start()

            @pl.when(i < pos)
            def _():
                side_copy(i).start()

            return carry

        lax.fori_loop(0, length, push, 0)
        side_copy(pos).start()

        def add(p, incoming, out):
            def body(r, carry):
                s = pl.ds(pl.multiple_of(r * tile, tile), tile)
                mine = pl.ds(pl.multiple_of((p * 2 + core) * rows + r * tile, tile), tile)
                total = p_ref[mine].astype(F32) + side_buf[p, s].astype(F32)
                for ref in incoming:
                    total = total + ref[p, s].astype(F32)
                if out is None:
                    o_ref[s] = total
                else:
                    out[p, s] = total.astype(out.dtype)
                return carry

            lax.fori_loop(0, rows // tile, body, 0)

        def move(p, right, first, source, target):
            side_copy(p).wait_recv()

            @pl.when(first)
            def _():
                add(p, [], target)

            @pl.when(jnp.logical_not(first))
            def _():
                line_copy(p, right).wait_recv()
                add(p, [source], target)

            line_copy(p, right).start()

        def slot(t):
            right_p, left_p = last - t + pos, t - (last - pos)

            @pl.when(t >= pos)
            def _():
                move(right_p, True, pos == 0, right_in, right_out)

            @pl.when(left_p >= 0)
            def _():
                move(left_p, False, pos == last, left_in, left_out)

        for t in range(last):
            yield
            slot(t)
        yield
        side_copy(pos).wait_recv()

        @pl.when(pos == 0)
        def _():
            line_copy(pos, False).wait_recv()
            add(pos, [left_in], None)

        @pl.when(pos == last)
        def _():
            line_copy(pos, True).wait_recv()
            add(pos, [right_in], None)

        @pl.when((pos > 0) & (pos < last))
        def _():
            line_copy(pos, False).wait_recv()
            line_copy(pos, True).wait_recv()
            add(pos, [left_in, right_in], None)

        def drain(p, carry):
            side_copy(p).wait_send()

            @pl.when(p > pos)
            def _():
                line_copy(p, True).wait_send()

            @pl.when(p < pos)
            def _():
                line_copy(p, False).wait_send()

            return carry

        lax.fori_loop(0, length, drain, 0)


class Across:
    line, across = False, True

    def __init__(self, x, parts, backwards):
        self.bits = parts.bit_length() - 1
        self.order = list(range(self.bits))[:: -1 if backwards else 1]
        rows, width = x.shape
        self.inputs = [(x, VMEM)]
        self.outputs = [(jax.ShapeDtypeStruct(x.shape, x.dtype), VMEM)]
        self.scratch = [pltpu.VMEM((rows, width), x.dtype)]
        self.scratch += [pltpu.VMEM((rows >> (s + 1), width), x.dtype) for s in range(self.bits)]
        self.scratch += [pltpu.SemaphoreType.DMA((2 * self.bits,))] * 2

    def run(self, here, x_ref, o_ref, sum_ref, *rest):
        taken, (send_sem, recv_sem) = rest[: self.bits], rest[self.bits :]
        rows = x_ref.shape[0]
        start, size, copies, tile = 0, rows, [], 16

        def part(ref, at, count):
            return ref.at[pl.ds(pl.multiple_of(at, count), count)]

        for s, bit in enumerate(self.order):
            mine, device = here.partner(bit)
            half = size // 2
            keep, give = start + mine * half, start + (1 - mine) * half
            source = x_ref if s == 0 else sum_ref
            target = o_ref if s == self.bits - 1 else sum_ref
            copy = remote(part(source, give, half), taken[s], send_sem.at[s], recv_sem.at[s], device)
            copy.start()
            copies.append(copy)
            yield
            copy.wait_recv()

            def body(r, carry):
                at = pl.ds(pl.multiple_of(keep + r * tile, tile), tile)
                got = taken[s][pl.ds(pl.multiple_of(r * tile, tile), tile)]
                target[at] = (source[at].astype(F32) + got.astype(F32)).astype(target.dtype)
                return carry

            lax.fori_loop(0, half // tile, body, 0)
            start, size = keep, half
        for s, bit in enumerate(self.order[::-1]):
            mine, device = here.partner(bit)
            n = self.bits + s
            copy = remote(part(o_ref, start, size), part(o_ref, start, size), send_sem.at[n], recv_sem.at[n], device)
            copy.start()
            copies.append(copy)
            yield
            copy.wait_recv()
            start, size = start - mine * size, size * 2
        yield
        for copy in copies:
            copy.wait_send()


def together(steps, members, parts, collective_id, vmem=48):
    counts = [(len(s.inputs), len(s.outputs), len(s.scratch)) for s in steps]

    def kernel(*refs):
        refs = list(refs)
        given = [[refs.pop(0) for _ in range(c[0])] for c in counts]
        made = [[refs.pop(0) for _ in range(c[1])] for c in counts]
        held = [[refs.pop(0) for _ in range(c[2])] for c in counts]
        here = Place(members, parts)
        here.meet(any(s.line for s in steps), any(s.across for s in steps))
        live = [s.run(here, *g, *m, *h) for s, g, m, h in zip(steps, given, made, held)]
        while live:
            live = [r for r in live if next(r, live) is not live]

    return pl.pallas_call(
        kernel,
        out_shape=[o for s in steps for o, _ in s.outputs],
        in_specs=[m for s in steps for _, m in s.inputs],
        out_specs=[m for s in steps for _, m in s.outputs],
        scratch_shapes=[h for s in steps for h in s.scratch],
        compiler_params=pltpu.CompilerParams(
            collective_id=collective_id, has_side_effects=True, vmem_limit_bytes=vmem << 20
        ),
        cost_estimate=pl.CostEstimate(flops=1, bytes_accessed=1, transcendentals=0),
    )(*[x for s in steps for x, _ in s.inputs])


def dot_nn(a, b):
    return lax.dot_general(a, b, (((1,), (0,)), ((), ())), preferred_element_type=F32)

def dot_nt(a, b):
    return lax.dot_general(a, b, (((1,), (1,)), ((), ())), preferred_element_type=F32)

def group_mean(x):
    width = x.shape[1]
    row = lax.broadcasted_iota(jnp.int32, (width, width), 0) // HD
    col = lax.broadcasted_iota(jnp.int32, (width, width), 1) // HD
    ones = jnp.where(row == col, 1.0 / HD, 0.0).astype(F32)
    return jnp.dot(x, ones, precision=lax.Precision.HIGHEST, preferred_element_type=F32)

def half_turn(x):
    width = x.shape[1]
    lane = lax.broadcasted_iota(jnp.int32, (1, width), 1)
    first = lax.rem(lane, HD) < HD // 2
    up = pltpu.roll(x, HD // 2, 1)
    down = pltpu.roll(x, width - HD // 2, 1)
    return jnp.where(first, -down, up)

def wide(table, width):
    return jnp.concatenate([table] * (width // table.shape[1]), 1)

def normed(x):
    inv = lax.rsqrt(group_mean(x * x) + EPSILON)
    return x * inv, inv

def turn(x, cosine, sine):
    return x * cosine + half_turn(x) * sine

def turn_back(x, cosine, sine):
    return x * cosine - half_turn(x) * sine

def attend_kernel(heads, proj_ref, cos_ref, sin_ref, gain_ref, pos_ref, ctx_ref, lse_ref, k_ref, v_ref, acc_ref):
    width = heads * HD
    scale = HD ** -0.5
    count = proj_ref.shape[0] // BLOCK
    lane = lax.broadcasted_iota(jnp.int32, (1, HD), 1)
    def outer(i, carry):
        rows = pl.ds(pl.multiple_of(i * BLOCK, BLOCK), BLOCK)
        x = proj_ref[rows]
        cosine, sine = wide(cos_ref[rows], width + 2 * HD), wide(sin_ref[rows], width + 2 * HD)
        unit, _ = normed(x)
        spun = turn(unit * gain_ref[...], cosine, sine)
        query = spun[:, :width].astype(BF16) * scale
        query = query.astype(BF16)
        stacked = jnp.concatenate([query[:, h * HD:(h + 1) * HD] for h in range(heads)], 0)
        k_ref[rows] = spun[:, width:width + HD].astype(BF16)
        value = x[:, width + HD:].astype(BF16)
        ones = jnp.broadcast_to(jnp.where(lane == 0, 1.0, 0.0), (BLOCK, HD)).astype(BF16)
        v_ref[rows] = jnp.concatenate([value, ones], 1)
        acc_ref[...] = jnp.zeros_like(acc_ref)
        index = i * BLOCK + lax.broadcasted_iota(jnp.int32, (BLOCK, 1), 0)
        start = index - pos_ref[rows]
        def inner(j, c):
            cols = pl.ds(pl.multiple_of(j * BLOCK, BLOCK), BLOCK)
            scores = dot_nt(stacked, k_ref[cols])
            place = j * BLOCK + lax.broadcasted_iota(jnp.int32, (1, BLOCK), 1)
            seen = (place >= start) & (place <= index)
            expo = jnp.concatenate(
                [jnp.where(seen, jnp.exp(scores[h * BLOCK:(h + 1) * BLOCK]), 0.0).astype(BF16) for h in range(heads)], 0)
            acc_ref[...] += dot_nn(expo, v_ref[cols])
            return c
        lax.fori_loop(0, i + 1, inner, 0)
        outs, logs = [], []
        for h in range(heads):
            acc = acc_ref[pl.ds(h * BLOCK, BLOCK)]
            total = acc[:, HD:HD + 1]
            outs.append((acc[:, :HD] * (1.0 / total)).astype(BF16))
            logs.append(jnp.log(acc.T[HD:HD + 1]))
        ctx_ref[rows] = jnp.concatenate(outs, 1)
        lse_ref[i] = jnp.concatenate(logs, 1)
        return carry
    lax.fori_loop(0, count, outer, 0)

def attend(proj, cosine, sine, gain, positions, heads):
    size = proj.shape[0]
    count = size // BLOCK
    vm = pl.BlockSpec(memory_space=pltpu.VMEM)
    return pl.pallas_call(
        functools.partial(attend_kernel, heads),
        out_shape=(jax.ShapeDtypeStruct((size, heads * HD), BF16), jax.ShapeDtypeStruct((count, 1, heads * BLOCK), F32)),
        in_specs=[vm] * 5, out_specs=(vm, vm),
        scratch_shapes=[pltpu.VMEM((size, HD), BF16), pltpu.VMEM((size, 2 * HD), BF16), pltpu.VMEM((heads * BLOCK, 2 * HD), F32)],
        compiler_params=pltpu.CompilerParams(vmem_limit_bytes=40 << 20),
        cost_estimate=pl.CostEstimate(flops=1, bytes_accessed=1, transcendentals=0),
    )(proj, cosine, sine, gain, positions.reshape(size, 1))

def stack_lanes(x, heads):
    return jnp.concatenate([x[h * HD:(h + 1) * HD] for h in range(heads)], 1)

def attend_back_kernel(heads, proj_ref, cos_ref, sin_ref, gain_ref, pos_ref, ctx_ref, grad_ref, lse_ref,
                       out_ref, sums_ref, k_ref, kt_ref, v_ref, dk_ref, dv_ref, dq_ref):
    width = heads * HD
    scale = HD ** -0.5
    count = proj_ref.shape[0] // BLOCK
    gain = gain_ref[...]
    def prepare(i, carry):
        rows = pl.ds(pl.multiple_of(i * BLOCK, BLOCK), BLOCK)
        x = proj_ref[rows, width:]
        unit, _ = normed(x)
        spun = turn(unit * gain[:, width:], cos_ref[rows], sin_ref[rows])
        k_ref[rows] = spun[:, :HD].astype(BF16)
        kt_ref[i] = spun.T[:HD].astype(BF16)
        v_ref[rows] = x[:, HD:].astype(BF16)
        dk_ref[rows] = jnp.zeros((BLOCK, HD), F32)
        dv_ref[rows] = jnp.zeros((BLOCK, HD), F32)
        return carry
    lax.fori_loop(0, count, prepare, 0)
    sums_ref[...] = jnp.zeros_like(sums_ref)
    def outer(i, carry):
        rows = pl.ds(pl.multiple_of(i * BLOCK, BLOCK), BLOCK)
        x = proj_ref[rows, :width]
        cosine, sine = wide(cos_ref[rows], width), wide(sin_ref[rows], width)
        unit, inv = normed(x)
        query = (turn(unit * gain[:, :width], cosine, sine).astype(BF16).astype(F32) * scale)
        query_t = stack_lanes(query.T, heads).astype(BF16)
        query = query.astype(BF16)
        query_s = jnp.concatenate([query[:, h * HD:(h + 1) * HD] for h in range(heads)], 0)
        grad = grad_ref[rows]
        grad_s = jnp.concatenate([grad[:, h * HD:(h + 1) * HD] for h in range(heads)], 0)
        grad_t = stack_lanes(grad.astype(F32).T, heads)
        ctx_t = stack_lanes(ctx_ref[rows].astype(F32).T, heads)
        delta = jnp.sum(grad_t * ctx_t, 0, keepdims=True)
        grad_t = grad_t.astype(BF16)
        lse = lse_ref[i]
        index = i * BLOCK + lax.broadcasted_iota(jnp.int32, (1, BLOCK), 1)
        start = index - pos_ref[i]
        dq_ref[...] = jnp.zeros_like(dq_ref)
        def inner(j, c):
            cols = pl.ds(pl.multiple_of(j * BLOCK, BLOCK), BLOCK)
            scores = dot_nn(k_ref[cols], query_t)
            grad_probs = dot_nn(v_ref[cols], grad_t)
            place = j * BLOCK + lax.broadcasted_iota(jnp.int32, (BLOCK, 1), 0)
            seen = (place >= start) & (place <= index)
            probs, back = [], []
            for h in range(heads):
                s = slice(h * BLOCK, (h + 1) * BLOCK)
                exact = jnp.where(seen, jnp.exp(scores[:, s] - lse[:, s]), 0.0)
                probs.append(exact.astype(BF16))
                back.append((exact * (grad_probs[:, s] - delta[:, s])).astype(BF16))
            probs = jnp.concatenate(probs, 1)
            back = jnp.concatenate(back, 1)
            dv_ref[cols] += dot_nn(probs, grad_s)
            dk_ref[cols] += dot_nn(back, query_s)
            dq_ref[...] += dot_nn(kt_ref[j], back)
            return c
        lax.fori_loop(0, i + 1, inner, 0)
        dq = jnp.concatenate([dq_ref[:, h * BLOCK:(h + 1) * BLOCK] for h in range(heads)], 0).T * scale
        dqn = turn_back(dq, cosine, sine)
        sums_ref[:, :width] += jnp.sum(dqn * unit, 0, keepdims=True)
        e = dqn * gain[:, :width]
        out_ref[rows, :width] = (inv * (e - unit * group_mean(e * unit))).astype(BF16)
        return carry
    lax.fori_loop(0, count, outer, 0)
    def finish(i, carry):
        rows = pl.ds(pl.multiple_of(i * BLOCK, BLOCK), BLOCK)
        x = proj_ref[rows, width:]
        unit, inv = normed(x)
        dv = dv_ref[rows]
        dk = jnp.concatenate([dk_ref[rows], dv], 1)
        dkn = turn_back(dk, cos_ref[rows], sin_ref[rows])
        sums_ref[:, width:] += jnp.sum(dkn * unit, 0, keepdims=True)
        e = dkn * gain[:, width:]
        dkp = inv * (e - unit * group_mean(e * unit))
        lane = lax.broadcasted_iota(jnp.int32, (1, 2 * HD), 1)
        out_ref[rows, width:] = jnp.where(lane < HD, dkp, dk).astype(BF16)
        return carry
    lax.fori_loop(0, count, finish, 0)

def attend_back(proj, cosine, sine, gain, positions, context, grad_context, lse, heads):
    size = proj.shape[0]
    count = size // BLOCK
    vm = pl.BlockSpec(memory_space=pltpu.VMEM)
    return pl.pallas_call(
        functools.partial(attend_back_kernel, heads),
        out_shape=(jax.ShapeDtypeStruct(proj.shape, BF16), jax.ShapeDtypeStruct((1, proj.shape[1]), F32)),
        in_specs=[vm] * 8, out_specs=(vm, vm),
        scratch_shapes=[pltpu.VMEM((size, HD), BF16), pltpu.VMEM((count, HD, BLOCK), BF16), pltpu.VMEM((size, HD), BF16),
                        pltpu.VMEM((size, HD), F32), pltpu.VMEM((size, HD), F32), pltpu.VMEM((HD, heads * BLOCK), F32)],
        compiler_params=pltpu.CompilerParams(vmem_limit_bytes=40 << 20),
        cost_estimate=pl.CostEstimate(flops=1, bytes_accessed=1, transcendentals=0),
    )(proj, cosine, sine, gain, positions.reshape(count, 1, BLOCK), context, grad_context, lse)


def matmul(left, right):
    return jnp.dot(left, right, preferred_element_type=F32)


def matmul_left_t(left, right):
    return lax.dot_general(left, right, (((0,), (0,)), ((), ())), preferred_element_type=F32)


def matmul_right_t(left, right):
    return lax.dot_general(left, right, (((1,), (1,)), ((), ())), preferred_element_type=F32)


def rope_tables(position_row):
    half = HD // 2
    freq = ROPE_BASE ** (-jnp.arange(half, dtype=F32) / half)
    angle = position_row.astype(F32)[:, None] * freq[None, :]
    return jnp.tile(jnp.cos(angle), (1, 4)), jnp.tile(jnp.sin(angle), (1, 4))


def norm_back(grad_normed, unit, inverse, gain):
    scaled = grad_normed * gain
    return inverse * (scaled - unit * jnp.mean(scaled * unit, -1, keepdims=True))


def after(first, *later):
    return lax.optimization_barrier((first,) + later)


def per_device(
    tokens,
    seg_ids,
    positions,
    w_query,
    w_key,
    w_value,
    w_output,
    w_gate,
    w_up,
    w_down,
    attn_gain,
    ffn_gain,
    query_gain,
    key_gain,
    out_grad,
):
    members, parts = lax.axis_size("mp"), lax.axis_size("dp")
    width = tokens.shape[1]
    query_width = w_query.shape[1]
    heads = query_width // HD
    ffn_width = w_gate.shape[1]
    share = members // KV
    group = lax.axis_index("mp") // share

    tokens_f = tokens.astype(F32)
    inv_one = lax.rsqrt(jnp.mean(tokens_f * tokens_f, -1, keepdims=True) + EPSILON)
    normed_one = tokens_f * inv_one
    h_one = (normed_one * attn_gain).astype(BF16)
    key_cols = lax.dynamic_slice_in_dim(w_key, group * HD, HD, 1)
    value_cols = lax.dynamic_slice_in_dim(w_value, group * HD, HD, 1)
    w_attn = jnp.concatenate([w_query, key_cols, value_cols], 1)
    cosine, sine = rope_tables(positions)
    gain = jnp.concatenate([jnp.tile(query_gain, heads), key_gain, jnp.ones(HD, F32)])[None]

    rows_one = together([Gather(h_one, members)], members, parts, 0)[0]
    rows_one, out_grad_late = after(rows_one, out_grad)
    grad_rows = lax.all_gather(out_grad_late, "mp", axis=0, tiled=True)
    projected = matmul(rows_one, w_attn)
    context, lse = attend(projected, cosine, sine, gain, positions, heads)
    attn_part = matmul(context, w_output).astype(BF16)
    attn_branch = together([Scatter(attn_part, members)], members, parts, 1)[0]
    residual_mid = tokens_f + attn_branch
    inv_two = lax.rsqrt(jnp.mean(residual_mid * residual_mid, -1, keepdims=True) + EPSILON)
    normed_two = residual_mid * inv_two
    h_two = (normed_two * ffn_gain).astype(BF16)
    w_ffn = jnp.concatenate([w_gate, w_up], 1)
    rows_two = together([Gather(h_two, members)], members, parts, 0)[0]
    gate_up = matmul(rows_two, w_ffn)
    gate = gate_up[:, :ffn_width]
    up = gate_up[:, ffn_width:]
    sigma = jax.nn.sigmoid(gate)
    silu_gate = gate * sigma
    hidden = (silu_gate * up).astype(BF16)
    grad_hidden = matmul_right_t(grad_rows, w_down)
    grad_gate = (grad_hidden * up * sigma * (1.0 + gate * (1.0 - sigma))).astype(BF16)
    grad_up = (grad_hidden * silu_gate).astype(BF16)
    grad_gate_up = jnp.concatenate([grad_gate, grad_up], 1)
    down_part = matmul_left_t(hidden, grad_rows).astype(BF16)
    gate_part = matmul_left_t(rows_two, grad_gate).astype(BF16)
    up_part = matmul_left_t(rows_two, grad_up).astype(BF16)
    down_part, gate_part, up_part, grad_gate_up, hidden = lax.optimization_barrier(
        (down_part, gate_part, up_part, grad_gate_up, hidden)
    )
    grad_w_down, grad_w_gate, grad_w_up = lax.psum((down_part, gate_part, up_part), "dp")

    grad_h_two_part = matmul_right_t(grad_gate_up, w_ffn).astype(BF16)
    grad_h_two = together([Scatter(grad_h_two_part, members)], members, parts, 1)[0]
    grad_ffn_gain = jnp.sum(grad_h_two * normed_two, 0)
    grad_mid = out_grad.astype(F32) + norm_back(grad_h_two, normed_two, inv_two, ffn_gain)
    ffn_part = matmul(hidden, w_down).astype(BF16)
    grad_attn_rows, ffn_branch = together(
        [Gather(grad_mid.astype(BF16), members), Scatter(ffn_part, members)], members, parts, 2
    )
    grad_context = matmul_right_t(grad_attn_rows, w_output).astype(BF16)
    grad_proj, gain_sums = attend_back(
        projected, cosine, sine, gain, positions, context, grad_context, lse, heads
    )
    output_part = matmul_left_t(context, grad_attn_rows).astype(BF16)
    grad_w_attn = matmul_left_t(rows_one, grad_proj)
    grad_attn_gain = jnp.sum(w_attn.astype(F32) * grad_w_attn, 1) / attn_gain

    small = jnp.concatenate(
        [
            grad_attn_gain,
            grad_ffn_gain,
            jnp.sum(gain_sums[0, :query_width].reshape(heads, HD), 0),
            gain_sums[0, query_width : query_width + HD],
            jnp.sum(tokens_f * tokens_f)[None],
        ]
    )
    columns = w_attn.shape[1]
    unit = 16 * parts
    extra = -(-small.shape[0] // (unit * columns)) * unit
    small_rows = jnp.pad(small, (0, extra * columns - small.shape[0])).reshape(extra, columns)
    attn_part = jnp.concatenate([grad_w_attn, small_rows], 0).astype(BF16)
    grad_h_one_part = matmul_right_t(grad_proj, w_attn).astype(BF16)
    grad_w_output, attn_sum, grad_h_one = together(
        [
            Across(output_part, parts, False),
            Across(attn_part, parts, True),
            Scatter(grad_h_one_part, members),
        ],
        members,
        parts,
        3,
    )
    payload = jnp.concatenate(
        [attn_sum[:width, query_width:], attn_sum[width:].reshape(-1, 2 * HD)], 0
    )
    every = together([Gather(payload, members)], members, parts, 4)[0]
    every = every.reshape(members, payload.shape[0], 2 * HD)
    kv = every[:, :width].astype(F32).reshape(KV, share, width, 2 * HD).sum(1)
    kv = jnp.transpose(kv, (1, 0, 2))
    grad_w_key = kv[:, :, :HD].reshape(width, KV * HD)
    grad_w_value = kv[:, :, HD:].reshape(width, KV * HD)
    small_sum = every[:, width:].astype(F32).sum(0).reshape(-1)
    entry_count = tokens.size * parts * members
    at = 2 * width
    residual_rms = jnp.sqrt(small_sum[at + 2 * HD : at + 2 * HD + 1] / entry_count)

    grad_tokens = (grad_mid + norm_back(grad_h_one, normed_one, inv_one, attn_gain)).astype(BF16)
    output = (residual_mid + ffn_branch).astype(BF16)
    branch_rms = jnp.stack(
        [
            jnp.sqrt(jnp.mean(attn_branch * attn_branch, -1)),
            jnp.sqrt(jnp.mean(ffn_branch * ffn_branch, -1)),
        ]
    )
    return (
        output,
        grad_tokens,
        attn_sum[:width, :query_width].astype(F32),
        grad_w_key,
        grad_w_value,
        grad_w_output.astype(F32),
        grad_w_gate.astype(F32),
        grad_w_up.astype(F32),
        grad_w_down.astype(F32),
        small_sum[:width],
        small_sum[width:at],
        small_sum[at : at + HD],
        small_sum[at + HD : at + 2 * HD],
        residual_rms,
        branch_rms,
    )


def solution(mesh):
    row, whole, column = P(("dp", "mp"), None), P(), P(None, "mp")
    lead = P("mp", None)
    return jax.shard_map(
        per_device,
        mesh=mesh,
        in_specs=(row, P("dp"), P("dp"), column, whole, whole, lead, column, column, lead)
        + (whole,) * 4
        + (row,),
        out_specs=(row, row, column, whole, whole, lead, column, column, lead)
        + (whole,) * 5
        + (P(None, ("dp", "mp")),),
        check_vma=False,
    )
```

```python
import functools

import jax
import jax.numpy as jnp
from jax import lax
from jax.experimental import pallas as pl
from jax.experimental.pallas import tpu as pltpu
from jax.sharding import PartitionSpec as P

HEADS = 32
KV = 8
HD = 64
EPSILON = 1e-06
ROPE_BASE = 10000.0
BLOCK = 256
F32 = jnp.float32
BF16 = jnp.bfloat16
MESH = pl.DeviceIdType.MESH


ANY = pl.BlockSpec(memory_space=pl.ANY)
VMEM = pl.BlockSpec(memory_space=pltpu.VMEM)


class Place:
    def __init__(self, members, parts):
        me = lax.axis_index("mp")
        self.dp, self.pos, self.core = lax.axis_index("dp"), me // 2, lax.rem(me, 2)
        self.length, self.parts = members // 2, parts
        self.last = self.length - 1

    def at(self, pos, core):
        return (self.dp, pos * 2 + core)

    def partner(self, bit):
        mine = lax.rem(self.dp // (1 << bit), 2)
        return mine, (self.dp + (1 - 2 * mine) * (1 << bit), self.pos * 2 + self.core)

    def bits(self):
        return self.parts.bit_length() - 1

    def meet(self, line, across):
        barrier = pltpu.get_barrier_semaphore()

        def tell(device):
            pl.semaphore_signal(barrier, inc=1, device_id=device, device_id_type=MESH)

        peers = 0
        if line:
            tell(self.at(self.pos, 1 - self.core))

            @pl.when(self.pos > 0)
            def _():
                tell(self.at(self.pos - 1, self.core))

            @pl.when(self.pos < self.last)
            def _():
                tell(self.at(self.pos + 1, self.core))

            peers = 1 + jnp.minimum(self.pos, 1) + jnp.minimum(self.last - self.pos, 1)
        if across:
            for bit in range(self.bits()):
                tell(self.partner(bit)[1])
            peers = peers + self.bits()
        pl.semaphore_wait(barrier, peers)


def remote(src, dst, send_sem, recv_sem, device):
    return pltpu.make_async_remote_copy(
        src_ref=src, dst_ref=dst, send_sem=send_sem, recv_sem=recv_sem, device_id=device, device_id_type=MESH
    )


class Gather:
    line, across = True, False

    def __init__(self, x, members):
        length = members // 2
        sems = pltpu.SemaphoreType.DMA((length,))
        self.inputs = [(x, ANY)]
        self.outputs = [(jax.ShapeDtypeStruct((members * x.shape[0],) + x.shape[1:], x.dtype), ANY)]
        self.scratch = [pltpu.SemaphoreType.DMA, sems, sems, sems, pltpu.SemaphoreType.DMA((members,))]

    def run(self, here, x_ref, o_ref, own_sem, left_sem, right_sem, side_sem, recv_sem):
        pos, core, length = here.pos, here.core, here.length
        rows = x_ref.shape[0]

        def block(p, c):
            return o_ref.at[pl.ds(pl.multiple_of((p * 2 + c) * rows, rows), rows)]

        def send(src, p, sem, to_p, to_c):
            remote(src, block(p, core), sem.at[p], recv_sem.at[p * 2 + core], here.at(to_p, to_c)).start()

        def arrived(p, c):
            pltpu.make_async_copy(x_ref, block(p, c), recv_sem.at[p * 2 + c]).wait()

        def sent(sem, p):
            pltpu.make_async_copy(x_ref, block(pos, core), sem.at[p]).wait()

        @pl.when(pos > 0)
        def _():
            send(x_ref, pos, left_sem, pos - 1, core)

        @pl.when(pos < here.last)
        def _():
            send(x_ref, pos, right_sem, pos + 1, core)

        send(x_ref, pos, side_sem, pos, 1 - core)
        own = pltpu.make_async_copy(x_ref, block(pos, core), own_sem)
        own.start()
        for step in range(1, length):
            yield
            right, left = pos + step, pos - step

            @pl.when(right < length)
            def _():
                arrived(right, core)

                @pl.when(pos > 0)
                def _():
                    send(block(right, core), right, left_sem, pos - 1, core)

                send(block(right, core), right, side_sem, pos, 1 - core)

            @pl.when(left >= 0)
            def _():
                arrived(left, core)

                @pl.when(pos < here.last)
                def _():
                    send(block(left, core), left, right_sem, pos + 1, core)

                send(block(left, core), left, side_sem, pos, 1 - core)

        yield
        own.wait()

        def drain(p, carry):
            arrived(p, 1 - core)
            sent(side_sem, p)

            @pl.when((p >= pos) & (pos > 0))
            def _():
                sent(left_sem, p)

            @pl.when((p <= pos) & (pos < here.last))
            def _():
                sent(right_sem, p)

            return carry

        lax.fori_loop(0, length, drain, 0)


class GatherFfn:
    line, across = True, False

    def __init__(self, x, grad_rows, w_gate, w_up, w_down, members):
        length, (rows, width), units = members // 2, x.shape, w_gate.shape[1]
        total = members * rows
        sems = pltpu.SemaphoreType.DMA((length,))
        self.units = units
        self.inputs = [(v, ANY) for v in (x, grad_rows, w_gate, w_up, w_down)]
        self.outputs = [
            (jax.ShapeDtypeStruct((total, width), BF16), VMEM),
            (jax.ShapeDtypeStruct((total, units), BF16), VMEM),
            (jax.ShapeDtypeStruct((total, 2 * units), BF16), VMEM),
        ]
        self.scratch = [pltpu.VMEM(v.shape, v.dtype) for v in (grad_rows, w_gate, w_up, w_down)]
        self.scratch += [pltpu.SemaphoreType.DMA((5,)), sems, sems, sems, pltpu.SemaphoreType.DMA((members,))]

    def run(self, here, x_ref, gr_ref, wg_ref, wu_ref, wd_ref, o_ref, hid_ref, ggu_ref,
            gr, wg, wu, wd, load_sem, left_sem, right_sem, side_sem, recv_sem):
        pos, core, length = here.pos, here.core, here.length
        rows, units, wide = x_ref.shape[0], self.units, 256

        def block(p, c):
            return o_ref.at[pl.ds(pl.multiple_of((p * 2 + c) * rows, rows), rows)]

        def send(src, p, sem, to_p, to_c):
            remote(src, block(p, core), sem.at[p], recv_sem.at[p * 2 + core], here.at(to_p, to_c)).start()

        def arrived(p, c):
            pltpu.make_async_copy(x_ref, block(p, c), recv_sem.at[p * 2 + c]).wait()

        def sent(sem, p):
            pltpu.make_async_copy(x_ref, block(pos, core), sem.at[p]).wait()

        @pl.when(pos > 0)
        def _():
            send(x_ref, pos, left_sem, pos - 1, core)

        @pl.when(pos < here.last)
        def _():
            send(x_ref, pos, right_sem, pos + 1, core)

        send(x_ref, pos, side_sem, pos, 1 - core)
        pairs = [(x_ref, block(pos, core)), (wg_ref, wg), (wu_ref, wu), (gr_ref, gr), (wd_ref, wd)]
        loads = [pltpu.make_async_copy(a, b, load_sem.at[i]) for i, (a, b) in enumerate(pairs)]
        for load in loads:
            load.start()
        yield
        for load in loads:
            load.wait()

        def use(p):
            at = pl.ds(pl.multiple_of(p * 2 * rows, 2 * rows), 2 * rows)

            def body(c, carry):
                cols = pl.ds(pl.multiple_of(c * wide, wide), wide)
                gate = dot_nn(o_ref[at], wg[:, cols])
                up = dot_nn(o_ref[at], wu[:, cols])
                back = dot_nt(gr[at], wd[cols])
                sigma = 1.0 / (1.0 + jnp.exp(-gate))
                silu = gate * sigma
                hid_ref[at, cols] = (silu * up).astype(BF16)
                ggu_ref[at, cols] = (back * up * sigma * (1.0 + gate * (1.0 - sigma))).astype(BF16)
                ggu_ref[at, pl.ds(pl.multiple_of(units + c * wide, wide), wide)] = (back * silu).astype(BF16)
                return carry

            lax.fori_loop(0, units // wide, body, 0)

        def hop(step, carry):
            right, left = pos + step, pos - step

            @pl.when((step > 0) & (right < length))
            def _():
                arrived(right, core)

                @pl.when(pos > 0)
                def _():
                    send(block(right, core), right, left_sem, pos - 1, core)

                send(block(right, core), right, side_sem, pos, 1 - core)

            @pl.when((step > 0) & (left >= 0))
            def _():
                arrived(left, core)

                @pl.when(pos < here.last)
                def _():
                    send(block(left, core), left, right_sem, pos + 1, core)

                send(block(left, core), left, side_sem, pos, 1 - core)

            def side(k, c):
                p = pos + (1 - 2 * k) * step

                @pl.when((p >= 0) & (p < length) & (step >= k))
                def _():
                    arrived(p, 1 - core)
                    use(p)

                return c

            lax.fori_loop(0, 2, side, 0)
            return carry

        lax.fori_loop(0, length, hop, 0)

        def drain(p, carry):
            sent(side_sem, p)

            @pl.when((p >= pos) & (pos > 0))
            def _():
                sent(left_sem, p)

            @pl.when((p <= pos) & (pos < here.last))
            def _():
                sent(right_sem, p)

            return carry

        lax.fori_loop(0, length, drain, 0)


class Scatter:
    line, across = True, False

    def __init__(self, terms, members):
        length = members // 2
        left, right, turned = terms[0]
        rows, width = left.shape[0] // members, right.shape[0 if turned else 1]
        self.rows, self.width, self.turned = rows, width, [t for _, _, t in terms]
        self.inputs = [(x, VMEM) for x, _, _ in terms] + [(w, ANY) for _, w, _ in terms]
        self.outputs = [(jax.ShapeDtypeStruct((rows, width), F32), VMEM)]
        self.scratch = [pltpu.VMEM(w.shape, w.dtype) for _, w, _ in terms]
        self.scratch += [pltpu.SemaphoreType.DMA((len(terms),)), pltpu.VMEM((members * rows, width), BF16)]
        self.scratch += [pltpu.VMEM((length, rows, width), BF16)] * 5
        self.scratch += [pltpu.SemaphoreType.DMA((length,))] * 6

    def run(self, here, *refs):
        n = len(self.turned)
        lefts, rights, (o_ref,), helds = refs[:n], refs[n : 2 * n], refs[2 * n : 2 * n + 1], refs[2 * n + 1 : 3 * n + 1]
        (load_sem, p_ref, side_buf, left_in, right_in, left_out, right_out,
         side_send, side_recv, right_send, right_recv, left_send, left_recv) = refs[3 * n + 1 :]
        pos, core, length, last = here.pos, here.core, here.length, here.last
        rows, tile, wide = self.rows, 32, 256
        loads = [pltpu.make_async_copy(w, h, load_sem.at[i]) for i, (w, h) in enumerate(zip(rights, helds))]
        for load in loads:
            load.start()

        def side_copy(p):
            block = p_ref.at[pl.ds(pl.multiple_of((p * 2 + 1 - core) * rows, rows), rows)]
            return remote(block, side_buf.at[p], side_send.at[p], side_recv.at[p], here.at(pos, 1 - core))

        def line_copy(p, right):
            if right:
                return remote(right_out.at[p], right_in.at[p], right_send.at[p], right_recv.at[p], here.at(pos + 1, core))
            return remote(left_out.at[p], left_in.at[p], left_send.at[p], left_recv.at[p], here.at(pos - 1, core))

        def multiply(p):
            at = pl.ds(pl.multiple_of(p * 2 * rows, 2 * rows), 2 * rows)

            def body(c, carry):
                cols = pl.ds(pl.multiple_of(c * wide, wide), wide)
                total = None
                for left, held, turned in zip(lefts, helds, self.turned):
                    part = dot_nt(left[at], held[cols]) if turned else dot_nn(left[at], held[:, cols])
                    total = part if total is None else total + part
                p_ref[at, cols] = total.astype(BF16)
                return carry

            lax.fori_loop(0, self.width // wide, body, 0)
            side_copy(p).start()

        def add(p, incoming, out):
            def body(r, carry):
                s = pl.ds(pl.multiple_of(r * tile, tile), tile)
                mine = pl.ds(pl.multiple_of((p * 2 + core) * rows + r * tile, tile), tile)
                total = p_ref[mine].astype(F32) + side_buf[p, s].astype(F32)
                for ref in incoming:
                    total = total + ref[p, s].astype(F32)
                if out is None:
                    o_ref[s] = total
                else:
                    out[p, s] = total.astype(out.dtype)
                return carry

            lax.fori_loop(0, rows // tile, body, 0)

        def move(p, right, first, source, target):
            side_copy(p).wait_recv()

            @pl.when(first)
            def _():
                add(p, [], target)

            @pl.when(jnp.logical_not(first))
            def _():
                line_copy(p, right).wait_recv()
                add(p, [source], target)

            line_copy(p, right).start()

        for load in loads:
            load.wait()
        for t in range(last):

            def side(k, carry):
                p = k * t + (1 - k) * (last - t)

                @pl.when((1 - 2 * k) * (p - pos) > 0)
                def _():
                    multiply(p)

                return carry

            lax.fori_loop(0, 2, side, 0)
            yield
            right_p, left_p = last - t + pos, t - (last - pos)

            @pl.when(t >= pos)
            def _():
                move(right_p, True, pos == 0, right_in, right_out)

            @pl.when(left_p >= 0)
            def _():
                move(left_p, False, pos == last, left_in, left_out)

        multiply(pos)
        yield
        side_copy(pos).wait_recv()

        @pl.when(pos == 0)
        def _():
            line_copy(pos, False).wait_recv()
            add(pos, [left_in], None)

        @pl.when(pos == last)
        def _():
            line_copy(pos, True).wait_recv()
            add(pos, [right_in], None)

        @pl.when((pos > 0) & (pos < last))
        def _():
            line_copy(pos, False).wait_recv()
            line_copy(pos, True).wait_recv()
            add(pos, [left_in, right_in], None)

        def drain(p, carry):
            side_copy(p).wait_send()

            @pl.when(p > pos)
            def _():
                line_copy(p, True).wait_send()

            @pl.when(p < pos)
            def _():
                line_copy(p, False).wait_send()

            return carry

        lax.fori_loop(0, length, drain, 0)


class Across:
    line, across = False, True

    def __init__(self, x, parts, backwards):
        self.bits = parts.bit_length() - 1
        self.order = list(range(self.bits))[:: -1 if backwards else 1]
        rows, width = x.shape
        self.inputs = [(x, VMEM)]
        self.outputs = [(jax.ShapeDtypeStruct(x.shape, x.dtype), VMEM)]
        self.scratch = [pltpu.VMEM((rows, width), x.dtype)]
        self.scratch += [pltpu.VMEM((rows >> (s + 1), width), x.dtype) for s in range(self.bits)]
        self.scratch += [pltpu.SemaphoreType.DMA((2 * self.bits,))] * 2

    def run(self, here, x_ref, o_ref, sum_ref, *rest):
        taken, (send_sem, recv_sem) = rest[: self.bits], rest[self.bits :]
        rows = x_ref.shape[0]
        start, size, copies, tile = 0, rows, [], 16

        def part(ref, at, count):
            return ref.at[pl.ds(pl.multiple_of(at, count), count)]

        for s, bit in enumerate(self.order):
            mine, device = here.partner(bit)
            half = size // 2
            keep, give = start + mine * half, start + (1 - mine) * half
            source = x_ref if s == 0 else sum_ref
            target = o_ref if s == self.bits - 1 else sum_ref
            copy = remote(part(source, give, half), taken[s], send_sem.at[s], recv_sem.at[s], device)
            copy.start()
            copies.append(copy)
            yield
            copy.wait_recv()

            def body(r, carry):
                at = pl.ds(pl.multiple_of(keep + r * tile, tile), tile)
                got = taken[s][pl.ds(pl.multiple_of(r * tile, tile), tile)]
                target[at] = (source[at].astype(F32) + got.astype(F32)).astype(target.dtype)
                return carry

            lax.fori_loop(0, half // tile, body, 0)
            start, size = keep, half
        for s, bit in enumerate(self.order[::-1]):
            mine, device = here.partner(bit)
            n = self.bits + s
            copy = remote(part(o_ref, start, size), part(o_ref, start, size), send_sem.at[n], recv_sem.at[n], device)
            copy.start()
            copies.append(copy)
            yield
            copy.wait_recv()
            start, size = start - mine * size, size * 2
        yield
        for copy in copies:
            copy.wait_send()


def together(steps, members, parts, collective_id, vmem=48):
    counts = [(len(s.inputs), len(s.outputs), len(s.scratch)) for s in steps]

    def kernel(*refs):
        refs = list(refs)
        given = [[refs.pop(0) for _ in range(c[0])] for c in counts]
        made = [[refs.pop(0) for _ in range(c[1])] for c in counts]
        held = [[refs.pop(0) for _ in range(c[2])] for c in counts]
        here = Place(members, parts)
        here.meet(any(s.line for s in steps), any(s.across for s in steps))
        live = [s.run(here, *g, *m, *h) for s, g, m, h in zip(steps, given, made, held)]
        while live:
            live = [r for r in live if next(r, live) is not live]

    return pl.pallas_call(
        kernel,
        out_shape=[o for s in steps for o, _ in s.outputs],
        in_specs=[m for s in steps for _, m in s.inputs],
        out_specs=[m for s in steps for _, m in s.outputs],
        scratch_shapes=[h for s in steps for h in s.scratch],
        compiler_params=pltpu.CompilerParams(
            collective_id=collective_id, has_side_effects=True, vmem_limit_bytes=vmem << 20
        ),
        cost_estimate=pl.CostEstimate(flops=1, bytes_accessed=1, transcendentals=0),
    )(*[x for s in steps for x, _ in s.inputs])


def dot_nn(a, b):
    return lax.dot_general(a, b, (((1,), (0,)), ((), ())), preferred_element_type=F32)

def dot_nt(a, b):
    return lax.dot_general(a, b, (((1,), (1,)), ((), ())), preferred_element_type=F32)

def group_mean(x):
    width = x.shape[1]
    row = lax.broadcasted_iota(jnp.int32, (width, width), 0) // HD
    col = lax.broadcasted_iota(jnp.int32, (width, width), 1) // HD
    ones = jnp.where(row == col, 1.0 / HD, 0.0).astype(F32)
    return jnp.dot(x, ones, precision=lax.Precision.HIGHEST, preferred_element_type=F32)

def half_turn(x):
    width = x.shape[1]
    lane = lax.broadcasted_iota(jnp.int32, (1, width), 1)
    first = lax.rem(lane, HD) < HD // 2
    up = pltpu.roll(x, HD // 2, 1)
    down = pltpu.roll(x, width - HD // 2, 1)
    return jnp.where(first, -down, up)

def wide(table, width):
    return jnp.concatenate([table] * (width // table.shape[1]), 1)

def normed(x):
    inv = lax.rsqrt(group_mean(x * x) + EPSILON)
    return x * inv, inv

def turn(x, cosine, sine):
    return x * cosine + half_turn(x) * sine

def turn_back(x, cosine, sine):
    return x * cosine - half_turn(x) * sine

def attend_kernel(heads, proj_ref, cos_ref, sin_ref, gain_ref, pos_ref, ctx_ref, lse_ref, k_ref, v_ref, acc_ref):
    width = heads * HD
    scale = HD ** -0.5
    count = proj_ref.shape[0] // BLOCK
    lane = lax.broadcasted_iota(jnp.int32, (1, HD), 1)
    def outer(i, carry):
        rows = pl.ds(pl.multiple_of(i * BLOCK, BLOCK), BLOCK)
        x = proj_ref[rows]
        cosine, sine = wide(cos_ref[rows], width + 2 * HD), wide(sin_ref[rows], width + 2 * HD)
        unit, _ = normed(x)
        spun = turn(unit * gain_ref[...], cosine, sine)
        query = spun[:, :width].astype(BF16) * scale
        query = query.astype(BF16)
        stacked = jnp.concatenate([query[:, h * HD:(h + 1) * HD] for h in range(heads)], 0)
        k_ref[rows] = spun[:, width:width + HD].astype(BF16)
        value = x[:, width + HD:].astype(BF16)
        ones = jnp.broadcast_to(jnp.where(lane == 0, 1.0, 0.0), (BLOCK, HD)).astype(BF16)
        v_ref[rows] = jnp.concatenate([value, ones], 1)
        acc_ref[...] = jnp.zeros_like(acc_ref)
        index = i * BLOCK + lax.broadcasted_iota(jnp.int32, (BLOCK, 1), 0)
        start = index - pos_ref[rows]
        def inner(j, c):
            cols = pl.ds(pl.multiple_of(j * BLOCK, BLOCK), BLOCK)
            scores = dot_nt(stacked, k_ref[cols])
            place = j * BLOCK + lax.broadcasted_iota(jnp.int32, (1, BLOCK), 1)
            seen = (place >= start) & (place <= index)
            expo = jnp.concatenate(
                [jnp.where(seen, jnp.exp(scores[h * BLOCK:(h + 1) * BLOCK]), 0.0).astype(BF16) for h in range(heads)], 0)
            acc_ref[...] += dot_nn(expo, v_ref[cols])
            return c
        lax.fori_loop(0, i + 1, inner, 0)
        outs, logs = [], []
        for h in range(heads):
            acc = acc_ref[pl.ds(h * BLOCK, BLOCK)]
            total = acc[:, HD:HD + 1]
            outs.append((acc[:, :HD] * (1.0 / total)).astype(BF16))
            logs.append(jnp.log(acc.T[HD:HD + 1]))
        ctx_ref[rows] = jnp.concatenate(outs, 1)
        lse_ref[i] = jnp.concatenate(logs, 1)
        return carry
    lax.fori_loop(0, count, outer, 0)

def attend(proj, cosine, sine, gain, positions, heads):
    size = proj.shape[0]
    count = size // BLOCK
    vm = pl.BlockSpec(memory_space=pltpu.VMEM)
    return pl.pallas_call(
        functools.partial(attend_kernel, heads),
        out_shape=(jax.ShapeDtypeStruct((size, heads * HD), BF16), jax.ShapeDtypeStruct((count, 1, heads * BLOCK), F32)),
        in_specs=[vm] * 5, out_specs=(vm, vm),
        scratch_shapes=[pltpu.VMEM((size, HD), BF16), pltpu.VMEM((size, 2 * HD), BF16), pltpu.VMEM((heads * BLOCK, 2 * HD), F32)],
        compiler_params=pltpu.CompilerParams(vmem_limit_bytes=40 << 20),
        cost_estimate=pl.CostEstimate(flops=1, bytes_accessed=1, transcendentals=0),
    )(proj, cosine, sine, gain, positions.reshape(size, 1))

def stack_lanes(x, heads):
    return jnp.concatenate([x[h * HD:(h + 1) * HD] for h in range(heads)], 1)

def attend_back_kernel(heads, proj_ref, cos_ref, sin_ref, gain_ref, pos_ref, ctx_ref, grad_ref, lse_ref,
                       out_ref, sums_ref, k_ref, kt_ref, v_ref, dk_ref, dv_ref, dq_ref):
    width = heads * HD
    scale = HD ** -0.5
    count = proj_ref.shape[0] // BLOCK
    gain = gain_ref[...]
    def prepare(i, carry):
        rows = pl.ds(pl.multiple_of(i * BLOCK, BLOCK), BLOCK)
        x = proj_ref[rows, width:]
        unit, _ = normed(x)
        spun = turn(unit * gain[:, width:], cos_ref[rows], sin_ref[rows])
        k_ref[rows] = spun[:, :HD].astype(BF16)
        kt_ref[i] = spun.T[:HD].astype(BF16)
        v_ref[rows] = x[:, HD:].astype(BF16)
        dk_ref[rows] = jnp.zeros((BLOCK, HD), F32)
        dv_ref[rows] = jnp.zeros((BLOCK, HD), F32)
        return carry
    lax.fori_loop(0, count, prepare, 0)
    sums_ref[...] = jnp.zeros_like(sums_ref)
    def outer(i, carry):
        rows = pl.ds(pl.multiple_of(i * BLOCK, BLOCK), BLOCK)
        x = proj_ref[rows, :width]
        cosine, sine = wide(cos_ref[rows], width), wide(sin_ref[rows], width)
        unit, inv = normed(x)
        query = (turn(unit * gain[:, :width], cosine, sine).astype(BF16).astype(F32) * scale)
        query_t = stack_lanes(query.T, heads).astype(BF16)
        query = query.astype(BF16)
        query_s = jnp.concatenate([query[:, h * HD:(h + 1) * HD] for h in range(heads)], 0)
        grad = grad_ref[rows]
        grad_s = jnp.concatenate([grad[:, h * HD:(h + 1) * HD] for h in range(heads)], 0)
        grad_t = stack_lanes(grad.astype(F32).T, heads)
        ctx_t = stack_lanes(ctx_ref[rows].astype(F32).T, heads)
        delta = jnp.sum(grad_t * ctx_t, 0, keepdims=True)
        grad_t = grad_t.astype(BF16)
        lse = lse_ref[i]
        index = i * BLOCK + lax.broadcasted_iota(jnp.int32, (1, BLOCK), 1)
        start = index - pos_ref[i]
        dq_ref[...] = jnp.zeros_like(dq_ref)
        def inner(j, c):
            cols = pl.ds(pl.multiple_of(j * BLOCK, BLOCK), BLOCK)
            scores = dot_nn(k_ref[cols], query_t)
            grad_probs = dot_nn(v_ref[cols], grad_t)
            place = j * BLOCK + lax.broadcasted_iota(jnp.int32, (BLOCK, 1), 0)
            seen = (place >= start) & (place <= index)
            probs, back = [], []
            for h in range(heads):
                s = slice(h * BLOCK, (h + 1) * BLOCK)
                exact = jnp.where(seen, jnp.exp(scores[:, s] - lse[:, s]), 0.0)
                probs.append(exact.astype(BF16))
                back.append((exact * (grad_probs[:, s] - delta[:, s])).astype(BF16))
            probs = jnp.concatenate(probs, 1)
            back = jnp.concatenate(back, 1)
            dv_ref[cols] += dot_nn(probs, grad_s)
            dk_ref[cols] += dot_nn(back, query_s)
            dq_ref[...] += dot_nn(kt_ref[j], back)
            return c
        lax.fori_loop(0, i + 1, inner, 0)
        dq = jnp.concatenate([dq_ref[:, h * BLOCK:(h + 1) * BLOCK] for h in range(heads)], 0).T * scale
        dqn = turn_back(dq, cosine, sine)
        sums_ref[:, :width] += jnp.sum(dqn * unit, 0, keepdims=True)
        e = dqn * gain[:, :width]
        out_ref[rows, :width] = (inv * (e - unit * group_mean(e * unit))).astype(BF16)
        return carry
    lax.fori_loop(0, count, outer, 0)
    def finish(i, carry):
        rows = pl.ds(pl.multiple_of(i * BLOCK, BLOCK), BLOCK)
        x = proj_ref[rows, width:]
        unit, inv = normed(x)
        dv = dv_ref[rows]
        dk = jnp.concatenate([dk_ref[rows], dv], 1)
        dkn = turn_back(dk, cos_ref[rows], sin_ref[rows])
        sums_ref[:, width:] += jnp.sum(dkn * unit, 0, keepdims=True)
        e = dkn * gain[:, width:]
        dkp = inv * (e - unit * group_mean(e * unit))
        lane = lax.broadcasted_iota(jnp.int32, (1, 2 * HD), 1)
        out_ref[rows, width:] = jnp.where(lane < HD, dkp, dk).astype(BF16)
        return carry
    lax.fori_loop(0, count, finish, 0)

def attend_back(proj, cosine, sine, gain, positions, context, grad_context, lse, heads):
    size = proj.shape[0]
    count = size // BLOCK
    vm = pl.BlockSpec(memory_space=pltpu.VMEM)
    return pl.pallas_call(
        functools.partial(attend_back_kernel, heads),
        out_shape=(jax.ShapeDtypeStruct(proj.shape, BF16), jax.ShapeDtypeStruct((1, proj.shape[1]), F32)),
        in_specs=[vm] * 8, out_specs=(vm, vm),
        scratch_shapes=[pltpu.VMEM((size, HD), BF16), pltpu.VMEM((count, HD, BLOCK), BF16), pltpu.VMEM((size, HD), BF16),
                        pltpu.VMEM((size, HD), F32), pltpu.VMEM((size, HD), F32), pltpu.VMEM((HD, heads * BLOCK), F32)],
        compiler_params=pltpu.CompilerParams(vmem_limit_bytes=40 << 20),
        cost_estimate=pl.CostEstimate(flops=1, bytes_accessed=1, transcendentals=0),
    )(proj, cosine, sine, gain, positions.reshape(count, 1, BLOCK), context, grad_context, lse)


def matmul(left, right):
    return jnp.dot(left, right, preferred_element_type=F32)


def matmul_left_t(left, right):
    return lax.dot_general(left, right, (((0,), (0,)), ((), ())), preferred_element_type=F32)


def matmul_right_t(left, right):
    return lax.dot_general(left, right, (((1,), (1,)), ((), ())), preferred_element_type=F32)


def rope_tables(position_row):
    half = HD // 2
    freq = ROPE_BASE ** (-jnp.arange(half, dtype=F32) / half)
    angle = position_row.astype(F32)[:, None] * freq[None, :]
    return jnp.tile(jnp.cos(angle), (1, 4)), jnp.tile(jnp.sin(angle), (1, 4))


def norm_back(grad_normed, unit, inverse, gain):
    scaled = grad_normed * gain
    return inverse * (scaled - unit * jnp.mean(scaled * unit, -1, keepdims=True))


def after(first, *later):
    return lax.optimization_barrier((first,) + later)


def per_device(
    tokens,
    seg_ids,
    positions,
    w_query,
    w_key,
    w_value,
    w_output,
    w_gate,
    w_up,
    w_down,
    attn_gain,
    ffn_gain,
    query_gain,
    key_gain,
    out_grad,
):
    members, parts = lax.axis_size("mp"), lax.axis_size("dp")
    width = tokens.shape[1]
    query_width = w_query.shape[1]
    heads = query_width // HD
    ffn_width = w_gate.shape[1]
    share = members // KV
    group = lax.axis_index("mp") // share

    tokens_f = tokens.astype(F32)
    inv_one = lax.rsqrt(jnp.mean(tokens_f * tokens_f, -1, keepdims=True) + EPSILON)
    normed_one = tokens_f * inv_one
    h_one = (normed_one * attn_gain).astype(BF16)
    key_cols = lax.dynamic_slice_in_dim(w_key, group * HD, HD, 1)
    value_cols = lax.dynamic_slice_in_dim(w_value, group * HD, HD, 1)
    w_attn = jnp.concatenate([w_query, key_cols, value_cols], 1)
    cosine, sine = rope_tables(positions)
    gain = jnp.concatenate([jnp.tile(query_gain, heads), key_gain, jnp.ones(HD, F32)])[None]

    rows_one = together([Gather(h_one, members)], members, parts, 0)[0]
    rows_one, out_grad_late = after(rows_one, out_grad)
    grad_rows = lax.all_gather(out_grad_late, "mp", axis=0, tiled=True)
    projected = matmul(rows_one, w_attn)
    context, lse = attend(projected, cosine, sine, gain, positions, heads)
    attn_branch = together([Scatter([(context, w_output, False)], members)], members, parts, 1)[0]
    residual_mid = tokens_f + attn_branch
    inv_two = lax.rsqrt(jnp.mean(residual_mid * residual_mid, -1, keepdims=True) + EPSILON)
    normed_two = residual_mid * inv_two
    h_two = (normed_two * ffn_gain).astype(BF16)
    rows_two, hidden, grad_gate_up = together(
        [GatherFfn(h_two, grad_rows, w_gate, w_up, w_down, members)], members, parts, 5, 58
    )
    ffn_parts = (
        matmul_left_t(rows_two, grad_gate_up).astype(BF16),
        matmul_left_t(hidden, grad_rows).astype(BF16),
    )
    ffn_parts, grad_gate_up, hidden = lax.optimization_barrier((ffn_parts, grad_gate_up, hidden))
    grad_w_ffn, grad_w_down = lax.psum(ffn_parts, "dp")

    grad_gate, grad_up = grad_gate_up[:, :ffn_width], grad_gate_up[:, ffn_width:]
    grad_h_two = together(
        [Scatter([(grad_gate, w_gate, True), (grad_up, w_up, True)], members)], members, parts, 6, 58
    )[0]
    grad_ffn_gain = jnp.sum(grad_h_two * normed_two, 0)
    grad_mid = out_grad.astype(F32) + norm_back(grad_h_two, normed_two, inv_two, ffn_gain)
    grad_attn_rows, ffn_branch = together(
        [Gather(grad_mid.astype(BF16), members), Scatter([(hidden, w_down, False)], members)],
        members,
        parts,
        2,
    )
    grad_context = matmul_right_t(grad_attn_rows, w_output).astype(BF16)
    grad_proj, gain_sums = attend_back(
        projected, cosine, sine, gain, positions, context, grad_context, lse, heads
    )
    output_part = matmul_left_t(context, grad_attn_rows).astype(BF16)
    grad_w_attn = matmul_left_t(rows_one, grad_proj)
    grad_attn_gain = jnp.sum(w_attn.astype(F32) * grad_w_attn, 1) / attn_gain

    small = jnp.concatenate(
        [
            grad_attn_gain,
            grad_ffn_gain,
            jnp.sum(gain_sums[0, :query_width].reshape(heads, HD), 0),
            gain_sums[0, query_width : query_width + HD],
            jnp.sum(tokens_f * tokens_f)[None],
        ]
    )
    columns = w_attn.shape[1]
    unit = 16 * parts
    extra = -(-small.shape[0] // (unit * columns)) * unit
    small_rows = jnp.pad(small, (0, extra * columns - small.shape[0])).reshape(extra, columns)
    attn_part = jnp.concatenate([grad_w_attn, small_rows], 0).astype(BF16)
    grad_w_output, attn_sum, grad_h_one = together(
        [
            Across(output_part, parts, False),
            Across(attn_part, parts, True),
            Scatter([(grad_proj, w_attn, True)], members),
        ],
        members,
        parts,
        3,
    )
    payload = jnp.concatenate(
        [attn_sum[:width, query_width:], attn_sum[width:].reshape(-1, 2 * HD)], 0
    )
    every = together([Gather(payload, members)], members, parts, 4)[0]
    every = every.reshape(members, payload.shape[0], 2 * HD)
    kv = every[:, :width].astype(F32).reshape(KV, share, width, 2 * HD).sum(1)
    kv = jnp.transpose(kv, (1, 0, 2))
    grad_w_key = kv[:, :, :HD].reshape(width, KV * HD)
    grad_w_value = kv[:, :, HD:].reshape(width, KV * HD)
    small_sum = every[:, width:].astype(F32).sum(0).reshape(-1)
    entry_count = tokens.size * parts * members
    at = 2 * width
    residual_rms = jnp.sqrt(small_sum[at + 2 * HD : at + 2 * HD + 1] / entry_count)

    grad_tokens = (grad_mid + norm_back(grad_h_one, normed_one, inv_one, attn_gain)).astype(BF16)
    output = (residual_mid + ffn_branch).astype(BF16)
    branch_rms = jnp.stack(
        [
            jnp.sqrt(jnp.mean(attn_branch * attn_branch, -1)),
            jnp.sqrt(jnp.mean(ffn_branch * ffn_branch, -1)),
        ]
    )
    return (
        output,
        grad_tokens,
        attn_sum[:width, :query_width].astype(F32),
        grad_w_key,
        grad_w_value,
        grad_w_output.astype(F32),
        grad_w_ffn[:, :ffn_width].astype(F32),
        grad_w_ffn[:, ffn_width:].astype(F32),
        grad_w_down.astype(F32),
        small_sum[:width],
        small_sum[width:at],
        small_sum[at : at + HD],
        small_sum[at + HD : at + 2 * HD],
        residual_rms,
        branch_rms,
    )


def solution(mesh):
    row, whole, column = P(("dp", "mp"), None), P(), P(None, "mp")
    lead = P("mp", None)
    return jax.shard_map(
        per_device,
        mesh=mesh,
        in_specs=(row, P("dp"), P("dp"), column, whole, whole, lead, column, column, lead)
        + (whole,) * 4
        + (row,),
        out_specs=(row, row, column, whole, whole, lead, column, column, lead)
        + (whole,) * 5
        + (P(None, ("dp", "mp")),),
        check_vma=False,
    )
```

```python
import functools

import jax
import jax.numpy as jnp
from jax import lax
from jax.experimental import pallas as pl
from jax.experimental.pallas import tpu as pltpu
from jax.sharding import PartitionSpec as P

HEADS = 32
KV = 8
HD = 64
EPSILON = 1e-06
ROPE_BASE = 10000.0
BLOCK = 256
F32 = jnp.float32
BF16 = jnp.bfloat16
MESH = pl.DeviceIdType.MESH


ANY = pl.BlockSpec(memory_space=pl.ANY)
VMEM = pl.BlockSpec(memory_space=pltpu.VMEM)


class Place:
    def __init__(self, members, parts):
        me = lax.axis_index("mp")
        self.dp, self.pos, self.core = lax.axis_index("dp"), me // 2, lax.rem(me, 2)
        self.length, self.parts = members // 2, parts
        self.last = self.length - 1

    def at(self, pos, core):
        return (self.dp, pos * 2 + core)

    def partner(self, bit):
        mine = lax.rem(self.dp // (1 << bit), 2)
        return mine, (self.dp + (1 - 2 * mine) * (1 << bit), self.pos * 2 + self.core)

    def bits(self):
        return self.parts.bit_length() - 1

    def greet(self, line, across):
        barrier = pltpu.get_barrier_semaphore()

        def tell(device):
            pl.semaphore_signal(barrier, inc=1, device_id=device, device_id_type=MESH)

        peers = 0
        if line:
            tell(self.at(self.pos, 1 - self.core))

            @pl.when(self.pos > 0)
            def _():
                tell(self.at(self.pos - 1, self.core))

            @pl.when(self.pos < self.last)
            def _():
                tell(self.at(self.pos + 1, self.core))

            peers = 1 + jnp.minimum(self.pos, 1) + jnp.minimum(self.last - self.pos, 1)
        if across:
            for bit in range(self.bits()):
                tell(self.partner(bit)[1])
            peers = peers + self.bits()
        return peers

    def meet(self, peers):
        pl.semaphore_wait(pltpu.get_barrier_semaphore(), peers)


def weave(live):
    while live:
        live = [r for r in live if next(r, live) is not live]


def remote(src, dst, send_sem, recv_sem, device):
    return pltpu.make_async_remote_copy(
        src_ref=src, dst_ref=dst, send_sem=send_sem, recv_sem=recv_sem, device_id=device, device_id_type=MESH
    )


class Step:
    def before(self, *refs):
        pass


class Gather(Step):
    line, across = True, False

    def __init__(self, x, members):
        length = members // 2
        sems = pltpu.SemaphoreType.DMA((length,))
        self.inputs = [(x, ANY)]
        self.outputs = [(jax.ShapeDtypeStruct((members * x.shape[0],) + x.shape[1:], x.dtype), ANY)]
        self.scratch = [pltpu.SemaphoreType.DMA, sems, sems, sems, pltpu.SemaphoreType.DMA((members,))]

    def run(self, here, x_ref, o_ref, own_sem, left_sem, right_sem, side_sem, recv_sem):
        pos, core, length = here.pos, here.core, here.length
        rows = x_ref.shape[0]

        def block(p, c):
            return o_ref.at[pl.ds(pl.multiple_of((p * 2 + c) * rows, rows), rows)]

        def send(src, p, sem, to_p, to_c):
            remote(src, block(p, core), sem.at[p], recv_sem.at[p * 2 + core], here.at(to_p, to_c)).start()

        def arrived(p, c):
            pltpu.make_async_copy(x_ref, block(p, c), recv_sem.at[p * 2 + c]).wait()

        def sent(sem, p):
            pltpu.make_async_copy(x_ref, block(pos, core), sem.at[p]).wait()

        @pl.when(pos > 0)
        def _():
            send(x_ref, pos, left_sem, pos - 1, core)

        @pl.when(pos < here.last)
        def _():
            send(x_ref, pos, right_sem, pos + 1, core)

        send(x_ref, pos, side_sem, pos, 1 - core)
        own = pltpu.make_async_copy(x_ref, block(pos, core), own_sem)
        own.start()
        for step in range(1, length):
            yield
            right, left = pos + step, pos - step

            @pl.when(right < length)
            def _():
                arrived(right, core)

                @pl.when(pos > 0)
                def _():
                    send(block(right, core), right, left_sem, pos - 1, core)

                send(block(right, core), right, side_sem, pos, 1 - core)

            @pl.when(left >= 0)
            def _():
                arrived(left, core)

                @pl.when(pos < here.last)
                def _():
                    send(block(left, core), left, right_sem, pos + 1, core)

                send(block(left, core), left, side_sem, pos, 1 - core)

        yield
        own.wait()

        def drain(p, carry):
            arrived(p, 1 - core)
            sent(side_sem, p)

            @pl.when((p >= pos) & (pos > 0))
            def _():
                sent(left_sem, p)

            @pl.when((p <= pos) & (pos < here.last))
            def _():
                sent(right_sem, p)

            return carry

        lax.fori_loop(0, length, drain, 0)


class GatherFfn(Step):
    line, across = True, False

    def __init__(self, x, grad_rows, w_gate, w_up, w_down, members):
        length, (rows, width), units = members // 2, x.shape, w_gate.shape[1]
        total = members * rows
        sems = pltpu.SemaphoreType.DMA((length,))
        self.units = units
        self.inputs = [(v, ANY) for v in (x, grad_rows, w_gate, w_up, w_down)]
        self.outputs = [
            (jax.ShapeDtypeStruct((total, width), BF16), VMEM),
            (jax.ShapeDtypeStruct((total, units), BF16), VMEM),
            (jax.ShapeDtypeStruct((total, units), BF16), VMEM),
            (jax.ShapeDtypeStruct((total, units), BF16), VMEM),
        ]
        self.scratch = [pltpu.VMEM(v.shape, v.dtype) for v in (grad_rows, w_gate, w_up, w_down)]
        self.scratch += [pltpu.SemaphoreType.DMA((5,)), sems, sems, sems, pltpu.SemaphoreType.DMA((members,))]

    def run(self, here, x_ref, gr_ref, wg_ref, wu_ref, wd_ref, o_ref, hid_ref, gg_ref, gu_ref,
            gr, wg, wu, wd, load_sem, left_sem, right_sem, side_sem, recv_sem):
        pos, core, length = here.pos, here.core, here.length
        rows, units, wide = x_ref.shape[0], self.units, 256

        def block(p, c):
            return o_ref.at[pl.ds(pl.multiple_of((p * 2 + c) * rows, rows), rows)]

        def send(src, p, sem, to_p, to_c):
            remote(src, block(p, core), sem.at[p], recv_sem.at[p * 2 + core], here.at(to_p, to_c)).start()

        def arrived(p, c):
            pltpu.make_async_copy(x_ref, block(p, c), recv_sem.at[p * 2 + c]).wait()

        def sent(sem, p):
            pltpu.make_async_copy(x_ref, block(pos, core), sem.at[p]).wait()

        @pl.when(pos > 0)
        def _():
            send(x_ref, pos, left_sem, pos - 1, core)

        @pl.when(pos < here.last)
        def _():
            send(x_ref, pos, right_sem, pos + 1, core)

        send(x_ref, pos, side_sem, pos, 1 - core)
        pairs = [(x_ref, block(pos, core)), (wg_ref, wg), (wu_ref, wu), (gr_ref, gr), (wd_ref, wd)]
        loads = [pltpu.make_async_copy(a, b, load_sem.at[i]) for i, (a, b) in enumerate(pairs)]
        for load in loads:
            load.start()
        yield
        for load in loads:
            load.wait()

        def use(p):
            at = pl.ds(pl.multiple_of(p * 2 * rows, 2 * rows), 2 * rows)

            def body(c, carry):
                cols = pl.ds(pl.multiple_of(c * wide, wide), wide)
                gate = dot_nn(o_ref[at], wg[:, cols])
                up = dot_nn(o_ref[at], wu[:, cols])
                back = dot_nt(gr[at], wd[cols])
                sigma = 1.0 / (1.0 + jnp.exp(-gate))
                silu = gate * sigma
                hid_ref[at, cols] = (silu * up).astype(BF16)
                gg_ref[at, cols] = (back * up * sigma * (1.0 + gate * (1.0 - sigma))).astype(BF16)
                gu_ref[at, cols] = (back * silu).astype(BF16)
                return carry

            lax.fori_loop(0, units // wide, body, 0)

        def hop(step, carry):
            right, left = pos + step, pos - step

            @pl.when((step > 0) & (right < length))
            def _():
                arrived(right, core)

                @pl.when(pos > 0)
                def _():
                    send(block(right, core), right, left_sem, pos - 1, core)

                send(block(right, core), right, side_sem, pos, 1 - core)

            @pl.when((step > 0) & (left >= 0))
            def _():
                arrived(left, core)

                @pl.when(pos < here.last)
                def _():
                    send(block(left, core), left, right_sem, pos + 1, core)

                send(block(left, core), left, side_sem, pos, 1 - core)

            def side(k, c):
                p = pos + (1 - 2 * k) * step

                @pl.when((p >= 0) & (p < length) & (step >= k))
                def _():
                    arrived(p, 1 - core)
                    use(p)

                return c

            lax.fori_loop(0, 2, side, 0)
            return carry

        lax.fori_loop(0, length, hop, 0)

        def drain(p, carry):
            sent(side_sem, p)

            @pl.when((p >= pos) & (pos > 0))
            def _():
                sent(left_sem, p)

            @pl.when((p <= pos) & (pos < here.last))
            def _():
                sent(right_sem, p)

            return carry

        lax.fori_loop(0, length, drain, 0)


class Scatter(Step):
    line, across = True, False

    def __init__(self, terms, members):
        left, right, turned = terms[0]
        rows, width = left.shape[0] // members, right.shape[0 if turned else 1]
        self.rows, self.width, self.turned = rows, width, [t[2] for t in terms]
        self.depth, self.start = right.shape[1 if turned else 0], [0] * len(terms)
        lefts = [t[0] for t in terms]
        if all(x is left for x in lefts) and len(terms) > 1:
            lefts, self.start = [left], [i * self.depth for i in range(len(terms))]
        self.inputs = [(x, VMEM) for x in lefts] + [(t[1], ANY) for t in terms]
        self.outputs = [(jax.ShapeDtypeStruct((rows, width), F32), VMEM)]
        self.scratch = [pltpu.VMEM(t[1].shape, t[1].dtype) for t in terms]
        self.scratch += [pltpu.SemaphoreType.DMA((len(terms),))] + line_sum_scratch(members, rows, width)

    def run(self, here, *refs):
        n = len(self.turned)
        m = len(self.inputs) - n
        lefts, refs = (refs[:m] * n)[:n], refs[m:]
        rights, o_ref, helds, load_sem, p_ref = refs[:n], refs[n], refs[n + 1 : 2 * n + 1], refs[2 * n + 1], refs[2 * n + 2]
        rows, wide = self.rows, 256
        loads = [pltpu.make_async_copy(w, h, load_sem.at[i]) for i, (w, h) in enumerate(zip(rights, helds))]
        for load in loads:
            load.start()

        def multiply(p):
            at = pl.ds(pl.multiple_of(p * 2 * rows, 2 * rows), 2 * rows)

            def body(c, carry):
                cols = pl.ds(pl.multiple_of(c * wide, wide), wide)
                total = None
                for left, held, turned, start in zip(lefts, helds, self.turned, self.start):
                    mine = left[at, start : start + self.depth]
                    part = dot_nt(mine, held[cols]) if turned else dot_nn(mine, held[:, cols])
                    total = part if total is None else total + part
                p_ref[at, cols] = total.astype(BF16)
                return carry

            lax.fori_loop(0, self.width // wide, body, 0)

        for load in loads:
            load.wait()
        yield from line_sum(here, rows, multiply, o_ref, p_ref, *refs[2 * n + 3 :])


def line_sum_scratch(members, rows, width):
    length = members // 2
    held = [pltpu.VMEM((members * rows, width), BF16), pltpu.VMEM((length, rows, width), BF16)]
    held += [pltpu.VMEM((length, rows, width), BF16)] * 2
    return held + [pltpu.SemaphoreType.DMA((length,))] * 6


def line_sum(here, rows, multiply, o_ref, p_ref, side_buf, left_in, right_in,
             side_send, side_recv, right_send, right_recv, left_send, left_recv):
    pos, core, length, last, tile = here.pos, here.core, here.length, here.last, 32

    def block(p, c):
        return p_ref.at[pl.ds(pl.multiple_of((p * 2 + c) * rows, rows), rows)]

    def side_copy(p):
        return remote(block(p, 1 - core), side_buf.at[p], side_send.at[p], side_recv.at[p], here.at(pos, 1 - core))

    def line_copy(p, right):
        if right:
            return remote(block(p, core), right_in.at[p], right_send.at[p], right_recv.at[p], here.at(pos + 1, core))
        return remote(block(p, core), left_in.at[p], left_send.at[p], left_recv.at[p], here.at(pos - 1, core))

    def make(p):
        multiply(p)
        side_copy(p).start()

    def add(p, incoming, final):
        def body(r, carry):
            s = pl.ds(pl.multiple_of(r * tile, tile), tile)
            mine = pl.ds(pl.multiple_of((p * 2 + core) * rows + r * tile, tile), tile)
            total = p_ref[mine].astype(F32) + side_buf[p, s].astype(F32)
            for ref in incoming:
                total = total + ref[p, s].astype(F32)
            if final:
                o_ref[s] = total
            else:
                p_ref[mine] = total.astype(BF16)
            return carry

        lax.fori_loop(0, rows // tile, body, 0)

    def move(p, right, first, source):
        side_copy(p).wait_recv()

        @pl.when(first)
        def _():
            add(p, [], False)

        @pl.when(jnp.logical_not(first))
        def _():
            line_copy(p, right).wait_recv()
            add(p, [source], False)

        line_copy(p, right).start()

    for t in range(last):

        def side(k, carry):
            p = k * t + (1 - k) * (last - t)

            @pl.when((1 - 2 * k) * (p - pos) > 0)
            def _():
                make(p)

            return carry

        lax.fori_loop(0, 2, side, 0)
        yield
        right_p, left_p = last - t + pos, t - (last - pos)

        @pl.when(t >= pos)
        def _():
            move(right_p, True, pos == 0, right_in)

        @pl.when(left_p >= 0)
        def _():
            move(left_p, False, pos == last, left_in)

    make(pos)
    yield
    side_copy(pos).wait_recv()

    @pl.when(pos == 0)
    def _():
        line_copy(pos, False).wait_recv()
        add(pos, [left_in], True)

    @pl.when(pos == last)
    def _():
        line_copy(pos, True).wait_recv()
        add(pos, [right_in], True)

    @pl.when((pos > 0) & (pos < last))
    def _():
        line_copy(pos, False).wait_recv()
        line_copy(pos, True).wait_recv()
        add(pos, [left_in, right_in], True)

    def drain(p, carry):
        side_copy(p).wait_send()

        @pl.when(p > pos)
        def _():
            line_copy(p, True).wait_send()

        @pl.when(p < pos)
        def _():
            line_copy(p, False).wait_send()

        return carry

    lax.fori_loop(0, length, drain, 0)


class Forward(Step):
    line, across = True, False

    def __init__(self, tokens, out_grad, attn_gain, ffn_gain, w_attn, w_output, cosine, sine, gain, positions, members):
        rows, width = tokens.shape
        length, size = members // 2, members * rows
        self.heads = w_output.shape[0] // HD
        inner, columns = w_output.shape[0], w_attn.shape[1]
        sems = pltpu.SemaphoreType.DMA((length,))
        self.grads = Gather(out_grad, members)
        self.inputs = [(tokens, VMEM), (out_grad, ANY), (attn_gain[None], VMEM), (ffn_gain[None], VMEM), (w_attn, ANY)]
        self.inputs += [(w_output, ANY)] + [(v, VMEM) for v in (cosine, sine, gain, positions.reshape(size, 1))]
        self.outputs = [
            (jax.ShapeDtypeStruct((size, width), BF16), ANY),
            (jax.ShapeDtypeStruct((size, columns), F32), VMEM),
            (jax.ShapeDtypeStruct((size, inner), BF16), VMEM),
            (jax.ShapeDtypeStruct((size // BLOCK, 1, self.heads * BLOCK), F32), VMEM),
            (jax.ShapeDtypeStruct((size, width), BF16), ANY),
            (jax.ShapeDtypeStruct((rows, width), F32), VMEM),
            (jax.ShapeDtypeStruct((rows, width), BF16), VMEM),
        ]
        self.scratch = [pltpu.VMEM((size, width), BF16), pltpu.VMEM(w_attn.shape, BF16), pltpu.VMEM(w_output.shape, BF16)]
        self.scratch += [pltpu.VMEM((size, inner), BF16), pltpu.VMEM((size, HD), BF16), pltpu.VMEM((size, 2 * HD), BF16)]
        self.scratch += [pltpu.VMEM((self.heads * BLOCK, 2 * HD), F32), pltpu.SemaphoreType.DMA((3,))]
        self.scratch += [sems, sems, sems, pltpu.SemaphoreType.DMA((members,))]
        self.scratch += self.grads.scratch + line_sum_scratch(members, rows, width)

    def before(self, here, tok_ref, og_ref, again_ref, fgain_ref, wa_ref, wo_ref, cos_ref, sin_ref, gain_ref, pos_ref,
               one_ref, proj_ref, ctx_ref, lse_ref, gr_ref, branch_ref, two_ref, all_ref, wa, wo, *rest):
        load_sem = rest[4]
        pltpu.make_async_copy(wa_ref, wa, load_sem.at[0]).start()
        pltpu.make_async_copy(wo_ref, wo, load_sem.at[1]).start()
        rows = tok_ref.shape[0]
        me = (here.pos * 2 + here.core) * rows

        def body(r, carry):
            at = pl.ds(pl.multiple_of(r * 32, 32), 32)
            x = tok_ref[at].astype(F32)
            inv = lax.rsqrt(jnp.mean(x * x, -1, keepdims=True) + EPSILON)
            all_ref[pl.ds(pl.multiple_of(me + r * 32, 32), 32)] = (x * inv * again_ref[...]).astype(BF16)
            return carry

        lax.fori_loop(0, rows // 32, body, 0)

    def run(self, here, tok_ref, og_ref, again_ref, fgain_ref, wa_ref, wo_ref, cos_ref, sin_ref, gain_ref, pos_ref,
            one_ref, proj_ref, ctx_ref, lse_ref, gr_ref, branch_ref, two_ref, all_ref, wa, wo,
            q_ref, k_ref, v_ref, acc_ref, load_sem, left_sem, right_sem, side_sem, recv_sem, *rest):
        pos, core, length = here.pos, here.core, here.length
        rows, heads, inner = tok_ref.shape[0], self.heads, self.heads * HD
        lane = lax.broadcasted_iota(jnp.int32, (1, HD), 1)

        def block(p, c):
            return all_ref.at[pl.ds(pl.multiple_of((p * 2 + c) * rows, rows), rows)]

        def send(p, sem, to_p, to_c):
            remote(block(p, core), block(p, core), sem.at[p], recv_sem.at[p * 2 + core], here.at(to_p, to_c)).start()

        def arrived(p, c):
            pltpu.make_async_copy(block(p, c), block(p, c), recv_sem.at[p * 2 + c]).wait()

        def sent(sem, p):
            pltpu.make_async_copy(block(p, core), block(p, core), sem.at[p]).wait()

        def use(p):
            at = pl.ds(pl.multiple_of(p * BLOCK, BLOCK), BLOCK)
            x = dot_nn(all_ref[at], wa[...])
            proj_ref[at] = x
            cosine, sine = wide(cos_ref[at], inner + 2 * HD), wide(sin_ref[at], inner + 2 * HD)
            unit, _ = normed(x)
            spun = turn(unit * gain_ref[...], cosine, sine)
            q_ref[at] = (spun[:, :inner].astype(BF16) * HD**-0.5).astype(BF16)
            k_ref[at] = spun[:, inner : inner + HD].astype(BF16)
            ones = jnp.broadcast_to(jnp.where(lane == 0, 1.0, 0.0), (BLOCK, HD)).astype(BF16)
            v_ref[at] = jnp.concatenate([x[:, inner + HD :].astype(BF16), ones], 1)

        def hop(step, carry):
            right, left = pos + step, pos - step

            @pl.when(right < length)
            def _():
                @pl.when(step > 0)
                def _():
                    arrived(right, core)

                @pl.when(pos > 0)
                def _():
                    send(right, left_sem, pos - 1, core)

                send(right, side_sem, pos, 1 - core)

            @pl.when(left >= 0)
            def _():
                @pl.when(step > 0)
                def _():
                    arrived(left, core)

                @pl.when(pos < here.last)
                def _():
                    send(left, right_sem, pos + 1, core)

                @pl.when(step > 0)
                def _():
                    send(left, side_sem, pos, 1 - core)

            def side(k, c):
                p = pos + (1 - 2 * k) * step

                @pl.when((p >= 0) & (p < length) & (step >= k))
                def _():
                    arrived(p, 1 - core)
                    use(p)

                return c

            lax.fori_loop(0, 2, side, 0)
            return carry

        pltpu.make_async_copy(wa_ref, wa, load_sem.at[0]).wait()
        lax.fori_loop(0, length, hop, 0)
        keep = pltpu.make_async_copy(all_ref, one_ref, load_sem.at[2])
        keep.start()
        pltpu.make_async_copy(wo_ref, wo, load_sem.at[1]).wait()

        def attend(i):
            at = pl.ds(pl.multiple_of(i * BLOCK, BLOCK), BLOCK)
            query = q_ref[at]
            stacked = jnp.concatenate([query[:, h * HD : (h + 1) * HD] for h in range(heads)], 0)
            acc_ref[...] = jnp.zeros_like(acc_ref)
            index = i * BLOCK + lax.broadcasted_iota(jnp.int32, (BLOCK, 1), 0)
            start = index - pos_ref[at]

            def keys(j, c):
                cols = pl.ds(pl.multiple_of(j * BLOCK, BLOCK), BLOCK)
                scores = dot_nt(stacked, k_ref[cols])
                place = j * BLOCK + lax.broadcasted_iota(jnp.int32, (1, BLOCK), 1)
                seen = (place >= start) & (place <= index)
                expo = [
                    jnp.where(seen, jnp.exp(scores[h * BLOCK : (h + 1) * BLOCK]), 0.0).astype(BF16)
                    for h in range(heads)
                ]
                acc_ref[...] += dot_nn(jnp.concatenate(expo, 0), v_ref[cols])
                return c

            lax.fori_loop(0, i + 1, keys, 0)
            outs, logs = [], []
            for h in range(heads):
                acc = acc_ref[pl.ds(h * BLOCK, BLOCK)]
                outs.append((acc[:, :HD] * (1.0 / acc[:, HD : HD + 1])).astype(BF16))
                logs.append(jnp.log(acc.T[HD : HD + 1]))
            ctx_ref[at] = jnp.concatenate(outs, 1)
            lse_ref[i] = jnp.concatenate(logs, 1)

        n = len(self.grads.scratch)
        held = rest[n:]
        p_ref, width = held[0], tok_ref.shape[1]

        def multiply(p):
            attend(p)
            at = pl.ds(pl.multiple_of(p * BLOCK, BLOCK), BLOCK)

            def body(c, carry):
                cols = pl.ds(pl.multiple_of(c * 512, 512), 512)
                p_ref[at, cols] = dot_nn(ctx_ref[at], wo[:, cols]).astype(BF16)
                return carry

            lax.fori_loop(0, width // 512, body, 0)

        weave([self.grads.run(here, og_ref, gr_ref, *rest[:n]), line_sum(here, rows, multiply, branch_ref, *held)])

        def body(r, carry):
            at = pl.ds(pl.multiple_of(r * 32, 32), 32)
            x = tok_ref[at].astype(F32) + branch_ref[at]
            inv = lax.rsqrt(jnp.mean(x * x, -1, keepdims=True) + EPSILON)
            two_ref[at] = (x * inv * fgain_ref[...]).astype(BF16)
            return carry

        lax.fori_loop(0, rows // 32, body, 0)

        def drain(p, carry):
            sent(side_sem, p)

            @pl.when((p >= pos) & (pos > 0))
            def _():
                sent(left_sem, p)

            @pl.when((p <= pos) & (pos < here.last))
            def _():
                sent(right_sem, p)

            return carry

        lax.fori_loop(0, length, drain, 0)
        keep.wait()
        yield


class Across(Step):
    line, across = False, True

    def __init__(self, x, parts, colours, late=0):
        self.bits, self.colours, self.late = parts.bit_length() - 1, colours, late
        rows, width = x.shape
        self.inputs = [(x, VMEM)]
        self.outputs = [(jax.ShapeDtypeStruct(x.shape, x.dtype), VMEM)]
        self.scratch = [pltpu.VMEM((rows, width), x.dtype)]
        for _ in colours:
            part = rows // len(colours)
            self.scratch += [pltpu.VMEM((part >> (s + 1), width), x.dtype) for s in range(self.bits)]
            self.scratch += [pltpu.SemaphoreType.DMA((2 * self.bits,))] * 2

    def run(self, here, x_ref, o_ref, sum_ref, *rest):
        for _ in range(self.late):
            yield
        n, rows = self.bits + 2, x_ref.shape[0] // len(self.colours)
        live = [
            self.one(here, backwards, i * rows, rows, x_ref, o_ref, sum_ref, *rest[i * n : (i + 1) * n])
            for i, backwards in enumerate(self.colours)
        ]
        while live:
            live = [r for r in live if next(r, live) is not live]
            yield

    def one(self, here, backwards, start, size, x_ref, o_ref, sum_ref, *rest):
        taken, (send_sem, recv_sem) = rest[: self.bits], rest[self.bits :]
        order = list(range(self.bits))[:: -1 if backwards else 1]
        copies, tile = [], 16

        def part(ref, at, count):
            return ref.at[pl.ds(pl.multiple_of(at, count), count)]

        for s, bit in enumerate(order):
            mine, device = here.partner(bit)
            half = size // 2
            keep, give = start + mine * half, start + (1 - mine) * half
            source = x_ref if s == 0 else sum_ref
            target = o_ref if s == self.bits - 1 else sum_ref
            copy = remote(part(source, give, half), taken[s], send_sem.at[s], recv_sem.at[s], device)
            copy.start()
            copies.append(copy)
            yield
            copy.wait_recv()

            def body(r, carry):
                at = pl.ds(pl.multiple_of(keep + r * tile, tile), tile)
                got = taken[s][pl.ds(pl.multiple_of(r * tile, tile), tile)]
                target[at] = (source[at].astype(F32) + got.astype(F32)).astype(target.dtype)
                return carry

            lax.fori_loop(0, half // tile, body, 0)
            start, size = keep, half
        for s, bit in enumerate(order[::-1]):
            mine, device = here.partner(bit)
            n = self.bits + s
            copy = remote(part(o_ref, start, size), part(o_ref, start, size), send_sem.at[n], recv_sem.at[n], device)
            copy.start()
            copies.append(copy)
            yield
            copy.wait_recv()
            start, size = start - mine * size, size * 2
        for copy in copies:
            copy.wait_send()


class KeyValue(Step):
    line, across = True, True

    def __init__(self, x, width, members, parts):
        self.width, self.extra, self.members = width, x.shape[0] - width, members
        self.sum, self.all = Across(x, parts, (False,)), Gather(x, members)
        self.inputs = [(x, VMEM)]
        flat = jax.ShapeDtypeStruct((width, KV * HD), BF16)
        self.outputs = [(flat, VMEM), (flat, VMEM), (jax.ShapeDtypeStruct((self.extra, 2 * HD), F32), VMEM)]
        self.scratch = [pltpu.VMEM(x.shape, x.dtype), pltpu.VMEM((members * x.shape[0], 2 * HD), x.dtype)]
        self.scratch += self.sum.scratch + self.all.scratch

    def run(self, here, x_ref, key_ref, value_ref, small_ref, sum_ref, all_ref, *rest):
        n = len(self.sum.scratch)
        first = self.sum.run(here, x_ref, sum_ref, *rest[:n])
        next(first)
        yield
        for _ in first:
            pass
        yield from self.all.run(here, sum_ref, all_ref, *rest[n:])
        rows, share, tile = self.width + self.extra, self.members // KV, 128

        def block(group, at, count):
            total = 0.0
            for k in range(share):
                begin = pl.multiple_of((group * share + k) * rows + at, 16)
                total = total + all_ref[pl.ds(begin, count)].astype(F32)
            return total

        for pair in range(KV // 2):
            cols = slice(2 * HD * pair, 2 * HD * (pair + 1))

            def body(r, carry):
                at = pl.ds(pl.multiple_of(r * tile, tile), tile)
                one, two = block(2 * pair, r * tile, tile), block(2 * pair + 1, r * tile, tile)
                key_ref[at, cols] = jnp.concatenate([one[:, :HD], two[:, :HD]], 1).astype(BF16)
                value_ref[at, cols] = jnp.concatenate([one[:, HD:], two[:, HD:]], 1).astype(BF16)
                return carry

            lax.fori_loop(0, self.width // tile, body, 0)
        small = 0.0
        for group in range(KV):
            small = small + block(group, self.width, self.extra)
        small_ref[...] = small


def together(steps, members, parts, collective_id, vmem=48):
    counts = [(len(s.inputs), len(s.outputs), len(s.scratch)) for s in steps]

    def kernel(*refs):
        refs = list(refs)
        given = [[refs.pop(0) for _ in range(c[0])] for c in counts]
        made = [[refs.pop(0) for _ in range(c[1])] for c in counts]
        held = [[refs.pop(0) for _ in range(c[2])] for c in counts]
        here = Place(members, parts)
        peers = here.greet(any(s.line for s in steps), any(s.across for s in steps))
        for s, g, m, h in zip(steps, given, made, held):
            s.before(here, *g, *m, *h)
        here.meet(peers)
        weave([s.run(here, *g, *m, *h) for s, g, m, h in zip(steps, given, made, held)])

    return pl.pallas_call(
        kernel,
        out_shape=[o for s in steps for o, _ in s.outputs],
        in_specs=[m for s in steps for _, m in s.inputs],
        out_specs=[m for s in steps for _, m in s.outputs],
        scratch_shapes=[h for s in steps for h in s.scratch],
        compiler_params=pltpu.CompilerParams(
            collective_id=collective_id, has_side_effects=True, vmem_limit_bytes=vmem << 20
        ),
        cost_estimate=pl.CostEstimate(flops=1, bytes_accessed=1, transcendentals=0),
    )(*[x for s in steps for x, _ in s.inputs])


def dot_nn(a, b):
    return lax.dot_general(a, b, (((1,), (0,)), ((), ())), preferred_element_type=F32)

def dot_nt(a, b):
    return lax.dot_general(a, b, (((1,), (1,)), ((), ())), preferred_element_type=F32)

def group_mean(x):
    width = x.shape[1]
    row = lax.broadcasted_iota(jnp.int32, (width, width), 0) // HD
    col = lax.broadcasted_iota(jnp.int32, (width, width), 1) // HD
    ones = jnp.where(row == col, 1.0 / HD, 0.0).astype(F32)
    return jnp.dot(x, ones, precision=lax.Precision.HIGHEST, preferred_element_type=F32)

def half_turn(x):
    width = x.shape[1]
    lane = lax.broadcasted_iota(jnp.int32, (1, width), 1)
    first = lax.rem(lane, HD) < HD // 2
    up = pltpu.roll(x, HD // 2, 1)
    down = pltpu.roll(x, width - HD // 2, 1)
    return jnp.where(first, -down, up)

def wide(table, width):
    return jnp.concatenate([table] * (width // table.shape[1]), 1)

def normed(x):
    inv = lax.rsqrt(group_mean(x * x) + EPSILON)
    return x * inv, inv

def turn(x, cosine, sine):
    return x * cosine + half_turn(x) * sine

def turn_back(x, cosine, sine):
    return x * cosine - half_turn(x) * sine

def stack_lanes(x, heads):
    return jnp.concatenate([x[h * HD:(h + 1) * HD] for h in range(heads)], 1)

def attend_back_kernel(heads, proj_ref, cos_ref, sin_ref, gain_ref, pos_ref, ctx_ref, grad_ref, lse_ref,
                       out_ref, sums_ref, k_ref, kt_ref, v_ref, dk_ref, dv_ref, dq_ref):
    width = heads * HD
    scale = HD ** -0.5
    count = proj_ref.shape[0] // BLOCK
    gain = gain_ref[...]
    def prepare(i, carry):
        rows = pl.ds(pl.multiple_of(i * BLOCK, BLOCK), BLOCK)
        x = proj_ref[rows, width:]
        unit, _ = normed(x)
        spun = turn(unit * gain[:, width:], cos_ref[rows], sin_ref[rows])
        k_ref[rows] = spun[:, :HD].astype(BF16)
        kt_ref[i] = spun.T[:HD].astype(BF16)
        v_ref[rows] = x[:, HD:].astype(BF16)
        dk_ref[rows] = jnp.zeros((BLOCK, HD), F32)
        dv_ref[rows] = jnp.zeros((BLOCK, HD), F32)
        return carry
    lax.fori_loop(0, count, prepare, 0)
    sums_ref[...] = jnp.zeros_like(sums_ref)
    def outer(i, carry):
        rows = pl.ds(pl.multiple_of(i * BLOCK, BLOCK), BLOCK)
        x = proj_ref[rows, :width]
        cosine, sine = wide(cos_ref[rows], width), wide(sin_ref[rows], width)
        unit, inv = normed(x)
        query = (turn(unit * gain[:, :width], cosine, sine).astype(BF16).astype(F32) * scale)
        query_t = stack_lanes(query.T, heads).astype(BF16)
        query = query.astype(BF16)
        query_s = jnp.concatenate([query[:, h * HD:(h + 1) * HD] for h in range(heads)], 0)
        grad = grad_ref[rows]
        grad_s = jnp.concatenate([grad[:, h * HD:(h + 1) * HD] for h in range(heads)], 0)
        grad_t = stack_lanes(grad.astype(F32).T, heads)
        ctx_t = stack_lanes(ctx_ref[rows].astype(F32).T, heads)
        delta = jnp.sum(grad_t * ctx_t, 0, keepdims=True)
        grad_t = grad_t.astype(BF16)
        lse = lse_ref[i]
        index = i * BLOCK + lax.broadcasted_iota(jnp.int32, (1, BLOCK), 1)
        start = index - pos_ref[i]
        dq_ref[...] = jnp.zeros_like(dq_ref)
        def inner(j, c):
            cols = pl.ds(pl.multiple_of(j * BLOCK, BLOCK), BLOCK)
            scores = dot_nn(k_ref[cols], query_t)
            grad_probs = dot_nn(v_ref[cols], grad_t)
            place = j * BLOCK + lax.broadcasted_iota(jnp.int32, (BLOCK, 1), 0)
            seen = (place >= start) & (place <= index)
            probs, back = [], []
            for h in range(heads):
                s = slice(h * BLOCK, (h + 1) * BLOCK)
                exact = jnp.where(seen, jnp.exp(scores[:, s] - lse[:, s]), 0.0)
                probs.append(exact.astype(BF16))
                back.append((exact * (grad_probs[:, s] - delta[:, s])).astype(BF16))
            probs = jnp.concatenate(probs, 1)
            back = jnp.concatenate(back, 1)
            dv_ref[cols] += dot_nn(probs, grad_s)
            dk_ref[cols] += dot_nn(back, query_s)
            dq_ref[...] += dot_nn(kt_ref[j], back)
            return c
        lax.fori_loop(0, i + 1, inner, 0)
        dq = jnp.concatenate([dq_ref[:, h * BLOCK:(h + 1) * BLOCK] for h in range(heads)], 0).T * scale
        dqn = turn_back(dq, cosine, sine)
        sums_ref[:, :width] += jnp.sum(dqn * unit, 0, keepdims=True)
        e = dqn * gain[:, :width]
        out_ref[rows, :width] = (inv * (e - unit * group_mean(e * unit))).astype(BF16)
        return carry
    lax.fori_loop(0, count, outer, 0)
    def finish(i, carry):
        rows = pl.ds(pl.multiple_of(i * BLOCK, BLOCK), BLOCK)
        x = proj_ref[rows, width:]
        unit, inv = normed(x)
        dv = dv_ref[rows]
        dk = jnp.concatenate([dk_ref[rows], dv], 1)
        dkn = turn_back(dk, cos_ref[rows], sin_ref[rows])
        sums_ref[:, width:] += jnp.sum(dkn * unit, 0, keepdims=True)
        e = dkn * gain[:, width:]
        dkp = inv * (e - unit * group_mean(e * unit))
        lane = lax.broadcasted_iota(jnp.int32, (1, 2 * HD), 1)
        out_ref[rows, width:] = jnp.where(lane < HD, dkp, dk).astype(BF16)
        return carry
    lax.fori_loop(0, count, finish, 0)

def attend_back(proj, cosine, sine, gain, positions, context, grad_context, lse, heads):
    size = proj.shape[0]
    count = size // BLOCK
    vm = pl.BlockSpec(memory_space=pltpu.VMEM)
    return pl.pallas_call(
        functools.partial(attend_back_kernel, heads),
        out_shape=(jax.ShapeDtypeStruct(proj.shape, BF16), jax.ShapeDtypeStruct((1, proj.shape[1]), F32)),
        in_specs=[vm] * 8, out_specs=(vm, vm),
        scratch_shapes=[pltpu.VMEM((size, HD), BF16), pltpu.VMEM((count, HD, BLOCK), BF16), pltpu.VMEM((size, HD), BF16),
                        pltpu.VMEM((size, HD), F32), pltpu.VMEM((size, HD), F32), pltpu.VMEM((HD, heads * BLOCK), F32)],
        compiler_params=pltpu.CompilerParams(vmem_limit_bytes=40 << 20),
        cost_estimate=pl.CostEstimate(flops=1, bytes_accessed=1, transcendentals=0),
    )(proj, cosine, sine, gain, positions.reshape(count, 1, BLOCK), context, grad_context, lse)


def matmul(left, right):
    return jnp.dot(left, right, preferred_element_type=F32)


def matmul_left_t(left, right):
    return lax.dot_general(left, right, (((0,), (0,)), ((), ())), preferred_element_type=F32)


def matmul_right_t(left, right):
    return lax.dot_general(left, right, (((1,), (1,)), ((), ())), preferred_element_type=F32)


def rope_tables(position_row):
    half = HD // 2
    freq = ROPE_BASE ** (-jnp.arange(half, dtype=F32) / half)
    angle = position_row.astype(F32)[:, None] * freq[None, :]
    return jnp.tile(jnp.cos(angle), (1, 4)), jnp.tile(jnp.sin(angle), (1, 4))


def norm_back(grad_normed, unit, inverse, gain):
    scaled = grad_normed * gain
    return inverse * (scaled - unit * jnp.mean(scaled * unit, -1, keepdims=True))


def after(first, *later):
    return lax.optimization_barrier((first,) + later)


def per_device(
    tokens,
    seg_ids,
    positions,
    w_query,
    w_key,
    w_value,
    w_output,
    w_gate,
    w_up,
    w_down,
    attn_gain,
    ffn_gain,
    query_gain,
    key_gain,
    out_grad,
):
    members, parts = lax.axis_size("mp"), lax.axis_size("dp")
    width = tokens.shape[1]
    query_width = w_query.shape[1]
    heads = query_width // HD
    ffn_width = w_gate.shape[1]
    share = members // KV
    group = lax.axis_index("mp") // share

    tokens_f = tokens.astype(F32)
    inv_one = lax.rsqrt(jnp.mean(tokens_f * tokens_f, -1, keepdims=True) + EPSILON)
    normed_one = tokens_f * inv_one
    key_cols = lax.dynamic_slice_in_dim(w_key, group * HD, HD, 1)
    value_cols = lax.dynamic_slice_in_dim(w_value, group * HD, HD, 1)
    w_attn = jnp.concatenate([w_query, key_cols, value_cols], 1)
    cosine, sine = rope_tables(positions)
    gain = jnp.concatenate([jnp.tile(query_gain, heads), key_gain, jnp.ones(HD, F32)])[None]

    rows_one, projected, context, lse, grad_rows, attn_branch, h_two = together(
        [
            Forward(
                tokens, out_grad, attn_gain, ffn_gain, w_attn, w_output, cosine, sine, gain, positions, members
            )
        ],
        members,
        parts,
        0,
        58,
    )
    rows_two, hidden, grad_gate, grad_up = together(
        [GatherFfn(h_two, grad_rows, w_gate, w_up, w_down, members)], members, parts, 5, 58
    )
    residual_mid = tokens_f + attn_branch
    inv_two = lax.rsqrt(jnp.mean(residual_mid * residual_mid, -1, keepdims=True) + EPSILON)
    normed_two = residual_mid * inv_two
    ffn_parts = (
        matmul_left_t(rows_two, grad_gate).astype(BF16),
        matmul_left_t(rows_two, grad_up).astype(BF16),
    )
    ffn_parts, grad_gate, grad_up, hidden = lax.optimization_barrier((ffn_parts, grad_gate, grad_up, hidden))
    grad_w_gate, grad_w_up = lax.psum(ffn_parts, "dp")
    down_part = matmul_left_t(hidden, grad_rows).astype(BF16)

    grad_h_two = together(
        [Scatter([(grad_gate, w_gate, True), (grad_up, w_up, True)], members)],
        members,
        parts,
        6,
        58,
    )[0]
    grad_ffn_gain = jnp.sum(grad_h_two * normed_two, 0)
    grad_mid = out_grad.astype(F32) + norm_back(grad_h_two, normed_two, inv_two, ffn_gain)
    grad_attn_rows, ffn_branch = together(
        [Gather(grad_mid.astype(BF16), members), Scatter([(hidden, w_down, False)], members)],
        members,
        parts,
        2,
    )
    grad_context = matmul_right_t(grad_attn_rows, w_output).astype(BF16)
    grad_proj, gain_sums = attend_back(
        projected, cosine, sine, gain, positions, context, grad_context, lse, heads
    )
    output_part = matmul_left_t(context, grad_attn_rows).astype(BF16)
    grad_w_attn = matmul_left_t(rows_one, grad_proj)
    grad_attn_gain = jnp.sum(w_attn.astype(F32) * grad_w_attn, 1) / attn_gain

    small = jnp.concatenate(
        [
            grad_attn_gain,
            grad_ffn_gain,
            jnp.sum(gain_sums[0, :query_width].reshape(heads, HD), 0),
            gain_sums[0, query_width : query_width + HD],
            jnp.sum(tokens_f * tokens_f)[None],
        ]
    )
    unit = 16 * parts
    extra = -(-small.shape[0] // (unit * 2 * HD)) * unit
    small_rows = jnp.pad(small, (0, extra * 2 * HD - small.shape[0])).reshape(extra, 2 * HD)
    kv_part = jnp.concatenate([grad_w_attn[:, query_width:], small_rows], 0).astype(BF16)
    query_part = grad_w_attn[:, :query_width].astype(BF16)
    grad_w_key, grad_w_value, small_sum, grad_h_one, grad_w_output, grad_w_query, grad_w_down = together(
        [
            KeyValue(kv_part, width, members, parts),
            Scatter([(grad_proj, w_attn, True)], members),
            Across(output_part, parts, (False,), 2),
            Across(query_part, parts, (True,), 2),
            Across(down_part, parts, (False, True), 2),
        ],
        members,
        parts,
        3,
        58,
    )
    small_sum = small_sum.reshape(-1)
    entry_count = tokens.size * parts * members
    at = 2 * width
    residual_rms = jnp.sqrt(small_sum[at + 2 * HD : at + 2 * HD + 1] / entry_count)

    grad_tokens = (grad_mid + norm_back(grad_h_one, normed_one, inv_one, attn_gain)).astype(BF16)
    output = (residual_mid + ffn_branch).astype(BF16)
    branch_rms = jnp.stack(
        [
            jnp.sqrt(jnp.mean(attn_branch * attn_branch, -1)),
            jnp.sqrt(jnp.mean(ffn_branch * ffn_branch, -1)),
        ]
    )
    return (
        output,
        grad_tokens,
        grad_w_query.astype(F32),
        grad_w_key.astype(F32),
        grad_w_value.astype(F32),
        grad_w_output.astype(F32),
        grad_w_gate.astype(F32),
        grad_w_up.astype(F32),
        grad_w_down.astype(F32),
        small_sum[:width],
        small_sum[width:at],
        small_sum[at : at + HD],
        small_sum[at + HD : at + 2 * HD],
        residual_rms,
        branch_rms,
    )


def solution(mesh):
    row, whole, column = P(("dp", "mp"), None), P(), P(None, "mp")
    lead = P("mp", None)
    return jax.shard_map(
        per_device,
        mesh=mesh,
        in_specs=(row, P("dp"), P("dp"), column, whole, whole, lead, column, column, lead)
        + (whole,) * 4
        + (row,),
        out_specs=(row, row, column, whole, whole, lead, column, column, lead)
        + (whole,) * 5
        + (P(None, ("dp", "mp")),),
        check_vma=False,
    )
```

```python
import functools

import jax
import jax.numpy as jnp
import numpy as np
from jax import lax
from jax.experimental import pallas as pl
from jax.experimental.pallas import tpu as pltpu
from jax.sharding import PartitionSpec as P

HEADS = 32
KV = 8
HD = 64
EPSILON = 1e-06
ROPE_BASE = 10000.0
BLOCK = 256
F32 = jnp.float32
BF16 = jnp.bfloat16
MESH = pl.DeviceIdType.MESH


ANY = pl.BlockSpec(memory_space=pl.ANY)
VMEM = pl.BlockSpec(memory_space=pltpu.VMEM)


class Place:
    def __init__(self, members, parts):
        me = lax.axis_index("mp")
        self.dp, self.pos, self.core = lax.axis_index("dp"), me // 2, lax.rem(me, 2)
        self.length, self.parts = members // 2, parts
        self.last = self.length - 1

    def at(self, pos, core):
        return (self.dp, pos * 2 + core)

    def partner(self, bit):
        mine = lax.rem(self.dp // (1 << bit), 2)
        return mine, (self.dp + (1 - 2 * mine) * (1 << bit), self.pos * 2 + self.core)

    def bits(self):
        return self.parts.bit_length() - 1

    def greet(self, line, across):
        barrier = pltpu.get_barrier_semaphore()

        def tell(device):
            pl.semaphore_signal(barrier, inc=1, device_id=device, device_id_type=MESH)

        peers = 0
        if line:
            tell(self.at(self.pos, 1 - self.core))

            @pl.when(self.pos > 0)
            def _():
                tell(self.at(self.pos - 1, self.core))

            @pl.when(self.pos < self.last)
            def _():
                tell(self.at(self.pos + 1, self.core))

            peers = 1 + jnp.minimum(self.pos, 1) + jnp.minimum(self.last - self.pos, 1)
        if across:
            for bit in range(self.bits()):
                tell(self.partner(bit)[1])
            peers = peers + self.bits()
        return peers

    def meet(self, peers):
        pl.semaphore_wait(pltpu.get_barrier_semaphore(), peers)


def weave(live):
    while live:
        live = [r for r in live if next(r, live) is not live]


def remote(src, dst, send_sem, recv_sem, device):
    return pltpu.make_async_remote_copy(
        src_ref=src, dst_ref=dst, send_sem=send_sem, recv_sem=recv_sem, device_id=device, device_id_type=MESH
    )


class Step:
    def before(self, *refs):
        pass


class Gather(Step):
    line, across = True, False

    def __init__(self, x, members):
        length = members // 2
        sems = pltpu.SemaphoreType.DMA((length,))
        self.inputs = [(x, ANY)]
        self.outputs = [(jax.ShapeDtypeStruct((members * x.shape[0],) + x.shape[1:], x.dtype), ANY)]
        self.scratch = [pltpu.SemaphoreType.DMA, sems, sems, sems, pltpu.SemaphoreType.DMA((members,))]

    def run(self, here, x_ref, o_ref, own_sem, left_sem, right_sem, side_sem, recv_sem):
        pos, core, length = here.pos, here.core, here.length
        rows = x_ref.shape[0]

        def block(p, c):
            return o_ref.at[pl.ds(pl.multiple_of((p * 2 + c) * rows, rows), rows)]

        def send(src, p, sem, to_p, to_c):
            remote(src, block(p, core), sem.at[p], recv_sem.at[p * 2 + core], here.at(to_p, to_c)).start()

        def arrived(p, c):
            pltpu.make_async_copy(x_ref, block(p, c), recv_sem.at[p * 2 + c]).wait()

        def sent(sem, p):
            pltpu.make_async_copy(x_ref, block(pos, core), sem.at[p]).wait()

        @pl.when(pos > 0)
        def _():
            send(x_ref, pos, left_sem, pos - 1, core)

        @pl.when(pos < here.last)
        def _():
            send(x_ref, pos, right_sem, pos + 1, core)

        send(x_ref, pos, side_sem, pos, 1 - core)
        own = pltpu.make_async_copy(x_ref, block(pos, core), own_sem)
        own.start()
        for step in range(1, length):
            yield
            right, left = pos + step, pos - step

            @pl.when(right < length)
            def _():
                arrived(right, core)

                @pl.when(pos > 0)
                def _():
                    send(block(right, core), right, left_sem, pos - 1, core)

                send(block(right, core), right, side_sem, pos, 1 - core)

            @pl.when(left >= 0)
            def _():
                arrived(left, core)

                @pl.when(pos < here.last)
                def _():
                    send(block(left, core), left, right_sem, pos + 1, core)

                send(block(left, core), left, side_sem, pos, 1 - core)

        yield
        own.wait()

        def drain(p, carry):
            arrived(p, 1 - core)
            sent(side_sem, p)

            @pl.when((p >= pos) & (pos > 0))
            def _():
                sent(left_sem, p)

            @pl.when((p <= pos) & (pos < here.last))
            def _():
                sent(right_sem, p)

            return carry

        lax.fori_loop(0, length, drain, 0)


class GatherFfn(Step):
    line, across = True, False

    def __init__(self, x, grad_rows, w_gate, w_up, w_down, members):
        length, (rows, width), units = members // 2, x.shape, w_gate.shape[1]
        total = members * rows
        sems = pltpu.SemaphoreType.DMA((length,))
        self.units = units
        self.inputs = [(v, ANY) for v in (x, grad_rows, w_gate, w_up, w_down)]
        self.outputs = [
            (jax.ShapeDtypeStruct((total, width), BF16), VMEM),
            (jax.ShapeDtypeStruct((total, units), BF16), VMEM),
            (jax.ShapeDtypeStruct((total, units), BF16), VMEM),
            (jax.ShapeDtypeStruct((total, units), BF16), VMEM),
        ]
        self.scratch = [pltpu.VMEM(v.shape, v.dtype) for v in (grad_rows, w_gate, w_up, w_down)]
        self.scratch += [pltpu.SemaphoreType.DMA((5,)), sems, sems, sems, pltpu.SemaphoreType.DMA((members,))]

    def run(self, here, x_ref, gr_ref, wg_ref, wu_ref, wd_ref, o_ref, hid_ref, gg_ref, gu_ref,
            gr, wg, wu, wd, load_sem, left_sem, right_sem, side_sem, recv_sem):
        pos, core, length = here.pos, here.core, here.length
        rows, units, wide = x_ref.shape[0], self.units, 256

        def block(p, c):
            return o_ref.at[pl.ds(pl.multiple_of((p * 2 + c) * rows, rows), rows)]

        def send(src, p, sem, to_p, to_c):
            remote(src, block(p, core), sem.at[p], recv_sem.at[p * 2 + core], here.at(to_p, to_c)).start()

        def arrived(p, c):
            pltpu.make_async_copy(x_ref, block(p, c), recv_sem.at[p * 2 + c]).wait()

        def sent(sem, p):
            pltpu.make_async_copy(x_ref, block(pos, core), sem.at[p]).wait()

        @pl.when(pos > 0)
        def _():
            send(x_ref, pos, left_sem, pos - 1, core)

        @pl.when(pos < here.last)
        def _():
            send(x_ref, pos, right_sem, pos + 1, core)

        send(x_ref, pos, side_sem, pos, 1 - core)
        pairs = [(x_ref, block(pos, core)), (wg_ref, wg), (wu_ref, wu), (gr_ref, gr), (wd_ref, wd)]
        loads = [pltpu.make_async_copy(a, b, load_sem.at[i]) for i, (a, b) in enumerate(pairs)]
        for load in loads:
            load.start()
        yield
        for load in loads:
            load.wait()

        def use(p):
            at = pl.ds(pl.multiple_of(p * 2 * rows, 2 * rows), 2 * rows)

            def body(c, carry):
                cols = pl.ds(pl.multiple_of(c * wide, wide), wide)
                gate = dot_nn(o_ref[at], wg[:, cols])
                up = dot_nn(o_ref[at], wu[:, cols])
                back = dot_nt(gr[at], wd[cols])
                sigma = 1.0 / (1.0 + jnp.exp(-gate))
                silu = gate * sigma
                hid_ref[at, cols] = (silu * up).astype(BF16)
                gg_ref[at, cols] = (back * up * sigma * (1.0 + gate * (1.0 - sigma))).astype(BF16)
                gu_ref[at, cols] = (back * silu).astype(BF16)
                return carry

            lax.fori_loop(0, units // wide, body, 0)

        def hop(step, carry):
            right, left = pos + step, pos - step

            @pl.when((step > 0) & (right < length))
            def _():
                arrived(right, core)

                @pl.when(pos > 0)
                def _():
                    send(block(right, core), right, left_sem, pos - 1, core)

                send(block(right, core), right, side_sem, pos, 1 - core)

            @pl.when((step > 0) & (left >= 0))
            def _():
                arrived(left, core)

                @pl.when(pos < here.last)
                def _():
                    send(block(left, core), left, right_sem, pos + 1, core)

                send(block(left, core), left, side_sem, pos, 1 - core)

            def side(k, c):
                p = pos + (1 - 2 * k) * step

                @pl.when((p >= 0) & (p < length) & (step >= k))
                def _():
                    arrived(p, 1 - core)
                    use(p)

                return c

            lax.fori_loop(0, 2, side, 0)
            return carry

        lax.fori_loop(0, length, hop, 0)

        def drain(p, carry):
            sent(side_sem, p)

            @pl.when((p >= pos) & (pos > 0))
            def _():
                sent(left_sem, p)

            @pl.when((p <= pos) & (pos < here.last))
            def _():
                sent(right_sem, p)

            return carry

        lax.fori_loop(0, length, drain, 0)


class Scatter(Step):
    line, across = True, False

    def __init__(self, terms, members):
        left, right, turned = terms[0]
        rows, width = left.shape[0] // members, right.shape[0 if turned else 1]
        self.rows, self.width, self.turned = rows, width, [t[2] for t in terms]
        self.depth, self.start = right.shape[1 if turned else 0], [0] * len(terms)
        lefts = [t[0] for t in terms]
        if all(x is left for x in lefts) and len(terms) > 1:
            lefts, self.start = [left], [i * self.depth for i in range(len(terms))]
        self.inputs = [(x, VMEM) for x in lefts] + [(t[1], ANY) for t in terms]
        self.outputs = [(jax.ShapeDtypeStruct((rows, width), F32), VMEM)]
        self.scratch = [pltpu.VMEM(t[1].shape, t[1].dtype) for t in terms]
        self.scratch += [pltpu.SemaphoreType.DMA((len(terms),))] + line_sum_scratch(members, rows, width)

    def run(self, here, *refs):
        n = len(self.turned)
        m = len(self.inputs) - n
        lefts, refs = (refs[:m] * n)[:n], refs[m:]
        rights, o_ref, helds, load_sem, p_ref = refs[:n], refs[n], refs[n + 1 : 2 * n + 1], refs[2 * n + 1], refs[2 * n + 2]
        rows, wide = self.rows, 256
        loads = [pltpu.make_async_copy(w, h, load_sem.at[i]) for i, (w, h) in enumerate(zip(rights, helds))]
        for load in loads:
            load.start()

        def multiply(p):
            at = pl.ds(pl.multiple_of(p * 2 * rows, 2 * rows), 2 * rows)

            def body(c, carry):
                cols = pl.ds(pl.multiple_of(c * wide, wide), wide)
                total = None
                for left, held, turned, start in zip(lefts, helds, self.turned, self.start):
                    mine = left[at, start : start + self.depth]
                    part = dot_nt(mine, held[cols]) if turned else dot_nn(mine, held[:, cols])
                    total = part if total is None else total + part
                p_ref[at, cols] = total.astype(BF16)
                return carry

            lax.fori_loop(0, self.width // wide, body, 0)

        for load in loads:
            load.wait()
        yield from line_sum(here, rows, multiply, o_ref, p_ref, *refs[2 * n + 3 :])


def line_sum_scratch(members, rows, width):
    length = members // 2
    held = [pltpu.VMEM((members * rows, width), BF16), pltpu.VMEM((length, rows, width), BF16)]
    held += [pltpu.VMEM((length, rows, width), BF16)] * 2
    return held + [pltpu.SemaphoreType.DMA((length,))] * 6


def line_sum(here, rows, multiply, o_ref, p_ref, side_buf, left_in, right_in,
             side_send, side_recv, right_send, right_recv, left_send, left_recv):
    pos, core, length, last, tile = here.pos, here.core, here.length, here.last, 32

    def block(p, c):
        return p_ref.at[pl.ds(pl.multiple_of((p * 2 + c) * rows, rows), rows)]

    def side_copy(p):
        return remote(block(p, 1 - core), side_buf.at[p], side_send.at[p], side_recv.at[p], here.at(pos, 1 - core))

    def line_copy(p, right):
        if right:
            return remote(block(p, core), right_in.at[p], right_send.at[p], right_recv.at[p], here.at(pos + 1, core))
        return remote(block(p, core), left_in.at[p], left_send.at[p], left_recv.at[p], here.at(pos - 1, core))

    def make(p):
        multiply(p)
        side_copy(p).start()

    def add(p, incoming, final):
        def body(r, carry):
            s = pl.ds(pl.multiple_of(r * tile, tile), tile)
            mine = pl.ds(pl.multiple_of((p * 2 + core) * rows + r * tile, tile), tile)
            total = p_ref[mine].astype(F32) + side_buf[p, s].astype(F32)
            for ref in incoming:
                total = total + ref[p, s].astype(F32)
            if final:
                o_ref[s] = total
            else:
                p_ref[mine] = total.astype(BF16)
            return carry

        lax.fori_loop(0, rows // tile, body, 0)

    def move(p, right, first, source):
        side_copy(p).wait_recv()

        @pl.when(first)
        def _():
            add(p, [], False)

        @pl.when(jnp.logical_not(first))
        def _():
            line_copy(p, right).wait_recv()
            add(p, [source], False)

        line_copy(p, right).start()

    for t in range(last):

        def side(k, carry):
            p = k * t + (1 - k) * (last - t)

            @pl.when((1 - 2 * k) * (p - pos) > 0)
            def _():
                make(p)

            return carry

        lax.fori_loop(0, 2, side, 0)
        yield
        right_p, left_p = last - t + pos, t - (last - pos)

        @pl.when(t >= pos)
        def _():
            move(right_p, True, pos == 0, right_in)

        @pl.when(left_p >= 0)
        def _():
            move(left_p, False, pos == last, left_in)

    make(pos)
    yield
    side_copy(pos).wait_recv()

    @pl.when(pos == 0)
    def _():
        line_copy(pos, False).wait_recv()
        add(pos, [left_in], True)

    @pl.when(pos == last)
    def _():
        line_copy(pos, True).wait_recv()
        add(pos, [right_in], True)

    @pl.when((pos > 0) & (pos < last))
    def _():
        line_copy(pos, False).wait_recv()
        line_copy(pos, True).wait_recv()
        add(pos, [left_in, right_in], True)

    def drain(p, carry):
        side_copy(p).wait_send()

        @pl.when(p > pos)
        def _():
            line_copy(p, True).wait_send()

        @pl.when(p < pos)
        def _():
            line_copy(p, False).wait_send()

        return carry

    lax.fori_loop(0, length, drain, 0)


class Forward(Step):
    line, across = True, False

    def __init__(self, tokens, out_grad, attn_gain, ffn_gain, query_gain, key_gain, w_query, w_key, w_value, w_output,
                 positions, members):
        rows, width = tokens.shape
        length, size, inner = members // 2, members * rows, w_query.shape[1]
        self.heads, self.share, columns = inner // HD, members // KV, inner + 2 * HD
        sems = pltpu.SemaphoreType.DMA((length,))
        self.grads = Gather(out_grad, members)
        freq = ROPE_BASE ** (-np.arange(HD // 2, dtype=np.float32) / (HD // 2))
        freq = jnp.asarray(np.tile(freq, 4)[None], F32)
        self.inputs = [(tokens, VMEM), (out_grad, ANY), (attn_gain[None], VMEM), (ffn_gain[None], VMEM)]
        self.inputs += [(query_gain[None], VMEM), (key_gain[None], VMEM), (w_query, ANY), (w_key, ANY), (w_value, ANY)]
        self.inputs += [(w_output, ANY), (positions.reshape(size // 128, 128), VMEM), (freq, VMEM)]
        self.outputs = [
            (jax.ShapeDtypeStruct((size, width), BF16), ANY),
            (jax.ShapeDtypeStruct((size, columns), F32), VMEM),
            (jax.ShapeDtypeStruct((size, inner), BF16), VMEM),
            (jax.ShapeDtypeStruct((size // BLOCK, 1, self.heads * BLOCK), F32), VMEM),
            (jax.ShapeDtypeStruct((size, width), BF16), ANY),
            (jax.ShapeDtypeStruct((rows, width), F32), VMEM),
            (jax.ShapeDtypeStruct((rows, width), BF16), VMEM),
            (jax.ShapeDtypeStruct((size, 2 * HD), F32), VMEM),
            (jax.ShapeDtypeStruct((size, 2 * HD), F32), VMEM),
        ]
        self.scratch = [pltpu.VMEM((size, width), BF16), pltpu.VMEM(w_query.shape, BF16), pltpu.VMEM((width, 2 * HD), BF16)]
        self.scratch += [pltpu.VMEM((width, 2 * HD), BF16), pltpu.VMEM((width, 2 * HD), BF16), pltpu.VMEM(w_output.shape, BF16)]
        self.scratch += [pltpu.VMEM((size, 2 * HD), jnp.int32)]
        self.scratch += [pltpu.VMEM((size, inner), BF16), pltpu.VMEM((size, HD), BF16), pltpu.VMEM((size, 2 * HD), BF16)]
        self.scratch += [pltpu.VMEM((self.heads * BLOCK, 2 * HD), F32), pltpu.SemaphoreType.DMA((5,))]
        self.scratch += [sems, sems, sems, pltpu.SemaphoreType.DMA((members,))]
        self.scratch += self.grads.scratch + line_sum_scratch(members, rows, width)

    def loads(self, here, wq_ref, wk_ref, wv_ref, wo_ref, wq, wk, wv, wo, load_sem):
        group = (here.pos * 2 + here.core) // self.share
        cols = pl.ds(pl.multiple_of(group // 2 * 2 * HD, 2 * HD), 2 * HD)
        pairs = [(wq_ref, wq), (wk_ref.at[:, cols], wk), (wv_ref.at[:, cols], wv), (wo_ref, wo)]
        return lax.rem(group, 2), [pltpu.make_async_copy(a, b, load_sem.at[i]) for i, (a, b) in enumerate(pairs)]

    def before(self, here, tok_ref, og_ref, again_ref, fgain_ref, qgain_ref, kgain_ref, wq_ref, wk_ref, wv_ref, wo_ref,
               pos_ref, freq_ref, one_ref, proj_ref, ctx_ref, lse_ref, gr_ref, branch_ref, two_ref, cos_ref, sin_ref,
               all_ref, wq, wk, wv, wkv, wo, *rest):
        for load in self.loads(here, wq_ref, wk_ref, wv_ref, wo_ref, wq, wk, wv, wo, rest[5])[1]:
            load.start()
        rows = tok_ref.shape[0]
        me = (here.pos * 2 + here.core) * rows

        def body(r, carry):
            at = pl.ds(pl.multiple_of(r * 32, 32), 32)
            x = tok_ref[at].astype(F32)
            inv = lax.rsqrt(jnp.mean(x * x, -1, keepdims=True) + EPSILON)
            all_ref[pl.ds(pl.multiple_of(me + r * 32, 32), 32)] = (x * inv * again_ref[...]).astype(BF16)
            return carry

        lax.fori_loop(0, rows // 32, body, 0)

    def run(self, here, tok_ref, og_ref, again_ref, fgain_ref, qgain_ref, kgain_ref, wq_ref, wk_ref, wv_ref, wo_ref,
            pos_ref, freq_ref, one_ref, proj_ref, ctx_ref, lse_ref, gr_ref, branch_ref, two_ref, cos_ref, sin_ref,
            all_ref, wq, wk, wv, wkv, wo, place_ref,
            q_ref, k_ref, v_ref, acc_ref, load_sem, left_sem, right_sem, side_sem, recv_sem, *rest):
        pos, core, length = here.pos, here.core, here.length
        rows, width = tok_ref.shape
        heads, inner, size = self.heads, self.heads * HD, proj_ref.shape[0]
        lane = lax.broadcasted_iota(jnp.int32, (1, HD), 1)

        def block(p, c):
            return all_ref.at[pl.ds(pl.multiple_of((p * 2 + c) * rows, rows), rows)]

        def send(p, sem, to_p, to_c):
            remote(block(p, core), block(p, core), sem.at[p], recv_sem.at[p * 2 + core], here.at(to_p, to_c)).start()

        def arrived(p, c):
            pltpu.make_async_copy(block(p, c), block(p, c), recv_sem.at[p * 2 + c]).wait()

        def sent(sem, p):
            pltpu.make_async_copy(block(p, core), block(p, core), sem.at[p]).wait()

        def prepare():
            odd, loads = self.loads(here, wq_ref, wk_ref, wv_ref, wo_ref, wq, wk, wv, wo, load_sem)
            for load in loads:
                load.wait()
            low = lax.broadcasted_iota(jnp.int32, (1, 2 * HD), 1) < HD

            def pick(r, carry):
                at = pl.ds(pl.multiple_of(r * 256, 256), 256)
                key, value = wk[at].astype(F32), wv[at].astype(F32)
                key = jnp.where(odd == 1, pltpu.roll(key, HD, 1), key)
                value = jnp.where(odd == 1, value, pltpu.roll(value, HD, 1))
                wkv[at] = jnp.where(low, key, value).astype(BF16)
                return carry

            lax.fori_loop(0, width // 256, pick, 0)

            def table(r, carry):
                at = pl.ds(pl.multiple_of(r * 128, 128), 128)
                place = jnp.broadcast_to(pos_ref[pl.ds(r, 1)].astype(F32), (128, 128)).T
                place_ref[at] = place.astype(jnp.int32)
                angle = place * freq_ref[...]
                cos_ref[at] = jnp.cos(angle)
                sin_ref[at] = jnp.sin(angle)
                return carry

            lax.fori_loop(0, size // 128, table, 0)

        def use(p):
            at = pl.ds(pl.multiple_of(p * BLOCK, BLOCK), BLOCK)
            x = jnp.concatenate([dot_nn(all_ref[at], wq[...]), dot_nn(all_ref[at], wkv[...])], 1)
            proj_ref[at] = x
            gain = jnp.concatenate([qgain_ref[...]] * heads + [kgain_ref[...], jnp.ones((1, HD), F32)], 1)
            cosine, sine = wide(cos_ref[at], inner + 2 * HD), wide(sin_ref[at], inner + 2 * HD)
            unit, _ = normed(x)
            spun = turn(unit * gain, cosine, sine)
            q_ref[at] = (spun[:, :inner].astype(BF16) * HD**-0.5).astype(BF16)
            k_ref[at] = spun[:, inner : inner + HD].astype(BF16)
            ones = jnp.broadcast_to(jnp.where(lane == 0, 1.0, 0.0), (BLOCK, HD)).astype(BF16)
            v_ref[at] = jnp.concatenate([x[:, inner + HD :].astype(BF16), ones], 1)

        def pass_on(step):
            right, left = pos + step, pos - step

            @pl.when(right < length)
            def _():
                @pl.when(step > 0)
                def _():
                    arrived(right, core)

                @pl.when(pos > 0)
                def _():
                    send(right, left_sem, pos - 1, core)

                send(right, side_sem, pos, 1 - core)

            @pl.when(left >= 0)
            def _():
                @pl.when(step > 0)
                def _():
                    arrived(left, core)

                @pl.when(pos < here.last)
                def _():
                    send(left, right_sem, pos + 1, core)

                @pl.when(step > 0)
                def _():
                    send(left, side_sem, pos, 1 - core)

        def use_both(step):
            def side(k, c):
                p = pos + (1 - 2 * k) * step

                @pl.when((p >= 0) & (p < length) & (step >= k))
                def _():
                    arrived(p, 1 - core)
                    use(p)

                return c

            lax.fori_loop(0, 2, side, 0)

        pass_on(0)
        prepare()

        def hop(step, carry):
            use_both(step)
            pass_on(step + 1)
            return carry

        lax.fori_loop(0, here.last, hop, 0)
        n = len(self.grads.scratch)
        held = rest[n:]
        p_ref = held[0]
        grads = self.grads.run(here, og_ref, gr_ref, *rest[:n])
        next(grads)
        use_both(here.last)
        keep = pltpu.make_async_copy(all_ref, one_ref, load_sem.at[4])
        keep.start()

        def attend(i):
            at = pl.ds(pl.multiple_of(i * BLOCK, BLOCK), BLOCK)
            query = q_ref[at]
            stacked = jnp.concatenate([query[:, h * HD : (h + 1) * HD] for h in range(heads)], 0)
            acc_ref[...] = jnp.zeros_like(acc_ref)
            index = i * BLOCK + lax.broadcasted_iota(jnp.int32, (BLOCK, 1), 0)
            start = index - place_ref[at, :1]

            def keys(j, c):
                cols = pl.ds(pl.multiple_of(j * BLOCK, BLOCK), BLOCK)
                scores = dot_nt(stacked, k_ref[cols])
                place = j * BLOCK + lax.broadcasted_iota(jnp.int32, (1, BLOCK), 1)
                seen = (place >= start) & (place <= index)
                expo = [
                    jnp.where(seen, jnp.exp(scores[h * BLOCK : (h + 1) * BLOCK]), 0.0).astype(BF16)
                    for h in range(heads)
                ]
                acc_ref[...] += dot_nn(jnp.concatenate(expo, 0), v_ref[cols])
                return c

            lax.fori_loop(0, i + 1, keys, 0)
            outs, logs = [], []
            for h in range(heads):
                acc = acc_ref[pl.ds(h * BLOCK, BLOCK)]
                outs.append((acc[:, :HD] * (1.0 / acc[:, HD : HD + 1])).astype(BF16))
                logs.append(jnp.log(acc.T[HD : HD + 1]))
            ctx_ref[at] = jnp.concatenate(outs, 1)
            lse_ref[i] = jnp.concatenate(logs, 1)

        def multiply(p):
            attend(p)
            at = pl.ds(pl.multiple_of(p * BLOCK, BLOCK), BLOCK)

            def body(c, carry):
                cols = pl.ds(pl.multiple_of(c * 512, 512), 512)
                p_ref[at, cols] = dot_nn(ctx_ref[at], wo[:, cols]).astype(BF16)
                return carry

            lax.fori_loop(0, width // 512, body, 0)

        weave([line_sum(here, rows, multiply, branch_ref, *held), grads])

        def body(r, carry):
            at = pl.ds(pl.multiple_of(r * 32, 32), 32)
            x = tok_ref[at].astype(F32) + branch_ref[at]
            inv = lax.rsqrt(jnp.mean(x * x, -1, keepdims=True) + EPSILON)
            two_ref[at] = (x * inv * fgain_ref[...]).astype(BF16)
            return carry

        lax.fori_loop(0, rows // 32, body, 0)

        def drain(p, carry):
            sent(side_sem, p)

            @pl.when((p >= pos) & (pos > 0))
            def _():
                sent(left_sem, p)

            @pl.when((p <= pos) & (pos < here.last))
            def _():
                sent(right_sem, p)

            return carry

        lax.fori_loop(0, length, drain, 0)
        keep.wait()
        yield


class Across(Step):
    line, across = False, True

    def __init__(self, x, parts, colours, late=0):
        self.bits, self.colours, self.late = parts.bit_length() - 1, colours, late
        rows, width = x.shape
        self.inputs = [(x, VMEM)]
        self.outputs = [(jax.ShapeDtypeStruct(x.shape, x.dtype), VMEM)]
        self.scratch = [pltpu.VMEM((rows, width), x.dtype)]
        for _ in colours:
            part = rows // len(colours)
            self.scratch += [pltpu.VMEM((part >> (s + 1), width), x.dtype) for s in range(self.bits)]
            self.scratch += [pltpu.SemaphoreType.DMA((2 * self.bits,))] * 2

    def run(self, here, x_ref, o_ref, sum_ref, *rest):
        for _ in range(self.late):
            yield
        n, rows = self.bits + 2, x_ref.shape[0] // len(self.colours)
        live = [
            self.one(here, backwards, i * rows, rows, x_ref, o_ref, sum_ref, *rest[i * n : (i + 1) * n])
            for i, backwards in enumerate(self.colours)
        ]
        while live:
            live = [r for r in live if next(r, live) is not live]
            yield

    def one(self, here, backwards, start, size, x_ref, o_ref, sum_ref, *rest):
        taken, (send_sem, recv_sem) = rest[: self.bits], rest[self.bits :]
        order = list(range(self.bits))[:: -1 if backwards else 1]
        copies, tile = [], 16

        def part(ref, at, count):
            return ref.at[pl.ds(pl.multiple_of(at, count), count)]

        for s, bit in enumerate(order):
            mine, device = here.partner(bit)
            half = size // 2
            keep, give = start + mine * half, start + (1 - mine) * half
            source = x_ref if s == 0 else sum_ref
            target = o_ref if s == self.bits - 1 else sum_ref
            copy = remote(part(source, give, half), taken[s], send_sem.at[s], recv_sem.at[s], device)
            copy.start()
            copies.append(copy)
            yield
            copy.wait_recv()

            def body(r, carry):
                at = pl.ds(pl.multiple_of(keep + r * tile, tile), tile)
                got = taken[s][pl.ds(pl.multiple_of(r * tile, tile), tile)]
                target[at] = (source[at].astype(F32) + got.astype(F32)).astype(target.dtype)
                return carry

            lax.fori_loop(0, half // tile, body, 0)
            start, size = keep, half
        for s, bit in enumerate(order[::-1]):
            mine, device = here.partner(bit)
            n = self.bits + s
            copy = remote(part(o_ref, start, size), part(o_ref, start, size), send_sem.at[n], recv_sem.at[n], device)
            copy.start()
            copies.append(copy)
            yield
            copy.wait_recv()
            start, size = start - mine * size, size * 2
        for copy in copies:
            copy.wait_send()


class KeyValue(Step):
    line, across = True, True

    def __init__(self, x, width, members, parts):
        self.width, self.extra, self.members = width, x.shape[0] - width, members
        self.sum, self.all = Across(x, parts, (False,)), Gather(x, members)
        self.inputs = [(x, VMEM)]
        flat = jax.ShapeDtypeStruct((width, KV * HD), BF16)
        self.outputs = [(flat, VMEM), (flat, VMEM), (jax.ShapeDtypeStruct((self.extra, 2 * HD), F32), VMEM)]
        self.scratch = [pltpu.VMEM(x.shape, x.dtype), pltpu.VMEM((members * x.shape[0], 2 * HD), x.dtype)]
        self.scratch += self.sum.scratch + self.all.scratch

    def run(self, here, x_ref, key_ref, value_ref, small_ref, sum_ref, all_ref, *rest):
        n = len(self.sum.scratch)
        first = self.sum.run(here, x_ref, sum_ref, *rest[:n])
        next(first)
        yield
        for _ in first:
            pass
        yield from self.all.run(here, sum_ref, all_ref, *rest[n:])
        rows, share, tile = self.width + self.extra, self.members // KV, 128

        def block(group, at, count):
            total = 0.0
            for k in range(share):
                begin = pl.multiple_of((group * share + k) * rows + at, 16)
                total = total + all_ref[pl.ds(begin, count)].astype(F32)
            return total

        for pair in range(KV // 2):
            cols = slice(2 * HD * pair, 2 * HD * (pair + 1))

            def body(r, carry):
                at = pl.ds(pl.multiple_of(r * tile, tile), tile)
                one, two = block(2 * pair, r * tile, tile), block(2 * pair + 1, r * tile, tile)
                key_ref[at, cols] = jnp.concatenate([one[:, :HD], two[:, :HD]], 1).astype(BF16)
                value_ref[at, cols] = jnp.concatenate([one[:, HD:], two[:, HD:]], 1).astype(BF16)
                return carry

            lax.fori_loop(0, self.width // tile, body, 0)
        small = 0.0
        for group in range(KV):
            small = small + block(group, self.width, self.extra)
        small_ref[...] = small


def together(steps, members, parts, collective_id, vmem=48):
    counts = [(len(s.inputs), len(s.outputs), len(s.scratch)) for s in steps]

    def kernel(*refs):
        refs = list(refs)
        given = [[refs.pop(0) for _ in range(c[0])] for c in counts]
        made = [[refs.pop(0) for _ in range(c[1])] for c in counts]
        held = [[refs.pop(0) for _ in range(c[2])] for c in counts]
        here = Place(members, parts)
        peers = here.greet(any(s.line for s in steps), any(s.across for s in steps))
        for s, g, m, h in zip(steps, given, made, held):
            s.before(here, *g, *m, *h)
        here.meet(peers)
        weave([s.run(here, *g, *m, *h) for s, g, m, h in zip(steps, given, made, held)])

    return pl.pallas_call(
        kernel,
        out_shape=[o for s in steps for o, _ in s.outputs],
        in_specs=[m for s in steps for _, m in s.inputs],
        out_specs=[m for s in steps for _, m in s.outputs],
        scratch_shapes=[h for s in steps for h in s.scratch],
        compiler_params=pltpu.CompilerParams(
            collective_id=collective_id, has_side_effects=True, vmem_limit_bytes=vmem << 20
        ),
        cost_estimate=pl.CostEstimate(flops=1, bytes_accessed=1, transcendentals=0),
    )(*[x for s in steps for x, _ in s.inputs])


def dot_nn(a, b):
    return lax.dot_general(a, b, (((1,), (0,)), ((), ())), preferred_element_type=F32)

def dot_nt(a, b):
    return lax.dot_general(a, b, (((1,), (1,)), ((), ())), preferred_element_type=F32)

def group_mean(x):
    width = x.shape[1]
    row = lax.broadcasted_iota(jnp.int32, (width, width), 0) // HD
    col = lax.broadcasted_iota(jnp.int32, (width, width), 1) // HD
    ones = jnp.where(row == col, 1.0 / HD, 0.0).astype(F32)
    return jnp.dot(x, ones, precision=lax.Precision.HIGHEST, preferred_element_type=F32)

def half_turn(x):
    width = x.shape[1]
    lane = lax.broadcasted_iota(jnp.int32, (1, width), 1)
    first = lax.rem(lane, HD) < HD // 2
    up = pltpu.roll(x, HD // 2, 1)
    down = pltpu.roll(x, width - HD // 2, 1)
    return jnp.where(first, -down, up)

def wide(table, width):
    return jnp.concatenate([table] * (width // table.shape[1]), 1)

def normed(x):
    inv = lax.rsqrt(group_mean(x * x) + EPSILON)
    return x * inv, inv

def turn(x, cosine, sine):
    return x * cosine + half_turn(x) * sine

def turn_back(x, cosine, sine):
    return x * cosine - half_turn(x) * sine

def stack_lanes(x, heads):
    return jnp.concatenate([x[h * HD:(h + 1) * HD] for h in range(heads)], 1)

def attend_back_kernel(heads, proj_ref, cos_ref, sin_ref, qgain_ref, kgain_ref, pos_ref, ctx_ref, grad_ref, lse_ref,
                       out_ref, sums_ref, k_ref, kt_ref, v_ref, dk_ref, dv_ref, dq_ref):
    width = heads * HD
    scale = HD ** -0.5
    count = proj_ref.shape[0] // BLOCK
    gain = jnp.concatenate([qgain_ref[...]] * heads + [kgain_ref[...], jnp.ones((1, HD), F32)], 1)
    def prepare(i, carry):
        rows = pl.ds(pl.multiple_of(i * BLOCK, BLOCK), BLOCK)
        x = proj_ref[rows, width:]
        unit, _ = normed(x)
        spun = turn(unit * gain[:, width:], cos_ref[rows], sin_ref[rows])
        k_ref[rows] = spun[:, :HD].astype(BF16)
        kt_ref[i] = spun.T[:HD].astype(BF16)
        v_ref[rows] = x[:, HD:].astype(BF16)
        dk_ref[rows] = jnp.zeros((BLOCK, HD), F32)
        dv_ref[rows] = jnp.zeros((BLOCK, HD), F32)
        return carry
    lax.fori_loop(0, count, prepare, 0)
    sums_ref[...] = jnp.zeros_like(sums_ref)
    def outer(i, carry):
        rows = pl.ds(pl.multiple_of(i * BLOCK, BLOCK), BLOCK)
        x = proj_ref[rows, :width]
        cosine, sine = wide(cos_ref[rows], width), wide(sin_ref[rows], width)
        unit, inv = normed(x)
        query = (turn(unit * gain[:, :width], cosine, sine).astype(BF16).astype(F32) * scale)
        query_t = stack_lanes(query.T, heads).astype(BF16)
        query = query.astype(BF16)
        query_s = jnp.concatenate([query[:, h * HD:(h + 1) * HD] for h in range(heads)], 0)
        grad = grad_ref[rows]
        grad_s = jnp.concatenate([grad[:, h * HD:(h + 1) * HD] for h in range(heads)], 0)
        grad_t = stack_lanes(grad.astype(F32).T, heads)
        ctx_t = stack_lanes(ctx_ref[rows].astype(F32).T, heads)
        delta = jnp.sum(grad_t * ctx_t, 0, keepdims=True)
        grad_t = grad_t.astype(BF16)
        lse = lse_ref[i]
        index = i * BLOCK + lax.broadcasted_iota(jnp.int32, (1, BLOCK), 1)
        start = index - pos_ref[i]
        dq_ref[...] = jnp.zeros_like(dq_ref)
        def inner(j, c):
            cols = pl.ds(pl.multiple_of(j * BLOCK, BLOCK), BLOCK)
            scores = dot_nn(k_ref[cols], query_t)
            grad_probs = dot_nn(v_ref[cols], grad_t)
            place = j * BLOCK + lax.broadcasted_iota(jnp.int32, (BLOCK, 1), 0)
            seen = (place >= start) & (place <= index)
            probs, back = [], []
            for h in range(heads):
                s = slice(h * BLOCK, (h + 1) * BLOCK)
                exact = jnp.where(seen, jnp.exp(scores[:, s] - lse[:, s]), 0.0)
                probs.append(exact.astype(BF16))
                back.append((exact * (grad_probs[:, s] - delta[:, s])).astype(BF16))
            probs = jnp.concatenate(probs, 1)
            back = jnp.concatenate(back, 1)
            dv_ref[cols] += dot_nn(probs, grad_s)
            dk_ref[cols] += dot_nn(back, query_s)
            dq_ref[...] += dot_nn(kt_ref[j], back)
            return c
        lax.fori_loop(0, i + 1, inner, 0)
        dq = jnp.concatenate([dq_ref[:, h * BLOCK:(h + 1) * BLOCK] for h in range(heads)], 0).T * scale
        dqn = turn_back(dq, cosine, sine)
        sums_ref[:, :width] += jnp.sum(dqn * unit, 0, keepdims=True)
        e = dqn * gain[:, :width]
        out_ref[rows, :width] = (inv * (e - unit * group_mean(e * unit))).astype(BF16)
        return carry
    lax.fori_loop(0, count, outer, 0)
    def finish(i, carry):
        rows = pl.ds(pl.multiple_of(i * BLOCK, BLOCK), BLOCK)
        x = proj_ref[rows, width:]
        unit, inv = normed(x)
        dv = dv_ref[rows]
        dk = jnp.concatenate([dk_ref[rows], dv], 1)
        dkn = turn_back(dk, cos_ref[rows], sin_ref[rows])
        sums_ref[:, width:] += jnp.sum(dkn * unit, 0, keepdims=True)
        e = dkn * gain[:, width:]
        dkp = inv * (e - unit * group_mean(e * unit))
        lane = lax.broadcasted_iota(jnp.int32, (1, 2 * HD), 1)
        out_ref[rows, width:] = jnp.where(lane < HD, dkp, dk).astype(BF16)
        return carry
    lax.fori_loop(0, count, finish, 0)

def attend_back(proj, cosine, sine, query_gain, key_gain, positions, context, grad_context, lse, heads):
    size = proj.shape[0]
    count = size // BLOCK
    vm = pl.BlockSpec(memory_space=pltpu.VMEM)
    return pl.pallas_call(
        functools.partial(attend_back_kernel, heads),
        out_shape=(jax.ShapeDtypeStruct(proj.shape, BF16), jax.ShapeDtypeStruct((1, proj.shape[1]), F32)),
        in_specs=[vm] * 9, out_specs=(vm, vm),
        scratch_shapes=[pltpu.VMEM((size, HD), BF16), pltpu.VMEM((count, HD, BLOCK), BF16), pltpu.VMEM((size, HD), BF16),
                        pltpu.VMEM((size, HD), F32), pltpu.VMEM((size, HD), F32), pltpu.VMEM((HD, heads * BLOCK), F32)],
        compiler_params=pltpu.CompilerParams(vmem_limit_bytes=40 << 20),
        cost_estimate=pl.CostEstimate(flops=1, bytes_accessed=1, transcendentals=0),
    )(proj, cosine, sine, query_gain[None], key_gain[None], positions.reshape(count, 1, BLOCK), context, grad_context, lse)


def matmul(left, right):
    return jnp.dot(left, right, preferred_element_type=F32)


def matmul_left_t(left, right):
    return lax.dot_general(left, right, (((0,), (0,)), ((), ())), preferred_element_type=F32)


def matmul_right_t(left, right):
    return lax.dot_general(left, right, (((1,), (1,)), ((), ())), preferred_element_type=F32)


def norm_back(grad_normed, unit, inverse, gain):
    scaled = grad_normed * gain
    return inverse * (scaled - unit * jnp.mean(scaled * unit, -1, keepdims=True))


def after(first, *later):
    return lax.optimization_barrier((first,) + later)


def per_device(
    tokens,
    seg_ids,
    positions,
    w_query,
    w_key,
    w_value,
    w_output,
    w_gate,
    w_up,
    w_down,
    attn_gain,
    ffn_gain,
    query_gain,
    key_gain,
    out_grad,
):
    members, parts = lax.axis_size("mp"), lax.axis_size("dp")
    width = tokens.shape[1]
    query_width = w_query.shape[1]
    heads = query_width // HD
    ffn_width = w_gate.shape[1]
    share = members // KV
    group = lax.axis_index("mp") // share

    rows_one, projected, context, lse, grad_rows, attn_branch, h_two, cosine, sine = together(
        [
            Forward(
                tokens,
                out_grad,
                attn_gain,
                ffn_gain,
                query_gain,
                key_gain,
                w_query,
                w_key,
                w_value,
                w_output,
                positions,
                members,
            )
        ],
        members,
        parts,
        0,
        58,
    )
    rows_two, hidden, grad_gate, grad_up = together(
        [GatherFfn(h_two, grad_rows, w_gate, w_up, w_down, members)], members, parts, 5, 58
    )
    rows_two, tokens_late, w_key, w_value = after(rows_two, tokens, w_key, w_value)
    tokens_f = tokens_late.astype(F32)
    inv_one = lax.rsqrt(jnp.mean(tokens_f * tokens_f, -1, keepdims=True) + EPSILON)
    normed_one = tokens_f * inv_one
    key_cols = lax.dynamic_slice_in_dim(w_key, group * HD, HD, 1)
    value_cols = lax.dynamic_slice_in_dim(w_value, group * HD, HD, 1)
    w_attn = jnp.concatenate([w_query, key_cols, value_cols], 1)
    residual_mid = tokens_f + attn_branch
    inv_two = lax.rsqrt(jnp.mean(residual_mid * residual_mid, -1, keepdims=True) + EPSILON)
    normed_two = residual_mid * inv_two
    ffn_parts = (
        matmul_left_t(hidden, grad_rows).astype(BF16),
        matmul_left_t(rows_two, grad_gate).astype(BF16),
        matmul_left_t(rows_two, grad_up).astype(BF16),
    )
    ffn_parts, grad_gate, grad_up, hidden = lax.optimization_barrier((ffn_parts, grad_gate, grad_up, hidden))
    grad_w_down, grad_w_gate, grad_w_up = lax.psum(ffn_parts, "dp")

    grad_h_two = together(
        [Scatter([(grad_gate, w_gate, True), (grad_up, w_up, True)], members)],
        members,
        parts,
        6,
        58,
    )[0]
    grad_ffn_gain = jnp.sum(grad_h_two * normed_two, 0)
    grad_mid = out_grad.astype(F32) + norm_back(grad_h_two, normed_two, inv_two, ffn_gain)
    grad_attn_rows, ffn_branch = together(
        [Gather(grad_mid.astype(BF16), members), Scatter([(hidden, w_down, False)], members)],
        members,
        parts,
        2,
    )
    grad_context = matmul_right_t(grad_attn_rows, w_output).astype(BF16)
    grad_proj, gain_sums = attend_back(
        projected, cosine, sine, query_gain, key_gain, positions, context, grad_context, lse, heads
    )
    output_part = matmul_left_t(context, grad_attn_rows).astype(BF16)
    grad_w_attn = matmul_left_t(rows_one, grad_proj)
    grad_attn_gain = jnp.sum(w_attn.astype(F32) * grad_w_attn, 1) / attn_gain

    small = jnp.concatenate(
        [
            grad_attn_gain,
            grad_ffn_gain,
            jnp.sum(gain_sums[0, :query_width].reshape(heads, HD), 0),
            gain_sums[0, query_width : query_width + HD],
            jnp.sum(tokens_f * tokens_f)[None],
        ]
    )
    unit = 16 * parts
    extra = -(-small.shape[0] // (unit * 2 * HD)) * unit
    small_rows = jnp.pad(small, (0, extra * 2 * HD - small.shape[0])).reshape(extra, 2 * HD)
    kv_part = jnp.concatenate([grad_w_attn[:, query_width:], small_rows], 0).astype(BF16)
    query_part = grad_w_attn[:, :query_width].astype(BF16)
    grad_w_key, grad_w_value, small_sum, grad_h_one, grad_w_output, grad_w_query = together(
        [
            KeyValue(kv_part, width, members, parts),
            Scatter([(grad_proj, w_attn, True)], members),
            Across(output_part, parts, (False,), 2),
            Across(query_part, parts, (True,), 2),
        ],
        members,
        parts,
        3,
        58,
    )
    small_sum = small_sum.reshape(-1)
    entry_count = tokens.size * parts * members
    at = 2 * width
    residual_rms = jnp.sqrt(small_sum[at + 2 * HD : at + 2 * HD + 1] / entry_count)

    grad_tokens = (grad_mid + norm_back(grad_h_one, normed_one, inv_one, attn_gain)).astype(BF16)
    output = (residual_mid + ffn_branch).astype(BF16)
    branch_rms = jnp.stack(
        [
            jnp.sqrt(jnp.mean(attn_branch * attn_branch, -1)),
            jnp.sqrt(jnp.mean(ffn_branch * ffn_branch, -1)),
        ]
    )
    return (
        output,
        grad_tokens,
        grad_w_query.astype(F32),
        grad_w_key.astype(F32),
        grad_w_value.astype(F32),
        grad_w_output.astype(F32),
        grad_w_gate.astype(F32),
        grad_w_up.astype(F32),
        grad_w_down.astype(F32),
        small_sum[:width],
        small_sum[width:at],
        small_sum[at : at + HD],
        small_sum[at + HD : at + 2 * HD],
        residual_rms,
        branch_rms,
    )


def solution(mesh):
    row, whole, column = P(("dp", "mp"), None), P(), P(None, "mp")
    lead = P("mp", None)
    return jax.shard_map(
        per_device,
        mesh=mesh,
        in_specs=(row, P("dp"), P("dp"), column, whole, whole, lead, column, column, lead)
        + (whole,) * 4
        + (row,),
        out_specs=(row, row, column, whole, whole, lead, column, column, lead)
        + (whole,) * 5
        + (P(None, ("dp", "mp")),),
        check_vma=False,
    )
```

```python
import functools

import jax
import jax.numpy as jnp
import numpy as np
from jax import lax
from jax.experimental import pallas as pl
from jax.experimental.pallas import tpu as pltpu
from jax.sharding import PartitionSpec as P

HEADS = 32
KV = 8
HD = 64
EPSILON = 1e-06
ROPE_BASE = 10000.0
BLOCK = 256
F32 = jnp.float32
BF16 = jnp.bfloat16
MESH = pl.DeviceIdType.MESH


ANY = pl.BlockSpec(memory_space=pl.ANY)
VMEM = pl.BlockSpec(memory_space=pltpu.VMEM)


class Place:
    def __init__(self, members, parts):
        me = lax.axis_index("mp")
        self.dp, self.pos, self.core = lax.axis_index("dp"), me // 2, lax.rem(me, 2)
        self.length, self.parts = members // 2, parts
        self.last = self.length - 1

    def at(self, pos, core):
        return (self.dp, pos * 2 + core)

    def partner(self, bit):
        mine = lax.rem(self.dp // (1 << bit), 2)
        return mine, (self.dp + (1 - 2 * mine) * (1 << bit), self.pos * 2 + self.core)

    def bits(self):
        return self.parts.bit_length() - 1

    def greet(self, line, across):
        barrier = pltpu.get_barrier_semaphore()

        def tell(device):
            pl.semaphore_signal(barrier, inc=1, device_id=device, device_id_type=MESH)

        peers = 0
        if line:
            tell(self.at(self.pos, 1 - self.core))

            @pl.when(self.pos > 0)
            def _():
                tell(self.at(self.pos - 1, self.core))

            @pl.when(self.pos < self.last)
            def _():
                tell(self.at(self.pos + 1, self.core))

            peers = 1 + jnp.minimum(self.pos, 1) + jnp.minimum(self.last - self.pos, 1)
        if across:
            for bit in range(self.bits()):
                tell(self.partner(bit)[1])
            peers = peers + self.bits()
        return peers

    def meet(self, peers):
        pl.semaphore_wait(pltpu.get_barrier_semaphore(), peers)


def weave(live):
    while live:
        live = [r for r in live if next(r, live) is not live]


def remote(src, dst, send_sem, recv_sem, device):
    return pltpu.make_async_remote_copy(
        src_ref=src, dst_ref=dst, send_sem=send_sem, recv_sem=recv_sem, device_id=device, device_id_type=MESH
    )


class Step:
    def before(self, *refs):
        pass


class Gather(Step):
    line, across = True, False

    def __init__(self, x, members):
        length = members // 2
        sems = pltpu.SemaphoreType.DMA((length,))
        self.inputs = [(x, ANY)]
        self.outputs = [(jax.ShapeDtypeStruct((members * x.shape[0],) + x.shape[1:], x.dtype), ANY)]
        self.scratch = [pltpu.SemaphoreType.DMA, sems, sems, sems, pltpu.SemaphoreType.DMA((members,))]

    def run(self, here, x_ref, o_ref, own_sem, left_sem, right_sem, side_sem, recv_sem):
        pos, core, length = here.pos, here.core, here.length
        rows = x_ref.shape[0]

        def block(p, c):
            return o_ref.at[pl.ds(pl.multiple_of((p * 2 + c) * rows, rows), rows)]

        def send(src, p, sem, to_p, to_c):
            remote(src, block(p, core), sem.at[p], recv_sem.at[p * 2 + core], here.at(to_p, to_c)).start()

        def arrived(p, c):
            pltpu.make_async_copy(x_ref, block(p, c), recv_sem.at[p * 2 + c]).wait()

        def sent(sem, p):
            pltpu.make_async_copy(x_ref, block(pos, core), sem.at[p]).wait()

        @pl.when(pos > 0)
        def _():
            send(x_ref, pos, left_sem, pos - 1, core)

        @pl.when(pos < here.last)
        def _():
            send(x_ref, pos, right_sem, pos + 1, core)

        send(x_ref, pos, side_sem, pos, 1 - core)
        own = pltpu.make_async_copy(x_ref, block(pos, core), own_sem)
        own.start()
        for step in range(1, length):
            yield
            right, left = pos + step, pos - step

            @pl.when(right < length)
            def _():
                arrived(right, core)

                @pl.when(pos > 0)
                def _():
                    send(block(right, core), right, left_sem, pos - 1, core)

                send(block(right, core), right, side_sem, pos, 1 - core)

            @pl.when(left >= 0)
            def _():
                arrived(left, core)

                @pl.when(pos < here.last)
                def _():
                    send(block(left, core), left, right_sem, pos + 1, core)

                send(block(left, core), left, side_sem, pos, 1 - core)

        yield
        own.wait()

        def drain(p, carry):
            arrived(p, 1 - core)
            sent(side_sem, p)

            @pl.when((p >= pos) & (pos > 0))
            def _():
                sent(left_sem, p)

            @pl.when((p <= pos) & (pos < here.last))
            def _():
                sent(right_sem, p)

            return carry

        lax.fori_loop(0, length, drain, 0)


class GatherFfn(Step):
    line, across = True, False

    def __init__(self, x, grad_rows, w_gate, w_up, w_down, members):
        length, (rows, width), units = members // 2, x.shape, w_gate.shape[1]
        total = members * rows
        sems = pltpu.SemaphoreType.DMA((length,))
        self.units = units
        self.inputs = [(v, ANY) for v in (x, grad_rows)] + [(v, ANY) for v in (w_gate, w_up, w_down)]
        self.outputs = [
            (jax.ShapeDtypeStruct((total, width), BF16), VMEM),
            (jax.ShapeDtypeStruct((total, units), BF16), VMEM),
            (jax.ShapeDtypeStruct((total, units), BF16), VMEM),
            (jax.ShapeDtypeStruct((total, units), BF16), VMEM),
        ]
        self.scratch = [pltpu.VMEM(v.shape, v.dtype) for v in (grad_rows, w_gate, w_up, w_down)]
        self.scratch += [pltpu.SemaphoreType.DMA((5,)), sems, sems, sems, pltpu.SemaphoreType.DMA((members,))]

    def run(self, here, x_ref, gr_ref, wg_ref, wu_ref, wd_ref, o_ref, hid_ref, gg_ref, gu_ref,
            gr, wg, wu, wd, load_sem, left_sem, right_sem, side_sem, recv_sem):
        pos, core, length = here.pos, here.core, here.length
        rows, units, wide = x_ref.shape[0], self.units, 256

        def block(p, c):
            return o_ref.at[pl.ds(pl.multiple_of((p * 2 + c) * rows, rows), rows)]

        def send(src, p, sem, to_p, to_c):
            remote(src, block(p, core), sem.at[p], recv_sem.at[p * 2 + core], here.at(to_p, to_c)).start()

        def arrived(p, c):
            pltpu.make_async_copy(x_ref, block(p, c), recv_sem.at[p * 2 + c]).wait()

        def sent(sem, p):
            pltpu.make_async_copy(x_ref, block(pos, core), sem.at[p]).wait()

        @pl.when(pos > 0)
        def _():
            send(x_ref, pos, left_sem, pos - 1, core)

        @pl.when(pos < here.last)
        def _():
            send(x_ref, pos, right_sem, pos + 1, core)

        send(x_ref, pos, side_sem, pos, 1 - core)
        pairs = [(x_ref, block(pos, core)), (wg_ref, wg), (wu_ref, wu), (gr_ref, gr), (wd_ref, wd)]
        loads = [pltpu.make_async_copy(a, b, load_sem.at[i]) for i, (a, b) in enumerate(pairs)]
        for load in loads:
            load.start()
        yield
        for load in loads:
            load.wait()

        def use(p):
            at = pl.ds(pl.multiple_of(p * 2 * rows, 2 * rows), 2 * rows)

            def body(c, carry):
                cols = pl.ds(pl.multiple_of(c * wide, wide), wide)
                gate = dot_nn(o_ref[at], wg[:, cols])
                up = dot_nn(o_ref[at], wu[:, cols])
                back = dot_nt(gr[at], wd[cols])
                sigma = 1.0 / (1.0 + jnp.exp(-gate))
                silu = gate * sigma
                hid_ref[at, cols] = (silu * up).astype(BF16)
                gg_ref[at, cols] = (back * up * sigma * (1.0 + gate * (1.0 - sigma))).astype(BF16)
                gu_ref[at, cols] = (back * silu).astype(BF16)
                return carry

            lax.fori_loop(0, units // wide, body, 0)

        def hop(step, carry):
            right, left = pos + step, pos - step

            @pl.when((step > 0) & (right < length))
            def _():
                arrived(right, core)

                @pl.when(pos > 0)
                def _():
                    send(block(right, core), right, left_sem, pos - 1, core)

                send(block(right, core), right, side_sem, pos, 1 - core)

            @pl.when((step > 0) & (left >= 0))
            def _():
                arrived(left, core)

                @pl.when(pos < here.last)
                def _():
                    send(block(left, core), left, right_sem, pos + 1, core)

                send(block(left, core), left, side_sem, pos, 1 - core)

            def side(k, c):
                p = pos + (1 - 2 * k) * step

                @pl.when((p >= 0) & (p < length) & (step >= k))
                def _():
                    arrived(p, 1 - core)
                    use(p)

                return c

            lax.fori_loop(0, 2, side, 0)
            return carry

        lax.fori_loop(0, length, hop, 0)

        def drain(p, carry):
            sent(side_sem, p)

            @pl.when((p >= pos) & (pos > 0))
            def _():
                sent(left_sem, p)

            @pl.when((p <= pos) & (pos < here.last))
            def _():
                sent(right_sem, p)

            return carry

        lax.fori_loop(0, length, drain, 0)


class Scatter(Step):
    line, across = True, False

    def __init__(self, terms, members):
        left, right, turned = terms[0]
        rows, width = left.shape[0] // members, right.shape[0 if turned else 1]
        self.rows, self.width, self.turned = rows, width, [t[2] for t in terms]
        self.depth, self.start = right.shape[1 if turned else 0], [0] * len(terms)
        lefts = [t[0] for t in terms]
        if all(x is left for x in lefts) and len(terms) > 1:
            lefts, self.start = [left], [i * self.depth for i in range(len(terms))]
        self.inputs = [(x, VMEM) for x in lefts] + [(t[1], ANY) for t in terms]
        self.outputs = [(jax.ShapeDtypeStruct((rows, width), F32), VMEM)]
        self.scratch = [pltpu.VMEM(t[1].shape, t[1].dtype) for t in terms]
        self.scratch += [pltpu.SemaphoreType.DMA((len(terms),))] + line_sum_scratch(members, rows, width)

    def run(self, here, *refs):
        n = len(self.turned)
        m = len(self.inputs) - n
        lefts, refs = (refs[:m] * n)[:n], refs[m:]
        rights, o_ref, helds, load_sem, p_ref = refs[:n], refs[n], refs[n + 1 : 2 * n + 1], refs[2 * n + 1], refs[2 * n + 2]
        rows, wide = self.rows, 256
        loads = [pltpu.make_async_copy(w, h, load_sem.at[i]) for i, (w, h) in enumerate(zip(rights, helds))]
        for load in loads:
            load.start()

        def multiply(p):
            at = pl.ds(pl.multiple_of(p * 2 * rows, 2 * rows), 2 * rows)

            def body(c, carry):
                cols = pl.ds(pl.multiple_of(c * wide, wide), wide)
                total = None
                for left, held, turned, start in zip(lefts, helds, self.turned, self.start):
                    mine = left[at, start : start + self.depth]
                    part = dot_nt(mine, held[cols]) if turned else dot_nn(mine, held[:, cols])
                    total = part if total is None else total + part
                p_ref[at, cols] = total.astype(BF16)
                return carry

            lax.fori_loop(0, self.width // wide, body, 0)

        for load in loads:
            load.wait()
        yield from line_sum(here, rows, multiply, o_ref, p_ref, *refs[2 * n + 3 :])


def line_sum_scratch(members, rows, width):
    length = members // 2
    held = [pltpu.VMEM((members * rows, width), BF16), pltpu.VMEM((length, rows, width), BF16)]
    held += [pltpu.VMEM((length, rows, width), BF16)] * 2
    return held + [pltpu.SemaphoreType.DMA((length,))] * 6


def line_sum(here, rows, multiply, o_ref, p_ref, side_buf, left_in, right_in,
             side_send, side_recv, right_send, right_recv, left_send, left_recv):
    pos, core, length, last, tile = here.pos, here.core, here.length, here.last, 32

    def block(p, c):
        return p_ref.at[pl.ds(pl.multiple_of((p * 2 + c) * rows, rows), rows)]

    def side_copy(p):
        return remote(block(p, 1 - core), side_buf.at[p], side_send.at[p], side_recv.at[p], here.at(pos, 1 - core))

    def line_copy(p, right):
        if right:
            return remote(block(p, core), right_in.at[p], right_send.at[p], right_recv.at[p], here.at(pos + 1, core))
        return remote(block(p, core), left_in.at[p], left_send.at[p], left_recv.at[p], here.at(pos - 1, core))

    def make(p):
        multiply(p)
        side_copy(p).start()

    def add(p, incoming, final):
        def body(r, carry):
            s = pl.ds(pl.multiple_of(r * tile, tile), tile)
            mine = pl.ds(pl.multiple_of((p * 2 + core) * rows + r * tile, tile), tile)
            total = p_ref[mine].astype(F32) + side_buf[p, s].astype(F32)
            for ref in incoming:
                total = total + ref[p, s].astype(F32)
            if final:
                o_ref[s] = total
            else:
                p_ref[mine] = total.astype(BF16)
            return carry

        lax.fori_loop(0, rows // tile, body, 0)

    def move(p, right, first, source):
        side_copy(p).wait_recv()

        @pl.when(first)
        def _():
            add(p, [], False)

        @pl.when(jnp.logical_not(first))
        def _():
            line_copy(p, right).wait_recv()
            add(p, [source], False)

        line_copy(p, right).start()

    for t in range(last):

        def side(k, carry):
            p = k * t + (1 - k) * (last - t)

            @pl.when((1 - 2 * k) * (p - pos) > 0)
            def _():
                make(p)

            return carry

        lax.fori_loop(0, 2, side, 0)
        yield
        right_p, left_p = last - t + pos, t - (last - pos)

        @pl.when(t >= pos)
        def _():
            move(right_p, True, pos == 0, right_in)

        @pl.when(left_p >= 0)
        def _():
            move(left_p, False, pos == last, left_in)

    make(pos)
    yield
    side_copy(pos).wait_recv()

    @pl.when(pos == 0)
    def _():
        line_copy(pos, False).wait_recv()
        add(pos, [left_in], True)

    @pl.when(pos == last)
    def _():
        line_copy(pos, True).wait_recv()
        add(pos, [right_in], True)

    @pl.when((pos > 0) & (pos < last))
    def _():
        line_copy(pos, False).wait_recv()
        line_copy(pos, True).wait_recv()
        add(pos, [left_in, right_in], True)

    def drain(p, carry):
        side_copy(p).wait_send()

        @pl.when(p > pos)
        def _():
            line_copy(p, True).wait_send()

        @pl.when(p < pos)
        def _():
            line_copy(p, False).wait_send()

        return carry

    lax.fori_loop(0, length, drain, 0)


class Forward(Step):
    line, across = True, False

    def __init__(self, tokens, out_grad, attn_gain, ffn_gain, query_gain, key_gain, w_query, w_key, w_value, w_output,
                 positions, members):
        rows, width = tokens.shape
        length, size, inner = members // 2, members * rows, w_query.shape[1]
        self.heads, self.share, columns = inner // HD, members // KV, inner + 2 * HD
        sems = pltpu.SemaphoreType.DMA((length,))
        self.grads = Gather(out_grad, members)
        freq = ROPE_BASE ** (-np.arange(HD // 2, dtype=np.float32) / (HD // 2))
        freq = jnp.asarray(np.tile(freq, 4)[None], F32)
        self.inputs = [(tokens, VMEM), (out_grad, ANY), (attn_gain[None], VMEM), (ffn_gain[None], VMEM)]
        self.inputs += [(query_gain[None], VMEM), (key_gain[None], VMEM), (w_query, ANY), (w_key, ANY), (w_value, ANY)]
        self.inputs += [(w_output, ANY), (positions.reshape(size // 128, 128), VMEM), (freq, VMEM)]
        self.outputs = [
            (jax.ShapeDtypeStruct((size, width), BF16), ANY),
            (jax.ShapeDtypeStruct((size, columns), F32), VMEM),
            (jax.ShapeDtypeStruct((size, inner), BF16), VMEM),
            (jax.ShapeDtypeStruct((size // BLOCK, 1, self.heads * BLOCK), F32), VMEM),
            (jax.ShapeDtypeStruct((size, width), BF16), ANY),
            (jax.ShapeDtypeStruct((rows, width), F32), VMEM),
            (jax.ShapeDtypeStruct((rows, width), BF16), VMEM),
            (jax.ShapeDtypeStruct((size, 2 * HD), F32), VMEM),
            (jax.ShapeDtypeStruct((size, 2 * HD), F32), VMEM),
        ]
        self.scratch = [pltpu.VMEM((size, width), BF16), pltpu.VMEM(w_query.shape, BF16), pltpu.VMEM((width, 2 * HD), BF16)]
        self.scratch += [pltpu.VMEM((width, 2 * HD), BF16), pltpu.VMEM((width, 2 * HD), BF16), pltpu.VMEM(w_output.shape, BF16)]
        self.scratch += [pltpu.VMEM((size, 2 * HD), jnp.int32)]
        self.scratch += [pltpu.VMEM((size, inner), BF16), pltpu.VMEM((size, HD), BF16), pltpu.VMEM((size, 2 * HD), BF16)]
        self.scratch += [pltpu.VMEM((self.heads * BLOCK, 2 * HD), F32), pltpu.SemaphoreType.DMA((5,))]
        self.scratch += [sems, sems, sems, pltpu.SemaphoreType.DMA((members,))]
        self.scratch += self.grads.scratch + line_sum_scratch(members, rows, width)

    def loads(self, here, wq_ref, wk_ref, wv_ref, wo_ref, wq, wk, wv, wo, load_sem):
        group = (here.pos * 2 + here.core) // self.share
        cols = pl.ds(pl.multiple_of(group // 2 * 2 * HD, 2 * HD), 2 * HD)
        pairs = [(wq_ref, wq), (wk_ref.at[:, cols], wk), (wv_ref.at[:, cols], wv), (wo_ref, wo)]
        return lax.rem(group, 2), [pltpu.make_async_copy(a, b, load_sem.at[i]) for i, (a, b) in enumerate(pairs)]

    def before(self, here, tok_ref, og_ref, again_ref, fgain_ref, qgain_ref, kgain_ref, wq_ref, wk_ref, wv_ref, wo_ref,
               pos_ref, freq_ref, one_ref, proj_ref, ctx_ref, lse_ref, gr_ref, branch_ref, two_ref, cos_ref, sin_ref,
               all_ref, wq, wk, wv, wkv, wo, *rest):
        for load in self.loads(here, wq_ref, wk_ref, wv_ref, wo_ref, wq, wk, wv, wo, rest[5])[1]:
            load.start()
        rows = tok_ref.shape[0]
        me = (here.pos * 2 + here.core) * rows

        def body(r, carry):
            at = pl.ds(pl.multiple_of(r * 32, 32), 32)
            x = tok_ref[at].astype(F32)
            inv = lax.rsqrt(jnp.mean(x * x, -1, keepdims=True) + EPSILON)
            all_ref[pl.ds(pl.multiple_of(me + r * 32, 32), 32)] = (x * inv * again_ref[...]).astype(BF16)
            return carry

        lax.fori_loop(0, rows // 32, body, 0)

    def run(self, here, tok_ref, og_ref, again_ref, fgain_ref, qgain_ref, kgain_ref, wq_ref, wk_ref, wv_ref, wo_ref,
            pos_ref, freq_ref, one_ref, proj_ref, ctx_ref, lse_ref, gr_ref, branch_ref, two_ref, cos_ref, sin_ref,
            all_ref, wq, wk, wv, wkv, wo, place_ref,
            q_ref, k_ref, v_ref, acc_ref, load_sem, left_sem, right_sem, side_sem, recv_sem, *rest):
        pos, core, length = here.pos, here.core, here.length
        rows, width = tok_ref.shape
        heads, inner, size = self.heads, self.heads * HD, proj_ref.shape[0]
        lane = lax.broadcasted_iota(jnp.int32, (1, HD), 1)

        def block(p, c):
            return all_ref.at[pl.ds(pl.multiple_of((p * 2 + c) * rows, rows), rows)]

        def send(p, sem, to_p, to_c):
            remote(block(p, core), block(p, core), sem.at[p], recv_sem.at[p * 2 + core], here.at(to_p, to_c)).start()

        def arrived(p, c):
            pltpu.make_async_copy(block(p, c), block(p, c), recv_sem.at[p * 2 + c]).wait()

        def sent(sem, p):
            pltpu.make_async_copy(block(p, core), block(p, core), sem.at[p]).wait()

        def prepare():
            odd, loads = self.loads(here, wq_ref, wk_ref, wv_ref, wo_ref, wq, wk, wv, wo, load_sem)
            for load in loads:
                load.wait()
            low = lax.broadcasted_iota(jnp.int32, (1, 2 * HD), 1) < HD

            def pick(r, carry):
                at = pl.ds(pl.multiple_of(r * 256, 256), 256)
                key, value = wk[at].astype(F32), wv[at].astype(F32)
                key = jnp.where(odd == 1, pltpu.roll(key, HD, 1), key)
                value = jnp.where(odd == 1, value, pltpu.roll(value, HD, 1))
                wkv[at] = jnp.where(low, key, value).astype(BF16)
                return carry

            lax.fori_loop(0, width // 256, pick, 0)

            def table(r, carry):
                at = pl.ds(pl.multiple_of(r * 128, 128), 128)
                place = jnp.broadcast_to(pos_ref[pl.ds(r, 1)].astype(F32), (128, 128)).T
                place_ref[at] = place.astype(jnp.int32)
                angle = place * freq_ref[...]
                cos_ref[at] = jnp.cos(angle)
                sin_ref[at] = jnp.sin(angle)
                return carry

            lax.fori_loop(0, size // 128, table, 0)

        def use(p):
            at = pl.ds(pl.multiple_of(p * BLOCK, BLOCK), BLOCK)
            x = jnp.concatenate([dot_nn(all_ref[at], wq[...]), dot_nn(all_ref[at], wkv[...])], 1)
            proj_ref[at] = x
            gain = jnp.concatenate([qgain_ref[...]] * heads + [kgain_ref[...], jnp.ones((1, HD), F32)], 1)
            cosine, sine = wide(cos_ref[at], inner + 2 * HD), wide(sin_ref[at], inner + 2 * HD)
            unit, _ = normed(x)
            spun = turn(unit * gain, cosine, sine)
            q_ref[at] = (spun[:, :inner].astype(BF16) * HD**-0.5).astype(BF16)
            k_ref[at] = spun[:, inner : inner + HD].astype(BF16)
            ones = jnp.broadcast_to(jnp.where(lane == 0, 1.0, 0.0), (BLOCK, HD)).astype(BF16)
            v_ref[at] = jnp.concatenate([x[:, inner + HD :].astype(BF16), ones], 1)

        def pass_on(step):
            right, left = pos + step, pos - step

            @pl.when(right < length)
            def _():
                @pl.when(step > 0)
                def _():
                    arrived(right, core)

                @pl.when(pos > 0)
                def _():
                    send(right, left_sem, pos - 1, core)

                send(right, side_sem, pos, 1 - core)

            @pl.when(left >= 0)
            def _():
                @pl.when(step > 0)
                def _():
                    arrived(left, core)

                @pl.when(pos < here.last)
                def _():
                    send(left, right_sem, pos + 1, core)

                @pl.when(step > 0)
                def _():
                    send(left, side_sem, pos, 1 - core)

        def use_both(step):
            def side(k, c):
                p = pos + (1 - 2 * k) * step

                @pl.when((p >= 0) & (p < length) & (step >= k))
                def _():
                    arrived(p, 1 - core)
                    use(p)

                return c

            lax.fori_loop(0, 2, side, 0)

        pass_on(0)
        prepare()

        def hop(step, carry):
            use_both(step)
            pass_on(step + 1)
            return carry

        lax.fori_loop(0, here.last, hop, 0)
        n = len(self.grads.scratch)
        held = rest[n:]
        p_ref = held[0]
        grads = self.grads.run(here, og_ref, gr_ref, *rest[:n])
        next(grads)
        use_both(here.last)
        keep = pltpu.make_async_copy(all_ref, one_ref, load_sem.at[4])
        keep.start()

        def attend(i):
            at = pl.ds(pl.multiple_of(i * BLOCK, BLOCK), BLOCK)
            query = q_ref[at]
            stacked = jnp.concatenate([query[:, h * HD : (h + 1) * HD] for h in range(heads)], 0)
            acc_ref[...] = jnp.zeros_like(acc_ref)
            index = i * BLOCK + lax.broadcasted_iota(jnp.int32, (BLOCK, 1), 0)
            start = index - place_ref[at, :1]

            def keys(j, c):
                cols = pl.ds(pl.multiple_of(j * BLOCK, BLOCK), BLOCK)
                scores = dot_nt(stacked, k_ref[cols])
                place = j * BLOCK + lax.broadcasted_iota(jnp.int32, (1, BLOCK), 1)
                seen = (place >= start) & (place <= index)
                expo = [
                    jnp.where(seen, jnp.exp(scores[h * BLOCK : (h + 1) * BLOCK]), 0.0).astype(BF16)
                    for h in range(heads)
                ]
                acc_ref[...] += dot_nn(jnp.concatenate(expo, 0), v_ref[cols])
                return c

            lax.fori_loop(0, i + 1, keys, 0)
            outs, logs = [], []
            for h in range(heads):
                acc = acc_ref[pl.ds(h * BLOCK, BLOCK)]
                outs.append((acc[:, :HD] * (1.0 / acc[:, HD : HD + 1])).astype(BF16))
                logs.append(jnp.log(acc.T[HD : HD + 1]))
            ctx_ref[at] = jnp.concatenate(outs, 1)
            lse_ref[i] = jnp.concatenate(logs, 1)

        def multiply(p):
            attend(p)
            at = pl.ds(pl.multiple_of(p * BLOCK, BLOCK), BLOCK)

            def body(c, carry):
                cols = pl.ds(pl.multiple_of(c * 512, 512), 512)
                p_ref[at, cols] = dot_nn(ctx_ref[at], wo[:, cols]).astype(BF16)
                return carry

            lax.fori_loop(0, width // 512, body, 0)

        weave([line_sum(here, rows, multiply, branch_ref, *held), grads])

        def body(r, carry):
            at = pl.ds(pl.multiple_of(r * 32, 32), 32)
            x = tok_ref[at].astype(F32) + branch_ref[at]
            inv = lax.rsqrt(jnp.mean(x * x, -1, keepdims=True) + EPSILON)
            two_ref[at] = (x * inv * fgain_ref[...]).astype(BF16)
            return carry

        lax.fori_loop(0, rows // 32, body, 0)

        def drain(p, carry):
            sent(side_sem, p)

            @pl.when((p >= pos) & (pos > 0))
            def _():
                sent(left_sem, p)

            @pl.when((p <= pos) & (pos < here.last))
            def _():
                sent(right_sem, p)

            return carry

        lax.fori_loop(0, length, drain, 0)
        keep.wait()
        yield


class Across(Step):
    line, across = False, True

    def __init__(self, x, parts, colours, late=0):
        self.bits, self.colours, self.late = parts.bit_length() - 1, colours, late
        rows, width = x.shape
        self.inputs = [(x, VMEM)]
        self.outputs = [(jax.ShapeDtypeStruct(x.shape, x.dtype), VMEM)]
        self.scratch = [pltpu.VMEM((rows, width), x.dtype)]
        for _ in colours:
            part = rows // len(colours)
            self.scratch += [pltpu.VMEM((part >> (s + 1), width), x.dtype) for s in range(self.bits)]
            self.scratch += [pltpu.SemaphoreType.DMA((2 * self.bits,))] * 2

    def run(self, here, x_ref, o_ref, sum_ref, *rest):
        for _ in range(self.late):
            yield
        n, rows = self.bits + 2, x_ref.shape[0] // len(self.colours)
        live = [
            self.one(here, backwards, i * rows, rows, x_ref, o_ref, sum_ref, *rest[i * n : (i + 1) * n])
            for i, backwards in enumerate(self.colours)
        ]
        while live:
            live = [r for r in live if next(r, live) is not live]
            yield

    def one(self, here, backwards, start, size, x_ref, o_ref, sum_ref, *rest):
        taken, (send_sem, recv_sem) = rest[: self.bits], rest[self.bits :]
        order = list(range(self.bits))[:: -1 if backwards else 1]
        copies, tile = [], 16

        def part(ref, at, count):
            return ref.at[pl.ds(pl.multiple_of(at, count), count)]

        for s, bit in enumerate(order):
            mine, device = here.partner(bit)
            half = size // 2
            keep, give = start + mine * half, start + (1 - mine) * half
            source = x_ref if s == 0 else sum_ref
            target = o_ref if s == self.bits - 1 else sum_ref
            copy = remote(part(source, give, half), taken[s], send_sem.at[s], recv_sem.at[s], device)
            copy.start()
            copies.append(copy)
            yield
            copy.wait_recv()

            def body(r, carry):
                at = pl.ds(pl.multiple_of(keep + r * tile, tile), tile)
                got = taken[s][pl.ds(pl.multiple_of(r * tile, tile), tile)]
                target[at] = (source[at].astype(F32) + got.astype(F32)).astype(target.dtype)
                return carry

            lax.fori_loop(0, half // tile, body, 0)
            start, size = keep, half
        for s, bit in enumerate(order[::-1]):
            mine, device = here.partner(bit)
            n = self.bits + s
            copy = remote(part(o_ref, start, size), part(o_ref, start, size), send_sem.at[n], recv_sem.at[n], device)
            copy.start()
            copies.append(copy)
            yield
            copy.wait_recv()
            start, size = start - mine * size, size * 2
        for copy in copies:
            copy.wait_send()


class KeyValue(Step):
    line, across = True, True

    def __init__(self, x, width, members, parts):
        self.width, self.extra, self.members = width, x.shape[0] - width, members
        self.sum, self.all = Across(x, parts, (False,)), Gather(x, members)
        self.inputs = [(x, VMEM)]
        flat = jax.ShapeDtypeStruct((width, KV * HD), BF16)
        self.outputs = [(flat, VMEM), (flat, VMEM), (jax.ShapeDtypeStruct((self.extra, 2 * HD), F32), VMEM)]
        self.scratch = [pltpu.VMEM(x.shape, x.dtype), pltpu.VMEM((members * x.shape[0], 2 * HD), x.dtype)]
        self.scratch += self.sum.scratch + self.all.scratch

    def run(self, here, x_ref, key_ref, value_ref, small_ref, sum_ref, all_ref, *rest):
        n = len(self.sum.scratch)
        first = self.sum.run(here, x_ref, sum_ref, *rest[:n])
        next(first)
        yield
        for _ in first:
            pass
        yield from self.all.run(here, sum_ref, all_ref, *rest[n:])
        rows, share, tile = self.width + self.extra, self.members // KV, 128

        def block(group, at, count):
            total = 0.0
            for k in range(share):
                begin = pl.multiple_of((group * share + k) * rows + at, 16)
                total = total + all_ref[pl.ds(begin, count)].astype(F32)
            return total

        for pair in range(KV // 2):
            cols = slice(2 * HD * pair, 2 * HD * (pair + 1))

            def body(r, carry):
                at = pl.ds(pl.multiple_of(r * tile, tile), tile)
                one, two = block(2 * pair, r * tile, tile), block(2 * pair + 1, r * tile, tile)
                key_ref[at, cols] = jnp.concatenate([one[:, :HD], two[:, :HD]], 1).astype(BF16)
                value_ref[at, cols] = jnp.concatenate([one[:, HD:], two[:, HD:]], 1).astype(BF16)
                return carry

            lax.fori_loop(0, self.width // tile, body, 0)
        small = 0.0
        for group in range(KV):
            small = small + block(group, self.width, self.extra)
        small_ref[...] = small


def held_bytes(shape, dtype):
    *lead, rows, columns = (1,) + tuple(shape)
    return int(np.prod(lead)) * -(-rows // 8) * 8 * -(-columns // 128) * 128 * jnp.dtype(dtype).itemsize


def together(steps, members, parts, collective_id, whole=False, spare=6):
    need = 0
    for s in steps:
        need += sum(held_bytes(x.shape, x.dtype) for x, m in s.inputs + s.outputs if m is VMEM)
        need += sum(held_bytes(h.shape, h.dtype) for h in s.scratch if h is not pltpu.SemaphoreType.DMA and h.memory_space == pltpu.VMEM)
    counts = [(len(s.inputs), len(s.outputs), len(s.scratch)) for s in steps]

    def kernel(*refs):
        refs = list(refs)
        given = [[refs.pop(0) for _ in range(c[0])] for c in counts]
        made = [[refs.pop(0) for _ in range(c[1])] for c in counts]
        held = [[refs.pop(0) for _ in range(c[2])] for c in counts]
        here = Place(members, parts)
        peers = here.greet(any(s.line for s in steps), any(s.across for s in steps))
        for s, g, m, h in zip(steps, given, made, held):
            s.before(here, *g, *m, *h)
        here.meet(peers)
        weave([s.run(here, *g, *m, *h) for s, g, m, h in zip(steps, given, made, held)])

    return pl.pallas_call(
        kernel,
        out_shape=[o for s in steps for o, _ in s.outputs],
        in_specs=[m for s in steps for _, m in s.inputs],
        out_specs=[m for s in steps for _, m in s.outputs],
        scratch_shapes=[h for s in steps for h in s.scratch],
        compiler_params=pltpu.CompilerParams(
            collective_id=collective_id, has_side_effects=True, vmem_limit_bytes=58 << 20 if whole else need + (spare << 20)
        ),
        cost_estimate=pl.CostEstimate(flops=1, bytes_accessed=1, transcendentals=0),
    )(*[x for s in steps for x, _ in s.inputs])


def dot_nn(a, b):
    return lax.dot_general(a, b, (((1,), (0,)), ((), ())), preferred_element_type=F32)

def dot_nt(a, b):
    return lax.dot_general(a, b, (((1,), (1,)), ((), ())), preferred_element_type=F32)

def dot_tn(a, b):
    return lax.dot_general(a, b, (((0,), (0,)), ((), ())), preferred_element_type=F32)

def group_mean(x):
    width = x.shape[1]
    row = lax.broadcasted_iota(jnp.int32, (width, width), 0) // HD
    col = lax.broadcasted_iota(jnp.int32, (width, width), 1) // HD
    ones = jnp.where(row == col, 1.0 / HD, 0.0).astype(F32)
    return jnp.dot(x, ones, precision=lax.Precision.HIGHEST, preferred_element_type=F32)

def half_turn(x):
    width = x.shape[1]
    lane = lax.broadcasted_iota(jnp.int32, (1, width), 1)
    first = lax.rem(lane, HD) < HD // 2
    up = pltpu.roll(x, HD // 2, 1)
    down = pltpu.roll(x, width - HD // 2, 1)
    return jnp.where(first, -down, up)

def wide(table, width):
    return jnp.concatenate([table] * (width // table.shape[1]), 1)

def normed(x):
    inv = lax.rsqrt(group_mean(x * x) + EPSILON)
    return x * inv, inv

def turn(x, cosine, sine):
    return x * cosine + half_turn(x) * sine

def turn_back(x, cosine, sine):
    return x * cosine - half_turn(x) * sine

def stack_lanes(x, heads):
    return jnp.concatenate([x[h * HD:(h + 1) * HD] for h in range(heads)], 1)

def attend_back_kernel(heads, proj_ref, cos_ref, sin_ref, qgain_ref, kgain_ref, pos_ref, ctx_ref, grad_ref, lse_ref,
                       out_ref, sums_ref, k_ref, kt_ref, v_ref, dk_ref, dv_ref, dq_ref):
    width = heads * HD
    scale = HD ** -0.5
    count = proj_ref.shape[0] // BLOCK
    gain = jnp.concatenate([qgain_ref[...]] * heads + [kgain_ref[...], jnp.ones((1, HD), F32)], 1)
    def prepare(i, carry):
        rows = pl.ds(pl.multiple_of(i * BLOCK, BLOCK), BLOCK)
        x = proj_ref[rows, width:]
        unit, _ = normed(x)
        spun = turn(unit * gain[:, width:], cos_ref[rows], sin_ref[rows])
        k_ref[rows] = spun[:, :HD].astype(BF16)
        kt_ref[i] = spun.T[:HD].astype(BF16)
        v_ref[rows] = x[:, HD:].astype(BF16)
        dk_ref[rows] = jnp.zeros((BLOCK, HD), F32)
        dv_ref[rows] = jnp.zeros((BLOCK, HD), F32)
        return carry
    lax.fori_loop(0, count, prepare, 0)
    sums_ref[...] = jnp.zeros_like(sums_ref)
    def outer(i, carry):
        rows = pl.ds(pl.multiple_of(i * BLOCK, BLOCK), BLOCK)
        x = proj_ref[rows, :width]
        cosine, sine = wide(cos_ref[rows], width), wide(sin_ref[rows], width)
        unit, inv = normed(x)
        query = (turn(unit * gain[:, :width], cosine, sine).astype(BF16).astype(F32) * scale)
        query_t = stack_lanes(query.T, heads).astype(BF16)
        query = query.astype(BF16)
        query_s = jnp.concatenate([query[:, h * HD:(h + 1) * HD] for h in range(heads)], 0)
        grad = grad_ref[rows]
        grad_s = jnp.concatenate([grad[:, h * HD:(h + 1) * HD] for h in range(heads)], 0)
        grad_t = stack_lanes(grad.astype(F32).T, heads)
        ctx_t = stack_lanes(ctx_ref[rows].astype(F32).T, heads)
        delta = jnp.sum(grad_t * ctx_t, 0, keepdims=True)
        grad_t = grad_t.astype(BF16)
        lse = lse_ref[i]
        index = i * BLOCK + lax.broadcasted_iota(jnp.int32, (1, BLOCK), 1)
        start = index - pos_ref[i]
        dq_ref[...] = jnp.zeros_like(dq_ref)
        def inner(j, c):
            cols = pl.ds(pl.multiple_of(j * BLOCK, BLOCK), BLOCK)
            scores = dot_nn(k_ref[cols], query_t)
            grad_probs = dot_nn(v_ref[cols], grad_t)
            place = j * BLOCK + lax.broadcasted_iota(jnp.int32, (BLOCK, 1), 0)
            seen = (place >= start) & (place <= index)
            probs, back = [], []
            for h in range(heads):
                s = slice(h * BLOCK, (h + 1) * BLOCK)
                exact = jnp.where(seen, jnp.exp(scores[:, s] - lse[:, s]), 0.0)
                probs.append(exact.astype(BF16))
                back.append((exact * (grad_probs[:, s] - delta[:, s])).astype(BF16))
            probs = jnp.concatenate(probs, 1)
            back = jnp.concatenate(back, 1)
            dv_ref[cols] += dot_nn(probs, grad_s)
            dk_ref[cols] += dot_nn(back, query_s)
            dq_ref[...] += dot_nn(kt_ref[j], back)
            return c
        lax.fori_loop(0, i + 1, inner, 0)
        dq = jnp.concatenate([dq_ref[:, h * BLOCK:(h + 1) * BLOCK] for h in range(heads)], 0).T * scale
        dqn = turn_back(dq, cosine, sine)
        sums_ref[:, :width] += jnp.sum(dqn * unit, 0, keepdims=True)
        e = dqn * gain[:, :width]
        out_ref[rows, :width] = (inv * (e - unit * group_mean(e * unit))).astype(BF16)
        return carry
    lax.fori_loop(0, count, outer, 0)
    def finish(i, carry):
        rows = pl.ds(pl.multiple_of(i * BLOCK, BLOCK), BLOCK)
        x = proj_ref[rows, width:]
        unit, inv = normed(x)
        dv = dv_ref[rows]
        dk = jnp.concatenate([dk_ref[rows], dv], 1)
        dkn = turn_back(dk, cos_ref[rows], sin_ref[rows])
        sums_ref[:, width:] += jnp.sum(dkn * unit, 0, keepdims=True)
        e = dkn * gain[:, width:]
        dkp = inv * (e - unit * group_mean(e * unit))
        lane = lax.broadcasted_iota(jnp.int32, (1, 2 * HD), 1)
        out_ref[rows, width:] = jnp.where(lane < HD, dkp, dk).astype(BF16)
        return carry
    lax.fori_loop(0, count, finish, 0)

def attend_back(proj, cosine, sine, query_gain, key_gain, positions, context, grad_context, lse, heads):
    size = proj.shape[0]
    count = size // BLOCK
    vm = pl.BlockSpec(memory_space=pltpu.VMEM)
    return pl.pallas_call(
        functools.partial(attend_back_kernel, heads),
        out_shape=(jax.ShapeDtypeStruct(proj.shape, BF16), jax.ShapeDtypeStruct((1, proj.shape[1]), F32)),
        in_specs=[vm] * 9, out_specs=(vm, vm),
        scratch_shapes=[pltpu.VMEM((size, HD), BF16), pltpu.VMEM((count, HD, BLOCK), BF16), pltpu.VMEM((size, HD), BF16),
                        pltpu.VMEM((size, HD), F32), pltpu.VMEM((size, HD), F32), pltpu.VMEM((HD, heads * BLOCK), F32)],
        compiler_params=pltpu.CompilerParams(vmem_limit_bytes=40 << 20),
        cost_estimate=pl.CostEstimate(flops=1, bytes_accessed=1, transcendentals=0),
    )(proj, cosine, sine, query_gain[None], key_gain[None], positions.reshape(count, 1, BLOCK), context, grad_context, lse)


def matmul(left, right):
    return jnp.dot(left, right, preferred_element_type=F32)


def matmul_left_t(left, right):
    return lax.dot_general(left, right, (((0,), (0,)), ((), ())), preferred_element_type=F32)


def matmul_right_t(left, right):
    return lax.dot_general(left, right, (((1,), (1,)), ((), ())), preferred_element_type=F32)


def norm_back(grad_normed, unit, inverse, gain):
    scaled = grad_normed * gain
    return inverse * (scaled - unit * jnp.mean(scaled * unit, -1, keepdims=True))


def after(first, *later):
    return lax.optimization_barrier((first,) + later)


def per_device(
    tokens,
    seg_ids,
    positions,
    w_query,
    w_key,
    w_value,
    w_output,
    w_gate,
    w_up,
    w_down,
    attn_gain,
    ffn_gain,
    query_gain,
    key_gain,
    out_grad,
):
    members, parts = lax.axis_size("mp"), lax.axis_size("dp")
    width = tokens.shape[1]
    query_width = w_query.shape[1]
    heads = query_width // HD
    ffn_width = w_gate.shape[1]
    share = members // KV
    group = lax.axis_index("mp") // share

    rows_one, projected, context, lse, grad_rows, attn_branch, h_two, cosine, sine = together(
        [
            Forward(
                tokens,
                out_grad,
                attn_gain,
                ffn_gain,
                query_gain,
                key_gain,
                w_query,
                w_key,
                w_value,
                w_output,
                positions,
                members,
            )
        ],
        members,
        parts,
        0,
        True,
    )
    rows_two, hidden, grad_gate, grad_up = together(
        [GatherFfn(h_two, grad_rows, w_gate, w_up, w_down, members)], members, parts, 5, False, 14
    )
    rows_two, tokens_late, w_key, w_value = after(rows_two, tokens, w_key, w_value)
    tokens_f = tokens_late.astype(F32)
    inv_one = lax.rsqrt(jnp.mean(tokens_f * tokens_f, -1, keepdims=True) + EPSILON)
    normed_one = tokens_f * inv_one
    key_cols = lax.dynamic_slice_in_dim(w_key, group * HD, HD, 1)
    value_cols = lax.dynamic_slice_in_dim(w_value, group * HD, HD, 1)
    w_attn = jnp.concatenate([w_query, key_cols, value_cols], 1)
    residual_mid = tokens_f + attn_branch
    inv_two = lax.rsqrt(jnp.mean(residual_mid * residual_mid, -1, keepdims=True) + EPSILON)
    normed_two = residual_mid * inv_two
    ffn_parts = (
        matmul_left_t(hidden, grad_rows).astype(BF16),
        matmul_left_t(rows_two, grad_gate).astype(BF16),
        matmul_left_t(rows_two, grad_up).astype(BF16),
    )
    ffn_parts, grad_gate, grad_up, hidden = lax.optimization_barrier((ffn_parts, grad_gate, grad_up, hidden))
    grad_w_down, grad_w_gate, grad_w_up = lax.psum(ffn_parts, "dp")

    grad_h_two = together(
        [Scatter([(grad_gate, w_gate, True), (grad_up, w_up, True)], members)],
        members,
        parts,
        6,
        True,
    )[0]
    grad_ffn_gain = jnp.sum(grad_h_two * normed_two, 0)
    grad_mid = out_grad.astype(F32) + norm_back(grad_h_two, normed_two, inv_two, ffn_gain)
    grad_attn_rows, ffn_branch = together(
        [Gather(grad_mid.astype(BF16), members), Scatter([(hidden, w_down, False)], members)],
        members,
        parts,
        2,
    )
    grad_context = matmul_right_t(grad_attn_rows, w_output).astype(BF16)
    grad_proj, gain_sums = attend_back(
        projected, cosine, sine, query_gain, key_gain, positions, context, grad_context, lse, heads
    )
    output_part = matmul_left_t(context, grad_attn_rows).astype(BF16)
    grad_w_attn = matmul_left_t(rows_one, grad_proj)
    grad_attn_gain = jnp.sum(w_attn.astype(F32) * grad_w_attn, 1) / attn_gain

    small = jnp.concatenate(
        [
            grad_attn_gain,
            grad_ffn_gain,
            jnp.sum(gain_sums[0, :query_width].reshape(heads, HD), 0),
            gain_sums[0, query_width : query_width + HD],
            jnp.sum(tokens_f * tokens_f)[None],
        ]
    )
    unit = 16 * parts
    extra = -(-small.shape[0] // (unit * 2 * HD)) * unit
    small_rows = jnp.pad(small, (0, extra * 2 * HD - small.shape[0])).reshape(extra, 2 * HD)
    kv_part = jnp.concatenate([grad_w_attn[:, query_width:], small_rows], 0).astype(BF16)
    query_part = grad_w_attn[:, :query_width].astype(BF16)
    grad_w_key, grad_w_value, small_sum, grad_h_one, grad_w_output, grad_w_query = together(
        [
            KeyValue(kv_part, width, members, parts),
            Scatter([(grad_proj, w_attn, True)], members),
            Across(output_part, parts, (False,), 2),
            Across(query_part, parts, (True,), 2),
        ],
        members,
        parts,
        3,
    )
    small_sum = small_sum.reshape(-1)
    entry_count = tokens.size * parts * members
    at = 2 * width
    residual_rms = jnp.sqrt(small_sum[at + 2 * HD : at + 2 * HD + 1] / entry_count)

    grad_tokens = (grad_mid + norm_back(grad_h_one, normed_one, inv_one, attn_gain)).astype(BF16)
    output = (residual_mid + ffn_branch).astype(BF16)
    branch_rms = jnp.stack(
        [
            jnp.sqrt(jnp.mean(attn_branch * attn_branch, -1)),
            jnp.sqrt(jnp.mean(ffn_branch * ffn_branch, -1)),
        ]
    )
    return (
        output,
        grad_tokens,
        grad_w_query.astype(F32),
        grad_w_key.astype(F32),
        grad_w_value.astype(F32),
        grad_w_output.astype(F32),
        grad_w_gate.astype(F32),
        grad_w_up.astype(F32),
        grad_w_down.astype(F32),
        small_sum[:width],
        small_sum[width:at],
        small_sum[at : at + HD],
        small_sum[at + HD : at + 2 * HD],
        residual_rms,
        branch_rms,
    )


def solution(mesh):
    row, whole, column = P(("dp", "mp"), None), P(), P(None, "mp")
    lead = P("mp", None)
    return jax.shard_map(
        per_device,
        mesh=mesh,
        in_specs=(row, P("dp"), P("dp"), column, whole, whole, lead, column, column, lead)
        + (whole,) * 4
        + (row,),
        out_specs=(row, row, column, whole, whole, lead, column, column, lead)
        + (whole,) * 5
        + (P(None, ("dp", "mp")),),
        check_vma=False,
    )
```

```python
import functools

import jax
import jax.numpy as jnp
import numpy as np
from jax import lax
from jax.experimental import pallas as pl
from jax.experimental.pallas import tpu as pltpu
from jax.sharding import PartitionSpec as P

HEADS = 32
KV = 8
HD = 64
EPSILON = 1e-06
ROPE_BASE = 10000.0
BLOCK = 256
F32 = jnp.float32
BF16 = jnp.bfloat16
MESH = pl.DeviceIdType.MESH


ANY = pl.BlockSpec(memory_space=pl.ANY)
VMEM = pl.BlockSpec(memory_space=pltpu.VMEM)


class Place:
    def __init__(self, members, parts):
        me = lax.axis_index("mp")
        self.dp, self.pos, self.core = lax.axis_index("dp"), me // 2, lax.rem(me, 2)
        self.length, self.parts = members // 2, parts
        self.last = self.length - 1

    def at(self, pos, core):
        return (self.dp, pos * 2 + core)

    def partner(self, bit):
        mine = lax.rem(self.dp // (1 << bit), 2)
        return mine, (self.dp + (1 - 2 * mine) * (1 << bit), self.pos * 2 + self.core)

    def bits(self):
        return self.parts.bit_length() - 1

    def greet(self, line, across):
        barrier = pltpu.get_barrier_semaphore()

        def tell(device):
            pl.semaphore_signal(barrier, inc=1, device_id=device, device_id_type=MESH)

        peers = 0
        if line:
            tell(self.at(self.pos, 1 - self.core))

            @pl.when(self.pos > 0)
            def _():
                tell(self.at(self.pos - 1, self.core))

            @pl.when(self.pos < self.last)
            def _():
                tell(self.at(self.pos + 1, self.core))

            peers = 1 + jnp.minimum(self.pos, 1) + jnp.minimum(self.last - self.pos, 1)
        if across:
            for bit in range(self.bits()):
                tell(self.partner(bit)[1])
            peers = peers + self.bits()
        return peers

    def meet(self, peers):
        pl.semaphore_wait(pltpu.get_barrier_semaphore(), peers)


def weave(live):
    while live:
        live = [r for r in live if next(r, live) is not live]


def remote(src, dst, send_sem, recv_sem, device):
    return pltpu.make_async_remote_copy(
        src_ref=src, dst_ref=dst, send_sem=send_sem, recv_sem=recv_sem, device_id=device, device_id_type=MESH
    )


class Step:
    def before(self, *refs):
        pass


class Gather(Step):
    line, across = True, False

    def __init__(self, x, members):
        length = members // 2
        sems = pltpu.SemaphoreType.DMA((length,))
        self.inputs = [(x, ANY)]
        self.outputs = [(jax.ShapeDtypeStruct((members * x.shape[0],) + x.shape[1:], x.dtype), ANY)]
        self.scratch = [pltpu.SemaphoreType.DMA, sems, sems, sems, pltpu.SemaphoreType.DMA((members,))]

    def run(self, here, *refs):
        self.begin(here, *refs)
        for step in range(1, here.length):
            yield
            self.hop(here, step, *refs)
        yield
        self.end(here, *refs)

    def parts(self, here, x_ref, o_ref, own_sem, left_sem, right_sem, side_sem, recv_sem):
        rows = x_ref.shape[0]

        def block(p, c):
            return o_ref.at[pl.ds(pl.multiple_of((p * 2 + c) * rows, rows), rows)]

        def send(src, p, sem, to_p, to_c):
            remote(src, block(p, here.core), sem.at[p], recv_sem.at[p * 2 + here.core], here.at(to_p, to_c)).start()

        def arrived(p, c):
            pltpu.make_async_copy(x_ref, block(p, c), recv_sem.at[p * 2 + c]).wait()

        own = pltpu.make_async_copy(x_ref, block(here.pos, here.core), own_sem)
        return block, send, arrived, own, left_sem, right_sem, side_sem

    def begin(self, here, x_ref, *refs):
        pos, core = here.pos, here.core
        block, send, arrived, own, left_sem, right_sem, side_sem = self.parts(here, x_ref, *refs)

        @pl.when(pos > 0)
        def _():
            send(x_ref, pos, left_sem, pos - 1, core)

        @pl.when(pos < here.last)
        def _():
            send(x_ref, pos, right_sem, pos + 1, core)

        send(x_ref, pos, side_sem, pos, 1 - core)
        own.start()

    def hop(self, here, step, x_ref, *refs):
        pos, core = here.pos, here.core
        block, send, arrived, own, left_sem, right_sem, side_sem = self.parts(here, x_ref, *refs)
        right, left = pos + step, pos - step

        @pl.when(right < here.length)
        def _():
            arrived(right, core)

            @pl.when(pos > 0)
            def _():
                send(block(right, core), right, left_sem, pos - 1, core)

            send(block(right, core), right, side_sem, pos, 1 - core)

        @pl.when(left >= 0)
        def _():
            arrived(left, core)

            @pl.when(pos < here.last)
            def _():
                send(block(left, core), left, right_sem, pos + 1, core)

            send(block(left, core), left, side_sem, pos, 1 - core)

    def end(self, here, x_ref, *refs):
        pos, core = here.pos, here.core
        block, send, arrived, own, left_sem, right_sem, side_sem = self.parts(here, x_ref, *refs)
        own.wait()

        def sent(sem, p):
            pltpu.make_async_copy(x_ref, block(pos, core), sem.at[p]).wait()

        def drain(p, carry):
            arrived(p, 1 - core)
            sent(side_sem, p)

            @pl.when((p >= pos) & (pos > 0))
            def _():
                sent(left_sem, p)

            @pl.when((p <= pos) & (pos < here.last))
            def _():
                sent(right_sem, p)

            return carry

        lax.fori_loop(0, here.length, drain, 0)


class GatherFfn(Step):
    line, across = True, False

    def __init__(self, x, grad_rows, w_gate, w_up, w_down, members):
        length, (rows, width), units = members // 2, x.shape, w_gate.shape[1]
        total = members * rows
        sems = pltpu.SemaphoreType.DMA((length,))
        self.units = units
        self.inputs = [(v, ANY) for v in (x, grad_rows)] + [(v, ANY) for v in (w_gate, w_up, w_down)]
        self.outputs = [
            (jax.ShapeDtypeStruct((total, width), BF16), VMEM),
            (jax.ShapeDtypeStruct((total, units), BF16), VMEM),
            (jax.ShapeDtypeStruct((total, units), BF16), VMEM),
            (jax.ShapeDtypeStruct((total, units), BF16), VMEM),
        ]
        self.scratch = [pltpu.VMEM(v.shape, v.dtype) for v in (grad_rows, w_gate, w_up, w_down)]
        self.scratch += [pltpu.SemaphoreType.DMA((5,)), sems, sems, sems, pltpu.SemaphoreType.DMA((members,))]

    def run(self, here, x_ref, gr_ref, wg_ref, wu_ref, wd_ref, o_ref, hid_ref, gg_ref, gu_ref,
            gr, wg, wu, wd, load_sem, left_sem, right_sem, side_sem, recv_sem):
        pos, core, length = here.pos, here.core, here.length
        rows, units, wide = x_ref.shape[0], self.units, 256

        def block(p, c):
            return o_ref.at[pl.ds(pl.multiple_of((p * 2 + c) * rows, rows), rows)]

        def send(src, p, sem, to_p, to_c):
            remote(src, block(p, core), sem.at[p], recv_sem.at[p * 2 + core], here.at(to_p, to_c)).start()

        def arrived(p, c):
            pltpu.make_async_copy(x_ref, block(p, c), recv_sem.at[p * 2 + c]).wait()

        def sent(sem, p):
            pltpu.make_async_copy(x_ref, block(pos, core), sem.at[p]).wait()

        @pl.when(pos > 0)
        def _():
            send(x_ref, pos, left_sem, pos - 1, core)

        @pl.when(pos < here.last)
        def _():
            send(x_ref, pos, right_sem, pos + 1, core)

        send(x_ref, pos, side_sem, pos, 1 - core)
        pairs = [(x_ref, block(pos, core)), (wg_ref, wg), (wu_ref, wu), (gr_ref, gr), (wd_ref, wd)]
        loads = [pltpu.make_async_copy(a, b, load_sem.at[i]) for i, (a, b) in enumerate(pairs)]
        for load in loads:
            load.start()
        yield
        for load in loads:
            load.wait()

        def use(p):
            at = pl.ds(pl.multiple_of(p * 2 * rows, 2 * rows), 2 * rows)

            def body(c, carry):
                cols = pl.ds(pl.multiple_of(c * wide, wide), wide)
                gate = dot_nn(o_ref[at], wg[:, cols])
                up = dot_nn(o_ref[at], wu[:, cols])
                back = dot_nt(gr[at], wd[cols])
                sigma = 1.0 / (1.0 + jnp.exp(-gate))
                silu = gate * sigma
                hid_ref[at, cols] = (silu * up).astype(BF16)
                gg_ref[at, cols] = (back * up * sigma * (1.0 + gate * (1.0 - sigma))).astype(BF16)
                gu_ref[at, cols] = (back * silu).astype(BF16)
                return carry

            lax.fori_loop(0, units // wide, body, 0)

        def hop(step, carry):
            right, left = pos + step, pos - step

            @pl.when((step > 0) & (right < length))
            def _():
                arrived(right, core)

                @pl.when(pos > 0)
                def _():
                    send(block(right, core), right, left_sem, pos - 1, core)

                send(block(right, core), right, side_sem, pos, 1 - core)

            @pl.when((step > 0) & (left >= 0))
            def _():
                arrived(left, core)

                @pl.when(pos < here.last)
                def _():
                    send(block(left, core), left, right_sem, pos + 1, core)

                send(block(left, core), left, side_sem, pos, 1 - core)

            def side(k, c):
                p = pos + (1 - 2 * k) * step

                @pl.when((p >= 0) & (p < length) & (step >= k))
                def _():
                    arrived(p, 1 - core)
                    use(p)

                return c

            lax.fori_loop(0, 2, side, 0)
            return carry

        lax.fori_loop(0, length, hop, 0)

        def drain(p, carry):
            sent(side_sem, p)

            @pl.when((p >= pos) & (pos > 0))
            def _():
                sent(left_sem, p)

            @pl.when((p <= pos) & (pos < here.last))
            def _():
                sent(right_sem, p)

            return carry

        lax.fori_loop(0, length, drain, 0)


class Scatter(Step):
    line, across = True, False

    def __init__(self, terms, members):
        left, right, turned = terms[0]
        rows, width = left.shape[0] // members, right.shape[0 if turned else 1]
        self.rows, self.width, self.turned = rows, width, [t[2] for t in terms]
        self.depth, self.start = right.shape[1 if turned else 0], [0] * len(terms)
        lefts = [t[0] for t in terms]
        if all(x is left for x in lefts) and len(terms) > 1:
            lefts, self.start = [left], [i * self.depth for i in range(len(terms))]
        self.inputs = [(x, VMEM) for x in lefts] + [(t[1], ANY) for t in terms]
        self.outputs = [(jax.ShapeDtypeStruct((rows, width), F32), VMEM)]
        self.scratch = [pltpu.VMEM(t[1].shape, t[1].dtype) for t in terms]
        self.scratch += [pltpu.SemaphoreType.DMA((len(terms),))] + line_sum_scratch(members, rows, width)

    def run(self, here, *refs):
        total = self.begin(here, *refs)
        for t in range(here.last):
            total.fill(t)
            yield
            total.slot(t)
        total.fill(here.last)
        yield
        total.end()

    def begin(self, here, *refs):
        n = len(self.turned)
        m = len(self.inputs) - n
        lefts, refs = (refs[:m] * n)[:n], refs[m:]
        rights, o_ref, helds, load_sem, p_ref = refs[:n], refs[n], refs[n + 1 : 2 * n + 1], refs[2 * n + 1], refs[2 * n + 2]
        rows, wide = self.rows, 256
        loads = [pltpu.make_async_copy(w, h, load_sem.at[i]) for i, (w, h) in enumerate(zip(rights, helds))]
        for load in loads:
            load.start()

        def multiply(p):
            at = pl.ds(pl.multiple_of(p * 2 * rows, 2 * rows), 2 * rows)

            def body(c, carry):
                cols = pl.ds(pl.multiple_of(c * wide, wide), wide)
                total = None
                for left, held, turned, start in zip(lefts, helds, self.turned, self.start):
                    mine = left[at, start : start + self.depth]
                    part = dot_nt(mine, held[cols]) if turned else dot_nn(mine, held[:, cols])
                    total = part if total is None else total + part
                p_ref[at, cols] = total.astype(BF16)
                return carry

            lax.fori_loop(0, self.width // wide, body, 0)

        for load in loads:
            load.wait()
        return LineSum(here, rows, multiply, o_ref, p_ref, *refs[2 * n + 3 :])


def line_sum_scratch(members, rows, width):
    length = members // 2
    held = [pltpu.VMEM((members * rows, width), BF16), pltpu.VMEM((length, rows, width), BF16)]
    held += [pltpu.VMEM((length, rows, width), BF16)] * 2
    return held + [pltpu.SemaphoreType.DMA((length,))] * 6


class LineSum:
    def __init__(self, here, rows, multiply, o_ref, p_ref, side_buf, left_in, right_in,
                 side_send, side_recv, right_send, right_recv, left_send, left_recv):
        self.here, self.rows, self.multiply, self.o_ref, self.p_ref = here, rows, multiply, o_ref, p_ref
        self.side_buf, self.left_in, self.right_in = side_buf, left_in, right_in
        self.side, self.right, self.left = (side_send, side_recv), (right_send, right_recv), (left_send, left_recv)

    def block(self, p, c):
        return self.p_ref.at[pl.ds(pl.multiple_of((p * 2 + c) * self.rows, self.rows), self.rows)]

    def side_copy(self, p):
        here = self.here
        sems = [s.at[p] for s in self.side]
        return remote(self.block(p, 1 - here.core), self.side_buf.at[p], *sems, here.at(here.pos, 1 - here.core))

    def line_copy(self, p, right):
        here = self.here
        buf, sems = (self.right_in, self.right) if right else (self.left_in, self.left)
        to = here.at(here.pos + 1 if right else here.pos - 1, here.core)
        return remote(self.block(p, here.core), buf.at[p], *[s.at[p] for s in sems], to)

    def add(self, p, incoming, final):
        tile, rows = 16, self.rows

        def body(r, carry):
            s = pl.ds(pl.multiple_of(r * tile, tile), tile)
            mine = pl.ds(pl.multiple_of((p * 2 + self.here.core) * rows + r * tile, tile), tile)
            total = self.p_ref[mine].astype(F32) + self.side_buf[p, s].astype(F32)
            for ref in incoming:
                total = total + ref[p, s].astype(F32)
            if final:
                self.o_ref[s] = total
            else:
                self.p_ref[mine] = total.astype(BF16)
            return carry

        lax.fori_loop(0, rows // tile, body, 0)

    def fill(self, t):
        pos, last = self.here.pos, self.here.last

        def side(k, carry):
            own = t == last
            p = jnp.where(own, pos, k * t + (1 - k) * (last - t))

            @pl.when(jnp.where(own, 1 - k, (1 - 2 * k) * (p - pos)) > 0)
            def _():
                self.multiply(p)
                self.side_copy(p).start()

            return carry

        lax.fori_loop(0, 2, side, 0)

    def move(self, p, right, first, source):
        self.side_copy(p).wait_recv()

        @pl.when(first)
        def _():
            self.add(p, [], False)

        @pl.when(jnp.logical_not(first))
        def _():
            self.line_copy(p, right).wait_recv()
            self.add(p, [source], False)

        self.line_copy(p, right).start()

    def slot(self, t):
        pos, last = self.here.pos, self.here.last
        right_p, left_p = last - t + pos, t - (last - pos)

        @pl.when(t >= pos)
        def _():
            self.move(right_p, True, pos == 0, self.right_in)

        @pl.when(left_p >= 0)
        def _():
            self.move(left_p, False, pos == last, self.left_in)

    def end(self):
        pos, last = self.here.pos, self.here.last
        self.side_copy(pos).wait_recv()

        @pl.when(pos == 0)
        def _():
            self.line_copy(pos, False).wait_recv()
            self.add(pos, [self.left_in], True)

        @pl.when(pos == last)
        def _():
            self.line_copy(pos, True).wait_recv()
            self.add(pos, [self.right_in], True)

        @pl.when((pos > 0) & (pos < last))
        def _():
            self.line_copy(pos, False).wait_recv()
            self.line_copy(pos, True).wait_recv()
            self.add(pos, [self.left_in, self.right_in], True)

        def drain(p, carry):
            self.side_copy(p).wait_send()

            @pl.when(p > pos)
            def _():
                self.line_copy(p, True).wait_send()

            @pl.when(p < pos)
            def _():
                self.line_copy(p, False).wait_send()

            return carry

        lax.fori_loop(0, self.here.length, drain, 0)


def rounds(here, total, hop=None):
    def body(t, carry):
        total.fill(t)

        @pl.when(t < here.last)
        def _():
            if hop is not None:
                hop(t + 1)
            total.slot(t)

        return carry

    lax.fori_loop(0, here.length, body, 0)


class ScatterAlone(Scatter):
    def __init__(self, terms, members, gathered=None):
        Scatter.__init__(self, terms, members)
        self.other = None if gathered is None else Gather(gathered, members)
        self.sizes = [len(v) for v in (self.inputs, self.outputs, self.scratch)]
        if gathered is not None:
            self.inputs = self.inputs + self.other.inputs
            self.outputs = self.outputs + self.other.outputs
            self.scratch = self.scratch + self.other.scratch

    def run(self, here, *refs):
        ends, mine, rest = [len(v) for v in (self.inputs, self.outputs, self.scratch)], [], []
        for size, end in zip(self.sizes, ends):
            mine += refs[:size]
            rest += refs[size:end]
            refs = refs[end:]
        if self.other is not None:
            self.other.begin(here, *rest)
        all_inputs, self.inputs = self.inputs, self.inputs[: self.sizes[0]]
        total = self.begin(here, *mine)
        self.inputs = all_inputs
        rounds(here, total, None if self.other is None else lambda step: self.other.hop(here, step, *rest))
        total.end()
        if self.other is not None:
            self.other.end(here, *rest)
        yield


class Forward(Step):
    line, across = True, False

    def __init__(self, tokens, out_grad, attn_gain, ffn_gain, query_gain, key_gain, w_query, w_key, w_value, w_output,
                 positions, members):
        rows, width = tokens.shape
        length, size, inner = members // 2, members * rows, w_query.shape[1]
        self.heads, self.share, columns = inner // HD, members // KV, inner + 2 * HD
        sems = pltpu.SemaphoreType.DMA((length,))
        self.grads = Gather(out_grad, members)
        freq = ROPE_BASE ** (-np.arange(HD // 2, dtype=np.float32) / (HD // 2))
        freq = jnp.asarray(np.tile(freq, 4)[None], F32)
        self.inputs = [(tokens, VMEM), (out_grad, ANY), (attn_gain[None], VMEM), (ffn_gain[None], VMEM)]
        self.inputs += [(query_gain[None], VMEM), (key_gain[None], VMEM), (w_query, ANY), (w_key, ANY), (w_value, ANY)]
        self.inputs += [(w_output, ANY), (positions.reshape(size // 128, 128), VMEM), (freq, VMEM)]
        self.outputs = [
            (jax.ShapeDtypeStruct((size, width), BF16), ANY),
            (jax.ShapeDtypeStruct((size, columns), F32), VMEM),
            (jax.ShapeDtypeStruct((size, inner), BF16), VMEM),
            (jax.ShapeDtypeStruct((size // BLOCK, 1, self.heads * BLOCK), F32), VMEM),
            (jax.ShapeDtypeStruct((size, width), BF16), ANY),
            (jax.ShapeDtypeStruct((rows, width), F32), VMEM),
            (jax.ShapeDtypeStruct((rows, width), BF16), VMEM),
            (jax.ShapeDtypeStruct((size, 2 * HD), F32), VMEM),
            (jax.ShapeDtypeStruct((size, 2 * HD), F32), VMEM),
        ]
        self.scratch = [pltpu.VMEM((size, width), BF16), pltpu.VMEM(w_query.shape, BF16), pltpu.VMEM((width, 2 * HD), BF16)]
        self.scratch += [pltpu.VMEM((width, 2 * HD), BF16), pltpu.VMEM((width, 2 * HD), BF16), pltpu.VMEM(w_output.shape, BF16)]
        self.scratch += [pltpu.VMEM((size, 2 * HD), jnp.int32)]
        self.scratch += [pltpu.VMEM((size, inner), BF16), pltpu.VMEM((size, HD), BF16), pltpu.VMEM((size, 2 * HD), BF16)]
        self.scratch += [pltpu.VMEM((self.heads * BLOCK, 2 * HD), F32), pltpu.SemaphoreType.DMA((5,))]
        self.scratch += [sems, sems, sems, pltpu.SemaphoreType.DMA((members,))]
        self.scratch += self.grads.scratch + line_sum_scratch(members, rows, width)

    def loads(self, here, wq_ref, wk_ref, wv_ref, wo_ref, wq, wk, wv, wo, load_sem):
        group = (here.pos * 2 + here.core) // self.share
        cols = pl.ds(pl.multiple_of(group // 2 * 2 * HD, 2 * HD), 2 * HD)
        pairs = [(wq_ref, wq), (wk_ref.at[:, cols], wk), (wv_ref.at[:, cols], wv), (wo_ref, wo)]
        return lax.rem(group, 2), [pltpu.make_async_copy(a, b, load_sem.at[i]) for i, (a, b) in enumerate(pairs)]

    def before(self, here, tok_ref, og_ref, again_ref, fgain_ref, qgain_ref, kgain_ref, wq_ref, wk_ref, wv_ref, wo_ref,
               pos_ref, freq_ref, one_ref, proj_ref, ctx_ref, lse_ref, gr_ref, branch_ref, two_ref, cos_ref, sin_ref,
               all_ref, wq, wk, wv, wkv, wo, *rest):
        for load in self.loads(here, wq_ref, wk_ref, wv_ref, wo_ref, wq, wk, wv, wo, rest[5])[1]:
            load.start()
        rows = tok_ref.shape[0]
        me = (here.pos * 2 + here.core) * rows

        def body(r, carry):
            at = pl.ds(pl.multiple_of(r * 32, 32), 32)
            x = tok_ref[at].astype(F32)
            inv = lax.rsqrt(jnp.mean(x * x, -1, keepdims=True) + EPSILON)
            all_ref[pl.ds(pl.multiple_of(me + r * 32, 32), 32)] = (x * inv * again_ref[...]).astype(BF16)
            return carry

        lax.fori_loop(0, rows // 32, body, 0)

    def run(self, here, tok_ref, og_ref, again_ref, fgain_ref, qgain_ref, kgain_ref, wq_ref, wk_ref, wv_ref, wo_ref,
            pos_ref, freq_ref, one_ref, proj_ref, ctx_ref, lse_ref, gr_ref, branch_ref, two_ref, cos_ref, sin_ref,
            all_ref, wq, wk, wv, wkv, wo, place_ref,
            q_ref, k_ref, v_ref, acc_ref, load_sem, left_sem, right_sem, side_sem, recv_sem, *rest):
        pos, core, length = here.pos, here.core, here.length
        rows, width = tok_ref.shape
        heads, inner, size = self.heads, self.heads * HD, proj_ref.shape[0]
        lane = lax.broadcasted_iota(jnp.int32, (1, HD), 1)

        def block(p, c):
            return all_ref.at[pl.ds(pl.multiple_of((p * 2 + c) * rows, rows), rows)]

        def send(p, sem, to_p, to_c):
            remote(block(p, core), block(p, core), sem.at[p], recv_sem.at[p * 2 + core], here.at(to_p, to_c)).start()

        def arrived(p, c):
            pltpu.make_async_copy(block(p, c), block(p, c), recv_sem.at[p * 2 + c]).wait()

        def sent(sem, p):
            pltpu.make_async_copy(block(p, core), block(p, core), sem.at[p]).wait()

        def prepare():
            odd, loads = self.loads(here, wq_ref, wk_ref, wv_ref, wo_ref, wq, wk, wv, wo, load_sem)
            for load in loads:
                load.wait()
            low = lax.broadcasted_iota(jnp.int32, (1, 2 * HD), 1) < HD

            def pick(r, carry):
                at = pl.ds(pl.multiple_of(r * 256, 256), 256)
                key, value = wk[at].astype(F32), wv[at].astype(F32)
                key = jnp.where(odd == 1, pltpu.roll(key, HD, 1), key)
                value = jnp.where(odd == 1, value, pltpu.roll(value, HD, 1))
                wkv[at] = jnp.where(low, key, value).astype(BF16)
                return carry

            lax.fori_loop(0, width // 256, pick, 0)

            def table(r, carry):
                at = pl.ds(pl.multiple_of(r * 128, 128), 128)
                place = jnp.broadcast_to(pos_ref[pl.ds(r, 1)].astype(F32), (128, 128)).T
                place_ref[at] = place.astype(jnp.int32)
                angle = place * freq_ref[...]
                cos_ref[at] = jnp.cos(angle)
                sin_ref[at] = jnp.sin(angle)
                return carry

            lax.fori_loop(0, size // 128, table, 0)

        def use(p):
            at = pl.ds(pl.multiple_of(p * BLOCK, BLOCK), BLOCK)
            x = jnp.concatenate([dot_nn(all_ref[at], wq[...]), dot_nn(all_ref[at], wkv[...])], 1)
            proj_ref[at] = x
            gain = jnp.concatenate([qgain_ref[...]] * heads + [kgain_ref[...], jnp.ones((1, HD), F32)], 1)
            cosine, sine = wide(cos_ref[at], inner + 2 * HD), wide(sin_ref[at], inner + 2 * HD)
            unit, _ = normed(x)
            spun = turn(unit * gain, cosine, sine)
            q_ref[at] = (spun[:, :inner].astype(BF16) * HD**-0.5).astype(BF16)
            k_ref[at] = spun[:, inner : inner + HD].astype(BF16)
            ones = jnp.broadcast_to(jnp.where(lane == 0, 1.0, 0.0), (BLOCK, HD)).astype(BF16)
            v_ref[at] = jnp.concatenate([x[:, inner + HD :].astype(BF16), ones], 1)

        def pass_on(step):
            right, left = pos + step, pos - step

            @pl.when(right < length)
            def _():
                @pl.when(step > 0)
                def _():
                    arrived(right, core)

                @pl.when(pos > 0)
                def _():
                    send(right, left_sem, pos - 1, core)

                send(right, side_sem, pos, 1 - core)

            @pl.when(left >= 0)
            def _():
                @pl.when(step > 0)
                def _():
                    arrived(left, core)

                @pl.when(pos < here.last)
                def _():
                    send(left, right_sem, pos + 1, core)

                @pl.when(step > 0)
                def _():
                    send(left, side_sem, pos, 1 - core)

        def use_both(step):
            def side(k, c):
                p = pos + (1 - 2 * k) * step

                @pl.when((p >= 0) & (p < length) & (step >= k))
                def _():
                    arrived(p, 1 - core)
                    use(p)

                return c

            lax.fori_loop(0, 2, side, 0)

        pass_on(0)
        prepare()

        def hop(step, carry):
            use_both(step)
            pass_on(step + 1)
            return carry

        lax.fori_loop(0, here.last, hop, 0)
        n = len(self.grads.scratch)
        held = rest[n:]
        p_ref = held[0]
        grads = (og_ref, gr_ref) + tuple(rest[:n])
        self.grads.begin(here, *grads)
        use_both(here.last)
        keep = pltpu.make_async_copy(all_ref, one_ref, load_sem.at[4])
        keep.start()

        def attend(i):
            at = pl.ds(pl.multiple_of(i * BLOCK, BLOCK), BLOCK)
            query = q_ref[at]
            stacked = jnp.concatenate([query[:, h * HD : (h + 1) * HD] for h in range(heads)], 0)
            acc_ref[...] = jnp.zeros_like(acc_ref)
            index = i * BLOCK + lax.broadcasted_iota(jnp.int32, (BLOCK, 1), 0)
            start = index - place_ref[at, :1]

            def keys(j, c):
                cols = pl.ds(pl.multiple_of(j * BLOCK, BLOCK), BLOCK)
                scores = dot_nt(stacked, k_ref[cols])
                place = j * BLOCK + lax.broadcasted_iota(jnp.int32, (1, BLOCK), 1)
                seen = (place >= start) & (place <= index)
                expo = [
                    jnp.where(seen, jnp.exp(scores[h * BLOCK : (h + 1) * BLOCK]), 0.0).astype(BF16)
                    for h in range(heads)
                ]
                acc_ref[...] += dot_nn(jnp.concatenate(expo, 0), v_ref[cols])
                return c

            lax.fori_loop(0, i + 1, keys, 0)
            outs, logs = [], []
            for h in range(heads):
                acc = acc_ref[pl.ds(h * BLOCK, BLOCK)]
                outs.append((acc[:, :HD] * (1.0 / acc[:, HD : HD + 1])).astype(BF16))
                logs.append(jnp.log(acc.T[HD : HD + 1]))
            ctx_ref[at] = jnp.concatenate(outs, 1)
            lse_ref[i] = jnp.concatenate(logs, 1)

        def multiply(p):
            attend(p)
            at = pl.ds(pl.multiple_of(p * BLOCK, BLOCK), BLOCK)

            def body(c, carry):
                cols = pl.ds(pl.multiple_of(c * 512, 512), 512)
                p_ref[at, cols] = dot_nn(ctx_ref[at], wo[:, cols]).astype(BF16)
                return carry

            lax.fori_loop(0, width // 512, body, 0)

        total = LineSum(here, rows, multiply, branch_ref, *held)
        rounds(here, total, lambda step: self.grads.hop(here, step, *grads))
        total.end()

        def body(r, carry):
            at = pl.ds(pl.multiple_of(r * 32, 32), 32)
            x = tok_ref[at].astype(F32) + branch_ref[at]
            inv = lax.rsqrt(jnp.mean(x * x, -1, keepdims=True) + EPSILON)
            two_ref[at] = (x * inv * fgain_ref[...]).astype(BF16)
            return carry

        lax.fori_loop(0, rows // 32, body, 0)

        def drain(p, carry):
            sent(side_sem, p)

            @pl.when((p >= pos) & (pos > 0))
            def _():
                sent(left_sem, p)

            @pl.when((p <= pos) & (pos < here.last))
            def _():
                sent(right_sem, p)

            return carry

        lax.fori_loop(0, length, drain, 0)
        self.grads.end(here, *grads)
        keep.wait()
        yield


class Across(Step):
    line, across = False, True

    def __init__(self, x, parts, colours, late=0):
        self.bits, self.colours, self.late = parts.bit_length() - 1, colours, late
        rows, width = x.shape
        self.inputs = [(x, VMEM)]
        self.outputs = [(jax.ShapeDtypeStruct(x.shape, x.dtype), VMEM)]
        self.scratch = [pltpu.VMEM((rows, width), x.dtype)]
        for _ in colours:
            part = rows // len(colours)
            self.scratch += [pltpu.VMEM((part >> (s + 1), width), x.dtype) for s in range(self.bits)]
            self.scratch += [pltpu.SemaphoreType.DMA((2 * self.bits,))] * 2

    def run(self, here, x_ref, o_ref, sum_ref, *rest):
        for _ in range(self.late):
            yield
        n, rows = self.bits + 2, x_ref.shape[0] // len(self.colours)
        live = [
            self.one(here, backwards, i * rows, rows, x_ref, o_ref, sum_ref, *rest[i * n : (i + 1) * n])
            for i, backwards in enumerate(self.colours)
        ]
        while live:
            live = [r for r in live if next(r, live) is not live]
            yield

    def one(self, here, backwards, start, size, x_ref, o_ref, sum_ref, *rest):
        taken, (send_sem, recv_sem) = rest[: self.bits], rest[self.bits :]
        order = list(range(self.bits))[:: -1 if backwards else 1]
        copies, tile = [], 16

        def part(ref, at, count):
            return ref.at[pl.ds(pl.multiple_of(at, count), count)]

        for s, bit in enumerate(order):
            mine, device = here.partner(bit)
            half = size // 2
            keep, give = start + mine * half, start + (1 - mine) * half
            source = x_ref if s == 0 else sum_ref
            target = o_ref if s == self.bits - 1 else sum_ref
            copy = remote(part(source, give, half), taken[s], send_sem.at[s], recv_sem.at[s], device)
            copy.start()
            copies.append(copy)
            yield
            copy.wait_recv()

            def body(r, carry):
                at = pl.ds(pl.multiple_of(keep + r * tile, tile), tile)
                got = taken[s][pl.ds(pl.multiple_of(r * tile, tile), tile)]
                target[at] = (source[at].astype(F32) + got.astype(F32)).astype(target.dtype)
                return carry

            lax.fori_loop(0, half // tile, body, 0)
            start, size = keep, half
        for s, bit in enumerate(order[::-1]):
            mine, device = here.partner(bit)
            n = self.bits + s
            copy = remote(part(o_ref, start, size), part(o_ref, start, size), send_sem.at[n], recv_sem.at[n], device)
            copy.start()
            copies.append(copy)
            yield
            copy.wait_recv()
            start, size = start - mine * size, size * 2
        for copy in copies:
            copy.wait_send()


class KeyValue(Step):
    line, across = True, True

    def __init__(self, x, width, members, parts):
        self.width, self.extra, self.members = width, x.shape[0] - width, members
        self.sum, self.all = Across(x, parts, (False,)), Gather(x, members)
        self.inputs = [(x, VMEM)]
        flat = jax.ShapeDtypeStruct((width, KV * HD), BF16)
        self.outputs = [(flat, VMEM), (flat, VMEM), (jax.ShapeDtypeStruct((self.extra, 2 * HD), F32), VMEM)]
        self.scratch = [pltpu.VMEM(x.shape, x.dtype), pltpu.VMEM((members * x.shape[0], 2 * HD), x.dtype)]
        self.scratch += self.sum.scratch + self.all.scratch

    def run(self, here, x_ref, key_ref, value_ref, small_ref, sum_ref, all_ref, *rest):
        n = len(self.sum.scratch)
        first = self.sum.run(here, x_ref, sum_ref, *rest[:n])
        next(first)
        yield
        for _ in first:
            pass
        yield from self.all.run(here, sum_ref, all_ref, *rest[n:])
        rows, share, tile = self.width + self.extra, self.members // KV, 128

        def block(group, at, count):
            total = 0.0
            for k in range(share):
                begin = pl.multiple_of((group * share + k) * rows + at, 16)
                total = total + all_ref[pl.ds(begin, count)].astype(F32)
            return total

        for pair in range(KV // 2):
            cols = slice(2 * HD * pair, 2 * HD * (pair + 1))

            def body(r, carry):
                at = pl.ds(pl.multiple_of(r * tile, tile), tile)
                one, two = block(2 * pair, r * tile, tile), block(2 * pair + 1, r * tile, tile)
                key_ref[at, cols] = jnp.concatenate([one[:, :HD], two[:, :HD]], 1).astype(BF16)
                value_ref[at, cols] = jnp.concatenate([one[:, HD:], two[:, HD:]], 1).astype(BF16)
                return carry

            lax.fori_loop(0, self.width // tile, body, 0)
        small = 0.0
        for group in range(KV):
            small = small + block(group, self.width, self.extra)
        small_ref[...] = small


def held_bytes(shape, dtype):
    *lead, rows, columns = (1,) + tuple(shape)
    return int(np.prod(lead)) * -(-rows // 8) * 8 * -(-columns // 128) * 128 * jnp.dtype(dtype).itemsize


def together(steps, members, parts, collective_id, whole=False, spare=6):
    need = 0
    for s in steps:
        need += sum(held_bytes(x.shape, x.dtype) for x, m in s.inputs + s.outputs if m is VMEM)
        need += sum(held_bytes(h.shape, h.dtype) for h in s.scratch if h is not pltpu.SemaphoreType.DMA and h.memory_space == pltpu.VMEM)
    counts = [(len(s.inputs), len(s.outputs), len(s.scratch)) for s in steps]

    def kernel(*refs):
        refs = list(refs)
        given = [[refs.pop(0) for _ in range(c[0])] for c in counts]
        made = [[refs.pop(0) for _ in range(c[1])] for c in counts]
        held = [[refs.pop(0) for _ in range(c[2])] for c in counts]
        here = Place(members, parts)
        peers = here.greet(any(s.line for s in steps), any(s.across for s in steps))
        for s, g, m, h in zip(steps, given, made, held):
            s.before(here, *g, *m, *h)
        here.meet(peers)
        weave([s.run(here, *g, *m, *h) for s, g, m, h in zip(steps, given, made, held)])

    return pl.pallas_call(
        kernel,
        out_shape=[o for s in steps for o, _ in s.outputs],
        in_specs=[m for s in steps for _, m in s.inputs],
        out_specs=[m for s in steps for _, m in s.outputs],
        scratch_shapes=[h for s in steps for h in s.scratch],
        compiler_params=pltpu.CompilerParams(
            collective_id=collective_id, has_side_effects=True, vmem_limit_bytes=58 << 20 if whole else need + (spare << 20)
        ),
        cost_estimate=pl.CostEstimate(flops=1, bytes_accessed=1, transcendentals=0),
    )(*[x for s in steps for x, _ in s.inputs])


def dot_nn(a, b):
    return lax.dot_general(a, b, (((1,), (0,)), ((), ())), preferred_element_type=F32)

def dot_nt(a, b):
    return lax.dot_general(a, b, (((1,), (1,)), ((), ())), preferred_element_type=F32)

def dot_tn(a, b):
    return lax.dot_general(a, b, (((0,), (0,)), ((), ())), preferred_element_type=F32)

def group_mean(x):
    width = x.shape[1]
    row = lax.broadcasted_iota(jnp.int32, (width, width), 0) // HD
    col = lax.broadcasted_iota(jnp.int32, (width, width), 1) // HD
    ones = jnp.where(row == col, 1.0 / HD, 0.0).astype(F32)
    return jnp.dot(x, ones, precision=lax.Precision.HIGHEST, preferred_element_type=F32)

def half_turn(x):
    width = x.shape[1]
    lane = lax.broadcasted_iota(jnp.int32, (1, width), 1)
    first = lax.rem(lane, HD) < HD // 2
    up = pltpu.roll(x, HD // 2, 1)
    down = pltpu.roll(x, width - HD // 2, 1)
    return jnp.where(first, -down, up)

def wide(table, width):
    return jnp.concatenate([table] * (width // table.shape[1]), 1)

def normed(x):
    inv = lax.rsqrt(group_mean(x * x) + EPSILON)
    return x * inv, inv

def turn(x, cosine, sine):
    return x * cosine + half_turn(x) * sine

def turn_back(x, cosine, sine):
    return x * cosine - half_turn(x) * sine

def stack_lanes(x, heads):
    return jnp.concatenate([x[h * HD:(h + 1) * HD] for h in range(heads)], 1)

def attend_back_kernel(heads, proj_ref, cos_ref, sin_ref, qgain_ref, kgain_ref, pos_ref, ctx_ref, grad_ref, lse_ref,
                       out_ref, sums_ref, k_ref, kt_ref, v_ref, dk_ref, dv_ref, dq_ref):
    width = heads * HD
    scale = HD ** -0.5
    count = proj_ref.shape[0] // BLOCK
    gain = jnp.concatenate([qgain_ref[...]] * heads + [kgain_ref[...], jnp.ones((1, HD), F32)], 1)
    def prepare(i, carry):
        rows = pl.ds(pl.multiple_of(i * BLOCK, BLOCK), BLOCK)
        x = proj_ref[rows, width:]
        unit, _ = normed(x)
        spun = turn(unit * gain[:, width:], cos_ref[rows], sin_ref[rows])
        k_ref[rows] = spun[:, :HD].astype(BF16)
        kt_ref[i] = spun.T[:HD].astype(BF16)
        v_ref[rows] = x[:, HD:].astype(BF16)
        dk_ref[rows] = jnp.zeros((BLOCK, HD), F32)
        dv_ref[rows] = jnp.zeros((BLOCK, HD), F32)
        return carry
    lax.fori_loop(0, count, prepare, 0)
    sums_ref[...] = jnp.zeros_like(sums_ref)
    def outer(i, carry):
        rows = pl.ds(pl.multiple_of(i * BLOCK, BLOCK), BLOCK)
        x = proj_ref[rows, :width]
        cosine, sine = wide(cos_ref[rows], width), wide(sin_ref[rows], width)
        unit, inv = normed(x)
        query = (turn(unit * gain[:, :width], cosine, sine).astype(BF16).astype(F32) * scale)
        query_t = stack_lanes(query.T, heads).astype(BF16)
        query = query.astype(BF16)
        query_s = jnp.concatenate([query[:, h * HD:(h + 1) * HD] for h in range(heads)], 0)
        grad = grad_ref[rows]
        grad_s = jnp.concatenate([grad[:, h * HD:(h + 1) * HD] for h in range(heads)], 0)
        grad_t = stack_lanes(grad.astype(F32).T, heads)
        ctx_t = stack_lanes(ctx_ref[rows].astype(F32).T, heads)
        delta = jnp.sum(grad_t * ctx_t, 0, keepdims=True)
        grad_t = grad_t.astype(BF16)
        lse = lse_ref[i]
        index = i * BLOCK + lax.broadcasted_iota(jnp.int32, (1, BLOCK), 1)
        start = index - pos_ref[i]
        dq_ref[...] = jnp.zeros_like(dq_ref)
        def inner(j, c):
            cols = pl.ds(pl.multiple_of(j * BLOCK, BLOCK), BLOCK)
            scores = dot_nn(k_ref[cols], query_t)
            grad_probs = dot_nn(v_ref[cols], grad_t)
            place = j * BLOCK + lax.broadcasted_iota(jnp.int32, (BLOCK, 1), 0)
            seen = (place >= start) & (place <= index)
            probs, back = [], []
            for h in range(heads):
                s = slice(h * BLOCK, (h + 1) * BLOCK)
                exact = jnp.where(seen, jnp.exp(scores[:, s] - lse[:, s]), 0.0)
                probs.append(exact.astype(BF16))
                back.append((exact * (grad_probs[:, s] - delta[:, s])).astype(BF16))
            probs = jnp.concatenate(probs, 1)
            back = jnp.concatenate(back, 1)
            dv_ref[cols] += dot_nn(probs, grad_s)
            dk_ref[cols] += dot_nn(back, query_s)
            dq_ref[...] += dot_nn(kt_ref[j], back)
            return c
        lax.fori_loop(0, i + 1, inner, 0)
        dq = jnp.concatenate([dq_ref[:, h * BLOCK:(h + 1) * BLOCK] for h in range(heads)], 0).T * scale
        dqn = turn_back(dq, cosine, sine)
        sums_ref[:, :width] += jnp.sum(dqn * unit, 0, keepdims=True)
        e = dqn * gain[:, :width]
        out_ref[rows, :width] = (inv * (e - unit * group_mean(e * unit))).astype(BF16)
        return carry
    lax.fori_loop(0, count, outer, 0)
    def finish(i, carry):
        rows = pl.ds(pl.multiple_of(i * BLOCK, BLOCK), BLOCK)
        x = proj_ref[rows, width:]
        unit, inv = normed(x)
        dv = dv_ref[rows]
        dk = jnp.concatenate([dk_ref[rows], dv], 1)
        dkn = turn_back(dk, cos_ref[rows], sin_ref[rows])
        sums_ref[:, width:] += jnp.sum(dkn * unit, 0, keepdims=True)
        e = dkn * gain[:, width:]
        dkp = inv * (e - unit * group_mean(e * unit))
        lane = lax.broadcasted_iota(jnp.int32, (1, 2 * HD), 1)
        out_ref[rows, width:] = jnp.where(lane < HD, dkp, dk).astype(BF16)
        return carry
    lax.fori_loop(0, count, finish, 0)

def attend_back(proj, cosine, sine, query_gain, key_gain, positions, context, grad_context, lse, heads):
    size = proj.shape[0]
    count = size // BLOCK
    vm = pl.BlockSpec(memory_space=pltpu.VMEM)
    return pl.pallas_call(
        functools.partial(attend_back_kernel, heads),
        out_shape=(jax.ShapeDtypeStruct(proj.shape, BF16), jax.ShapeDtypeStruct((1, proj.shape[1]), F32)),
        in_specs=[vm] * 9, out_specs=(vm, vm),
        scratch_shapes=[pltpu.VMEM((size, HD), BF16), pltpu.VMEM((count, HD, BLOCK), BF16), pltpu.VMEM((size, HD), BF16),
                        pltpu.VMEM((size, HD), F32), pltpu.VMEM((size, HD), F32), pltpu.VMEM((HD, heads * BLOCK), F32)],
        compiler_params=pltpu.CompilerParams(vmem_limit_bytes=40 << 20),
        cost_estimate=pl.CostEstimate(flops=1, bytes_accessed=1, transcendentals=0),
    )(proj, cosine, sine, query_gain[None], key_gain[None], positions.reshape(count, 1, BLOCK), context, grad_context, lse)


def matmul(left, right):
    return jnp.dot(left, right, preferred_element_type=F32)


def matmul_left_t(left, right):
    return lax.dot_general(left, right, (((0,), (0,)), ((), ())), preferred_element_type=F32)


def matmul_right_t(left, right):
    return lax.dot_general(left, right, (((1,), (1,)), ((), ())), preferred_element_type=F32)


def norm_back(grad_normed, unit, inverse, gain):
    scaled = grad_normed * gain
    return inverse * (scaled - unit * jnp.mean(scaled * unit, -1, keepdims=True))


def after(first, *later):
    return lax.optimization_barrier((first,) + later)


def per_device(
    tokens,
    seg_ids,
    positions,
    w_query,
    w_key,
    w_value,
    w_output,
    w_gate,
    w_up,
    w_down,
    attn_gain,
    ffn_gain,
    query_gain,
    key_gain,
    out_grad,
):
    members, parts = lax.axis_size("mp"), lax.axis_size("dp")
    width = tokens.shape[1]
    query_width = w_query.shape[1]
    heads = query_width // HD
    ffn_width = w_gate.shape[1]
    share = members // KV
    group = lax.axis_index("mp") // share

    rows_one, projected, context, lse, grad_rows, attn_branch, h_two, cosine, sine = together(
        [
            Forward(
                tokens,
                out_grad,
                attn_gain,
                ffn_gain,
                query_gain,
                key_gain,
                w_query,
                w_key,
                w_value,
                w_output,
                positions,
                members,
            )
        ],
        members,
        parts,
        0,
        True,
    )
    rows_two, hidden, grad_gate, grad_up = together(
        [GatherFfn(h_two, grad_rows, w_gate, w_up, w_down, members)], members, parts, 5, False, 14
    )
    rows_two, tokens_late, w_key, w_value = after(rows_two, tokens, w_key, w_value)
    tokens_f = tokens_late.astype(F32)
    inv_one = lax.rsqrt(jnp.mean(tokens_f * tokens_f, -1, keepdims=True) + EPSILON)
    normed_one = tokens_f * inv_one
    key_cols = lax.dynamic_slice_in_dim(w_key, group * HD, HD, 1)
    value_cols = lax.dynamic_slice_in_dim(w_value, group * HD, HD, 1)
    w_attn = jnp.concatenate([w_query, key_cols, value_cols], 1)
    residual_mid = tokens_f + attn_branch
    inv_two = lax.rsqrt(jnp.mean(residual_mid * residual_mid, -1, keepdims=True) + EPSILON)
    normed_two = residual_mid * inv_two
    ffn_parts = (
        matmul_left_t(hidden, grad_rows).astype(BF16),
        matmul_left_t(rows_two, grad_gate).astype(BF16),
        matmul_left_t(rows_two, grad_up).astype(BF16),
    )
    ffn_parts, grad_gate, grad_up, hidden = lax.optimization_barrier((ffn_parts, grad_gate, grad_up, hidden))
    grad_w_down, grad_w_gate, grad_w_up = lax.psum(ffn_parts, "dp")

    grad_h_two = together(
        [ScatterAlone([(grad_gate, w_gate, True), (grad_up, w_up, True)], members)],
        members,
        parts,
        6,
        True,
    )[0]
    grad_ffn_gain = jnp.sum(grad_h_two * normed_two, 0)
    grad_mid = out_grad.astype(F32) + norm_back(grad_h_two, normed_two, inv_two, ffn_gain)
    ffn_branch, grad_attn_rows = together(
        [ScatterAlone([(hidden, w_down, False)], members, grad_mid.astype(BF16))],
        members,
        parts,
        2,
    )
    grad_context = matmul_right_t(grad_attn_rows, w_output).astype(BF16)
    grad_proj, gain_sums = attend_back(
        projected, cosine, sine, query_gain, key_gain, positions, context, grad_context, lse, heads
    )
    output_part = matmul_left_t(context, grad_attn_rows).astype(BF16)
    grad_w_attn = matmul_left_t(rows_one, grad_proj)
    grad_attn_gain = jnp.sum(w_attn.astype(F32) * grad_w_attn, 1) / attn_gain

    small = jnp.concatenate(
        [
            grad_attn_gain,
            grad_ffn_gain,
            jnp.sum(gain_sums[0, :query_width].reshape(heads, HD), 0),
            gain_sums[0, query_width : query_width + HD],
            jnp.sum(tokens_f * tokens_f)[None],
        ]
    )
    unit = 16 * parts
    extra = -(-small.shape[0] // (unit * 2 * HD)) * unit
    small_rows = jnp.pad(small, (0, extra * 2 * HD - small.shape[0])).reshape(extra, 2 * HD)
    kv_part = jnp.concatenate([grad_w_attn[:, query_width:], small_rows], 0).astype(BF16)
    query_part = grad_w_attn[:, :query_width].astype(BF16)
    grad_w_key, grad_w_value, small_sum, grad_h_one, grad_w_output, grad_w_query = together(
        [
            KeyValue(kv_part, width, members, parts),
            Scatter([(grad_proj, w_attn, True)], members),
            Across(output_part, parts, (False,), 2),
            Across(query_part, parts, (True,), 2),
        ],
        members,
        parts,
        3,
    )
    small_sum = small_sum.reshape(-1)
    entry_count = tokens.size * parts * members
    at = 2 * width
    residual_rms = jnp.sqrt(small_sum[at + 2 * HD : at + 2 * HD + 1] / entry_count)

    grad_tokens = (grad_mid + norm_back(grad_h_one, normed_one, inv_one, attn_gain)).astype(BF16)
    output = (residual_mid + ffn_branch).astype(BF16)
    branch_rms = jnp.stack(
        [
            jnp.sqrt(jnp.mean(attn_branch * attn_branch, -1)),
            jnp.sqrt(jnp.mean(ffn_branch * ffn_branch, -1)),
        ]
    )
    return (
        output,
        grad_tokens,
        grad_w_query.astype(F32),
        grad_w_key.astype(F32),
        grad_w_value.astype(F32),
        grad_w_output.astype(F32),
        grad_w_gate.astype(F32),
        grad_w_up.astype(F32),
        grad_w_down.astype(F32),
        small_sum[:width],
        small_sum[width:at],
        small_sum[at : at + HD],
        small_sum[at + HD : at + 2 * HD],
        residual_rms,
        branch_rms,
    )


def solution(mesh):
    row, whole, column = P(("dp", "mp"), None), P(), P(None, "mp")
    lead = P("mp", None)
    return jax.shard_map(
        per_device,
        mesh=mesh,
        in_specs=(row, P("dp"), P("dp"), column, whole, whole, lead, column, column, lead)
        + (whole,) * 4
        + (row,),
        out_specs=(row, row, column, whole, whole, lead, column, column, lead)
        + (whole,) * 5
        + (P(None, ("dp", "mp")),),
        check_vma=False,
    )
```

```python
import functools

import jax
import jax.numpy as jnp
import numpy as np
from jax import lax
from jax.experimental import pallas as pl
from jax.experimental.pallas import tpu as pltpu
from jax.sharding import PartitionSpec as P

HEADS = 32
KV = 8
HD = 64
EPSILON = 1e-06
ROPE_BASE = 10000.0
BLOCK = 256
F32 = jnp.float32
BF16 = jnp.bfloat16
MESH = pl.DeviceIdType.MESH


ANY = pl.BlockSpec(memory_space=pl.ANY)
VMEM = pl.BlockSpec(memory_space=pltpu.VMEM)


class Place:
    def __init__(self, members, parts):
        me = lax.axis_index("mp")
        self.dp, self.pos, self.core = lax.axis_index("dp"), me // 2, lax.rem(me, 2)
        self.length, self.parts = members // 2, parts
        self.last = self.length - 1

    def at(self, pos, core):
        return (self.dp, pos * 2 + core)

    def partner(self, bit):
        mine = lax.rem(self.dp // (1 << bit), 2)
        return mine, (self.dp + (1 - 2 * mine) * (1 << bit), self.pos * 2 + self.core)

    def bits(self):
        return self.parts.bit_length() - 1

    def greet(self, line, across):
        barrier = pltpu.get_barrier_semaphore()

        def tell(device):
            pl.semaphore_signal(barrier, inc=1, device_id=device, device_id_type=MESH)

        peers = 0
        if line:
            tell(self.at(self.pos, 1 - self.core))

            @pl.when(self.pos > 0)
            def _():
                tell(self.at(self.pos - 1, self.core))

            @pl.when(self.pos < self.last)
            def _():
                tell(self.at(self.pos + 1, self.core))

            peers = 1 + jnp.minimum(self.pos, 1) + jnp.minimum(self.last - self.pos, 1)
        if across:
            for bit in range(self.bits()):
                tell(self.partner(bit)[1])
            peers = peers + self.bits()
        return peers

    def meet(self, peers):
        pl.semaphore_wait(pltpu.get_barrier_semaphore(), peers)


def weave(live):
    while live:
        live = [r for r in live if next(r, live) is not live]


def remote(src, dst, send_sem, recv_sem, device):
    return pltpu.make_async_remote_copy(
        src_ref=src, dst_ref=dst, send_sem=send_sem, recv_sem=recv_sem, device_id=device, device_id_type=MESH
    )


class Step:
    def before(self, *refs):
        pass


class Gather(Step):
    line, across = True, False

    def __init__(self, x, members):
        length = members // 2
        sems = pltpu.SemaphoreType.DMA((length,))
        self.inputs = [(x, ANY)]
        self.outputs = [(jax.ShapeDtypeStruct((members * x.shape[0],) + x.shape[1:], x.dtype), ANY)]
        self.scratch = [pltpu.SemaphoreType.DMA, sems, sems, sems, pltpu.SemaphoreType.DMA((members,))]

    def run(self, here, *refs):
        self.begin(here, *refs)
        for step in range(1, here.length):
            yield
            self.hop(here, step, *refs)
        yield
        self.end(here, *refs)

    def parts(self, here, x_ref, o_ref, own_sem, left_sem, right_sem, side_sem, recv_sem):
        rows = x_ref.shape[0]

        def block(p, c):
            return o_ref.at[pl.ds(pl.multiple_of((p * 2 + c) * rows, rows), rows)]

        def send(src, p, sem, to_p, to_c):
            remote(src, block(p, here.core), sem.at[p], recv_sem.at[p * 2 + here.core], here.at(to_p, to_c)).start()

        def arrived(p, c):
            pltpu.make_async_copy(x_ref, block(p, c), recv_sem.at[p * 2 + c]).wait()

        own = pltpu.make_async_copy(x_ref, block(here.pos, here.core), own_sem)
        return block, send, arrived, own, left_sem, right_sem, side_sem

    def begin(self, here, x_ref, *refs):
        pos, core = here.pos, here.core
        block, send, arrived, own, left_sem, right_sem, side_sem = self.parts(here, x_ref, *refs)

        @pl.when(pos > 0)
        def _():
            send(x_ref, pos, left_sem, pos - 1, core)

        @pl.when(pos < here.last)
        def _():
            send(x_ref, pos, right_sem, pos + 1, core)

        send(x_ref, pos, side_sem, pos, 1 - core)
        own.start()

    def hop(self, here, step, x_ref, *refs):
        pos, core = here.pos, here.core
        block, send, arrived, own, left_sem, right_sem, side_sem = self.parts(here, x_ref, *refs)
        right, left = pos + step, pos - step

        @pl.when(right < here.length)
        def _():
            arrived(right, core)

            @pl.when(pos > 0)
            def _():
                send(block(right, core), right, left_sem, pos - 1, core)

            send(block(right, core), right, side_sem, pos, 1 - core)

        @pl.when(left >= 0)
        def _():
            arrived(left, core)

            @pl.when(pos < here.last)
            def _():
                send(block(left, core), left, right_sem, pos + 1, core)

            send(block(left, core), left, side_sem, pos, 1 - core)

    def end(self, here, x_ref, *refs):
        pos, core = here.pos, here.core
        block, send, arrived, own, left_sem, right_sem, side_sem = self.parts(here, x_ref, *refs)
        own.wait()

        def sent(sem, p):
            pltpu.make_async_copy(x_ref, block(pos, core), sem.at[p]).wait()

        def drain(p, carry):
            arrived(p, 1 - core)
            sent(side_sem, p)

            @pl.when((p >= pos) & (pos > 0))
            def _():
                sent(left_sem, p)

            @pl.when((p <= pos) & (pos < here.last))
            def _():
                sent(right_sem, p)

            return carry

        lax.fori_loop(0, here.length, drain, 0)


class GatherFfn(Step):
    line, across = True, False

    def __init__(self, x, grad_rows, w_gate, w_up, w_down, members):
        length, (rows, width), units = members // 2, x.shape, w_gate.shape[1]
        total = members * rows
        sems = pltpu.SemaphoreType.DMA((length,))
        self.units = units
        self.inputs = [(v, ANY) for v in (x, grad_rows)] + [(v, ANY) for v in (w_gate, w_up, w_down)]
        self.outputs = [
            (jax.ShapeDtypeStruct((total, width), BF16), VMEM),
            (jax.ShapeDtypeStruct((total, units), BF16), VMEM),
            (jax.ShapeDtypeStruct((total, units), BF16), VMEM),
            (jax.ShapeDtypeStruct((total, units), BF16), VMEM),
        ]
        self.scratch = [pltpu.VMEM(v.shape, v.dtype) for v in (grad_rows, w_gate, w_up, w_down)]
        self.scratch += [pltpu.SemaphoreType.DMA((5,)), sems, sems, sems, pltpu.SemaphoreType.DMA((members,))]

    def run(self, here, x_ref, gr_ref, wg_ref, wu_ref, wd_ref, o_ref, hid_ref, gg_ref, gu_ref,
            gr, wg, wu, wd, load_sem, left_sem, right_sem, side_sem, recv_sem):
        pos, core, length = here.pos, here.core, here.length
        rows, units, wide = x_ref.shape[0], self.units, 256

        def block(p, c):
            return o_ref.at[pl.ds(pl.multiple_of((p * 2 + c) * rows, rows), rows)]

        def send(src, p, sem, to_p, to_c):
            remote(src, block(p, core), sem.at[p], recv_sem.at[p * 2 + core], here.at(to_p, to_c)).start()

        def arrived(p, c):
            pltpu.make_async_copy(x_ref, block(p, c), recv_sem.at[p * 2 + c]).wait()

        def sent(sem, p):
            pltpu.make_async_copy(x_ref, block(pos, core), sem.at[p]).wait()

        @pl.when(pos > 0)
        def _():
            send(x_ref, pos, left_sem, pos - 1, core)

        @pl.when(pos < here.last)
        def _():
            send(x_ref, pos, right_sem, pos + 1, core)

        send(x_ref, pos, side_sem, pos, 1 - core)
        pairs = [(x_ref, block(pos, core)), (wg_ref, wg), (wu_ref, wu), (gr_ref, gr), (wd_ref, wd)]
        loads = [pltpu.make_async_copy(a, b, load_sem.at[i]) for i, (a, b) in enumerate(pairs)]
        for load in loads:
            load.start()
        yield
        for load in loads:
            load.wait()

        def use(p):
            at = pl.ds(pl.multiple_of(p * 2 * rows, 2 * rows), 2 * rows)

            def body(c, carry):
                cols = pl.ds(pl.multiple_of(c * wide, wide), wide)
                gate = dot_nn(o_ref[at], wg[:, cols])
                up = dot_nn(o_ref[at], wu[:, cols])
                back = dot_nt(gr[at], wd[cols])
                sigma = 1.0 / (1.0 + jnp.exp(-gate))
                silu = gate * sigma
                hid_ref[at, cols] = (silu * up).astype(BF16)
                gg_ref[at, cols] = (back * up * sigma * (1.0 + gate * (1.0 - sigma))).astype(BF16)
                gu_ref[at, cols] = (back * silu).astype(BF16)
                return carry

            lax.fori_loop(0, units // wide, body, 0)

        def hop(step, carry):
            right, left = pos + step, pos - step

            @pl.when((step > 0) & (right < length))
            def _():
                arrived(right, core)

                @pl.when(pos > 0)
                def _():
                    send(block(right, core), right, left_sem, pos - 1, core)

                send(block(right, core), right, side_sem, pos, 1 - core)

            @pl.when((step > 0) & (left >= 0))
            def _():
                arrived(left, core)

                @pl.when(pos < here.last)
                def _():
                    send(block(left, core), left, right_sem, pos + 1, core)

                send(block(left, core), left, side_sem, pos, 1 - core)

            def side(k, c):
                p = pos + (1 - 2 * k) * step

                @pl.when((p >= 0) & (p < length) & (step >= k))
                def _():
                    arrived(p, 1 - core)
                    use(p)

                return c

            lax.fori_loop(0, 2, side, 0)
            return carry

        lax.fori_loop(0, length, hop, 0)

        def drain(p, carry):
            sent(side_sem, p)

            @pl.when((p >= pos) & (pos > 0))
            def _():
                sent(left_sem, p)

            @pl.when((p <= pos) & (pos < here.last))
            def _():
                sent(right_sem, p)

            return carry

        lax.fori_loop(0, length, drain, 0)


class Scatter(Step):
    line, across = True, False

    def __init__(self, terms, members):
        left, right, turned = terms[0]
        rows, width = left.shape[0] // members, right.shape[0 if turned else 1]
        self.rows, self.width, self.turned = rows, width, [t[2] for t in terms]
        self.depth, self.start = right.shape[1 if turned else 0], [0] * len(terms)
        lefts = [t[0] for t in terms]
        if all(x is left for x in lefts) and len(terms) > 1:
            lefts, self.start = [left], [i * self.depth for i in range(len(terms))]
        self.inputs = [(x, VMEM) for x in lefts] + [(t[1], ANY) for t in terms]
        self.outputs = [(jax.ShapeDtypeStruct((rows, width), F32), VMEM)]
        self.scratch = [pltpu.VMEM(t[1].shape, t[1].dtype) for t in terms]
        self.scratch += [pltpu.SemaphoreType.DMA((len(terms),))] + line_sum_scratch(members, rows, width)

    def run(self, here, *refs):
        total = self.begin(here, *refs)
        for t in range(here.last):
            total.fill(t)
            yield
            total.slot(t)
        total.fill(here.last)
        yield
        total.end()

    def begin(self, here, *refs):
        n = len(self.turned)
        m = len(self.inputs) - n
        lefts, refs = (refs[:m] * n)[:n], refs[m:]
        rights, o_ref, helds, load_sem, p_ref = refs[:n], refs[n], refs[n + 1 : 2 * n + 1], refs[2 * n + 1], refs[2 * n + 2]
        rows, wide = self.rows, 256
        loads = [pltpu.make_async_copy(w, h, load_sem.at[i]) for i, (w, h) in enumerate(zip(rights, helds))]
        for load in loads:
            load.start()

        def multiply(p):
            at = pl.ds(pl.multiple_of(p * 2 * rows, 2 * rows), 2 * rows)

            def body(c, carry):
                cols = pl.ds(pl.multiple_of(c * wide, wide), wide)
                total = None
                for left, held, turned, start in zip(lefts, helds, self.turned, self.start):
                    mine = left[at, start : start + self.depth]
                    part = dot_nt(mine, held[cols]) if turned else dot_nn(mine, held[:, cols])
                    total = part if total is None else total + part
                p_ref[at, cols] = total.astype(BF16)
                return carry

            lax.fori_loop(0, self.width // wide, body, 0)

        for load in loads:
            load.wait()
        return LineSum(here, rows, multiply, o_ref, p_ref, *refs[2 * n + 3 :])


def line_sum_scratch(members, rows, width):
    length = members // 2
    held = [pltpu.VMEM((members * rows, width), BF16), pltpu.VMEM((length, rows, width), BF16)]
    held += [pltpu.VMEM((length, rows, width), BF16)] * 2
    return held + [pltpu.SemaphoreType.DMA((length,))] * 6


class LineSum:
    def __init__(self, here, rows, multiply, o_ref, p_ref, side_buf, left_in, right_in,
                 side_send, side_recv, right_send, right_recv, left_send, left_recv):
        self.here, self.rows, self.multiply, self.o_ref, self.p_ref = here, rows, multiply, o_ref, p_ref
        self.side_buf, self.left_in, self.right_in = side_buf, left_in, right_in
        self.side, self.right, self.left = (side_send, side_recv), (right_send, right_recv), (left_send, left_recv)

    def block(self, p, c):
        return self.p_ref.at[pl.ds(pl.multiple_of((p * 2 + c) * self.rows, self.rows), self.rows)]

    def side_copy(self, p):
        here = self.here
        sems = [s.at[p] for s in self.side]
        return remote(self.block(p, 1 - here.core), self.side_buf.at[p], *sems, here.at(here.pos, 1 - here.core))

    def line_copy(self, p, right):
        here = self.here
        buf, sems = (self.right_in, self.right) if right else (self.left_in, self.left)
        to = here.at(here.pos + 1 if right else here.pos - 1, here.core)
        return remote(self.block(p, here.core), buf.at[p], *[s.at[p] for s in sems], to)

    def add(self, p, incoming, final):
        tile, rows = 16, self.rows

        def body(r, carry):
            s = pl.ds(pl.multiple_of(r * tile, tile), tile)
            mine = pl.ds(pl.multiple_of((p * 2 + self.here.core) * rows + r * tile, tile), tile)
            total = self.p_ref[mine].astype(F32) + self.side_buf[p, s].astype(F32)
            for ref in incoming:
                total = total + ref[p, s].astype(F32)
            if final:
                self.o_ref[s] = total
            else:
                self.p_ref[mine] = total.astype(BF16)
            return carry

        lax.fori_loop(0, rows // tile, body, 0)

    def fill(self, t):
        pos, last = self.here.pos, self.here.last

        def side(k, carry):
            own = t == last
            p = jnp.where(own, pos, k * t + (1 - k) * (last - t))

            @pl.when(jnp.where(own, 1 - k, (1 - 2 * k) * (p - pos)) > 0)
            def _():
                self.multiply(p)
                self.side_copy(p).start()

            return carry

        lax.fori_loop(0, 2, side, 0)

    def move(self, p, right, first, source):
        self.side_copy(p).wait_recv()

        @pl.when(first)
        def _():
            self.add(p, [], False)

        @pl.when(jnp.logical_not(first))
        def _():
            self.line_copy(p, right).wait_recv()
            self.add(p, [source], False)

        self.line_copy(p, right).start()

    def slot(self, t):
        pos, last = self.here.pos, self.here.last
        right_p, left_p = last - t + pos, t - (last - pos)

        @pl.when(t >= pos)
        def _():
            self.move(right_p, True, pos == 0, self.right_in)

        @pl.when(left_p >= 0)
        def _():
            self.move(left_p, False, pos == last, self.left_in)

    def end(self):
        pos, last = self.here.pos, self.here.last
        self.side_copy(pos).wait_recv()

        @pl.when(pos == 0)
        def _():
            self.line_copy(pos, False).wait_recv()
            self.add(pos, [self.left_in], True)

        @pl.when(pos == last)
        def _():
            self.line_copy(pos, True).wait_recv()
            self.add(pos, [self.right_in], True)

        @pl.when((pos > 0) & (pos < last))
        def _():
            self.line_copy(pos, False).wait_recv()
            self.line_copy(pos, True).wait_recv()
            self.add(pos, [self.left_in, self.right_in], True)

        def drain(p, carry):
            self.side_copy(p).wait_send()

            @pl.when(p > pos)
            def _():
                self.line_copy(p, True).wait_send()

            @pl.when(p < pos)
            def _():
                self.line_copy(p, False).wait_send()

            return carry

        lax.fori_loop(0, self.here.length, drain, 0)


def rounds(here, total, hop=None):
    def body(t, carry):
        total.fill(t)

        @pl.when(t < here.last)
        def _():
            if hop is not None:
                hop(t + 1)
            total.slot(t)

        return carry

    lax.fori_loop(0, here.length, body, 0)


class ScatterAlone(Scatter):
    def __init__(self, terms, members, gathered=None):
        Scatter.__init__(self, terms, members)
        self.other = None if gathered is None else Gather(gathered, members)
        self.sizes = [len(v) for v in (self.inputs, self.outputs, self.scratch)]
        if gathered is not None:
            self.inputs = self.inputs + self.other.inputs
            self.outputs = self.outputs + self.other.outputs
            self.scratch = self.scratch + self.other.scratch

    def run(self, here, *refs):
        ends, mine, rest = [len(v) for v in (self.inputs, self.outputs, self.scratch)], [], []
        for size, end in zip(self.sizes, ends):
            mine += refs[:size]
            rest += refs[size:end]
            refs = refs[end:]
        if self.other is not None:
            self.other.begin(here, *rest)
        all_inputs, self.inputs = self.inputs, self.inputs[: self.sizes[0]]
        total = self.begin(here, *mine)
        self.inputs = all_inputs
        rounds(here, total, None if self.other is None else lambda step: self.other.hop(here, step, *rest))
        total.end()
        if self.other is not None:
            self.other.end(here, *rest)
        yield


class Forward(Step):
    line, across = True, False

    def __init__(self, tokens, out_grad, attn_gain, ffn_gain, query_gain, key_gain, w_query, w_key, w_value, w_output,
                 positions, members):
        rows, width = tokens.shape
        length, size, inner = members // 2, members * rows, w_query.shape[1]
        self.heads, self.share, columns = inner // HD, members // KV, inner + 2 * HD
        sems = pltpu.SemaphoreType.DMA((length,))
        self.grads = Gather(out_grad, members)
        freq = ROPE_BASE ** (-np.arange(HD // 2, dtype=np.float32) / (HD // 2))
        freq = jnp.asarray(np.tile(freq, 4)[None], F32)
        self.inputs = [(tokens, VMEM), (out_grad, ANY), (attn_gain[None], VMEM), (ffn_gain[None], VMEM)]
        self.inputs += [(query_gain[None], VMEM), (key_gain[None], VMEM), (w_query, ANY), (w_key, ANY), (w_value, ANY)]
        self.inputs += [(w_output, ANY), (positions.reshape(size // 128, 128), VMEM), (freq, VMEM)]
        self.outputs = [
            (jax.ShapeDtypeStruct((size, width), BF16), ANY),
            (jax.ShapeDtypeStruct((size, columns), F32), VMEM),
            (jax.ShapeDtypeStruct((size, inner), BF16), VMEM),
            (jax.ShapeDtypeStruct((size // BLOCK, 1, self.heads * BLOCK), F32), VMEM),
            (jax.ShapeDtypeStruct((size, width), BF16), ANY),
            (jax.ShapeDtypeStruct((rows, width), F32), VMEM),
            (jax.ShapeDtypeStruct((rows, width), BF16), VMEM),
            (jax.ShapeDtypeStruct((size, 2 * HD), F32), VMEM),
            (jax.ShapeDtypeStruct((size, 2 * HD), F32), VMEM),
        ]
        self.scratch = [pltpu.VMEM((size, width), BF16), pltpu.VMEM(w_query.shape, BF16), pltpu.VMEM((width, 2 * HD), BF16)]
        self.scratch += [pltpu.VMEM((width, 2 * HD), BF16), pltpu.VMEM((width, 2 * HD), BF16), pltpu.VMEM(w_output.shape, BF16)]
        self.scratch += [pltpu.VMEM((size, 2 * HD), jnp.int32)]
        self.scratch += [pltpu.VMEM((size, inner), BF16), pltpu.VMEM((size, HD), BF16), pltpu.VMEM((size, 2 * HD), BF16)]
        self.scratch += [pltpu.VMEM((self.heads * BLOCK, 2 * HD), F32), pltpu.SemaphoreType.DMA((5,))]
        self.scratch += [sems, sems, sems, pltpu.SemaphoreType.DMA((members,))]
        self.scratch += self.grads.scratch + line_sum_scratch(members, rows, width)

    def loads(self, here, wq_ref, wk_ref, wv_ref, wo_ref, wq, wk, wv, wo, load_sem):
        group = (here.pos * 2 + here.core) // self.share
        cols = pl.ds(pl.multiple_of(group // 2 * 2 * HD, 2 * HD), 2 * HD)
        pairs = [(wq_ref, wq), (wk_ref.at[:, cols], wk), (wv_ref.at[:, cols], wv), (wo_ref, wo)]
        return lax.rem(group, 2), [pltpu.make_async_copy(a, b, load_sem.at[i]) for i, (a, b) in enumerate(pairs)]

    def before(self, here, tok_ref, og_ref, again_ref, fgain_ref, qgain_ref, kgain_ref, wq_ref, wk_ref, wv_ref, wo_ref,
               pos_ref, freq_ref, one_ref, proj_ref, ctx_ref, lse_ref, gr_ref, branch_ref, two_ref, cos_ref, sin_ref,
               all_ref, wq, wk, wv, wkv, wo, *rest):
        for load in self.loads(here, wq_ref, wk_ref, wv_ref, wo_ref, wq, wk, wv, wo, rest[5])[1]:
            load.start()
        rows = tok_ref.shape[0]
        me = (here.pos * 2 + here.core) * rows

        def body(r, carry):
            at = pl.ds(pl.multiple_of(r * 32, 32), 32)
            x = tok_ref[at].astype(F32)
            inv = lax.rsqrt(jnp.mean(x * x, -1, keepdims=True) + EPSILON)
            all_ref[pl.ds(pl.multiple_of(me + r * 32, 32), 32)] = (x * inv * again_ref[...]).astype(BF16)
            return carry

        lax.fori_loop(0, rows // 32, body, 0)

    def run(self, here, tok_ref, og_ref, again_ref, fgain_ref, qgain_ref, kgain_ref, wq_ref, wk_ref, wv_ref, wo_ref,
            pos_ref, freq_ref, one_ref, proj_ref, ctx_ref, lse_ref, gr_ref, branch_ref, two_ref, cos_ref, sin_ref,
            all_ref, wq, wk, wv, wkv, wo, place_ref,
            q_ref, k_ref, v_ref, acc_ref, load_sem, left_sem, right_sem, side_sem, recv_sem, *rest):
        pos, core, length = here.pos, here.core, here.length
        rows, width = tok_ref.shape
        heads, inner, size = self.heads, self.heads * HD, proj_ref.shape[0]
        lane = lax.broadcasted_iota(jnp.int32, (1, HD), 1)

        def block(p, c):
            return all_ref.at[pl.ds(pl.multiple_of((p * 2 + c) * rows, rows), rows)]

        def send(p, sem, to_p, to_c):
            remote(block(p, core), block(p, core), sem.at[p], recv_sem.at[p * 2 + core], here.at(to_p, to_c)).start()

        def arrived(p, c):
            pltpu.make_async_copy(block(p, c), block(p, c), recv_sem.at[p * 2 + c]).wait()

        def sent(sem, p):
            pltpu.make_async_copy(block(p, core), block(p, core), sem.at[p]).wait()

        def prepare():
            odd, loads = self.loads(here, wq_ref, wk_ref, wv_ref, wo_ref, wq, wk, wv, wo, load_sem)
            for load in loads:
                load.wait()
            low = lax.broadcasted_iota(jnp.int32, (1, 2 * HD), 1) < HD

            def pick(r, carry):
                at = pl.ds(pl.multiple_of(r * 256, 256), 256)
                key, value = wk[at].astype(F32), wv[at].astype(F32)
                key = jnp.where(odd == 1, pltpu.roll(key, HD, 1), key)
                value = jnp.where(odd == 1, value, pltpu.roll(value, HD, 1))
                wkv[at] = jnp.where(low, key, value).astype(BF16)
                return carry

            lax.fori_loop(0, width // 256, pick, 0)

            def table(r, carry):
                at = pl.ds(pl.multiple_of(r * 128, 128), 128)
                place = jnp.broadcast_to(pos_ref[pl.ds(r, 1)].astype(F32), (128, 128)).T
                place_ref[at] = place.astype(jnp.int32)
                angle = place * freq_ref[...]
                cos_ref[at] = jnp.cos(angle)
                sin_ref[at] = jnp.sin(angle)
                return carry

            lax.fori_loop(0, size // 128, table, 0)

        def use(p):
            at = pl.ds(pl.multiple_of(p * BLOCK, BLOCK), BLOCK)
            x = jnp.concatenate([dot_nn(all_ref[at], wq[...]), dot_nn(all_ref[at], wkv[...])], 1)
            proj_ref[at] = x
            gain = jnp.concatenate([qgain_ref[...]] * heads + [kgain_ref[...], jnp.ones((1, HD), F32)], 1)
            cosine, sine = wide(cos_ref[at], inner + 2 * HD), wide(sin_ref[at], inner + 2 * HD)
            unit, _ = normed(x)
            spun = turn(unit * gain, cosine, sine)
            q_ref[at] = (spun[:, :inner].astype(BF16) * HD**-0.5).astype(BF16)
            k_ref[at] = spun[:, inner : inner + HD].astype(BF16)
            ones = jnp.broadcast_to(jnp.where(lane == 0, 1.0, 0.0), (BLOCK, HD)).astype(BF16)
            v_ref[at] = jnp.concatenate([x[:, inner + HD :].astype(BF16), ones], 1)

        def pass_on(step):
            right, left = pos + step, pos - step

            @pl.when(right < length)
            def _():
                @pl.when(step > 0)
                def _():
                    arrived(right, core)

                @pl.when(pos > 0)
                def _():
                    send(right, left_sem, pos - 1, core)

                send(right, side_sem, pos, 1 - core)

            @pl.when(left >= 0)
            def _():
                @pl.when(step > 0)
                def _():
                    arrived(left, core)

                @pl.when(pos < here.last)
                def _():
                    send(left, right_sem, pos + 1, core)

                @pl.when(step > 0)
                def _():
                    send(left, side_sem, pos, 1 - core)

        def use_both(step):
            def side(k, c):
                p = pos + (1 - 2 * k) * step

                @pl.when((p >= 0) & (p < length) & (step >= k))
                def _():
                    arrived(p, 1 - core)
                    use(p)

                return c

            lax.fori_loop(0, 2, side, 0)

        pass_on(0)
        prepare()

        def hop(step, carry):
            use_both(step)
            pass_on(step + 1)
            return carry

        lax.fori_loop(0, here.last, hop, 0)
        n = len(self.grads.scratch)
        held = rest[n:]
        p_ref = held[0]
        grads = (og_ref, gr_ref) + tuple(rest[:n])
        self.grads.begin(here, *grads)
        use_both(here.last)
        keep = pltpu.make_async_copy(all_ref, one_ref, load_sem.at[4])
        keep.start()

        def attend(i):
            at = pl.ds(pl.multiple_of(i * BLOCK, BLOCK), BLOCK)
            query = q_ref[at]
            stacked = jnp.concatenate([query[:, h * HD : (h + 1) * HD] for h in range(heads)], 0)
            acc_ref[...] = jnp.zeros_like(acc_ref)
            index = i * BLOCK + lax.broadcasted_iota(jnp.int32, (BLOCK, 1), 0)
            start = index - place_ref[at, :1]

            def keys(j, c):
                cols = pl.ds(pl.multiple_of(j * BLOCK, BLOCK), BLOCK)
                scores = dot_nt(stacked, k_ref[cols])
                place = j * BLOCK + lax.broadcasted_iota(jnp.int32, (1, BLOCK), 1)
                seen = (place >= start) & (place <= index)
                expo = [
                    jnp.where(seen, jnp.exp(scores[h * BLOCK : (h + 1) * BLOCK]), 0.0).astype(BF16)
                    for h in range(heads)
                ]
                acc_ref[...] += dot_nn(jnp.concatenate(expo, 0), v_ref[cols])
                return c

            lax.fori_loop(0, i + 1, keys, 0)
            outs, logs = [], []
            for h in range(heads):
                acc = acc_ref[pl.ds(h * BLOCK, BLOCK)]
                outs.append((acc[:, :HD] * (1.0 / acc[:, HD : HD + 1])).astype(BF16))
                logs.append(jnp.log(acc.T[HD : HD + 1]))
            ctx_ref[at] = jnp.concatenate(outs, 1)
            lse_ref[i] = jnp.concatenate(logs, 1)

        def multiply(p):
            attend(p)
            at = pl.ds(pl.multiple_of(p * BLOCK, BLOCK), BLOCK)

            def body(c, carry):
                cols = pl.ds(pl.multiple_of(c * 512, 512), 512)
                p_ref[at, cols] = dot_nn(ctx_ref[at], wo[:, cols]).astype(BF16)
                return carry

            lax.fori_loop(0, width // 512, body, 0)

        total = LineSum(here, rows, multiply, branch_ref, *held)
        rounds(here, total, lambda step: self.grads.hop(here, step, *grads))
        total.end()

        def body(r, carry):
            at = pl.ds(pl.multiple_of(r * 32, 32), 32)
            x = tok_ref[at].astype(F32) + branch_ref[at]
            inv = lax.rsqrt(jnp.mean(x * x, -1, keepdims=True) + EPSILON)
            two_ref[at] = (x * inv * fgain_ref[...]).astype(BF16)
            return carry

        lax.fori_loop(0, rows // 32, body, 0)

        def drain(p, carry):
            sent(side_sem, p)

            @pl.when((p >= pos) & (pos > 0))
            def _():
                sent(left_sem, p)

            @pl.when((p <= pos) & (pos < here.last))
            def _():
                sent(right_sem, p)

            return carry

        lax.fori_loop(0, length, drain, 0)
        self.grads.end(here, *grads)
        keep.wait()
        yield


class Across(Step):
    line, across = False, True

    def __init__(self, x, parts, colours, late=0):
        self.bits, self.colours, self.late = parts.bit_length() - 1, colours, late
        rows, width = x.shape
        self.inputs = [(x, VMEM)]
        self.outputs = [(jax.ShapeDtypeStruct(x.shape, x.dtype), VMEM)]
        self.scratch = [pltpu.VMEM((rows, width), x.dtype)]
        for _ in colours:
            part = rows // len(colours)
            self.scratch += [pltpu.VMEM((part >> (s + 1), width), x.dtype) for s in range(self.bits)]
            self.scratch += [pltpu.SemaphoreType.DMA((2 * self.bits,))] * 2

    def run(self, here, x_ref, o_ref, sum_ref, *rest):
        for _ in range(self.late):
            yield
        n, rows = self.bits + 2, x_ref.shape[0] // len(self.colours)
        live = [
            self.one(here, backwards, i * rows, rows, x_ref, o_ref, sum_ref, *rest[i * n : (i + 1) * n])
            for i, backwards in enumerate(self.colours)
        ]
        while live:
            live = [r for r in live if next(r, live) is not live]
            yield

    def one(self, here, backwards, start, size, x_ref, o_ref, sum_ref, *rest):
        taken, (send_sem, recv_sem) = rest[: self.bits], rest[self.bits :]
        order = list(range(self.bits))[:: -1 if backwards else 1]
        copies, tile = [], 16

        def part(ref, at, count):
            return ref.at[pl.ds(pl.multiple_of(at, count), count)]

        for s, bit in enumerate(order):
            mine, device = here.partner(bit)
            half = size // 2
            keep, give = start + mine * half, start + (1 - mine) * half
            source = x_ref if s == 0 else sum_ref
            target = o_ref if s == self.bits - 1 else sum_ref
            copy = remote(part(source, give, half), taken[s], send_sem.at[s], recv_sem.at[s], device)
            copy.start()
            copies.append(copy)
            yield
            copy.wait_recv()

            def body(r, carry):
                at = pl.ds(pl.multiple_of(keep + r * tile, tile), tile)
                got = taken[s][pl.ds(pl.multiple_of(r * tile, tile), tile)]
                target[at] = (source[at].astype(F32) + got.astype(F32)).astype(target.dtype)
                return carry

            lax.fori_loop(0, half // tile, body, 0)
            start, size = keep, half
        for s, bit in enumerate(order[::-1]):
            mine, device = here.partner(bit)
            n = self.bits + s
            copy = remote(part(o_ref, start, size), part(o_ref, start, size), send_sem.at[n], recv_sem.at[n], device)
            copy.start()
            copies.append(copy)
            yield
            copy.wait_recv()
            start, size = start - mine * size, size * 2
        for copy in copies:
            copy.wait_send()


class KeyValue(Step):
    line, across = True, True

    def __init__(self, x, width, members, parts):
        self.width, self.extra, self.members = width, x.shape[0] - width, members
        self.sum, self.all = Across(x, parts, (False,)), Gather(x, members)
        self.inputs = [(x, VMEM)]
        flat = jax.ShapeDtypeStruct((width, KV * HD), BF16)
        self.outputs = [(flat, VMEM), (flat, VMEM), (jax.ShapeDtypeStruct((self.extra, 2 * HD), F32), VMEM)]
        self.scratch = [pltpu.VMEM(x.shape, x.dtype), pltpu.VMEM((members * x.shape[0], 2 * HD), x.dtype)]
        self.scratch += self.sum.scratch + self.all.scratch

    def run(self, here, x_ref, key_ref, value_ref, small_ref, sum_ref, all_ref, *rest):
        n = len(self.sum.scratch)
        first = self.sum.run(here, x_ref, sum_ref, *rest[:n])
        next(first)
        yield
        for _ in first:
            pass
        yield from self.all.run(here, sum_ref, all_ref, *rest[n:])
        rows, share, tile = self.width + self.extra, self.members // KV, 128

        def block(group, at, count):
            total = 0.0
            for k in range(share):
                begin = pl.multiple_of((group * share + k) * rows + at, 16)
                total = total + all_ref[pl.ds(begin, count)].astype(F32)
            return total

        for pair in range(KV // 2):
            cols = slice(2 * HD * pair, 2 * HD * (pair + 1))

            def body(r, carry):
                at = pl.ds(pl.multiple_of(r * tile, tile), tile)
                one, two = block(2 * pair, r * tile, tile), block(2 * pair + 1, r * tile, tile)
                key_ref[at, cols] = jnp.concatenate([one[:, :HD], two[:, :HD]], 1).astype(BF16)
                value_ref[at, cols] = jnp.concatenate([one[:, HD:], two[:, HD:]], 1).astype(BF16)
                return carry

            lax.fori_loop(0, self.width // tile, body, 0)
        small = 0.0
        for group in range(KV):
            small = small + block(group, self.width, self.extra)
        small_ref[...] = small


def held_bytes(shape, dtype):
    *lead, rows, columns = (1,) + tuple(shape)
    return int(np.prod(lead)) * -(-rows // 8) * 8 * -(-columns // 128) * 128 * jnp.dtype(dtype).itemsize


def together(steps, members, parts, collective_id, whole=False, spare=6):
    need = 0
    for s in steps:
        need += sum(held_bytes(x.shape, x.dtype) for x, m in s.inputs + s.outputs if m is VMEM)
        need += sum(held_bytes(h.shape, h.dtype) for h in s.scratch if h is not pltpu.SemaphoreType.DMA and h.memory_space == pltpu.VMEM)
    counts = [(len(s.inputs), len(s.outputs), len(s.scratch)) for s in steps]

    def kernel(*refs):
        refs = list(refs)
        given = [[refs.pop(0) for _ in range(c[0])] for c in counts]
        made = [[refs.pop(0) for _ in range(c[1])] for c in counts]
        held = [[refs.pop(0) for _ in range(c[2])] for c in counts]
        here = Place(members, parts)
        peers = here.greet(any(s.line for s in steps), any(s.across for s in steps))
        for s, g, m, h in zip(steps, given, made, held):
            s.before(here, *g, *m, *h)
        here.meet(peers)
        weave([s.run(here, *g, *m, *h) for s, g, m, h in zip(steps, given, made, held)])

    return pl.pallas_call(
        kernel,
        out_shape=[o for s in steps for o, _ in s.outputs],
        in_specs=[m for s in steps for _, m in s.inputs],
        out_specs=[m for s in steps for _, m in s.outputs],
        scratch_shapes=[h for s in steps for h in s.scratch],
        compiler_params=pltpu.CompilerParams(
            collective_id=collective_id, has_side_effects=True, vmem_limit_bytes=58 << 20 if whole else need + (spare << 20)
        ),
        cost_estimate=pl.CostEstimate(flops=1, bytes_accessed=1, transcendentals=0),
    )(*[x for s in steps for x, _ in s.inputs])


def dot_nn(a, b):
    return lax.dot_general(a, b, (((1,), (0,)), ((), ())), preferred_element_type=F32)

def dot_nt(a, b):
    return lax.dot_general(a, b, (((1,), (1,)), ((), ())), preferred_element_type=F32)

def dot_tn(a, b):
    return lax.dot_general(a, b, (((0,), (0,)), ((), ())), preferred_element_type=F32)

def group_mean(x):
    width = x.shape[1]
    row = lax.broadcasted_iota(jnp.int32, (width, width), 0) // HD
    col = lax.broadcasted_iota(jnp.int32, (width, width), 1) // HD
    ones = jnp.where(row == col, 1.0 / HD, 0.0).astype(F32)
    return jnp.dot(x, ones, precision=lax.Precision.HIGHEST, preferred_element_type=F32)

def half_turn(x):
    width = x.shape[1]
    lane = lax.broadcasted_iota(jnp.int32, (1, width), 1)
    first = lax.rem(lane, HD) < HD // 2
    up = pltpu.roll(x, HD // 2, 1)
    down = pltpu.roll(x, width - HD // 2, 1)
    return jnp.where(first, -down, up)

def wide(table, width):
    return jnp.concatenate([table] * (width // table.shape[1]), 1)

def normed(x):
    inv = lax.rsqrt(group_mean(x * x) + EPSILON)
    return x * inv, inv

def turn(x, cosine, sine):
    return x * cosine + half_turn(x) * sine

def turn_back(x, cosine, sine):
    return x * cosine - half_turn(x) * sine

def stack_lanes(x, heads):
    return jnp.concatenate([x[h * HD:(h + 1) * HD] for h in range(heads)], 1)

def attend_back_kernel(heads, proj_ref, cos_ref, sin_ref, qgain_ref, kgain_ref, pos_ref, ctx_ref, grad_ref, lse_ref,
                       out_ref, sums_ref, k_ref, kt_ref, v_ref, dk_ref, dv_ref, dq_ref):
    width = heads * HD
    scale = HD ** -0.5
    count = proj_ref.shape[0] // BLOCK
    gain = jnp.concatenate([qgain_ref[...]] * heads + [kgain_ref[...], jnp.ones((1, HD), F32)], 1)
    def prepare(i, carry):
        rows = pl.ds(pl.multiple_of(i * BLOCK, BLOCK), BLOCK)
        x = proj_ref[rows, width:]
        unit, _ = normed(x)
        spun = turn(unit * gain[:, width:], cos_ref[rows], sin_ref[rows])
        k_ref[rows] = spun[:, :HD].astype(BF16)
        kt_ref[i] = spun.T[:HD].astype(BF16)
        v_ref[rows] = x[:, HD:].astype(BF16)
        dk_ref[rows] = jnp.zeros((BLOCK, HD), F32)
        dv_ref[rows] = jnp.zeros((BLOCK, HD), F32)
        return carry
    lax.fori_loop(0, count, prepare, 0)
    sums_ref[...] = jnp.zeros_like(sums_ref)
    def outer(i, carry):
        rows = pl.ds(pl.multiple_of(i * BLOCK, BLOCK), BLOCK)
        x = proj_ref[rows, :width]
        cosine, sine = wide(cos_ref[rows], width), wide(sin_ref[rows], width)
        unit, inv = normed(x)
        query = (turn(unit * gain[:, :width], cosine, sine).astype(BF16).astype(F32) * scale)
        query_t = stack_lanes(query.T, heads).astype(BF16)
        query = query.astype(BF16)
        query_s = jnp.concatenate([query[:, h * HD:(h + 1) * HD] for h in range(heads)], 0)
        grad = grad_ref[rows]
        grad_s = jnp.concatenate([grad[:, h * HD:(h + 1) * HD] for h in range(heads)], 0)
        grad_t = stack_lanes(grad.astype(F32).T, heads)
        ctx_t = stack_lanes(ctx_ref[rows].astype(F32).T, heads)
        delta = jnp.sum(grad_t * ctx_t, 0, keepdims=True)
        grad_t = grad_t.astype(BF16)
        lse = lse_ref[i]
        index = i * BLOCK + lax.broadcasted_iota(jnp.int32, (1, BLOCK), 1)
        start = index - pos_ref[i]
        dq_ref[...] = jnp.zeros_like(dq_ref)
        def inner(j, c):
            cols = pl.ds(pl.multiple_of(j * BLOCK, BLOCK), BLOCK)
            scores = dot_nn(k_ref[cols], query_t)
            grad_probs = dot_nn(v_ref[cols], grad_t)
            place = j * BLOCK + lax.broadcasted_iota(jnp.int32, (BLOCK, 1), 0)
            seen = (place >= start) & (place <= index)
            probs, back = [], []
            for h in range(heads):
                s = slice(h * BLOCK, (h + 1) * BLOCK)
                exact = jnp.where(seen, jnp.exp(scores[:, s] - lse[:, s]), 0.0)
                probs.append(exact.astype(BF16))
                back.append((exact * (grad_probs[:, s] - delta[:, s])).astype(BF16))
            probs = jnp.concatenate(probs, 1)
            back = jnp.concatenate(back, 1)
            dv_ref[cols] += dot_nn(probs, grad_s)
            dk_ref[cols] += dot_nn(back, query_s)
            dq_ref[...] += dot_nn(kt_ref[j], back)
            return c
        lax.fori_loop(0, i + 1, inner, 0)
        dq = jnp.concatenate([dq_ref[:, h * BLOCK:(h + 1) * BLOCK] for h in range(heads)], 0).T * scale
        dqn = turn_back(dq, cosine, sine)
        sums_ref[:, :width] += jnp.sum(dqn * unit, 0, keepdims=True)
        e = dqn * gain[:, :width]
        out_ref[rows, :width] = (inv * (e - unit * group_mean(e * unit))).astype(BF16)
        return carry
    lax.fori_loop(0, count, outer, 0)
    def finish(i, carry):
        rows = pl.ds(pl.multiple_of(i * BLOCK, BLOCK), BLOCK)
        x = proj_ref[rows, width:]
        unit, inv = normed(x)
        dv = dv_ref[rows]
        dk = jnp.concatenate([dk_ref[rows], dv], 1)
        dkn = turn_back(dk, cos_ref[rows], sin_ref[rows])
        sums_ref[:, width:] += jnp.sum(dkn * unit, 0, keepdims=True)
        e = dkn * gain[:, width:]
        dkp = inv * (e - unit * group_mean(e * unit))
        lane = lax.broadcasted_iota(jnp.int32, (1, 2 * HD), 1)
        out_ref[rows, width:] = jnp.where(lane < HD, dkp, dk).astype(BF16)
        return carry
    lax.fori_loop(0, count, finish, 0)

def attend_back(proj, cosine, sine, query_gain, key_gain, positions, context, grad_context, lse, heads):
    size = proj.shape[0]
    count = size // BLOCK
    vm = pl.BlockSpec(memory_space=pltpu.VMEM)
    return pl.pallas_call(
        functools.partial(attend_back_kernel, heads),
        out_shape=(jax.ShapeDtypeStruct(proj.shape, BF16), jax.ShapeDtypeStruct((1, proj.shape[1]), F32)),
        in_specs=[vm] * 9, out_specs=(vm, vm),
        scratch_shapes=[pltpu.VMEM((size, HD), BF16), pltpu.VMEM((count, HD, BLOCK), BF16), pltpu.VMEM((size, HD), BF16),
                        pltpu.VMEM((size, HD), F32), pltpu.VMEM((size, HD), F32), pltpu.VMEM((HD, heads * BLOCK), F32)],
        compiler_params=pltpu.CompilerParams(vmem_limit_bytes=40 << 20),
        cost_estimate=pl.CostEstimate(flops=1, bytes_accessed=1, transcendentals=0),
    )(proj, cosine, sine, query_gain[None], key_gain[None], positions.reshape(count, 1, BLOCK), context, grad_context, lse)


def matmul(left, right):
    return jnp.dot(left, right, preferred_element_type=F32)


def matmul_left_t(left, right):
    return lax.dot_general(left, right, (((0,), (0,)), ((), ())), preferred_element_type=F32)


def matmul_right_t(left, right):
    return lax.dot_general(left, right, (((1,), (1,)), ((), ())), preferred_element_type=F32)


def norm_back(grad_normed, unit, inverse, gain):
    scaled = grad_normed * gain
    return inverse * (scaled - unit * jnp.mean(scaled * unit, -1, keepdims=True))


def after(first, *later):
    return lax.optimization_barrier((first,) + later)


def per_device(
    tokens,
    seg_ids,
    positions,
    w_query,
    w_key,
    w_value,
    w_output,
    w_gate,
    w_up,
    w_down,
    attn_gain,
    ffn_gain,
    query_gain,
    key_gain,
    out_grad,
):
    members, parts = lax.axis_size("mp"), lax.axis_size("dp")
    width = tokens.shape[1]
    query_width = w_query.shape[1]
    heads = query_width // HD
    ffn_width = w_gate.shape[1]
    share = members // KV
    group = lax.axis_index("mp") // share

    rows_one, projected, context, lse, grad_rows, attn_branch, h_two, cosine, sine = together(
        [
            Forward(
                tokens,
                out_grad,
                attn_gain,
                ffn_gain,
                query_gain,
                key_gain,
                w_query,
                w_key,
                w_value,
                w_output,
                positions,
                members,
            )
        ],
        members,
        parts,
        0,
        True,
    )
    rows_two, hidden, grad_gate, grad_up = together(
        [GatherFfn(h_two, grad_rows, w_gate, w_up, w_down, members)], members, parts, 5, False, 14
    )
    rows_two, tokens_late, w_key, w_value = after(rows_two, tokens, w_key, w_value)
    tokens_f = tokens_late.astype(F32)
    inv_one = lax.rsqrt(jnp.mean(tokens_f * tokens_f, -1, keepdims=True) + EPSILON)
    normed_one = tokens_f * inv_one
    key_cols = lax.dynamic_slice_in_dim(w_key, group * HD, HD, 1)
    value_cols = lax.dynamic_slice_in_dim(w_value, group * HD, HD, 1)
    w_attn = jnp.concatenate([w_query, key_cols, value_cols], 1)
    residual_mid = tokens_f + attn_branch
    inv_two = lax.rsqrt(jnp.mean(residual_mid * residual_mid, -1, keepdims=True) + EPSILON)
    normed_two = residual_mid * inv_two
    ffn_parts = (
        matmul_left_t(hidden, grad_rows).astype(BF16),
        matmul_left_t(rows_two, grad_gate).astype(BF16),
        matmul_left_t(rows_two, grad_up).astype(BF16),
    )
    ffn_parts, grad_gate, grad_up, hidden = lax.optimization_barrier((ffn_parts, grad_gate, grad_up, hidden))
    grad_w_down, grad_w_gate, grad_w_up = lax.psum(ffn_parts, "dp")

    grad_h_two = together(
        [ScatterAlone([(grad_gate, w_gate, True), (grad_up, w_up, True)], members)],
        members,
        parts,
        6,
        True,
    )[0]
    grad_ffn_gain = jnp.sum(grad_h_two * normed_two, 0)
    grad_mid = out_grad.astype(F32) + norm_back(grad_h_two, normed_two, inv_two, ffn_gain)
    ffn_branch, grad_attn_rows = together(
        [ScatterAlone([(hidden, w_down, False)], members, grad_mid.astype(BF16))],
        members,
        parts,
        2,
    )
    grad_context = matmul_right_t(grad_attn_rows, w_output).astype(BF16)
    grad_proj, gain_sums = attend_back(
        projected, cosine, sine, query_gain, key_gain, positions, context, grad_context, lse, heads
    )
    output_part = matmul_left_t(context, grad_attn_rows).astype(BF16)
    grad_w_attn = matmul_left_t(rows_one, grad_proj)
    grad_attn_gain = jnp.sum(w_attn.astype(F32) * grad_w_attn, 1) / attn_gain

    small = jnp.concatenate(
        [
            grad_attn_gain,
            grad_ffn_gain,
            jnp.sum(gain_sums[0, :query_width].reshape(heads, HD), 0),
            gain_sums[0, query_width : query_width + HD],
            jnp.sum(tokens_f * tokens_f)[None],
        ]
    )
    unit = 16 * parts
    extra = -(-small.shape[0] // (unit * 2 * HD)) * unit
    small_rows = jnp.pad(small, (0, extra * 2 * HD - small.shape[0])).reshape(extra, 2 * HD)
    kv_part = jnp.concatenate([grad_w_attn[:, query_width:], small_rows], 0).astype(BF16)
    query_part = grad_w_attn[:, :query_width].astype(BF16)
    grad_w_key, grad_w_value, small_sum, grad_h_one, grad_w_output, grad_w_query = together(
        [
            KeyValue(kv_part, width, members, parts),
            Scatter([(grad_proj, w_attn, True)], members),
            Across(output_part, parts, (False,)),
            Across(query_part, parts, (True,)),
        ],
        members,
        parts,
        3,
    )
    small_sum = small_sum.reshape(-1)
    entry_count = tokens.size * parts * members
    at = 2 * width
    residual_rms = jnp.sqrt(small_sum[at + 2 * HD : at + 2 * HD + 1] / entry_count)

    grad_tokens = (grad_mid + norm_back(grad_h_one, normed_one, inv_one, attn_gain)).astype(BF16)
    output = (residual_mid + ffn_branch).astype(BF16)
    branch_rms = jnp.stack(
        [
            jnp.sqrt(jnp.mean(attn_branch * attn_branch, -1)),
            jnp.sqrt(jnp.mean(ffn_branch * ffn_branch, -1)),
        ]
    )
    return (
        output,
        grad_tokens,
        grad_w_query.astype(F32),
        grad_w_key.astype(F32),
        grad_w_value.astype(F32),
        grad_w_output.astype(F32),
        grad_w_gate.astype(F32),
        grad_w_up.astype(F32),
        grad_w_down.astype(F32),
        small_sum[:width],
        small_sum[width:at],
        small_sum[at : at + HD],
        small_sum[at + HD : at + 2 * HD],
        residual_rms,
        branch_rms,
    )


def solution(mesh):
    row, whole, column = P(("dp", "mp"), None), P(), P(None, "mp")
    lead = P("mp", None)
    return jax.shard_map(
        per_device,
        mesh=mesh,
        in_specs=(row, P("dp"), P("dp"), column, whole, whole, lead, column, column, lead)
        + (whole,) * 4
        + (row,),
        out_specs=(row, row, column, whole, whole, lead, column, column, lead)
        + (whole,) * 5
        + (P(None, ("dp", "mp")),),
        check_vma=False,
    )
```

```python
import functools

import jax
import jax.numpy as jnp
import numpy as np
from jax import lax
from jax.experimental import pallas as pl
from jax.experimental.pallas import tpu as pltpu
from jax.sharding import PartitionSpec as P

HEADS = 32
KV = 8
HD = 64
EPSILON = 1e-06
ROPE_BASE = 10000.0
BLOCK = 256
F32 = jnp.float32
BF16 = jnp.bfloat16
MESH = pl.DeviceIdType.MESH


ANY = pl.BlockSpec(memory_space=pl.ANY)
VMEM = pl.BlockSpec(memory_space=pltpu.VMEM)


class Place:
    def __init__(self, members, parts):
        me = lax.axis_index("mp")
        self.dp, self.pos, self.core = lax.axis_index("dp"), me // 2, lax.rem(me, 2)
        self.length, self.parts = members // 2, parts
        self.last = self.length - 1

    def at(self, pos, core):
        return (self.dp, pos * 2 + core)

    def partner(self, bit):
        mine = lax.rem(self.dp // (1 << bit), 2)
        return mine, (self.dp + (1 - 2 * mine) * (1 << bit), self.pos * 2 + self.core)

    def bits(self):
        return self.parts.bit_length() - 1

    def greet(self, line, across):
        barrier = pltpu.get_barrier_semaphore()

        def tell(device):
            pl.semaphore_signal(barrier, inc=1, device_id=device, device_id_type=MESH)

        peers = 0
        if line:
            tell(self.at(self.pos, 1 - self.core))

            @pl.when(self.pos > 0)
            def _():
                tell(self.at(self.pos - 1, self.core))

            @pl.when(self.pos < self.last)
            def _():
                tell(self.at(self.pos + 1, self.core))

            peers = 1 + jnp.minimum(self.pos, 1) + jnp.minimum(self.last - self.pos, 1)
        if across:
            for bit in range(self.bits()):
                tell(self.partner(bit)[1])
            peers = peers + self.bits()
        return peers

    def meet(self, peers):
        pl.semaphore_wait(pltpu.get_barrier_semaphore(), peers)


def weave(live):
    while live:
        live = [r for r in live if next(r, live) is not live]


def remote(src, dst, send_sem, recv_sem, device):
    return pltpu.make_async_remote_copy(
        src_ref=src, dst_ref=dst, send_sem=send_sem, recv_sem=recv_sem, device_id=device, device_id_type=MESH
    )


class Step:
    def before(self, *refs):
        pass


class Gather(Step):
    line, across = True, False

    def __init__(self, x, members):
        length = members // 2
        sems = pltpu.SemaphoreType.DMA((length,))
        self.inputs = [(x, ANY)]
        self.outputs = [(jax.ShapeDtypeStruct((members * x.shape[0],) + x.shape[1:], x.dtype), ANY)]
        self.scratch = [pltpu.SemaphoreType.DMA, sems, sems, sems, pltpu.SemaphoreType.DMA((members,))]

    def run(self, here, *refs):
        self.begin(here, *refs)
        for step in range(1, here.length):
            yield
            self.hop(here, step, *refs)
        yield
        self.end(here, *refs)

    def parts(self, here, x_ref, o_ref, own_sem, left_sem, right_sem, side_sem, recv_sem):
        rows = x_ref.shape[0]

        def block(p, c):
            return o_ref.at[pl.ds(pl.multiple_of((p * 2 + c) * rows, rows), rows)]

        def send(src, p, sem, to_p, to_c):
            remote(src, block(p, here.core), sem.at[p], recv_sem.at[p * 2 + here.core], here.at(to_p, to_c)).start()

        def arrived(p, c):
            pltpu.make_async_copy(x_ref, block(p, c), recv_sem.at[p * 2 + c]).wait()

        own = pltpu.make_async_copy(x_ref, block(here.pos, here.core), own_sem)
        return block, send, arrived, own, left_sem, right_sem, side_sem

    def begin(self, here, x_ref, *refs):
        pos, core = here.pos, here.core
        block, send, arrived, own, left_sem, right_sem, side_sem = self.parts(here, x_ref, *refs)

        @pl.when(pos > 0)
        def _():
            send(x_ref, pos, left_sem, pos - 1, core)

        @pl.when(pos < here.last)
        def _():
            send(x_ref, pos, right_sem, pos + 1, core)

        send(x_ref, pos, side_sem, pos, 1 - core)
        own.start()

    def hop(self, here, step, x_ref, *refs):
        pos, core = here.pos, here.core
        block, send, arrived, own, left_sem, right_sem, side_sem = self.parts(here, x_ref, *refs)
        right, left = pos + step, pos - step

        @pl.when(right < here.length)
        def _():
            arrived(right, core)

            @pl.when(pos > 0)
            def _():
                send(block(right, core), right, left_sem, pos - 1, core)

            send(block(right, core), right, side_sem, pos, 1 - core)

        @pl.when(left >= 0)
        def _():
            arrived(left, core)

            @pl.when(pos < here.last)
            def _():
                send(block(left, core), left, right_sem, pos + 1, core)

            send(block(left, core), left, side_sem, pos, 1 - core)

    def end(self, here, x_ref, *refs):
        pos, core = here.pos, here.core
        block, send, arrived, own, left_sem, right_sem, side_sem = self.parts(here, x_ref, *refs)
        own.wait()

        def sent(sem, p):
            pltpu.make_async_copy(x_ref, block(pos, core), sem.at[p]).wait()

        def drain(p, carry):
            arrived(p, 1 - core)
            sent(side_sem, p)

            @pl.when((p >= pos) & (pos > 0))
            def _():
                sent(left_sem, p)

            @pl.when((p <= pos) & (pos < here.last))
            def _():
                sent(right_sem, p)

            return carry

        lax.fori_loop(0, here.length, drain, 0)


class GatherFfn(Step):
    line, across = True, False

    def __init__(self, x, grad_rows, w_gate, w_up, w_down, members):
        length, (rows, width), units = members // 2, x.shape, w_gate.shape[1]
        total = members * rows
        sems = pltpu.SemaphoreType.DMA((length,))
        self.units = units
        self.inputs = [(v, ANY) for v in (x, grad_rows)] + [(v, ANY) for v in (w_gate, w_up, w_down)]
        self.outputs = [
            (jax.ShapeDtypeStruct((total, width), BF16), VMEM),
            (jax.ShapeDtypeStruct((total, units), BF16), VMEM),
            (jax.ShapeDtypeStruct((total, units), BF16), VMEM),
            (jax.ShapeDtypeStruct((total, units), BF16), VMEM),
        ]
        self.scratch = [pltpu.VMEM(v.shape, v.dtype) for v in (grad_rows, w_gate, w_up, w_down)]
        self.scratch += [pltpu.SemaphoreType.DMA((5,)), sems, sems, sems, pltpu.SemaphoreType.DMA((members,))]

    def run(self, here, x_ref, gr_ref, wg_ref, wu_ref, wd_ref, o_ref, hid_ref, gg_ref, gu_ref,
            gr, wg, wu, wd, load_sem, left_sem, right_sem, side_sem, recv_sem):
        pos, core, length = here.pos, here.core, here.length
        rows, units, wide = x_ref.shape[0], self.units, 256

        def block(p, c):
            return o_ref.at[pl.ds(pl.multiple_of((p * 2 + c) * rows, rows), rows)]

        def send(src, p, sem, to_p, to_c):
            remote(src, block(p, core), sem.at[p], recv_sem.at[p * 2 + core], here.at(to_p, to_c)).start()

        def arrived(p, c):
            pltpu.make_async_copy(x_ref, block(p, c), recv_sem.at[p * 2 + c]).wait()

        def sent(sem, p):
            pltpu.make_async_copy(x_ref, block(pos, core), sem.at[p]).wait()

        @pl.when(pos > 0)
        def _():
            send(x_ref, pos, left_sem, pos - 1, core)

        @pl.when(pos < here.last)
        def _():
            send(x_ref, pos, right_sem, pos + 1, core)

        send(x_ref, pos, side_sem, pos, 1 - core)
        pairs = [(x_ref, block(pos, core)), (wg_ref, wg), (wu_ref, wu), (gr_ref, gr), (wd_ref, wd)]
        loads = [pltpu.make_async_copy(a, b, load_sem.at[i]) for i, (a, b) in enumerate(pairs)]
        for load in loads:
            load.start()
        yield
        for load in loads:
            load.wait()

        def use(p):
            at = pl.ds(pl.multiple_of(p * 2 * rows, 2 * rows), 2 * rows)

            def body(c, carry):
                cols = pl.ds(pl.multiple_of(c * wide, wide), wide)
                gate = dot_nn(o_ref[at], wg[:, cols])
                up = dot_nn(o_ref[at], wu[:, cols])
                back = dot_nt(gr[at], wd[cols])
                sigma = 1.0 / (1.0 + jnp.exp(-gate))
                silu = gate * sigma
                hid_ref[at, cols] = (silu * up).astype(BF16)
                gg_ref[at, cols] = (back * up * sigma * (1.0 + gate * (1.0 - sigma))).astype(BF16)
                gu_ref[at, cols] = (back * silu).astype(BF16)
                return carry

            lax.fori_loop(0, units // wide, body, 0)

        def hop(step, carry):
            right, left = pos + step, pos - step

            @pl.when((step > 0) & (right < length))
            def _():
                arrived(right, core)

                @pl.when(pos > 0)
                def _():
                    send(block(right, core), right, left_sem, pos - 1, core)

                send(block(right, core), right, side_sem, pos, 1 - core)

            @pl.when((step > 0) & (left >= 0))
            def _():
                arrived(left, core)

                @pl.when(pos < here.last)
                def _():
                    send(block(left, core), left, right_sem, pos + 1, core)

                send(block(left, core), left, side_sem, pos, 1 - core)

            def side(k, c):
                p = pos + (1 - 2 * k) * step

                @pl.when((p >= 0) & (p < length) & (step >= k))
                def _():
                    arrived(p, 1 - core)
                    use(p)

                return c

            lax.fori_loop(0, 2, side, 0)
            return carry

        lax.fori_loop(0, length, hop, 0)

        def drain(p, carry):
            sent(side_sem, p)

            @pl.when((p >= pos) & (pos > 0))
            def _():
                sent(left_sem, p)

            @pl.when((p <= pos) & (pos < here.last))
            def _():
                sent(right_sem, p)

            return carry

        lax.fori_loop(0, length, drain, 0)


class Scatter(Step):
    line, across = True, False

    def __init__(self, terms, members):
        left, right, turned = terms[0]
        rows, width = left.shape[0] // members, right.shape[0 if turned else 1]
        self.rows, self.width, self.turned = rows, width, [t[2] for t in terms]
        self.depth, self.start = right.shape[1 if turned else 0], [0] * len(terms)
        lefts = [t[0] for t in terms]
        if all(x is left for x in lefts) and len(terms) > 1:
            lefts, self.start = [left], [i * self.depth for i in range(len(terms))]
        self.inputs = [(x, VMEM) for x in lefts] + [(t[1], ANY) for t in terms]
        self.outputs = [(jax.ShapeDtypeStruct((rows, width), F32), VMEM)]
        self.scratch = [pltpu.VMEM(t[1].shape, t[1].dtype) for t in terms]
        self.scratch += [pltpu.SemaphoreType.DMA((len(terms),))] + line_sum_scratch(members, rows, width)

    def run(self, here, *refs):
        total = self.begin(here, *refs)
        for t in range(here.last):
            total.fill(t)
            yield
            total.slot(t)
        total.fill(here.last)
        yield
        total.end()

    def begin(self, here, *refs):
        n = len(self.turned)
        m = len(self.inputs) - n
        lefts, refs = (refs[:m] * n)[:n], refs[m:]
        rights, o_ref, helds, load_sem, p_ref = refs[:n], refs[n], refs[n + 1 : 2 * n + 1], refs[2 * n + 1], refs[2 * n + 2]
        rows, wide = self.rows, 256
        loads = [pltpu.make_async_copy(w, h, load_sem.at[i]) for i, (w, h) in enumerate(zip(rights, helds))]
        for load in loads:
            load.start()

        def multiply(p):
            at = pl.ds(pl.multiple_of(p * 2 * rows, 2 * rows), 2 * rows)

            def body(c, carry):
                cols = pl.ds(pl.multiple_of(c * wide, wide), wide)
                total = None
                for left, held, turned, start in zip(lefts, helds, self.turned, self.start):
                    mine = left[at, start : start + self.depth]
                    part = dot_nt(mine, held[cols]) if turned else dot_nn(mine, held[:, cols])
                    total = part if total is None else total + part
                p_ref[at, cols] = total.astype(BF16)
                return carry

            lax.fori_loop(0, self.width // wide, body, 0)

        for load in loads:
            load.wait()
        return LineSum(here, rows, multiply, o_ref, p_ref, *refs[2 * n + 3 :])


def line_sum_scratch(members, rows, width):
    length = members // 2
    held = [pltpu.VMEM((members * rows, width), BF16), pltpu.VMEM((length, rows, width), BF16)]
    held += [pltpu.VMEM((length, rows, width), BF16)] * 2
    return held + [pltpu.SemaphoreType.DMA((length,))] * 6


class LineSum:
    def __init__(self, here, rows, multiply, o_ref, p_ref, side_buf, left_in, right_in,
                 side_send, side_recv, right_send, right_recv, left_send, left_recv):
        self.here, self.rows, self.multiply, self.o_ref, self.p_ref = here, rows, multiply, o_ref, p_ref
        self.side_buf, self.left_in, self.right_in = side_buf, left_in, right_in
        self.side, self.right, self.left = (side_send, side_recv), (right_send, right_recv), (left_send, left_recv)

    def block(self, p, c):
        return self.p_ref.at[pl.ds(pl.multiple_of((p * 2 + c) * self.rows, self.rows), self.rows)]

    def side_copy(self, p):
        here = self.here
        sems = [s.at[p] for s in self.side]
        return remote(self.block(p, 1 - here.core), self.side_buf.at[p], *sems, here.at(here.pos, 1 - here.core))

    def line_copy(self, p, right):
        here = self.here
        buf, sems = (self.right_in, self.right) if right else (self.left_in, self.left)
        to = here.at(here.pos + 1 if right else here.pos - 1, here.core)
        return remote(self.block(p, here.core), buf.at[p], *[s.at[p] for s in sems], to)

    def add(self, p, incoming, final):
        tile, rows = 16, self.rows

        def body(r, carry):
            s = pl.ds(pl.multiple_of(r * tile, tile), tile)
            mine = pl.ds(pl.multiple_of((p * 2 + self.here.core) * rows + r * tile, tile), tile)
            total = self.p_ref[mine].astype(F32) + self.side_buf[p, s].astype(F32)
            for ref in incoming:
                total = total + ref[p, s].astype(F32)
            if final:
                self.o_ref[s] = total
            else:
                self.p_ref[mine] = total.astype(BF16)
            return carry

        lax.fori_loop(0, rows // tile, body, 0)

    def fill(self, t):
        pos, last = self.here.pos, self.here.last

        def side(k, carry):
            own = t == last
            p = jnp.where(own, pos, k * t + (1 - k) * (last - t))

            @pl.when(jnp.where(own, 1 - k, (1 - 2 * k) * (p - pos)) > 0)
            def _():
                self.multiply(p)
                self.side_copy(p).start()

            return carry

        lax.fori_loop(0, 2, side, 0)

    def move(self, p, right, first, source):
        self.side_copy(p).wait_recv()

        @pl.when(first)
        def _():
            self.add(p, [], False)

        @pl.when(jnp.logical_not(first))
        def _():
            self.line_copy(p, right).wait_recv()
            self.add(p, [source], False)

        self.line_copy(p, right).start()

    def slot(self, t):
        pos, last = self.here.pos, self.here.last
        right_p, left_p = last - t + pos, t - (last - pos)

        @pl.when(t >= pos)
        def _():
            self.move(right_p, True, pos == 0, self.right_in)

        @pl.when(left_p >= 0)
        def _():
            self.move(left_p, False, pos == last, self.left_in)

    def end(self):
        pos, last = self.here.pos, self.here.last
        self.side_copy(pos).wait_recv()

        @pl.when(pos == 0)
        def _():
            self.line_copy(pos, False).wait_recv()
            self.add(pos, [self.left_in], True)

        @pl.when(pos == last)
        def _():
            self.line_copy(pos, True).wait_recv()
            self.add(pos, [self.right_in], True)

        @pl.when((pos > 0) & (pos < last))
        def _():
            self.line_copy(pos, False).wait_recv()
            self.line_copy(pos, True).wait_recv()
            self.add(pos, [self.left_in, self.right_in], True)

        def drain(p, carry):
            self.side_copy(p).wait_send()

            @pl.when(p > pos)
            def _():
                self.line_copy(p, True).wait_send()

            @pl.when(p < pos)
            def _():
                self.line_copy(p, False).wait_send()

            return carry

        lax.fori_loop(0, self.here.length, drain, 0)


def rounds(here, total, hop=None):
    def body(t, carry):
        total.fill(t)

        @pl.when(t < here.last)
        def _():
            if hop is not None:
                hop(t + 1)
            total.slot(t)

        return carry

    lax.fori_loop(0, here.length, body, 0)


class ScatterAlone(Scatter):
    def __init__(self, terms, members, gathered=None):
        Scatter.__init__(self, terms, members)
        self.other = None if gathered is None else Gather(gathered, members)
        self.sizes = [len(v) for v in (self.inputs, self.outputs, self.scratch)]
        if gathered is not None:
            self.inputs = self.inputs + self.other.inputs
            self.outputs = self.outputs + self.other.outputs
            self.scratch = self.scratch + self.other.scratch

    def run(self, here, *refs):
        ends, mine, rest = [len(v) for v in (self.inputs, self.outputs, self.scratch)], [], []
        for size, end in zip(self.sizes, ends):
            mine += refs[:size]
            rest += refs[size:end]
            refs = refs[end:]
        if self.other is not None:
            self.other.begin(here, *rest)
        all_inputs, self.inputs = self.inputs, self.inputs[: self.sizes[0]]
        total = self.begin(here, *mine)
        self.inputs = all_inputs
        rounds(here, total, None if self.other is None else lambda step: self.other.hop(here, step, *rest))
        total.end()
        if self.other is not None:
            self.other.end(here, *rest)
        yield


class Forward(Step):
    line, across = True, False

    def __init__(self, tokens, out_grad, attn_gain, ffn_gain, query_gain, key_gain, w_query, w_key, w_value, w_output,
                 positions, members):
        rows, width = tokens.shape
        length, size, inner = members // 2, members * rows, w_query.shape[1]
        self.heads, self.share, columns = inner // HD, members // KV, inner + 2 * HD
        sems = pltpu.SemaphoreType.DMA((length,))
        self.grads = Gather(out_grad, members)
        freq = ROPE_BASE ** (-np.arange(HD // 2, dtype=np.float32) / (HD // 2))
        freq = jnp.asarray(np.tile(freq, 4)[None], F32)
        self.inputs = [(tokens, VMEM), (out_grad, ANY), (attn_gain[None], VMEM), (ffn_gain[None], VMEM)]
        self.inputs += [(query_gain[None], VMEM), (key_gain[None], VMEM), (w_query, ANY), (w_key, ANY), (w_value, ANY)]
        self.inputs += [(w_output, ANY), (positions.reshape(size // 128, 128), VMEM), (freq, VMEM)]
        self.outputs = [
            (jax.ShapeDtypeStruct((size, width), BF16), ANY),
            (jax.ShapeDtypeStruct((size, columns), F32), VMEM),
            (jax.ShapeDtypeStruct((size, inner), BF16), VMEM),
            (jax.ShapeDtypeStruct((size // BLOCK, 1, self.heads * BLOCK), F32), VMEM),
            (jax.ShapeDtypeStruct((size, width), BF16), ANY),
            (jax.ShapeDtypeStruct((rows, width), F32), VMEM),
            (jax.ShapeDtypeStruct((rows, width), BF16), VMEM),
            (jax.ShapeDtypeStruct((size, 2 * HD), F32), VMEM),
            (jax.ShapeDtypeStruct((size, 2 * HD), F32), VMEM),
        ]
        self.scratch = [pltpu.VMEM((size, width), BF16), pltpu.VMEM(w_query.shape, BF16), pltpu.VMEM((width, 2 * HD), BF16)]
        self.scratch += [pltpu.VMEM((width, 2 * HD), BF16), pltpu.VMEM((width, 2 * HD), BF16), pltpu.VMEM(w_output.shape, BF16)]
        self.scratch += [pltpu.VMEM((size, 2 * HD), jnp.int32)]
        self.scratch += [pltpu.VMEM((size, inner), BF16), pltpu.VMEM((size, HD), BF16), pltpu.VMEM((size, 2 * HD), BF16)]
        self.scratch += [pltpu.VMEM((self.heads * BLOCK, 2 * HD), F32), pltpu.SemaphoreType.DMA((5,))]
        self.scratch += [sems, sems, sems, pltpu.SemaphoreType.DMA((members,))]
        self.scratch += self.grads.scratch + line_sum_scratch(members, rows, width)

    def loads(self, here, wq_ref, wk_ref, wv_ref, wo_ref, wq, wk, wv, wo, load_sem):
        group = (here.pos * 2 + here.core) // self.share
        cols = pl.ds(pl.multiple_of(group // 2 * 2 * HD, 2 * HD), 2 * HD)
        pairs = [(wq_ref, wq), (wk_ref.at[:, cols], wk), (wv_ref.at[:, cols], wv), (wo_ref, wo)]
        return lax.rem(group, 2), [pltpu.make_async_copy(a, b, load_sem.at[i]) for i, (a, b) in enumerate(pairs)]

    def before(self, here, tok_ref, og_ref, again_ref, fgain_ref, qgain_ref, kgain_ref, wq_ref, wk_ref, wv_ref, wo_ref,
               pos_ref, freq_ref, one_ref, proj_ref, ctx_ref, lse_ref, gr_ref, branch_ref, two_ref, cos_ref, sin_ref,
               all_ref, wq, wk, wv, wkv, wo, *rest):
        for load in self.loads(here, wq_ref, wk_ref, wv_ref, wo_ref, wq, wk, wv, wo, rest[5])[1]:
            load.start()
        rows = tok_ref.shape[0]
        me = (here.pos * 2 + here.core) * rows

        def body(r, carry):
            at = pl.ds(pl.multiple_of(r * 32, 32), 32)
            x = tok_ref[at].astype(F32)
            inv = lax.rsqrt(jnp.mean(x * x, -1, keepdims=True) + EPSILON)
            all_ref[pl.ds(pl.multiple_of(me + r * 32, 32), 32)] = (x * inv * again_ref[...]).astype(BF16)
            return carry

        lax.fori_loop(0, rows // 32, body, 0)

    def run(self, here, tok_ref, og_ref, again_ref, fgain_ref, qgain_ref, kgain_ref, wq_ref, wk_ref, wv_ref, wo_ref,
            pos_ref, freq_ref, one_ref, proj_ref, ctx_ref, lse_ref, gr_ref, branch_ref, two_ref, cos_ref, sin_ref,
            all_ref, wq, wk, wv, wkv, wo, place_ref,
            q_ref, k_ref, v_ref, acc_ref, load_sem, left_sem, right_sem, side_sem, recv_sem, *rest):
        pos, core, length = here.pos, here.core, here.length
        rows, width = tok_ref.shape
        heads, inner, size = self.heads, self.heads * HD, proj_ref.shape[0]
        lane = lax.broadcasted_iota(jnp.int32, (1, HD), 1)

        def block(p, c):
            return all_ref.at[pl.ds(pl.multiple_of((p * 2 + c) * rows, rows), rows)]

        def send(p, sem, to_p, to_c):
            remote(block(p, core), block(p, core), sem.at[p], recv_sem.at[p * 2 + core], here.at(to_p, to_c)).start()

        def arrived(p, c):
            pltpu.make_async_copy(block(p, c), block(p, c), recv_sem.at[p * 2 + c]).wait()

        def sent(sem, p):
            pltpu.make_async_copy(block(p, core), block(p, core), sem.at[p]).wait()

        def prepare():
            odd, loads = self.loads(here, wq_ref, wk_ref, wv_ref, wo_ref, wq, wk, wv, wo, load_sem)
            for load in loads:
                load.wait()
            low = lax.broadcasted_iota(jnp.int32, (1, 2 * HD), 1) < HD

            def pick(r, carry):
                at = pl.ds(pl.multiple_of(r * 256, 256), 256)
                key, value = wk[at].astype(F32), wv[at].astype(F32)
                key = jnp.where(odd == 1, pltpu.roll(key, HD, 1), key)
                value = jnp.where(odd == 1, value, pltpu.roll(value, HD, 1))
                wkv[at] = jnp.where(low, key, value).astype(BF16)
                return carry

            lax.fori_loop(0, width // 256, pick, 0)

            def table(r, carry):
                at = pl.ds(pl.multiple_of(r * 128, 128), 128)
                place = jnp.broadcast_to(pos_ref[pl.ds(r, 1)].astype(F32), (128, 128)).T
                place_ref[at] = place.astype(jnp.int32)
                angle = place * freq_ref[...]
                cos_ref[at] = jnp.cos(angle)
                sin_ref[at] = jnp.sin(angle)
                return carry

            lax.fori_loop(0, size // 128, table, 0)

        def use(p):
            at = pl.ds(pl.multiple_of(p * BLOCK, BLOCK), BLOCK)
            x = jnp.concatenate([dot_nn(all_ref[at], wq[...]), dot_nn(all_ref[at], wkv[...])], 1)
            proj_ref[at] = x
            gain = jnp.concatenate([qgain_ref[...]] * heads + [kgain_ref[...], jnp.ones((1, HD), F32)], 1)
            cosine, sine = wide(cos_ref[at], inner + 2 * HD), wide(sin_ref[at], inner + 2 * HD)
            unit, _ = normed(x)
            spun = turn(unit * gain, cosine, sine)
            q_ref[at] = (spun[:, :inner].astype(BF16) * HD**-0.5).astype(BF16)
            k_ref[at] = spun[:, inner : inner + HD].astype(BF16)
            ones = jnp.broadcast_to(jnp.where(lane == 0, 1.0, 0.0), (BLOCK, HD)).astype(BF16)
            v_ref[at] = jnp.concatenate([x[:, inner + HD :].astype(BF16), ones], 1)

        def pass_on(step):
            right, left = pos + step, pos - step

            @pl.when(right < length)
            def _():
                @pl.when(step > 0)
                def _():
                    arrived(right, core)

                @pl.when(pos > 0)
                def _():
                    send(right, left_sem, pos - 1, core)

                send(right, side_sem, pos, 1 - core)

            @pl.when(left >= 0)
            def _():
                @pl.when(step > 0)
                def _():
                    arrived(left, core)

                @pl.when(pos < here.last)
                def _():
                    send(left, right_sem, pos + 1, core)

                @pl.when(step > 0)
                def _():
                    send(left, side_sem, pos, 1 - core)

        def use_both(step):
            def side(k, c):
                p = pos + (1 - 2 * k) * step

                @pl.when((p >= 0) & (p < length) & (step >= k))
                def _():
                    arrived(p, 1 - core)
                    use(p)

                return c

            lax.fori_loop(0, 2, side, 0)

        pass_on(0)
        prepare()

        def hop(step, carry):
            use_both(step)
            pass_on(step + 1)
            return carry

        lax.fori_loop(0, here.last, hop, 0)
        n = len(self.grads.scratch)
        held = rest[n:]
        p_ref = held[0]
        grads = (og_ref, gr_ref) + tuple(rest[:n])
        self.grads.begin(here, *grads)
        use_both(here.last)
        keep = pltpu.make_async_copy(all_ref, one_ref, load_sem.at[4])
        keep.start()

        def attend(i):
            at = pl.ds(pl.multiple_of(i * BLOCK, BLOCK), BLOCK)
            query = q_ref[at]
            stacked = jnp.concatenate([query[:, h * HD : (h + 1) * HD] for h in range(heads)], 0)
            acc_ref[...] = jnp.zeros_like(acc_ref)
            index = i * BLOCK + lax.broadcasted_iota(jnp.int32, (BLOCK, 1), 0)
            start = index - place_ref[at, :1]

            def keys(j, c):
                cols = pl.ds(pl.multiple_of(j * BLOCK, BLOCK), BLOCK)
                scores = dot_nt(stacked, k_ref[cols])
                place = j * BLOCK + lax.broadcasted_iota(jnp.int32, (1, BLOCK), 1)
                seen = (place >= start) & (place <= index)
                expo = [
                    jnp.where(seen, jnp.exp(scores[h * BLOCK : (h + 1) * BLOCK]), 0.0).astype(BF16)
                    for h in range(heads)
                ]
                acc_ref[...] += dot_nn(jnp.concatenate(expo, 0), v_ref[cols])
                return c

            lax.fori_loop(0, i + 1, keys, 0)
            outs, logs = [], []
            for h in range(heads):
                acc = acc_ref[pl.ds(h * BLOCK, BLOCK)]
                outs.append((acc[:, :HD] * (1.0 / acc[:, HD : HD + 1])).astype(BF16))
                logs.append(jnp.log(acc.T[HD : HD + 1]))
            ctx_ref[at] = jnp.concatenate(outs, 1)
            lse_ref[i] = jnp.concatenate(logs, 1)

        def multiply(p):
            attend(p)
            at = pl.ds(pl.multiple_of(p * BLOCK, BLOCK), BLOCK)

            def body(c, carry):
                cols = pl.ds(pl.multiple_of(c * 512, 512), 512)
                p_ref[at, cols] = dot_nn(ctx_ref[at], wo[:, cols]).astype(BF16)
                return carry

            lax.fori_loop(0, width // 512, body, 0)

        total = LineSum(here, rows, multiply, branch_ref, *held)
        rounds(here, total, lambda step: self.grads.hop(here, step, *grads))
        total.end()

        def body(r, carry):
            at = pl.ds(pl.multiple_of(r * 32, 32), 32)
            x = tok_ref[at].astype(F32) + branch_ref[at]
            inv = lax.rsqrt(jnp.mean(x * x, -1, keepdims=True) + EPSILON)
            two_ref[at] = (x * inv * fgain_ref[...]).astype(BF16)
            return carry

        lax.fori_loop(0, rows // 32, body, 0)

        def drain(p, carry):
            sent(side_sem, p)

            @pl.when((p >= pos) & (pos > 0))
            def _():
                sent(left_sem, p)

            @pl.when((p <= pos) & (pos < here.last))
            def _():
                sent(right_sem, p)

            return carry

        lax.fori_loop(0, length, drain, 0)
        self.grads.end(here, *grads)
        keep.wait()
        yield


class Across(Step):
    line, across = False, True

    def __init__(self, x, parts, colours, late=0):
        self.bits, self.colours, self.late = parts.bit_length() - 1, colours, late
        rows, width = x.shape
        self.inputs = [(x, VMEM)]
        self.outputs = [(jax.ShapeDtypeStruct(x.shape, x.dtype), VMEM)]
        self.scratch = [pltpu.VMEM((rows, width), x.dtype)]
        for _ in colours:
            part = rows // len(colours)
            self.scratch += [pltpu.VMEM((part >> (s + 1), width), x.dtype) for s in range(self.bits)]
            self.scratch += [pltpu.SemaphoreType.DMA((2 * self.bits,))] * 2

    def run(self, here, x_ref, o_ref, sum_ref, *rest):
        for _ in range(self.late):
            yield
        n, rows = self.bits + 2, x_ref.shape[0] // len(self.colours)
        live = [
            self.one(here, backwards, i * rows, rows, x_ref, o_ref, sum_ref, *rest[i * n : (i + 1) * n])
            for i, backwards in enumerate(self.colours)
        ]
        while live:
            live = [r for r in live if next(r, live) is not live]
            yield

    def one(self, here, backwards, start, size, x_ref, o_ref, sum_ref, *rest):
        taken, (send_sem, recv_sem) = rest[: self.bits], rest[self.bits :]
        order = list(range(self.bits))[:: -1 if backwards else 1]
        copies, tile = [], 16

        def part(ref, at, count):
            return ref.at[pl.ds(pl.multiple_of(at, count), count)]

        for s, bit in enumerate(order):
            mine, device = here.partner(bit)
            half = size // 2
            keep, give = start + mine * half, start + (1 - mine) * half
            source = x_ref if s == 0 else sum_ref
            target = o_ref if s == self.bits - 1 else sum_ref
            copy = remote(part(source, give, half), taken[s], send_sem.at[s], recv_sem.at[s], device)
            copy.start()
            copies.append(copy)
            yield
            copy.wait_recv()

            def body(r, carry):
                at = pl.ds(pl.multiple_of(keep + r * tile, tile), tile)
                got = taken[s][pl.ds(pl.multiple_of(r * tile, tile), tile)]
                target[at] = (source[at].astype(F32) + got.astype(F32)).astype(target.dtype)
                return carry

            lax.fori_loop(0, half // tile, body, 0)
            start, size = keep, half
        for s, bit in enumerate(order[::-1]):
            mine, device = here.partner(bit)
            n = self.bits + s
            copy = remote(part(o_ref, start, size), part(o_ref, start, size), send_sem.at[n], recv_sem.at[n], device)
            copy.start()
            copies.append(copy)
            yield
            copy.wait_recv()
            start, size = start - mine * size, size * 2
        for copy in copies:
            copy.wait_send()


class KeyValue(Step):
    line, across = True, True

    def __init__(self, x, width, members, parts):
        self.width, self.extra, self.members = width, x.shape[0] - width, members
        self.sum, self.all = Across(x, parts, (False,)), Gather(x, members)
        self.inputs = [(x, VMEM)]
        flat = jax.ShapeDtypeStruct((width, KV * HD), BF16)
        self.outputs = [(flat, VMEM), (flat, VMEM), (jax.ShapeDtypeStruct((self.extra, 2 * HD), F32), VMEM)]
        self.scratch = [pltpu.VMEM(x.shape, x.dtype), pltpu.VMEM((members * x.shape[0], 2 * HD), x.dtype)]
        self.scratch += self.sum.scratch + self.all.scratch

    def run(self, here, x_ref, key_ref, value_ref, small_ref, sum_ref, all_ref, *rest):
        n = len(self.sum.scratch)
        first = self.sum.run(here, x_ref, sum_ref, *rest[:n])
        next(first)
        yield
        for _ in first:
            pass
        yield from self.all.run(here, sum_ref, all_ref, *rest[n:])
        rows, share, tile = self.width + self.extra, self.members // KV, 128

        def block(group, at, count):
            total = 0.0
            for k in range(share):
                begin = pl.multiple_of((group * share + k) * rows + at, 16)
                total = total + all_ref[pl.ds(begin, count)].astype(F32)
            return total

        for pair in range(KV // 2):
            cols = slice(2 * HD * pair, 2 * HD * (pair + 1))

            def body(r, carry):
                at = pl.ds(pl.multiple_of(r * tile, tile), tile)
                one, two = block(2 * pair, r * tile, tile), block(2 * pair + 1, r * tile, tile)
                key_ref[at, cols] = jnp.concatenate([one[:, :HD], two[:, :HD]], 1).astype(BF16)
                value_ref[at, cols] = jnp.concatenate([one[:, HD:], two[:, HD:]], 1).astype(BF16)
                return carry

            lax.fori_loop(0, self.width // tile, body, 0)
        small = 0.0
        for group in range(KV):
            small = small + block(group, self.width, self.extra)
        small_ref[...] = small


def held_bytes(shape, dtype):
    *lead, rows, columns = (1,) + tuple(shape)
    return int(np.prod(lead)) * -(-rows // 8) * 8 * -(-columns // 128) * 128 * jnp.dtype(dtype).itemsize


def together(steps, members, parts, collective_id, whole=False, spare=6):
    need = 0
    for s in steps:
        need += sum(held_bytes(x.shape, x.dtype) for x, m in s.inputs + s.outputs if m is VMEM)
        need += sum(held_bytes(h.shape, h.dtype) for h in s.scratch if h is not pltpu.SemaphoreType.DMA and h.memory_space == pltpu.VMEM)
    counts = [(len(s.inputs), len(s.outputs), len(s.scratch)) for s in steps]

    def kernel(*refs):
        refs = list(refs)
        given = [[refs.pop(0) for _ in range(c[0])] for c in counts]
        made = [[refs.pop(0) for _ in range(c[1])] for c in counts]
        held = [[refs.pop(0) for _ in range(c[2])] for c in counts]
        here = Place(members, parts)
        peers = here.greet(any(s.line for s in steps), any(s.across for s in steps))
        for s, g, m, h in zip(steps, given, made, held):
            s.before(here, *g, *m, *h)
        here.meet(peers)
        weave([s.run(here, *g, *m, *h) for s, g, m, h in zip(steps, given, made, held)])

    return pl.pallas_call(
        kernel,
        out_shape=[o for s in steps for o, _ in s.outputs],
        in_specs=[m for s in steps for _, m in s.inputs],
        out_specs=[m for s in steps for _, m in s.outputs],
        scratch_shapes=[h for s in steps for h in s.scratch],
        compiler_params=pltpu.CompilerParams(
            collective_id=collective_id, has_side_effects=True, vmem_limit_bytes=58 << 20 if whole else need + (spare << 20)
        ),
        cost_estimate=pl.CostEstimate(flops=1, bytes_accessed=1, transcendentals=0),
    )(*[x for s in steps for x, _ in s.inputs])


def dot_nn(a, b):
    return lax.dot_general(a, b, (((1,), (0,)), ((), ())), preferred_element_type=F32)

def dot_nt(a, b):
    return lax.dot_general(a, b, (((1,), (1,)), ((), ())), preferred_element_type=F32)

def dot_tn(a, b):
    return lax.dot_general(a, b, (((0,), (0,)), ((), ())), preferred_element_type=F32)

def group_mean(x):
    width = x.shape[1]
    row = lax.broadcasted_iota(jnp.int32, (width, width), 0) // HD
    col = lax.broadcasted_iota(jnp.int32, (width, width), 1) // HD
    ones = jnp.where(row == col, 1.0 / HD, 0.0).astype(F32)
    return jnp.dot(x, ones, precision=lax.Precision.HIGHEST, preferred_element_type=F32)

def half_turn(x):
    width = x.shape[1]
    lane = lax.broadcasted_iota(jnp.int32, (1, width), 1)
    first = lax.rem(lane, HD) < HD // 2
    up = pltpu.roll(x, HD // 2, 1)
    down = pltpu.roll(x, width - HD // 2, 1)
    return jnp.where(first, -down, up)

def wide(table, width):
    return jnp.concatenate([table] * (width // table.shape[1]), 1)

def normed(x):
    inv = lax.rsqrt(group_mean(x * x) + EPSILON)
    return x * inv, inv

def turn(x, cosine, sine):
    return x * cosine + half_turn(x) * sine

def turn_back(x, cosine, sine):
    return x * cosine - half_turn(x) * sine

def stack_lanes(x, heads):
    return jnp.concatenate([x[h * HD:(h + 1) * HD] for h in range(heads)], 1)

def attend_back_kernel(heads, proj_ref, cos_ref, sin_ref, qgain_ref, kgain_ref, pos_ref, ctx_ref, grad_ref, lse_ref,
                       out_ref, sums_ref, k_ref, kt_ref, v_ref, dk_ref, dv_ref, dq_ref):
    width = heads * HD
    scale = HD ** -0.5
    count = proj_ref.shape[0] // BLOCK
    gain = jnp.concatenate([qgain_ref[...]] * heads + [kgain_ref[...], jnp.ones((1, HD), F32)], 1)
    def prepare(i, carry):
        rows = pl.ds(pl.multiple_of(i * BLOCK, BLOCK), BLOCK)
        x = proj_ref[rows, width:]
        unit, _ = normed(x)
        spun = turn(unit * gain[:, width:], cos_ref[rows], sin_ref[rows])
        k_ref[rows] = spun[:, :HD].astype(BF16)
        kt_ref[i] = spun.T[:HD].astype(BF16)
        v_ref[rows] = x[:, HD:].astype(BF16)
        dk_ref[rows] = jnp.zeros((BLOCK, HD), F32)
        dv_ref[rows] = jnp.zeros((BLOCK, HD), F32)
        return carry
    lax.fori_loop(0, count, prepare, 0)
    sums_ref[...] = jnp.zeros_like(sums_ref)
    def outer(i, carry):
        rows = pl.ds(pl.multiple_of(i * BLOCK, BLOCK), BLOCK)
        x = proj_ref[rows, :width]
        cosine, sine = wide(cos_ref[rows], width), wide(sin_ref[rows], width)
        unit, inv = normed(x)
        query = (turn(unit * gain[:, :width], cosine, sine).astype(BF16).astype(F32) * scale)
        query_t = stack_lanes(query.T, heads).astype(BF16)
        query = query.astype(BF16)
        query_s = jnp.concatenate([query[:, h * HD:(h + 1) * HD] for h in range(heads)], 0)
        grad = grad_ref[rows]
        grad_s = jnp.concatenate([grad[:, h * HD:(h + 1) * HD] for h in range(heads)], 0)
        grad_t = stack_lanes(grad.astype(F32).T, heads)
        ctx_t = stack_lanes(ctx_ref[rows].astype(F32).T, heads)
        delta = jnp.sum(grad_t * ctx_t, 0, keepdims=True)
        grad_t = grad_t.astype(BF16)
        lse = lse_ref[i]
        index = i * BLOCK + lax.broadcasted_iota(jnp.int32, (1, BLOCK), 1)
        start = index - pos_ref[i]
        dq_ref[...] = jnp.zeros_like(dq_ref)
        def inner(j, c):
            cols = pl.ds(pl.multiple_of(j * BLOCK, BLOCK), BLOCK)
            scores = dot_nn(k_ref[cols], query_t)
            grad_probs = dot_nn(v_ref[cols], grad_t)
            place = j * BLOCK + lax.broadcasted_iota(jnp.int32, (BLOCK, 1), 0)
            seen = (place >= start) & (place <= index)
            probs, back = [], []
            for h in range(heads):
                s = slice(h * BLOCK, (h + 1) * BLOCK)
                exact = jnp.where(seen, jnp.exp(scores[:, s] - lse[:, s]), 0.0)
                probs.append(exact.astype(BF16))
                back.append((exact * (grad_probs[:, s] - delta[:, s])).astype(BF16))
            probs = jnp.concatenate(probs, 1)
            back = jnp.concatenate(back, 1)
            dv_ref[cols] += dot_nn(probs, grad_s)
            dk_ref[cols] += dot_nn(back, query_s)
            dq_ref[...] += dot_nn(kt_ref[j], back)
            return c
        lax.fori_loop(0, i + 1, inner, 0)
        dq = jnp.concatenate([dq_ref[:, h * BLOCK:(h + 1) * BLOCK] for h in range(heads)], 0).T * scale
        dqn = turn_back(dq, cosine, sine)
        sums_ref[:, :width] += jnp.sum(dqn * unit, 0, keepdims=True)
        e = dqn * gain[:, :width]
        out_ref[rows, :width] = (inv * (e - unit * group_mean(e * unit))).astype(BF16)
        return carry
    for first in range(2):
        lax.fori_loop(first * count // 2, (first + 1) * count // 2, outer, 0)
        yield
    def finish(i, carry):
        rows = pl.ds(pl.multiple_of(i * BLOCK, BLOCK), BLOCK)
        x = proj_ref[rows, width:]
        unit, inv = normed(x)
        dv = dv_ref[rows]
        dk = jnp.concatenate([dk_ref[rows], dv], 1)
        dkn = turn_back(dk, cos_ref[rows], sin_ref[rows])
        sums_ref[:, width:] += jnp.sum(dkn * unit, 0, keepdims=True)
        e = dkn * gain[:, width:]
        dkp = inv * (e - unit * group_mean(e * unit))
        lane = lax.broadcasted_iota(jnp.int32, (1, 2 * HD), 1)
        out_ref[rows, width:] = jnp.where(lane < HD, dkp, dk).astype(BF16)
        return carry
    lax.fori_loop(0, count, finish, 0)
    yield

class AttendBack(Step):
    line, across = False, False

    def __init__(self, proj, cosine, sine, query_gain, key_gain, positions, context, grad_context, lse, heads):
        size = proj.shape[0]
        count = size // BLOCK
        self.heads = heads
        args = (proj, cosine, sine, query_gain[None], key_gain[None], positions.reshape(count, 1, BLOCK), context, grad_context, lse)
        self.inputs = [(x, VMEM) for x in args]
        self.outputs = [(jax.ShapeDtypeStruct(proj.shape, BF16), VMEM), (jax.ShapeDtypeStruct((1, proj.shape[1]), F32), VMEM)]
        self.scratch = [pltpu.VMEM((size, HD), BF16), pltpu.VMEM((count, HD, BLOCK), BF16), pltpu.VMEM((size, HD), BF16)]
        self.scratch += [pltpu.VMEM((size, HD), F32), pltpu.VMEM((size, HD), F32), pltpu.VMEM((HD, heads * BLOCK), F32)]

    def run(self, here, *refs):
        yield from attend_back_kernel(self.heads, *refs)


def matmul(left, right):
    return jnp.dot(left, right, preferred_element_type=F32)


def matmul_left_t(left, right):
    return lax.dot_general(left, right, (((0,), (0,)), ((), ())), preferred_element_type=F32)


def matmul_right_t(left, right):
    return lax.dot_general(left, right, (((1,), (1,)), ((), ())), preferred_element_type=F32)


def norm_back(grad_normed, unit, inverse, gain):
    scaled = grad_normed * gain
    return inverse * (scaled - unit * jnp.mean(scaled * unit, -1, keepdims=True))


def after(first, *later):
    return lax.optimization_barrier((first,) + later)


def per_device(
    tokens,
    seg_ids,
    positions,
    w_query,
    w_key,
    w_value,
    w_output,
    w_gate,
    w_up,
    w_down,
    attn_gain,
    ffn_gain,
    query_gain,
    key_gain,
    out_grad,
):
    members, parts = lax.axis_size("mp"), lax.axis_size("dp")
    width = tokens.shape[1]
    query_width = w_query.shape[1]
    heads = query_width // HD
    ffn_width = w_gate.shape[1]
    share = members // KV
    group = lax.axis_index("mp") // share

    rows_one, projected, context, lse, grad_rows, attn_branch, h_two, cosine, sine = together(
        [
            Forward(
                tokens,
                out_grad,
                attn_gain,
                ffn_gain,
                query_gain,
                key_gain,
                w_query,
                w_key,
                w_value,
                w_output,
                positions,
                members,
            )
        ],
        members,
        parts,
        0,
        True,
    )
    rows_two, hidden, grad_gate, grad_up = together(
        [GatherFfn(h_two, grad_rows, w_gate, w_up, w_down, members)], members, parts, 5, False, 14
    )
    rows_two, tokens_late, w_key, w_value = after(rows_two, tokens, w_key, w_value)
    tokens_f = tokens_late.astype(F32)
    inv_one = lax.rsqrt(jnp.mean(tokens_f * tokens_f, -1, keepdims=True) + EPSILON)
    normed_one = tokens_f * inv_one
    key_cols = lax.dynamic_slice_in_dim(w_key, group * HD, HD, 1)
    value_cols = lax.dynamic_slice_in_dim(w_value, group * HD, HD, 1)
    w_attn = jnp.concatenate([w_query, key_cols, value_cols], 1)
    residual_mid = tokens_f + attn_branch
    inv_two = lax.rsqrt(jnp.mean(residual_mid * residual_mid, -1, keepdims=True) + EPSILON)
    normed_two = residual_mid * inv_two
    ffn_parts = (
        matmul_left_t(hidden, grad_rows).astype(BF16),
        matmul_left_t(rows_two, grad_gate).astype(BF16),
        matmul_left_t(rows_two, grad_up).astype(BF16),
    )
    ffn_parts, grad_gate, grad_up, hidden = lax.optimization_barrier((ffn_parts, grad_gate, grad_up, hidden))
    grad_w_down, grad_w_gate, grad_w_up = lax.psum(ffn_parts, "dp")

    grad_h_two = together(
        [ScatterAlone([(grad_gate, w_gate, True), (grad_up, w_up, True)], members)],
        members,
        parts,
        6,
        True,
    )[0]
    grad_ffn_gain = jnp.sum(grad_h_two * normed_two, 0)
    grad_mid = out_grad.astype(F32) + norm_back(grad_h_two, normed_two, inv_two, ffn_gain)
    ffn_branch, grad_attn_rows = together(
        [ScatterAlone([(hidden, w_down, False)], members, grad_mid.astype(BF16))],
        members,
        parts,
        2,
    )
    grad_context = matmul_right_t(grad_attn_rows, w_output).astype(BF16)
    output_part = matmul_left_t(context, grad_attn_rows).astype(BF16)
    grad_proj, gain_sums, grad_w_output = together(
        [
            AttendBack(
                projected, cosine, sine, query_gain, key_gain, positions, context, grad_context, lse, heads
            ),
            Across(output_part, parts, (False, True) if output_part.shape[0] % (32 * parts) == 0 else (False,)),
        ],
        members,
        parts,
        7,
    )
    grad_w_attn = matmul_left_t(rows_one, grad_proj)
    grad_attn_gain = jnp.sum(w_attn.astype(F32) * grad_w_attn, 1) / attn_gain

    small = jnp.concatenate(
        [
            grad_attn_gain,
            grad_ffn_gain,
            jnp.sum(gain_sums[0, :query_width].reshape(heads, HD), 0),
            gain_sums[0, query_width : query_width + HD],
            jnp.sum(tokens_f * tokens_f)[None],
        ]
    )
    unit = 16 * parts
    extra = -(-small.shape[0] // (unit * 2 * HD)) * unit
    small_rows = jnp.pad(small, (0, extra * 2 * HD - small.shape[0])).reshape(extra, 2 * HD)
    kv_part = jnp.concatenate([grad_w_attn[:, query_width:], small_rows], 0).astype(BF16)
    query_part = grad_w_attn[:, :query_width].astype(BF16)
    grad_w_key, grad_w_value, small_sum, grad_h_one, grad_w_query = together(
        [
            KeyValue(kv_part, width, members, parts),
            Scatter([(grad_proj, w_attn, True)], members),
            Across(query_part, parts, (False, True)),
        ],
        members,
        parts,
        3,
    )
    small_sum = small_sum.reshape(-1)
    entry_count = tokens.size * parts * members
    at = 2 * width
    residual_rms = jnp.sqrt(small_sum[at + 2 * HD : at + 2 * HD + 1] / entry_count)

    grad_tokens = (grad_mid + norm_back(grad_h_one, normed_one, inv_one, attn_gain)).astype(BF16)
    output = (residual_mid + ffn_branch).astype(BF16)
    branch_rms = jnp.stack(
        [
            jnp.sqrt(jnp.mean(attn_branch * attn_branch, -1)),
            jnp.sqrt(jnp.mean(ffn_branch * ffn_branch, -1)),
        ]
    )
    return (
        output,
        grad_tokens,
        grad_w_query.astype(F32),
        grad_w_key.astype(F32),
        grad_w_value.astype(F32),
        grad_w_output.astype(F32),
        grad_w_gate.astype(F32),
        grad_w_up.astype(F32),
        grad_w_down.astype(F32),
        small_sum[:width],
        small_sum[width:at],
        small_sum[at : at + HD],
        small_sum[at + HD : at + 2 * HD],
        residual_rms,
        branch_rms,
    )


def solution(mesh):
    row, whole, column = P(("dp", "mp"), None), P(), P(None, "mp")
    lead = P("mp", None)
    return jax.shard_map(
        per_device,
        mesh=mesh,
        in_specs=(row, P("dp"), P("dp"), column, whole, whole, lead, column, column, lead)
        + (whole,) * 4
        + (row,),
        out_specs=(row, row, column, whole, whole, lead, column, column, lead)
        + (whole,) * 5
        + (P(None, ("dp", "mp")),),
        check_vma=False,
    )
```

```python
import functools

import jax
import jax.numpy as jnp
import numpy as np
from jax import lax
from jax.experimental import pallas as pl
from jax.experimental.pallas import tpu as pltpu
from jax.sharding import PartitionSpec as P

HEADS = 32
KV = 8
HD = 64
EPSILON = 1e-06
ROPE_BASE = 10000.0
BLOCK = 256
F32 = jnp.float32
BF16 = jnp.bfloat16
MESH = pl.DeviceIdType.MESH


ANY = pl.BlockSpec(memory_space=pl.ANY)
VMEM = pl.BlockSpec(memory_space=pltpu.VMEM)


class Place:
    def __init__(self, members, parts):
        me = lax.axis_index("mp")
        self.dp, self.pos, self.core = lax.axis_index("dp"), me // 2, lax.rem(me, 2)
        self.length, self.parts = members // 2, parts
        self.last = self.length - 1

    def at(self, pos, core):
        return (self.dp, pos * 2 + core)

    def partner(self, bit):
        mine = lax.rem(self.dp // (1 << bit), 2)
        return mine, (self.dp + (1 - 2 * mine) * (1 << bit), self.pos * 2 + self.core)

    def bits(self):
        return self.parts.bit_length() - 1

    def greet(self, line, across):
        barrier = pltpu.get_barrier_semaphore()

        def tell(device):
            pl.semaphore_signal(barrier, inc=1, device_id=device, device_id_type=MESH)

        peers = 0
        if line:
            tell(self.at(self.pos, 1 - self.core))

            @pl.when(self.pos > 0)
            def _():
                tell(self.at(self.pos - 1, self.core))

            @pl.when(self.pos < self.last)
            def _():
                tell(self.at(self.pos + 1, self.core))

            peers = 1 + jnp.minimum(self.pos, 1) + jnp.minimum(self.last - self.pos, 1)
        if across:
            for bit in range(self.bits()):
                tell(self.partner(bit)[1])
            peers = peers + self.bits()
        return peers

    def meet(self, peers):
        pl.semaphore_wait(pltpu.get_barrier_semaphore(), peers)


def weave(live):
    while live:
        live = [r for r in live if next(r, live) is not live]


def remote(src, dst, send_sem, recv_sem, device):
    return pltpu.make_async_remote_copy(
        src_ref=src, dst_ref=dst, send_sem=send_sem, recv_sem=recv_sem, device_id=device, device_id_type=MESH
    )


class Step:
    def before(self, *refs):
        pass


class Gather(Step):
    line, across = True, False

    def __init__(self, x, members):
        length = members // 2
        sems = pltpu.SemaphoreType.DMA((length,))
        self.inputs = [(x, ANY)]
        self.outputs = [(jax.ShapeDtypeStruct((members * x.shape[0],) + x.shape[1:], x.dtype), ANY)]
        self.scratch = [pltpu.SemaphoreType.DMA, sems, sems, sems, pltpu.SemaphoreType.DMA((members,))]

    def run(self, here, *refs):
        self.begin(here, *refs)
        for step in range(1, here.length):
            yield
            self.hop(here, step, *refs)
        yield
        self.end(here, *refs)

    def parts(self, here, x_ref, o_ref, own_sem, left_sem, right_sem, side_sem, recv_sem):
        rows = x_ref.shape[0]

        def block(p, c):
            return o_ref.at[pl.ds(pl.multiple_of((p * 2 + c) * rows, rows), rows)]

        def send(src, p, sem, to_p, to_c):
            remote(src, block(p, here.core), sem.at[p], recv_sem.at[p * 2 + here.core], here.at(to_p, to_c)).start()

        def arrived(p, c):
            pltpu.make_async_copy(x_ref, block(p, c), recv_sem.at[p * 2 + c]).wait()

        own = pltpu.make_async_copy(x_ref, block(here.pos, here.core), own_sem)
        return block, send, arrived, own, left_sem, right_sem, side_sem

    def begin(self, here, x_ref, *refs):
        pos, core = here.pos, here.core
        block, send, arrived, own, left_sem, right_sem, side_sem = self.parts(here, x_ref, *refs)

        @pl.when(pos > 0)
        def _():
            send(x_ref, pos, left_sem, pos - 1, core)

        @pl.when(pos < here.last)
        def _():
            send(x_ref, pos, right_sem, pos + 1, core)

        send(x_ref, pos, side_sem, pos, 1 - core)
        own.start()

    def hop(self, here, step, x_ref, *refs):
        pos, core = here.pos, here.core
        block, send, arrived, own, left_sem, right_sem, side_sem = self.parts(here, x_ref, *refs)
        right, left = pos + step, pos - step

        @pl.when(right < here.length)
        def _():
            arrived(right, core)

            @pl.when(pos > 0)
            def _():
                send(block(right, core), right, left_sem, pos - 1, core)

            send(block(right, core), right, side_sem, pos, 1 - core)

        @pl.when(left >= 0)
        def _():
            arrived(left, core)

            @pl.when(pos < here.last)
            def _():
                send(block(left, core), left, right_sem, pos + 1, core)

            send(block(left, core), left, side_sem, pos, 1 - core)

    def end(self, here, x_ref, *refs):
        pos, core = here.pos, here.core
        block, send, arrived, own, left_sem, right_sem, side_sem = self.parts(here, x_ref, *refs)
        own.wait()

        def sent(sem, p):
            pltpu.make_async_copy(x_ref, block(pos, core), sem.at[p]).wait()

        def drain(p, carry):
            arrived(p, 1 - core)
            sent(side_sem, p)

            @pl.when((p >= pos) & (pos > 0))
            def _():
                sent(left_sem, p)

            @pl.when((p <= pos) & (pos < here.last))
            def _():
                sent(right_sem, p)

            return carry

        lax.fori_loop(0, here.length, drain, 0)


class GatherFfn(Step):
    line, across = True, False

    def __init__(self, x, grad_rows, w_gate, w_up, w_down, members):
        length, (rows, width), units = members // 2, x.shape, w_gate.shape[1]
        total = members * rows
        sems = pltpu.SemaphoreType.DMA((length,))
        self.units = units
        self.inputs = [(v, ANY) for v in (x, grad_rows)] + [(v, ANY) for v in (w_gate, w_up, w_down)]
        self.outputs = [
            (jax.ShapeDtypeStruct((total, width), BF16), VMEM),
            (jax.ShapeDtypeStruct((total, units), BF16), VMEM),
            (jax.ShapeDtypeStruct((total, units), BF16), VMEM),
            (jax.ShapeDtypeStruct((total, units), BF16), VMEM),
        ]
        self.scratch = [pltpu.VMEM(v.shape, v.dtype) for v in (grad_rows, w_gate, w_up, w_down)]
        self.scratch += [pltpu.SemaphoreType.DMA((5,)), sems, sems, sems, pltpu.SemaphoreType.DMA((members,))]

    def run(self, here, x_ref, gr_ref, wg_ref, wu_ref, wd_ref, o_ref, hid_ref, gg_ref, gu_ref,
            gr, wg, wu, wd, load_sem, left_sem, right_sem, side_sem, recv_sem):
        pos, core, length = here.pos, here.core, here.length
        rows, units, wide = x_ref.shape[0], self.units, 256

        def block(p, c):
            return o_ref.at[pl.ds(pl.multiple_of((p * 2 + c) * rows, rows), rows)]

        def send(src, p, sem, to_p, to_c):
            remote(src, block(p, core), sem.at[p], recv_sem.at[p * 2 + core], here.at(to_p, to_c)).start()

        def arrived(p, c):
            pltpu.make_async_copy(x_ref, block(p, c), recv_sem.at[p * 2 + c]).wait()

        def sent(sem, p):
            pltpu.make_async_copy(x_ref, block(pos, core), sem.at[p]).wait()

        @pl.when(pos > 0)
        def _():
            send(x_ref, pos, left_sem, pos - 1, core)

        @pl.when(pos < here.last)
        def _():
            send(x_ref, pos, right_sem, pos + 1, core)

        send(x_ref, pos, side_sem, pos, 1 - core)
        pairs = [(x_ref, block(pos, core)), (wg_ref, wg), (wu_ref, wu), (gr_ref, gr), (wd_ref, wd)]
        loads = [pltpu.make_async_copy(a, b, load_sem.at[i]) for i, (a, b) in enumerate(pairs)]
        for load in loads:
            load.start()
        yield
        for load in loads:
            load.wait()

        def use(p):
            at = pl.ds(pl.multiple_of(p * 2 * rows, 2 * rows), 2 * rows)

            def body(c, carry):
                cols = pl.ds(pl.multiple_of(c * wide, wide), wide)
                gate = dot_nn(o_ref[at], wg[:, cols])
                up = dot_nn(o_ref[at], wu[:, cols])
                back = dot_nt(gr[at], wd[cols])
                sigma = 1.0 / (1.0 + jnp.exp(-gate))
                silu = gate * sigma
                hid_ref[at, cols] = (silu * up).astype(BF16)
                gg_ref[at, cols] = (back * up * sigma * (1.0 + gate * (1.0 - sigma))).astype(BF16)
                gu_ref[at, cols] = (back * silu).astype(BF16)
                return carry

            lax.fori_loop(0, units // wide, body, 0)

        def hop(step, carry):
            right, left = pos + step, pos - step

            @pl.when((step > 0) & (right < length))
            def _():
                arrived(right, core)

                @pl.when(pos > 0)
                def _():
                    send(block(right, core), right, left_sem, pos - 1, core)

                send(block(right, core), right, side_sem, pos, 1 - core)

            @pl.when((step > 0) & (left >= 0))
            def _():
                arrived(left, core)

                @pl.when(pos < here.last)
                def _():
                    send(block(left, core), left, right_sem, pos + 1, core)

                send(block(left, core), left, side_sem, pos, 1 - core)

            def side(k, c):
                p = pos + (1 - 2 * k) * step

                @pl.when((p >= 0) & (p < length) & (step >= k))
                def _():
                    arrived(p, 1 - core)
                    use(p)

                return c

            lax.fori_loop(0, 2, side, 0)
            return carry

        lax.fori_loop(0, length, hop, 0)

        def drain(p, carry):
            sent(side_sem, p)

            @pl.when((p >= pos) & (pos > 0))
            def _():
                sent(left_sem, p)

            @pl.when((p <= pos) & (pos < here.last))
            def _():
                sent(right_sem, p)

            return carry

        lax.fori_loop(0, length, drain, 0)


class Scatter(Step):
    line, across = True, False

    def __init__(self, terms, members):
        left, right, turned = terms[0]
        rows, width = left.shape[0] // members, right.shape[0 if turned else 1]
        self.rows, self.width, self.turned = rows, width, [t[2] for t in terms]
        self.depth, self.start = right.shape[1 if turned else 0], [0] * len(terms)
        lefts = [t[0] for t in terms]
        if all(x is left for x in lefts) and len(terms) > 1:
            lefts, self.start = [left], [i * self.depth for i in range(len(terms))]
        self.inputs = [(x, VMEM) for x in lefts] + [(t[1], ANY) for t in terms]
        self.outputs = [(jax.ShapeDtypeStruct((rows, width), F32), VMEM)]
        self.scratch = [pltpu.VMEM(t[1].shape, t[1].dtype) for t in terms]
        self.scratch += [pltpu.SemaphoreType.DMA((len(terms),))] + line_sum_scratch(members, rows, width)

    def run(self, here, *refs):
        total = self.begin(here, *refs)
        for t in range(here.last):
            total.fill(t)
            yield
            total.slot(t)
        total.fill(here.last)
        yield
        total.end()

    def begin(self, here, *refs):
        n = len(self.turned)
        m = len(self.inputs) - n
        lefts, refs = (refs[:m] * n)[:n], refs[m:]
        rights, o_ref, helds, load_sem, p_ref = refs[:n], refs[n], refs[n + 1 : 2 * n + 1], refs[2 * n + 1], refs[2 * n + 2]
        rows, wide = self.rows, 256
        loads = [pltpu.make_async_copy(w, h, load_sem.at[i]) for i, (w, h) in enumerate(zip(rights, helds))]
        for load in loads:
            load.start()

        def multiply(p):
            at = pl.ds(pl.multiple_of(p * 2 * rows, 2 * rows), 2 * rows)

            def body(c, carry):
                cols = pl.ds(pl.multiple_of(c * wide, wide), wide)
                total = None
                for left, held, turned, start in zip(lefts, helds, self.turned, self.start):
                    mine = left[at, start : start + self.depth]
                    part = dot_nt(mine, held[cols]) if turned else dot_nn(mine, held[:, cols])
                    total = part if total is None else total + part
                p_ref[at, cols] = total.astype(BF16)
                return carry

            lax.fori_loop(0, self.width // wide, body, 0)

        for load in loads:
            load.wait()
        return LineSum(here, rows, multiply, o_ref, p_ref, *refs[2 * n + 3 :])


def line_sum_scratch(members, rows, width):
    length = members // 2
    held = [pltpu.VMEM((members * rows, width), BF16), pltpu.VMEM((length, rows, width), BF16)]
    held += [pltpu.VMEM((length, rows, width), BF16)] * 2
    return held + [pltpu.SemaphoreType.DMA((length,))] * 6


class LineSum:
    def __init__(self, here, rows, multiply, o_ref, p_ref, side_buf, left_in, right_in,
                 side_send, side_recv, right_send, right_recv, left_send, left_recv):
        self.here, self.rows, self.multiply, self.o_ref, self.p_ref = here, rows, multiply, o_ref, p_ref
        self.side_buf, self.left_in, self.right_in = side_buf, left_in, right_in
        self.side, self.right, self.left = (side_send, side_recv), (right_send, right_recv), (left_send, left_recv)

    def block(self, p, c):
        return self.p_ref.at[pl.ds(pl.multiple_of((p * 2 + c) * self.rows, self.rows), self.rows)]

    def side_copy(self, p):
        here = self.here
        sems = [s.at[p] for s in self.side]
        return remote(self.block(p, 1 - here.core), self.side_buf.at[p], *sems, here.at(here.pos, 1 - here.core))

    def line_copy(self, p, right):
        here = self.here
        buf, sems = (self.right_in, self.right) if right else (self.left_in, self.left)
        to = here.at(here.pos + 1 if right else here.pos - 1, here.core)
        return remote(self.block(p, here.core), buf.at[p], *[s.at[p] for s in sems], to)

    def add(self, p, incoming, final):
        tile, rows = 16, self.rows

        def body(r, carry):
            s = pl.ds(pl.multiple_of(r * tile, tile), tile)
            mine = pl.ds(pl.multiple_of((p * 2 + self.here.core) * rows + r * tile, tile), tile)
            total = self.p_ref[mine].astype(F32) + self.side_buf[p, s].astype(F32)
            for ref in incoming:
                total = total + ref[p, s].astype(F32)
            if final:
                self.o_ref[s] = total
            else:
                self.p_ref[mine] = total.astype(BF16)
            return carry

        lax.fori_loop(0, rows // tile, body, 0)

    def fill(self, t):
        pos, last = self.here.pos, self.here.last

        def side(k, carry):
            own = t == last
            p = jnp.where(own, pos, k * t + (1 - k) * (last - t))

            @pl.when(jnp.where(own, 1 - k, (1 - 2 * k) * (p - pos)) > 0)
            def _():
                self.multiply(p)
                self.side_copy(p).start()

            return carry

        lax.fori_loop(0, 2, side, 0)

    def move(self, p, right, first, source):
        self.side_copy(p).wait_recv()

        @pl.when(first)
        def _():
            self.add(p, [], False)

        @pl.when(jnp.logical_not(first))
        def _():
            self.line_copy(p, right).wait_recv()
            self.add(p, [source], False)

        self.line_copy(p, right).start()

    def slot(self, t):
        pos, last = self.here.pos, self.here.last
        right_p, left_p = last - t + pos, t - (last - pos)

        @pl.when(t >= pos)
        def _():
            self.move(right_p, True, pos == 0, self.right_in)

        @pl.when(left_p >= 0)
        def _():
            self.move(left_p, False, pos == last, self.left_in)

    def end(self):
        pos, last = self.here.pos, self.here.last
        self.side_copy(pos).wait_recv()

        @pl.when(pos == 0)
        def _():
            self.line_copy(pos, False).wait_recv()
            self.add(pos, [self.left_in], True)

        @pl.when(pos == last)
        def _():
            self.line_copy(pos, True).wait_recv()
            self.add(pos, [self.right_in], True)

        @pl.when((pos > 0) & (pos < last))
        def _():
            self.line_copy(pos, False).wait_recv()
            self.line_copy(pos, True).wait_recv()
            self.add(pos, [self.left_in, self.right_in], True)

        def drain(p, carry):
            self.side_copy(p).wait_send()

            @pl.when(p > pos)
            def _():
                self.line_copy(p, True).wait_send()

            @pl.when(p < pos)
            def _():
                self.line_copy(p, False).wait_send()

            return carry

        lax.fori_loop(0, self.here.length, drain, 0)


def rounds(here, total, hop=None):
    def body(t, carry):
        total.fill(t)

        @pl.when(t < here.last)
        def _():
            if hop is not None:
                hop(t + 1)
            total.slot(t)

        return carry

    lax.fori_loop(0, here.length, body, 0)


class ScatterAlone(Scatter):
    def __init__(self, terms, members, gathered=None):
        Scatter.__init__(self, terms, members)
        self.other = None if gathered is None else Gather(gathered, members)
        self.sizes = [len(v) for v in (self.inputs, self.outputs, self.scratch)]
        if gathered is not None:
            self.inputs = self.inputs + self.other.inputs
            self.outputs = self.outputs + self.other.outputs
            self.scratch = self.scratch + self.other.scratch

    def run(self, here, *refs):
        ends, mine, rest = [len(v) for v in (self.inputs, self.outputs, self.scratch)], [], []
        for size, end in zip(self.sizes, ends):
            mine += refs[:size]
            rest += refs[size:end]
            refs = refs[end:]
        if self.other is not None:
            self.other.begin(here, *rest)
        all_inputs, self.inputs = self.inputs, self.inputs[: self.sizes[0]]
        total = self.begin(here, *mine)
        self.inputs = all_inputs
        rounds(here, total, None if self.other is None else lambda step: self.other.hop(here, step, *rest))
        total.end()
        if self.other is not None:
            self.other.end(here, *rest)
        yield


class Forward(Step):
    line, across = True, False

    def __init__(self, tokens, out_grad, attn_gain, ffn_gain, query_gain, key_gain, w_query, w_key, w_value, w_output,
                 positions, members):
        rows, width = tokens.shape
        length, size, inner = members // 2, members * rows, w_query.shape[1]
        self.heads, self.share, columns = inner // HD, members // KV, inner + 2 * HD
        sems = pltpu.SemaphoreType.DMA((length,))
        self.grads = Gather(out_grad, members)
        freq = ROPE_BASE ** (-np.arange(HD // 2, dtype=np.float32) / (HD // 2))
        freq = jnp.asarray(np.tile(freq, 4)[None], F32)
        self.inputs = [(tokens, VMEM), (out_grad, ANY), (attn_gain[None], VMEM), (ffn_gain[None], VMEM)]
        self.inputs += [(query_gain[None], VMEM), (key_gain[None], VMEM), (w_query, ANY), (w_key, ANY), (w_value, ANY)]
        self.inputs += [(w_output, ANY), (positions.reshape(size // 128, 128), VMEM), (freq, VMEM)]
        self.outputs = [
            (jax.ShapeDtypeStruct((size, width), BF16), ANY),
            (jax.ShapeDtypeStruct((size, columns), F32), VMEM),
            (jax.ShapeDtypeStruct((size, inner), BF16), VMEM),
            (jax.ShapeDtypeStruct((size // BLOCK, 1, self.heads * BLOCK), F32), VMEM),
            (jax.ShapeDtypeStruct((size, width), BF16), ANY),
            (jax.ShapeDtypeStruct((rows, width), F32), VMEM),
            (jax.ShapeDtypeStruct((rows, width), BF16), VMEM),
            (jax.ShapeDtypeStruct((size, 2 * HD), F32), VMEM),
            (jax.ShapeDtypeStruct((size, 2 * HD), F32), VMEM),
        ]
        self.scratch = [pltpu.VMEM((size, width), BF16), pltpu.VMEM(w_query.shape, BF16), pltpu.VMEM((width, 2 * HD), BF16)]
        self.scratch += [pltpu.VMEM((width, 2 * HD), BF16), pltpu.VMEM((width, 2 * HD), BF16), pltpu.VMEM(w_output.shape, BF16)]
        self.scratch += [pltpu.VMEM((size, 2 * HD), jnp.int32)]
        self.scratch += [pltpu.VMEM((size, inner), BF16), pltpu.VMEM((size, HD), BF16), pltpu.VMEM((size, 2 * HD), BF16)]
        self.scratch += [pltpu.VMEM((self.heads * BLOCK, 2 * HD), F32), pltpu.SemaphoreType.DMA((5,))]
        self.scratch += [sems, sems, sems, pltpu.SemaphoreType.DMA((members,))]
        self.scratch += self.grads.scratch + line_sum_scratch(members, rows, width)

    def loads(self, here, wq_ref, wk_ref, wv_ref, wo_ref, wq, wk, wv, wo, load_sem):
        group = (here.pos * 2 + here.core) // self.share
        cols = pl.ds(pl.multiple_of(group // 2 * 2 * HD, 2 * HD), 2 * HD)
        pairs = [(wq_ref, wq), (wk_ref.at[:, cols], wk), (wv_ref.at[:, cols], wv), (wo_ref, wo)]
        return lax.rem(group, 2), [pltpu.make_async_copy(a, b, load_sem.at[i]) for i, (a, b) in enumerate(pairs)]

    def before(self, here, tok_ref, og_ref, again_ref, fgain_ref, qgain_ref, kgain_ref, wq_ref, wk_ref, wv_ref, wo_ref,
               pos_ref, freq_ref, one_ref, proj_ref, ctx_ref, lse_ref, gr_ref, branch_ref, two_ref, cos_ref, sin_ref,
               all_ref, wq, wk, wv, wkv, wo, *rest):
        for load in self.loads(here, wq_ref, wk_ref, wv_ref, wo_ref, wq, wk, wv, wo, rest[5])[1]:
            load.start()
        rows = tok_ref.shape[0]
        me = (here.pos * 2 + here.core) * rows

        def body(r, carry):
            at = pl.ds(pl.multiple_of(r * 32, 32), 32)
            x = tok_ref[at].astype(F32)
            inv = lax.rsqrt(jnp.mean(x * x, -1, keepdims=True) + EPSILON)
            all_ref[pl.ds(pl.multiple_of(me + r * 32, 32), 32)] = (x * inv * again_ref[...]).astype(BF16)
            return carry

        lax.fori_loop(0, rows // 32, body, 0)

    def run(self, here, tok_ref, og_ref, again_ref, fgain_ref, qgain_ref, kgain_ref, wq_ref, wk_ref, wv_ref, wo_ref,
            pos_ref, freq_ref, one_ref, proj_ref, ctx_ref, lse_ref, gr_ref, branch_ref, two_ref, cos_ref, sin_ref,
            all_ref, wq, wk, wv, wkv, wo, place_ref,
            q_ref, k_ref, v_ref, acc_ref, load_sem, left_sem, right_sem, side_sem, recv_sem, *rest):
        pos, core, length = here.pos, here.core, here.length
        rows, width = tok_ref.shape
        heads, inner, size = self.heads, self.heads * HD, proj_ref.shape[0]
        lane = lax.broadcasted_iota(jnp.int32, (1, HD), 1)

        def block(p, c):
            return all_ref.at[pl.ds(pl.multiple_of((p * 2 + c) * rows, rows), rows)]

        def send(p, sem, to_p, to_c):
            remote(block(p, core), block(p, core), sem.at[p], recv_sem.at[p * 2 + core], here.at(to_p, to_c)).start()

        def arrived(p, c):
            pltpu.make_async_copy(block(p, c), block(p, c), recv_sem.at[p * 2 + c]).wait()

        def sent(sem, p):
            pltpu.make_async_copy(block(p, core), block(p, core), sem.at[p]).wait()

        def prepare():
            odd, loads = self.loads(here, wq_ref, wk_ref, wv_ref, wo_ref, wq, wk, wv, wo, load_sem)
            for load in loads:
                load.wait()
            low = lax.broadcasted_iota(jnp.int32, (1, 2 * HD), 1) < HD

            def pick(r, carry):
                at = pl.ds(pl.multiple_of(r * 256, 256), 256)
                key, value = wk[at].astype(F32), wv[at].astype(F32)
                key = jnp.where(odd == 1, pltpu.roll(key, HD, 1), key)
                value = jnp.where(odd == 1, value, pltpu.roll(value, HD, 1))
                wkv[at] = jnp.where(low, key, value).astype(BF16)
                return carry

            lax.fori_loop(0, width // 256, pick, 0)

            def table(r, carry):
                at = pl.ds(pl.multiple_of(r * 128, 128), 128)
                place = jnp.broadcast_to(pos_ref[pl.ds(r, 1)].astype(F32), (128, 128)).T
                place_ref[at] = place.astype(jnp.int32)
                angle = place * freq_ref[...]
                cos_ref[at] = jnp.cos(angle)
                sin_ref[at] = jnp.sin(angle)
                return carry

            lax.fori_loop(0, size // 128, table, 0)

        def use(p):
            at = pl.ds(pl.multiple_of(p * BLOCK, BLOCK), BLOCK)
            x = jnp.concatenate([dot_nn(all_ref[at], wq[...]), dot_nn(all_ref[at], wkv[...])], 1)
            proj_ref[at] = x
            gain = jnp.concatenate([qgain_ref[...]] * heads + [kgain_ref[...], jnp.ones((1, HD), F32)], 1)
            cosine, sine = wide(cos_ref[at], inner + 2 * HD), wide(sin_ref[at], inner + 2 * HD)
            unit, _ = normed(x)
            spun = turn(unit * gain, cosine, sine)
            q_ref[at] = (spun[:, :inner].astype(BF16) * HD**-0.5).astype(BF16)
            k_ref[at] = spun[:, inner : inner + HD].astype(BF16)
            ones = jnp.broadcast_to(jnp.where(lane == 0, 1.0, 0.0), (BLOCK, HD)).astype(BF16)
            v_ref[at] = jnp.concatenate([x[:, inner + HD :].astype(BF16), ones], 1)

        def pass_on(step):
            right, left = pos + step, pos - step

            @pl.when(right < length)
            def _():
                @pl.when(step > 0)
                def _():
                    arrived(right, core)

                @pl.when(pos > 0)
                def _():
                    send(right, left_sem, pos - 1, core)

                send(right, side_sem, pos, 1 - core)

            @pl.when(left >= 0)
            def _():
                @pl.when(step > 0)
                def _():
                    arrived(left, core)

                @pl.when(pos < here.last)
                def _():
                    send(left, right_sem, pos + 1, core)

                @pl.when(step > 0)
                def _():
                    send(left, side_sem, pos, 1 - core)

        def use_both(step):
            def side(k, c):
                p = pos + (1 - 2 * k) * step

                @pl.when((p >= 0) & (p < length) & (step >= k))
                def _():
                    arrived(p, 1 - core)
                    use(p)

                return c

            lax.fori_loop(0, 2, side, 0)

        pass_on(0)
        prepare()

        def hop(step, carry):
            use_both(step)
            pass_on(step + 1)
            return carry

        lax.fori_loop(0, here.last, hop, 0)
        n = len(self.grads.scratch)
        held = rest[n:]
        p_ref = held[0]
        grads = (og_ref, gr_ref) + tuple(rest[:n])
        self.grads.begin(here, *grads)
        use_both(here.last)
        keep = pltpu.make_async_copy(all_ref, one_ref, load_sem.at[4])
        keep.start()

        def attend(i):
            at = pl.ds(pl.multiple_of(i * BLOCK, BLOCK), BLOCK)
            query = q_ref[at]
            stacked = jnp.concatenate([query[:, h * HD : (h + 1) * HD] for h in range(heads)], 0)
            acc_ref[...] = jnp.zeros_like(acc_ref)
            index = i * BLOCK + lax.broadcasted_iota(jnp.int32, (BLOCK, 1), 0)
            start = index - place_ref[at, :1]

            def keys(j, c):
                cols = pl.ds(pl.multiple_of(j * BLOCK, BLOCK), BLOCK)
                scores = dot_nt(stacked, k_ref[cols])
                place = j * BLOCK + lax.broadcasted_iota(jnp.int32, (1, BLOCK), 1)
                seen = (place >= start) & (place <= index)
                expo = [
                    jnp.where(seen, jnp.exp(scores[h * BLOCK : (h + 1) * BLOCK]), 0.0).astype(BF16)
                    for h in range(heads)
                ]
                acc_ref[...] += dot_nn(jnp.concatenate(expo, 0), v_ref[cols])
                return c

            lax.fori_loop(0, i + 1, keys, 0)
            outs, logs = [], []
            for h in range(heads):
                acc = acc_ref[pl.ds(h * BLOCK, BLOCK)]
                outs.append((acc[:, :HD] * (1.0 / acc[:, HD : HD + 1])).astype(BF16))
                logs.append(jnp.log(acc.T[HD : HD + 1]))
            ctx_ref[at] = jnp.concatenate(outs, 1)
            lse_ref[i] = jnp.concatenate(logs, 1)

        def multiply(p):
            attend(p)
            at = pl.ds(pl.multiple_of(p * BLOCK, BLOCK), BLOCK)

            def body(c, carry):
                cols = pl.ds(pl.multiple_of(c * 512, 512), 512)
                p_ref[at, cols] = dot_nn(ctx_ref[at], wo[:, cols]).astype(BF16)
                return carry

            lax.fori_loop(0, width // 512, body, 0)

        total = LineSum(here, rows, multiply, branch_ref, *held)
        rounds(here, total, lambda step: self.grads.hop(here, step, *grads))
        total.end()

        def body(r, carry):
            at = pl.ds(pl.multiple_of(r * 32, 32), 32)
            x = tok_ref[at].astype(F32) + branch_ref[at]
            inv = lax.rsqrt(jnp.mean(x * x, -1, keepdims=True) + EPSILON)
            two_ref[at] = (x * inv * fgain_ref[...]).astype(BF16)
            return carry

        lax.fori_loop(0, rows // 32, body, 0)

        def drain(p, carry):
            sent(side_sem, p)

            @pl.when((p >= pos) & (pos > 0))
            def _():
                sent(left_sem, p)

            @pl.when((p <= pos) & (pos < here.last))
            def _():
                sent(right_sem, p)

            return carry

        lax.fori_loop(0, length, drain, 0)
        self.grads.end(here, *grads)
        keep.wait()
        yield


class Across(Step):
    line, across = False, True

    def __init__(self, x, parts, colours, late=0):
        self.bits, self.colours, self.late = parts.bit_length() - 1, colours, late
        rows, width = x.shape
        self.inputs = [(x, VMEM)]
        self.outputs = [(jax.ShapeDtypeStruct(x.shape, x.dtype), VMEM)]
        self.scratch = [pltpu.VMEM((rows, width), x.dtype)]
        for _ in colours:
            part = rows // len(colours)
            self.scratch += [pltpu.VMEM((part >> (s + 1), width), x.dtype) for s in range(self.bits)]
            self.scratch += [pltpu.SemaphoreType.DMA((2 * self.bits,))] * 2

    def run(self, here, x_ref, o_ref, sum_ref, *rest):
        for _ in range(self.late):
            yield
        n, rows = self.bits + 2, x_ref.shape[0] // len(self.colours)
        live = [
            self.one(here, backwards, i * rows, rows, x_ref, o_ref, sum_ref, *rest[i * n : (i + 1) * n])
            for i, backwards in enumerate(self.colours)
        ]
        while live:
            live = [r for r in live if next(r, live) is not live]
            yield

    def one(self, here, backwards, start, size, x_ref, o_ref, sum_ref, *rest):
        taken, (send_sem, recv_sem) = rest[: self.bits], rest[self.bits :]
        order = list(range(self.bits))[:: -1 if backwards else 1]
        copies, tile = [], 16

        def part(ref, at, count):
            return ref.at[pl.ds(pl.multiple_of(at, count), count)]

        for s, bit in enumerate(order):
            mine, device = here.partner(bit)
            half = size // 2
            keep, give = start + mine * half, start + (1 - mine) * half
            source = x_ref if s == 0 else sum_ref
            target = o_ref if s == self.bits - 1 else sum_ref
            copy = remote(part(source, give, half), taken[s], send_sem.at[s], recv_sem.at[s], device)
            copy.start()
            copies.append(copy)
            yield
            copy.wait_recv()

            def body(r, carry):
                at = pl.ds(pl.multiple_of(keep + r * tile, tile), tile)
                got = taken[s][pl.ds(pl.multiple_of(r * tile, tile), tile)]
                target[at] = (source[at].astype(F32) + got.astype(F32)).astype(target.dtype)
                return carry

            lax.fori_loop(0, half // tile, body, 0)
            start, size = keep, half
        for s, bit in enumerate(order[::-1]):
            mine, device = here.partner(bit)
            n = self.bits + s
            copy = remote(part(o_ref, start, size), part(o_ref, start, size), send_sem.at[n], recv_sem.at[n], device)
            copy.start()
            copies.append(copy)
            yield
            copy.wait_recv()
            start, size = start - mine * size, size * 2
        for copy in copies:
            copy.wait_send()


class KeyValue(Step):
    line, across = True, True

    def __init__(self, x, width, members, parts):
        self.width, self.extra, self.members = width, x.shape[0] - width, members
        self.sum, self.all = Across(x, parts, (False,)), Gather(x, members)
        self.inputs = [(x, VMEM)]
        flat = jax.ShapeDtypeStruct((width, KV * HD), BF16)
        self.outputs = [(flat, VMEM), (flat, VMEM), (jax.ShapeDtypeStruct((self.extra, 2 * HD), F32), VMEM)]
        self.scratch = [pltpu.VMEM(x.shape, x.dtype), pltpu.VMEM((members * x.shape[0], 2 * HD), x.dtype)]
        self.scratch += self.sum.scratch + self.all.scratch

    def run(self, here, x_ref, key_ref, value_ref, small_ref, sum_ref, all_ref, *rest):
        n = len(self.sum.scratch)
        first = self.sum.run(here, x_ref, sum_ref, *rest[:n])
        next(first)
        yield
        for _ in first:
            pass
        yield from self.all.run(here, sum_ref, all_ref, *rest[n:])
        rows, share, tile = self.width + self.extra, self.members // KV, 128

        def block(group, at, count):
            total = 0.0
            for k in range(share):
                begin = pl.multiple_of((group * share + k) * rows + at, 16)
                total = total + all_ref[pl.ds(begin, count)].astype(F32)
            return total

        for pair in range(KV // 2):
            cols = slice(2 * HD * pair, 2 * HD * (pair + 1))

            def body(r, carry):
                at = pl.ds(pl.multiple_of(r * tile, tile), tile)
                one, two = block(2 * pair, r * tile, tile), block(2 * pair + 1, r * tile, tile)
                key_ref[at, cols] = jnp.concatenate([one[:, :HD], two[:, :HD]], 1).astype(BF16)
                value_ref[at, cols] = jnp.concatenate([one[:, HD:], two[:, HD:]], 1).astype(BF16)
                return carry

            lax.fori_loop(0, self.width // tile, body, 0)
        small = 0.0
        for group in range(KV):
            small = small + block(group, self.width, self.extra)
        small_ref[...] = small


def held_bytes(shape, dtype):
    *lead, rows, columns = (1,) + tuple(shape)
    return int(np.prod(lead)) * -(-rows // 8) * 8 * -(-columns // 128) * 128 * jnp.dtype(dtype).itemsize


def together(steps, members, parts, collective_id, whole=False, spare=6):
    need = 0
    for s in steps:
        need += sum(held_bytes(x.shape, x.dtype) for x, m in s.inputs + s.outputs if m is VMEM)
        need += sum(held_bytes(h.shape, h.dtype) for h in s.scratch if h is not pltpu.SemaphoreType.DMA and h.memory_space == pltpu.VMEM)
    counts = [(len(s.inputs), len(s.outputs), len(s.scratch)) for s in steps]

    def kernel(*refs):
        refs = list(refs)
        given = [[refs.pop(0) for _ in range(c[0])] for c in counts]
        made = [[refs.pop(0) for _ in range(c[1])] for c in counts]
        held = [[refs.pop(0) for _ in range(c[2])] for c in counts]
        here = Place(members, parts)
        peers = here.greet(any(s.line for s in steps), any(s.across for s in steps))
        for s, g, m, h in zip(steps, given, made, held):
            s.before(here, *g, *m, *h)
        here.meet(peers)
        weave([s.run(here, *g, *m, *h) for s, g, m, h in zip(steps, given, made, held)])

    return pl.pallas_call(
        kernel,
        out_shape=[o for s in steps for o, _ in s.outputs],
        in_specs=[m for s in steps for _, m in s.inputs],
        out_specs=[m for s in steps for _, m in s.outputs],
        scratch_shapes=[h for s in steps for h in s.scratch],
        compiler_params=pltpu.CompilerParams(
            collective_id=collective_id, has_side_effects=True, vmem_limit_bytes=58 << 20 if whole else need + (spare << 20)
        ),
        cost_estimate=pl.CostEstimate(flops=1, bytes_accessed=1, transcendentals=0),
    )(*[x for s in steps for x, _ in s.inputs])


def dot_nn(a, b):
    return lax.dot_general(a, b, (((1,), (0,)), ((), ())), preferred_element_type=F32)

def dot_nt(a, b):
    return lax.dot_general(a, b, (((1,), (1,)), ((), ())), preferred_element_type=F32)

def dot_tn(a, b):
    return lax.dot_general(a, b, (((0,), (0,)), ((), ())), preferred_element_type=F32)

def group_mean(x):
    width = x.shape[1]
    row = lax.broadcasted_iota(jnp.int32, (width, width), 0) // HD
    col = lax.broadcasted_iota(jnp.int32, (width, width), 1) // HD
    ones = jnp.where(row == col, 1.0 / HD, 0.0).astype(F32)
    return jnp.dot(x, ones, precision=lax.Precision.HIGHEST, preferred_element_type=F32)

def half_turn(x):
    width = x.shape[1]
    lane = lax.broadcasted_iota(jnp.int32, (1, width), 1)
    first = lax.rem(lane, HD) < HD // 2
    up = pltpu.roll(x, HD // 2, 1)
    down = pltpu.roll(x, width - HD // 2, 1)
    return jnp.where(first, -down, up)

def wide(table, width):
    return jnp.concatenate([table] * (width // table.shape[1]), 1)

def normed(x):
    inv = lax.rsqrt(group_mean(x * x) + EPSILON)
    return x * inv, inv

def turn(x, cosine, sine):
    return x * cosine + half_turn(x) * sine

def turn_back(x, cosine, sine):
    return x * cosine - half_turn(x) * sine

def stack_lanes(x, heads):
    return jnp.concatenate([x[h * HD:(h + 1) * HD] for h in range(heads)], 1)

def attend_back_kernel(heads, proj_ref, cos_ref, sin_ref, qgain_ref, kgain_ref, pos_ref, ctx_ref, grad_ref, lse_ref,
                       out_ref, sums_ref, k_ref, kt_ref, v_ref, dk_ref, dv_ref, dq_ref):
    width = heads * HD
    scale = HD ** -0.5
    count = proj_ref.shape[0] // BLOCK
    gain = jnp.concatenate([qgain_ref[...]] * heads + [kgain_ref[...], jnp.ones((1, HD), F32)], 1)
    def prepare(i, carry):
        rows = pl.ds(pl.multiple_of(i * BLOCK, BLOCK), BLOCK)
        x = proj_ref[rows, width:]
        unit, _ = normed(x)
        spun = turn(unit * gain[:, width:], cos_ref[rows], sin_ref[rows])
        k_ref[rows] = spun[:, :HD].astype(BF16)
        kt_ref[i] = spun.T[:HD].astype(BF16)
        v_ref[rows] = x[:, HD:].astype(BF16)
        dk_ref[rows] = jnp.zeros((BLOCK, HD), F32)
        dv_ref[rows] = jnp.zeros((BLOCK, HD), F32)
        return carry
    lax.fori_loop(0, count, prepare, 0)
    sums_ref[...] = jnp.zeros_like(sums_ref)
    def outer(i, carry):
        rows = pl.ds(pl.multiple_of(i * BLOCK, BLOCK), BLOCK)
        x = proj_ref[rows, :width]
        cosine, sine = wide(cos_ref[rows], width), wide(sin_ref[rows], width)
        unit, inv = normed(x)
        query = (turn(unit * gain[:, :width], cosine, sine).astype(BF16).astype(F32) * scale)
        query_t = stack_lanes(query.T, heads).astype(BF16)
        query = query.astype(BF16)
        query_s = jnp.concatenate([query[:, h * HD:(h + 1) * HD] for h in range(heads)], 0)
        grad = grad_ref[rows]
        grad_s = jnp.concatenate([grad[:, h * HD:(h + 1) * HD] for h in range(heads)], 0)
        grad_t = stack_lanes(grad.astype(F32).T, heads)
        ctx_t = stack_lanes(ctx_ref[rows].astype(F32).T, heads)
        delta = jnp.sum(grad_t * ctx_t, 0, keepdims=True)
        grad_t = grad_t.astype(BF16)
        lse = lse_ref[i]
        index = i * BLOCK + lax.broadcasted_iota(jnp.int32, (1, BLOCK), 1)
        start = index - pos_ref[i]
        dq_ref[...] = jnp.zeros_like(dq_ref)
        def inner(j, c):
            cols = pl.ds(pl.multiple_of(j * BLOCK, BLOCK), BLOCK)
            scores = dot_nn(k_ref[cols], query_t)
            grad_probs = dot_nn(v_ref[cols], grad_t)
            place = j * BLOCK + lax.broadcasted_iota(jnp.int32, (BLOCK, 1), 0)
            seen = (place >= start) & (place <= index)
            probs, back = [], []
            for h in range(heads):
                s = slice(h * BLOCK, (h + 1) * BLOCK)
                exact = jnp.where(seen, jnp.exp(scores[:, s] - lse[:, s]), 0.0)
                probs.append(exact.astype(BF16))
                back.append((exact * (grad_probs[:, s] - delta[:, s])).astype(BF16))
            probs = jnp.concatenate(probs, 1)
            back = jnp.concatenate(back, 1)
            dv_ref[cols] += dot_nn(probs, grad_s)
            dk_ref[cols] += dot_nn(back, query_s)
            dq_ref[...] += dot_nn(kt_ref[j], back)
            return c
        lax.fori_loop(0, i + 1, inner, 0)
        dq = jnp.concatenate([dq_ref[:, h * BLOCK:(h + 1) * BLOCK] for h in range(heads)], 0).T * scale
        dqn = turn_back(dq, cosine, sine)
        sums_ref[:, :width] += jnp.sum(dqn * unit, 0, keepdims=True)
        e = dqn * gain[:, :width]
        out_ref[rows, :width] = (inv * (e - unit * group_mean(e * unit))).astype(BF16)
        return carry
    for first in range(2):
        lax.fori_loop(first * count // 2, (first + 1) * count // 2, outer, 0)
        yield
    def finish(i, carry):
        rows = pl.ds(pl.multiple_of(i * BLOCK, BLOCK), BLOCK)
        x = proj_ref[rows, width:]
        unit, inv = normed(x)
        dv = dv_ref[rows]
        dk = jnp.concatenate([dk_ref[rows], dv], 1)
        dkn = turn_back(dk, cos_ref[rows], sin_ref[rows])
        sums_ref[:, width:] += jnp.sum(dkn * unit, 0, keepdims=True)
        e = dkn * gain[:, width:]
        dkp = inv * (e - unit * group_mean(e * unit))
        lane = lax.broadcasted_iota(jnp.int32, (1, 2 * HD), 1)
        out_ref[rows, width:] = jnp.where(lane < HD, dkp, dk).astype(BF16)
        return carry
    lax.fori_loop(0, count, finish, 0)
    yield

class AttendBack(Step):
    line, across = False, False

    def __init__(self, proj, cosine, sine, query_gain, key_gain, positions, context, grad_context, lse, heads):
        size = proj.shape[0]
        count = size // BLOCK
        self.heads = heads
        args = (proj, cosine, sine, query_gain[None], key_gain[None], positions.reshape(count, 1, BLOCK), context, grad_context, lse)
        self.inputs = [(x, VMEM) for x in args]
        self.outputs = [(jax.ShapeDtypeStruct(proj.shape, BF16), VMEM), (jax.ShapeDtypeStruct((1, proj.shape[1]), F32), VMEM)]
        self.scratch = [pltpu.VMEM((size, HD), BF16), pltpu.VMEM((count, HD, BLOCK), BF16), pltpu.VMEM((size, HD), BF16)]
        self.scratch += [pltpu.VMEM((size, HD), F32), pltpu.VMEM((size, HD), F32), pltpu.VMEM((HD, heads * BLOCK), F32)]

    def run(self, here, *refs):
        yield from attend_back_kernel(self.heads, *refs)


def matmul(left, right):
    return jnp.dot(left, right, preferred_element_type=F32)


def matmul_left_t(left, right):
    return lax.dot_general(left, right, (((0,), (0,)), ((), ())), preferred_element_type=F32)


def matmul_right_t(left, right):
    return lax.dot_general(left, right, (((1,), (1,)), ((), ())), preferred_element_type=F32)


def norm_back(grad_normed, unit, inverse, gain):
    scaled = grad_normed * gain
    return inverse * (scaled - unit * jnp.mean(scaled * unit, -1, keepdims=True))


def after(first, *later):
    return lax.optimization_barrier((first,) + later)


def widen_kernel(*refs):
    for low, high in zip(refs[:3], refs[3:]):
        high[...] = low[...].astype(F32)


def widen(*arrays):
    steps = 8
    specs = [pl.BlockSpec((x.shape[0] // steps, x.shape[1]), lambda i: (i, 0)) for x in arrays]
    return pl.pallas_call(
        widen_kernel,
        grid=(steps,),
        out_shape=[jax.ShapeDtypeStruct(x.shape, F32) for x in arrays],
        in_specs=specs,
        out_specs=specs,
        compiler_params=pltpu.CompilerParams(vmem_limit_bytes=32 << 20),
        cost_estimate=pl.CostEstimate(flops=1, bytes_accessed=1, transcendentals=0),
    )(*arrays)


def per_device(
    tokens,
    seg_ids,
    positions,
    w_query,
    w_key,
    w_value,
    w_output,
    w_gate,
    w_up,
    w_down,
    attn_gain,
    ffn_gain,
    query_gain,
    key_gain,
    out_grad,
):
    members, parts = lax.axis_size("mp"), lax.axis_size("dp")
    width = tokens.shape[1]
    query_width = w_query.shape[1]
    heads = query_width // HD
    ffn_width = w_gate.shape[1]
    share = members // KV
    group = lax.axis_index("mp") // share

    rows_one, projected, context, lse, grad_rows, attn_branch, h_two, cosine, sine = together(
        [
            Forward(
                tokens,
                out_grad,
                attn_gain,
                ffn_gain,
                query_gain,
                key_gain,
                w_query,
                w_key,
                w_value,
                w_output,
                positions,
                members,
            )
        ],
        members,
        parts,
        0,
        True,
    )
    rows_two, hidden, grad_gate, grad_up = together(
        [GatherFfn(h_two, grad_rows, w_gate, w_up, w_down, members)], members, parts, 5, False, 14
    )
    rows_two, tokens_late, w_key, w_value = after(rows_two, tokens, w_key, w_value)
    tokens_f = tokens_late.astype(F32)
    inv_one = lax.rsqrt(jnp.mean(tokens_f * tokens_f, -1, keepdims=True) + EPSILON)
    normed_one = tokens_f * inv_one
    key_cols = lax.dynamic_slice_in_dim(w_key, group * HD, HD, 1)
    value_cols = lax.dynamic_slice_in_dim(w_value, group * HD, HD, 1)
    w_attn = jnp.concatenate([w_query, key_cols, value_cols], 1)
    residual_mid = tokens_f + attn_branch
    inv_two = lax.rsqrt(jnp.mean(residual_mid * residual_mid, -1, keepdims=True) + EPSILON)
    normed_two = residual_mid * inv_two
    ffn_parts = (
        matmul_left_t(hidden, grad_rows).astype(BF16),
        matmul_left_t(rows_two, grad_gate).astype(BF16),
        matmul_left_t(rows_two, grad_up).astype(BF16),
    )
    ffn_parts, grad_gate, grad_up, hidden = lax.optimization_barrier((ffn_parts, grad_gate, grad_up, hidden))
    grad_w_down, grad_w_gate, grad_w_up = lax.psum(ffn_parts, "dp")

    grad_h_two = together(
        [ScatterAlone([(grad_gate, w_gate, True), (grad_up, w_up, True)], members)],
        members,
        parts,
        6,
        True,
    )[0]
    grad_ffn_gain = jnp.sum(grad_h_two * normed_two, 0)
    grad_mid = out_grad.astype(F32) + norm_back(grad_h_two, normed_two, inv_two, ffn_gain)
    ffn_branch, grad_attn_rows = together(
        [ScatterAlone([(hidden, w_down, False)], members, grad_mid.astype(BF16))],
        members,
        parts,
        2,
    )
    grad_context = matmul_right_t(grad_attn_rows, w_output).astype(BF16)
    output_part = matmul_left_t(context, grad_attn_rows).astype(BF16)
    grad_proj, gain_sums, grad_w_output = together(
        [
            AttendBack(
                projected, cosine, sine, query_gain, key_gain, positions, context, grad_context, lse, heads
            ),
            Across(output_part, parts, (False, True) if output_part.shape[0] % (32 * parts) == 0 else (False,)),
        ],
        members,
        parts,
        7,
    )
    grad_w_attn = matmul_left_t(rows_one, grad_proj)
    grad_attn_gain = jnp.sum(w_attn.astype(F32) * grad_w_attn, 1) / attn_gain

    small = jnp.concatenate(
        [
            grad_attn_gain,
            grad_ffn_gain,
            jnp.sum(gain_sums[0, :query_width].reshape(heads, HD), 0),
            gain_sums[0, query_width : query_width + HD],
            jnp.sum(tokens_f * tokens_f)[None],
        ]
    )
    unit = 16 * parts
    extra = -(-small.shape[0] // (unit * 2 * HD)) * unit
    small_rows = jnp.pad(small, (0, extra * 2 * HD - small.shape[0])).reshape(extra, 2 * HD)
    kv_part = jnp.concatenate([grad_w_attn[:, query_width:], small_rows], 0).astype(BF16)
    query_part = grad_w_attn[:, :query_width].astype(BF16)
    grad_w_key, grad_w_value, small_sum, grad_h_one, grad_w_query = together(
        [
            KeyValue(kv_part, width, members, parts),
            Scatter([(grad_proj, w_attn, True)], members),
            Across(query_part, parts, (False, True)),
        ],
        members,
        parts,
        3,
    )
    small_sum = small_sum.reshape(-1)
    entry_count = tokens.size * parts * members
    at = 2 * width
    residual_rms = jnp.sqrt(small_sum[at + 2 * HD : at + 2 * HD + 1] / entry_count)

    grad_w_gate, grad_w_up, grad_w_down = widen(grad_w_gate, grad_w_up, grad_w_down)
    grad_tokens = (grad_mid + norm_back(grad_h_one, normed_one, inv_one, attn_gain)).astype(BF16)
    output = (residual_mid + ffn_branch).astype(BF16)
    branch_rms = jnp.stack(
        [
            jnp.sqrt(jnp.mean(attn_branch * attn_branch, -1)),
            jnp.sqrt(jnp.mean(ffn_branch * ffn_branch, -1)),
        ]
    )
    return (
        output,
        grad_tokens,
        grad_w_query.astype(F32),
        grad_w_key.astype(F32),
        grad_w_value.astype(F32),
        grad_w_output.astype(F32),
        grad_w_gate,
        grad_w_up,
        grad_w_down,
        small_sum[:width],
        small_sum[width:at],
        small_sum[at : at + HD],
        small_sum[at + HD : at + 2 * HD],
        residual_rms,
        branch_rms,
    )


def solution(mesh):
    row, whole, column = P(("dp", "mp"), None), P(), P(None, "mp")
    lead = P("mp", None)
    return jax.shard_map(
        per_device,
        mesh=mesh,
        in_specs=(row, P("dp"), P("dp"), column, whole, whole, lead, column, column, lead)
        + (whole,) * 4
        + (row,),
        out_specs=(row, row, column, whole, whole, lead, column, column, lead)
        + (whole,) * 5
        + (P(None, ("dp", "mp")),),
        check_vma=False,
    )
```
